32 devices in a mesh: face: 4 (over z), row: 4 (over y, core), col: 2 (over x).
Axes of the slice: x: 2, y: 2, z: 4, core: 2. Of those that a mesh axis runs over, the one named last changes fastest.
Arguments:
- field: bfloat16 [12, 256, 256, 128], P('face', 'row', 'col'), may hold values from -6 to 6
- conv1_w: bfloat16 [3, 3, 128, 128], replicated, may hold values from -0.1875 to 0.1875
- conv1_b: float32 [128], replicated, may hold values from -3 to 3
- conv2_w: bfloat16 [3, 3, 128, 128], replicated, may hold values from -0.1875 to 0.1875
- conv2_b: float32 [128], replicated, may hold values from -3 to 3
- down_w: bfloat16 [2, 2, 128, 256], replicated, may hold values from -0.25 to 0.25
- down_b: float32 [256], replicated, may hold values from -3 to 3
- neighbour_face: int32 [12, 8], replicated, may hold values from 0 to 12, as said below
- orientation: int32 [12, 8], replicated, may hold values from 0 to 7, as said below
Outputs:
- skip: bfloat16 [12, 256, 256, 128], P('face', 'row', 'col')
- coarse: bfloat16 [12, 128, 128, 256], P('face', 'row', 'col')
The draws below stay inside these ranges and needn't reach their ends.
Inputs may be any that keep to these rules, and one draw needn't show every extreme that they name: `neighbour_face`: entries 0 to 3 of a row name the face across the top, right, bottom and left edge; entries 4 to 7 name the face diagonally across the top-left, top-right, bottom-right and bottom-left corner point, or 12 where only three faces meet there. Edge neighbours are mutual: if face f names face n across edge e, face n names f across the edge that orientation gives. `orientation`: entries 0 to 3 are 2 * e + r, where e is the neighbour's edge (0 top, 1 right, 2 bottom, 3 left) that meets this edge and r is 1 where positions along the two edges run opposite ways; entries 4 to 7 are the neighbour's corner (0 top-left, 1 top-right, 2 bottom-right, 3 bottom-left) that touches this corner, 0 where there is no such neighbour.
All inputs are finite; a program needn't handle non-finite values.
Results may differ from the reference program's by a relative error of at most 0.005.
Values may be sent and summed in bfloat16 or wider, within the bound.
No kernel may reach another device: no remote copies, remote signals or barrier semaphores. Data moves between devices by JAX's collectives and lax.ppermute only.
A program may use at most 128 MiB of HBM per device.

```python
import jax
import jax.numpy as jnp
import numpy as np
from jax import lax

FACES = 12
CH = 128
CO = 256
SIDE = 256


def dihedral_tables():
    normals = [(-1, 0), (0, 1), (1, 0), (0, -1)]
    alongs = [(0, 1), (1, 0), (0, 1), (1, 0)]
    points = [(-1, -1), (-1, 1), (1, 1), (1, -1)]
    edge_map = np.zeros((8, 4), np.int32)
    edge_rev = np.zeros((8, 4), np.int32)
    corner_map = np.zeros((8, 4), np.int32)
    for turning in range(8):

        def moved(vector):
            row_step, col_step = vector
            if turning >= 4:
                row_step, col_step = (col_step, row_step)
            for quarter in range(turning % 4):
                row_step, col_step = (col_step, -row_step)
            return (row_step, col_step)
        for which in range(4):
            target = normals.index(moved(normals[which]))
            edge_map[turning, which] = target
            edge_rev[turning, which] = int(moved(alongs[which]) != alongs[target])
            corner_map[turning, which] = points.index(moved(points[which]))
    edge_inverse = np.argsort(edge_map, axis=1).astype(np.int32)
    corner_inverse = np.argsort(corner_map, axis=1).astype(np.int32)
    return (edge_map, edge_rev, corner_map, edge_inverse, corner_inverse)


def base_links():
    edge_face = np.zeros((12, 4), np.int32)
    edge_side = np.zeros((12, 4), np.int32)
    corner_face = np.full((12, 4), 12, np.int32)
    corner_point = np.zeros((12, 4), np.int32)
    for which in range(4):
        following = (which + 1) % 4
        preceding = (which + 3) % 4
        opposite = (which + 2) % 4
        edge_face[which] = [following, 4 + following, 4 + which, preceding]
        edge_side[which] = [3, 3, 0, 0]
        edge_face[4 + which] = [which, 8 + which, 8 + preceding, preceding]
        edge_side[4 + which] = [2, 3, 0, 1]
        edge_face[8 + which] = [4 + following, 8 + following, 8 + preceding, 4 + which]
        edge_side[8 + which] = [2, 2, 1, 1]
        corner_face[which, 0] = opposite
        corner_point[which, 0] = 0
        corner_face[which, 2] = 8 + which
        corner_point[which, 2] = 0
        corner_face[4 + which, 1] = 4 + following
        corner_point[4 + which, 1] = 3
        corner_face[4 + which, 3] = 4 + preceding
        corner_point[4 + which, 3] = 1
        corner_face[8 + which, 0] = which
        corner_point[8 + which, 0] = 2
        corner_face[8 + which, 2] = 8 + opposite
        corner_point[8 + which, 2] = 2
    return (edge_face, edge_side, corner_face, corner_point)


def linked(key):
    edge_map, edge_rev, corner_map, edge_inverse, corner_inverse = [jnp.asarray(table) for table in dihedral_tables()]
    edge_face, edge_side, corner_face, corner_point = [jnp.asarray(table) for table in base_links()]
    placing = jax.random.permutation(jax.random.fold_in(key, 11), 12).astype(jnp.int32)
    turning = jax.random.randint(jax.random.fold_in(key, 12), (12,), 0, 8).astype(jnp.int32)
    slot_of = jnp.zeros((12,), jnp.int32).at[placing].set(jnp.arange(12, dtype=jnp.int32))
    sides = jnp.arange(4, dtype=jnp.int32)[None, :]
    own_turn = turning[:, None]
    base_face = placing[:, None]
    base_side = edge_inverse[own_turn, sides]
    far_base = edge_face[base_face, base_side]
    far_base_side = edge_side[base_face, base_side]
    far_slot = slot_of[far_base]
    far_turn = turning[far_slot]
    far_side = edge_map[far_turn, far_base_side]
    flipped = (edge_rev[own_turn, base_side] + edge_rev[far_turn, far_base_side]) % 2
    base_point = corner_inverse[own_turn, sides]
    corner_base = corner_face[base_face, base_point]
    present = corner_base < 12
    corner_slot = jnp.where(present, slot_of[jnp.minimum(corner_base, 11)], 12)
    corner_turn = turning[jnp.minimum(corner_slot, 11)]
    corner_code = jnp.where(present, corner_map[corner_turn, corner_point[base_face, base_point]], 0)
    faces = jnp.concatenate([far_slot, corner_slot], axis=1).astype(jnp.int32)
    codes = jnp.concatenate([2 * far_side + flipped, corner_code], axis=1).astype(jnp.int32)
    return (faces, codes)


def draw_neighbour_face(key, part):
    return linked(key)[0]


def draw_orientation(key, part):
    return linked(key)[1]


def levels(key, shape, shards, smallest, high):
    level, own = 1.0, jax.random.fold_in(key, 6)
    for dim, blocks in shards:
        draws = jnp.exp(jax.random.uniform(jax.random.fold_in(own, dim), (blocks,), jnp.float32, smallest / len(shards), high / len(shards)))
        level = level * jnp.repeat(draws, shape[dim] // blocks).reshape([-1 if axis == dim else 1 for axis in range(len(shape))])
    return level


def noise(rng, extent, spread, reach, pieces=(), kind=jnp.bfloat16):
    drawn = jax.random.normal(rng, extent, jnp.float32) * spread
    if len(pieces) > 0:
        drawn = levels(rng, extent, pieces, -0.22, 0.18) * drawn
    return jnp.clip(drawn, min=-reach, max=reach).astype(kind)


def setup_inputs(seed: int = 0) -> dict:
    arg_keys = jax.random.split(jax.random.key(seed), 10)
    return {
        "field": noise(arg_keys[0], (FACES, SIDE, SIDE, CH), 1.0, 6.0, ((0, 4), (1, 4), (2, 2))),
        "conv1_w": noise(arg_keys[1], (3, 3, CH, CH), (9 * CH) ** -0.5, 0.1875),
        "conv1_b": noise(arg_keys[2], (CH,), 0.5, 3.0, (), jnp.float32),
        "conv2_w": noise(arg_keys[3], (3, 3, CH, CH), (9 * CH) ** -0.5, 0.1875),
        "conv2_b": noise(arg_keys[4], (CH,), 0.5, 3.0, (), jnp.float32),
        "down_w": noise(arg_keys[5], (2, 2, CH, CO), (4 * CH) ** -0.5, 0.25),
        "down_b": noise(arg_keys[6], (CO,), 0.5, 3.0, (), jnp.float32),
        "neighbour_face": draw_neighbour_face(jax.random.fold_in(arg_keys[9], 71), 0),
        "orientation": draw_orientation(jax.random.fold_in(arg_keys[9], 71), 0),
    }


layout = ("NHWC", "HWIO", "NHWC")


def face_edges(values):
    return jnp.stack([values[:, 0], values[:, :, -1], values[:, -1], values[:, :, 0]], axis=1)


def seam_parts(edges, neighbours, codes):
    seam_faces = neighbours[:, :4]
    seam_codes = codes[:, :4]
    seams = edges[seam_faces, seam_codes // 2]
    seams = jnp.where((seam_codes % 2 == 1)[:, :, None, None], seams[:, :, ::-1], seams)
    corner_values = jnp.stack([edges[:, 0, 0], edges[:, 0, -1], edges[:, 2, -1], edges[:, 2, 0]], axis=1)
    corner_faces = neighbours[:, 4:]
    picked = corner_values[jnp.minimum(corner_faces, FACES - 1), codes[:, 4:]]
    picked = jnp.where((corner_faces < FACES)[:, :, None], picked, jnp.zeros_like(picked))
    return seams, picked


def surround(face_values, seams, corners):
    upper = jnp.concatenate([corners[0:1], seams[0], corners[1:2]], 0)
    lower = jnp.concatenate([corners[3:4], seams[2], corners[2:3]], 0)
    middle = jnp.concatenate([seams[3][:, None], face_values, seams[1][:, None]], 1)
    return jnp.concatenate([upper[None], middle, lower[None]], 0)


def convolve(padded, weight, bias):
    summed = lax.conv_general_dilated(padded, weight, (1, 1), "VALID", dimension_numbers=layout, preferred_element_type=jnp.float32)
    return jax.nn.gelu(summed + bias, approximate=False).astype(jnp.bfloat16)


def level(values, weight, bias, neighbours, codes):
    seams, corners = seam_parts(face_edges(values), neighbours, codes)

    def single(items):
        face_values, face_seams, face_corners = items
        return convolve(surround(face_values, face_seams, face_corners)[None], weight, bias)[0]

    return lax.map(single, (values, seams, corners))


def reference(field, conv1_w, conv1_b, conv2_w, conv2_b, down_w, down_b, neighbour_face, orientation):
    hidden = level(field, conv1_w, conv1_b, neighbour_face, orientation)
    skip = level(hidden, conv2_w, conv2_b, neighbour_face, orientation)

    def shrink(face_values):
        summed = lax.conv_general_dilated(face_values[None], down_w, (2, 2), "VALID", dimension_numbers=layout, preferred_element_type=jnp.float32)
        return (summed + down_b)[0].astype(jnp.bfloat16)

    coarse = lax.map(shrink, skip)
    return skip, coarse
```

```python
import functools

import jax
import jax.numpy as jnp
import numpy as np
from jax import lax
from jax.experimental import pallas as pl
from jax.experimental.pallas import tpu as pltpu
from jax.sharding import PartitionSpec as P

FACES = 12
BF = jnp.bfloat16
F32 = jnp.float32
STEP = 16
EXTRA = 16

layout = ("NHWC", "HWIO", "NHWC")


def padded_2(block, sides, width):
    for axis, dim in sides:
        count = lax.axis_size(axis)
        forward = [(i, i + 1) for i in range(count - 1)]
        backward = [(target, source) for source, target in forward]
        low = lax.ppermute(
            lax.slice_in_dim(block, block.shape[dim] - width, None, axis=dim), axis, forward
        )
        high = lax.ppermute(lax.slice_in_dim(block, 0, width, axis=dim), axis, backward)
        block = jnp.concatenate([low, block, high], axis=dim)
    return block


def seam_parts(edges, neighbours, codes):
    seam_faces = neighbours[:, :4]
    seam_codes = codes[:, :4]
    seams = edges[seam_faces, seam_codes // 2]
    seams = jnp.where((seam_codes % 2 == 1)[:, :, None, None], seams[:, :, ::-1], seams)
    corner_values = jnp.stack(
        [edges[:, 0, 0], edges[:, 0, -1], edges[:, 2, -1], edges[:, 2, 0]], axis=1
    )
    corner_faces = neighbours[:, 4:]
    picked = corner_values[jnp.minimum(corner_faces, FACES - 1), codes[:, 4:]]
    picked = jnp.where((corner_faces < FACES)[:, :, None], picked, jnp.zeros_like(picked))
    return (seams, picked)


def convolve(padded, weight, bias):
    summed = lax.conv_general_dilated(
        padded,
        weight,
        (1, 1),
        "VALID",
        dimension_numbers=layout,
        preferred_element_type=jnp.float32,
    )
    return jax.nn.gelu(summed + bias, approximate=False).astype(jnp.bfloat16)


def general_layer(block, weight, bias, neighbour_face, orientation):
    face_count, row_size, col_size, channels = block.shape
    row_total = lax.axis_size("row")
    col_total = lax.axis_size("col")
    row_place = lax.axis_index("row")
    col_place = lax.axis_index("col")
    face_side = row_size * row_total
    padded = padded_2(block, (("row", 1), ("col", 2)), 1)
    top_live = row_place == 0
    bottom_live = row_place == row_total - 1
    left_live = col_place == 0
    right_live = col_place == col_total - 1
    empty_line = jnp.zeros((face_count, face_side, channels), jnp.float32)

    def place(strip, offset, live):
        scaled = strip.astype(jnp.float32) * live.astype(jnp.float32)
        return lax.dynamic_update_slice_in_dim(empty_line, scaled, offset, 1)

    lines = jnp.stack(
        [
            place(block[:, 0], col_place * col_size, top_live),
            place(block[:, :, -1], row_place * row_size, right_live),
            place(block[:, -1], col_place * col_size, bottom_live),
            place(block[:, :, 0], row_place * row_size, left_live),
        ],
        axis=1,
    )
    complete = lax.psum(lax.psum(lines.astype(jnp.bfloat16), "col"), "row").astype(jnp.float32)
    every_edge = lax.all_gather(complete.astype(jnp.bfloat16), "face", axis=0, tiled=True)
    first_face = lax.axis_index("face") * face_count
    own_faces = lax.dynamic_slice_in_dim(neighbour_face, first_face, face_count, 0)
    own_codes = lax.dynamic_slice_in_dim(orientation, first_face, face_count, 0)
    seams, corners = seam_parts(every_edge, own_faces, own_codes)
    upper = jnp.concatenate([corners[:, 0:1], seams[:, 0], corners[:, 1:2]], 1)
    lower = jnp.concatenate([corners[:, 3:4], seams[:, 2], corners[:, 2:3]], 1)
    leftward = jnp.concatenate([corners[:, 0:1], seams[:, 3], corners[:, 3:4]], 1)
    rightward = jnp.concatenate([corners[:, 1:2], seams[:, 1], corners[:, 2:3]], 1)
    upper_cut = lax.dynamic_slice_in_dim(upper, col_place * col_size, col_size + 2, 1)
    lower_cut = lax.dynamic_slice_in_dim(lower, col_place * col_size, col_size + 2, 1)
    left_cut = lax.dynamic_slice_in_dim(leftward, row_place * row_size, row_size + 2, 1)
    right_cut = lax.dynamic_slice_in_dim(rightward, row_place * row_size, row_size + 2, 1)
    padded = padded.at[:, 0].set(jnp.where(top_live, upper_cut, padded[:, 0]))
    padded = padded.at[:, -1].set(jnp.where(bottom_live, lower_cut, padded[:, -1]))
    padded = padded.at[:, :, 0].set(jnp.where(left_live, left_cut, padded[:, :, 0]))
    padded = padded.at[:, :, -1].set(jnp.where(right_live, right_cut, padded[:, :, -1]))
    return convolve(padded, weight, bias)


def general_device(
    field, conv1_w, conv1_b, conv2_w, conv2_b, down_w, down_b, neighbour_face, orientation
):
    hidden = general_layer(field, conv1_w, conv1_b, neighbour_face, orientation)
    skip = general_layer(hidden, conv2_w, conv2_b, neighbour_face, orientation)
    summed = lax.conv_general_dilated(
        skip, down_w, (2, 2), "VALID", dimension_numbers=layout, preferred_element_type=jnp.float32
    )
    coarse = (summed + down_b).astype(jnp.bfloat16)
    return (skip, coarse)


def gelu(v):
    return 0.5 * v * (1.0 + lax.erf(v * np.float32(np.sqrt(0.5))))


def shifted(v, before, after):
    n = v.shape[0]
    spot = lax.broadcasted_iota(jnp.int32, (n, 1), 0)
    low = jnp.where(spot == 0, before, pltpu.roll(v, 1, 0))
    high = jnp.where(spot == n - 1, after, pltpu.roll(v, n - 1, 0))
    return low.astype(BF), v.astype(BF), high.astype(BF)


def conv_kernel(x_ref, next_ref, w_ref, b_ref, *refs):
    o_ref, taps, w_low, w_high = refs[-4:]
    rows, cols, ch = x_ref.shape[1:]
    pairs = rows // 2
    step = pl.program_id(1)
    zero_row = jnp.zeros((1, ch), F32)
    half = 3 * ch

    @pl.when((pl.program_id(0) == 0) & (step == 0))
    def _():
        zero = jnp.zeros((ch, ch), BF)
        for d in range(3):
            first = slice(d * ch, (d + 1) * ch)
            second = slice(half + d * ch, half + (d + 1) * ch)
            w_low[first, :ch] = w_ref[0, d]
            w_low[first, ch:] = zero
            w_low[second, :ch] = w_ref[1, d]
            w_low[second, ch:] = w_ref[0, d]
            w_high[first, :ch] = w_ref[2, d]
            w_high[first, ch:] = w_ref[1, d]
            w_high[second, :ch] = zero
            w_high[second, ch:] = w_ref[2, d]

    def put(v, pair, side):
        low, same, high = shifted(v.astype(F32), zero_row, zero_row)
        start = side * half
        taps[pair, :, start : start + ch] = low
        taps[pair, :, start + ch : start + 2 * ch] = same
        taps[pair, :, start + 2 * ch : start + 3 * ch] = high

    @pl.when(step == 0)
    def _():
        taps[0, :, :half] = jnp.zeros((cols, half), BF)
        put(x_ref[0, 0], 0, 1)

    @pl.when(step > 0)
    def _():
        taps[0] = taps[pairs]

    for pair in range(1, pairs + 1):
        put(x_ref[0, 2 * pair - 1], pair, 0)
        if pair < pairs:
            put(x_ref[0, 2 * pair], pair, 1)
    last = (step == pl.num_programs(1) - 1).astype(F32)
    put(next_ref[0, 0].astype(F32) * (1.0 - last), pairs, 1)

    lower = taps[pl.ds(0, pairs)].reshape(pairs * cols, 2 * half)
    upper = taps[pl.ds(1, pairs)].reshape(pairs * cols, 2 * half)
    total = jnp.dot(lower, w_low[...], preferred_element_type=F32)
    total += jnp.dot(upper, w_high[...], preferred_element_type=F32)
    total = total.reshape(pairs, cols, 2 * ch)
    bias = b_ref[...]
    for side in range(2):
        out = gelu(total[:, :, side * ch : (side + 1) * ch] + bias[None]).astype(BF)
        for pair in range(pairs):
            o_ref[0, 2 * pair + side] = out[pair]


def in_hbm(x):
    return pltpu.with_memory_space_constraint(x, pltpu.HBM)


def conv_faces(x, weight, bias, first, count, into=None):
    faces, rows, cols, ch = x.shape
    steps = rows // STEP
    in_specs = [
        pl.BlockSpec((1, STEP, cols, ch), lambda f, s: (first + f, s, 0, 0)),
        pl.BlockSpec(
            (1, 1, cols, ch), lambda f, s: (first + f, jnp.minimum((s + 1) * STEP, rows - 1), 0, 0)
        ),
        pl.BlockSpec(weight.shape, lambda f, s: (0, 0, 0, 0)),
        pl.BlockSpec((1, ch), lambda f, s: (0, 0)),
    ]
    args = [in_hbm(x), in_hbm(x), weight, bias]
    aliases = {}
    if into is not None:
        in_specs.append(pl.BlockSpec(memory_space=pltpu.HBM))
        args.append(into)
        aliases = {4: 0}
    pixels = count * rows * cols
    return pl.pallas_call(
        conv_kernel,
        grid=(count, steps),
        in_specs=in_specs,
        out_specs=pl.BlockSpec((1, STEP, cols, ch), lambda f, s: (first + f, s, 0, 0)),
        out_shape=pltpu.HBM(x.shape, BF),
        scratch_shapes=[
            pltpu.VMEM((STEP // 2 + 1, cols, 6 * ch), BF),
            pltpu.VMEM((6 * ch, 2 * ch), BF),
            pltpu.VMEM((6 * ch, 2 * ch), BF),
        ],
        input_output_aliases=aliases,
        cost_estimate=pl.CostEstimate(
            flops=pixels * ch * ch * 24, bytes_accessed=4 * pixels * ch, transcendentals=0
        ),
        compiler_params=pltpu.CompilerParams(vmem_limit_bytes=14 * 2**20),
        name="conv_faces",
    )(*args)


def column(tile, place):
    return tile[pl.ds(place, tile.shape[0] // STEP, stride=STEP), :]


def put_strips(i, r, c, lines, top, bottom, u_ref, v_ref, turn_ref, line_ref):
    left, left_in, right_in, right = lines
    size = left.shape[0]
    for place, value in enumerate(lines):
        line_ref[i, place] = value.astype(BF)
    side = jnp.where(c == 0, left, right).astype(BF)
    inner = jnp.where(c == 0, right, left).astype(BF)
    even = lax.rem(r, 2) == 0
    line = jnp.where(even, top, bottom).astype(BF)
    turn_ref[i] = jnp.where(even, bottom, top).astype(BF)
    for ref in (u_ref, v_ref):
        ref[i, 0] = side
        ref[i, 1] = line[:size]
        ref[i, 2] = line[size:]
    u_ref[i, 3] = inner


def strip_shapes(faces, rows, cols, ch):
    return (
        jax.ShapeDtypeStruct((faces, 4, rows, ch), BF),
        jax.ShapeDtypeStruct((faces, 3, rows, ch), BF),
        jax.ShapeDtypeStruct((faces, cols, ch), BF),
        jax.ShapeDtypeStruct((faces, 4, rows, ch), BF),
    )


def whole(shape):
    return pl.BlockSpec(shape, lambda *_: (0,) * len(shape))


def tile_copies(array, tiles, sems, back=False):
    cols = array.shape[2]
    out = []
    for side, start in enumerate((0, cols - STEP)):
        far, near = array.at[:, :, pl.ds(start, STEP), :], tiles.at[side]
        out.append(pltpu.make_async_copy(*((near, far) if back else (far, near)), sems.at[side]))
    return out


def strips_kernel(x_ref, u_ref, v_ref, turn_ref, line_ref, tiles, outer, left, right, sems):
    faces, rows, cols, ch = x_ref.shape
    r, c = lax.axis_index("row"), lax.axis_index("col")
    copies = tile_copies(x_ref, tiles, sems)
    for k, row in enumerate((0, rows - 1)):
        copies.append(pltpu.make_async_copy(x_ref.at[:, row], outer.at[k], sems.at[2 + k]))
    for copy in copies:
        copy.start()
    for copy in copies:
        copy.wait()

    def face(i, carry):
        left[...] = tiles[0, i].astype(F32).reshape(rows * STEP, ch)
        right[...] = tiles[1, i].astype(F32).reshape(rows * STEP, ch)
        lines = (column(left, 0), column(left, 1), column(right, STEP - 2), column(right, STEP - 1))
        put_strips(
            i, r, c, lines, outer[0, i].astype(F32), outer[1, i].astype(F32),
            u_ref, v_ref, turn_ref, line_ref,
        )
        return carry

    lax.fori_loop(0, faces, face, 0)


def strips_of(x):
    faces, rows, cols, ch = x.shape
    shapes = strip_shapes(faces, rows, cols, ch)
    return pl.pallas_call(
        strips_kernel,
        grid=(1,),
        in_specs=[pl.BlockSpec(memory_space=pltpu.HBM)],
        out_specs=tuple(whole(s.shape) for s in shapes),
        out_shape=shapes,
        scratch_shapes=[
            pltpu.VMEM((2, faces, rows, STEP, ch), BF),
            pltpu.VMEM((2, faces, cols, ch), BF),
            pltpu.VMEM((rows * STEP, ch), F32),
            pltpu.VMEM((rows * STEP, ch), F32),
            pltpu.SemaphoreType.DMA((4,)),
        ],
        cost_estimate=pl.CostEstimate(flops=0, bytes_accessed=4 * 2**20, transcendentals=0),
        compiler_params=pltpu.CompilerParams(vmem_limit_bytes=10 * 2**20),
        name="strips_of",
    )(in_hbm(x))


def select_kernel(near_ref, code_ref, *refs):
    stores, outs, (held, sems) = refs[:8], refs[8:-2], refs[-2:]
    faces, _, size, ch = held.shape[1:]
    me, r, c = lax.axis_index("face"), lax.axis_index("row"), lax.axis_index("col")
    copies = [
        pltpu.make_async_copy(store.at[:, pl.ds(0, 3)], held.at[k], sems.at[k])
        for k, store in enumerate(stores)
    ]
    for copy in copies:
        copy.start()
    for copy in copies:
        copy.wait()

    def slot(row, col):
        return ((r ^ row) << 1) | (c ^ col)

    def quarter(edge, q):
        upright = lax.rem(edge, 2) == 1
        row = jnp.where(upright, q, jnp.where(edge == 0, 0, 3))
        col = jnp.where(upright, jnp.where(edge == 3, 0, 1), q >> 1)
        return slot(row, col), jnp.where(upright, 0, 1 + (q & 1))

    def end(n, where, block, last):
        head = held[where, n, block, 0:EXTRA].astype(F32)
        tail = held[where, n, block, size - EXTRA : size].astype(F32)
        return jnp.where(last, tail[EXTRA - 1 : EXTRA], head[0:1])

    spot = lax.broadcasted_iota(jnp.int32, (EXTRA, 1), 0)
    for k, out in enumerate(outs):
        target = me ^ k

        def face(i, carry, out=out, target=target):
            f = target * faces + i
            edge = 3 - 2 * c
            code = code_ref[f, edge]
            far, flip = code >> 1, code & 1
            n = lax.rem(near_ref[f, edge], faces)
            where, block = quarter(far, jnp.where(flip == 1, 3 - r, r))
            out[i, 0:size] = held[where, n, block]
            corner = jnp.where(r < 2, c, 3 - c)
            tip = code_ref[f, 4 + corner]
            tip_n = lax.rem(near_ref[f, 4 + corner], faces)
            tip_row = jnp.where(tip < 2, 0, 3)
            tip_col = jnp.where((tip == 1) | (tip == 2), 1, 0)
            tip_pixel = end(tip_n, slot(tip_row, tip_col), 0, tip_row == 3)
            q = jnp.where(flip == 1, 4 - r, r - 1)
            where, block = quarter(far, jnp.clip(q, 0, 3))
            before = jnp.where(r == 0, tip_pixel, end(n, where, block, flip == 0))
            q = jnp.where(flip == 1, 2 - r, r + 1)
            where, block = quarter(far, jnp.clip(q, 0, 3))
            after = jnp.where(r == 3, tip_pixel, end(n, where, block, flip == 1))

            edge = jnp.where(r < 2, 0, 2)
            code = code_ref[f, edge]
            far, flip = code >> 1, code & 1
            n = lax.rem(near_ref[f, edge], faces)
            part = c ^ flip
            for h in range(2):
                where, block = quarter(far, 2 * part + h)
                out[i, (1 + h) * size : (2 + h) * size] = held[where, n, block]
            where, block = quarter(far, jnp.where(part == 0, 2, 1))
            middle = end(n, where, block, part == 1)
            single = jnp.where(spot == 0, before, jnp.where(spot == 1, after, middle))
            out[i, 3 * size : 3 * size + EXTRA] = single.astype(BF)
            return carry

        lax.fori_loop(0, faces, face, 0)


def select_strips(neighbour_face, orientation, stores, groups):
    faces, _, size, ch = stores[0].shape
    shape = jax.ShapeDtypeStruct((faces, 3 * size + EXTRA, ch), BF)
    smem = pl.BlockSpec(memory_space=pltpu.SMEM)
    return pl.pallas_call(
        select_kernel,
        grid=(1,),
        in_specs=[smem, smem] + [pl.BlockSpec(memory_space=pl.ANY)] * 8,
        out_specs=tuple(whole(shape.shape) for _ in range(groups)),
        out_shape=(shape,) * groups,
        scratch_shapes=[
            pltpu.VMEM((8, faces, 3, size, ch), BF),
            pltpu.SemaphoreType.DMA((8,)),
        ],
        cost_estimate=pl.CostEstimate(flops=0, bytes_accessed=4 * 2**20, transcendentals=0),
        compiler_params=pltpu.CompilerParams(vmem_limit_bytes=10 * 2**20),
        name="select_strips",
    )(neighbour_face, orientation, *stores)


def ring_kernel(near_ref, code_ref, x_ref, line_in, y_in, beside, diagonal, across, far_diagonal,
                turned, w_ref, b_ref, *refs, groups, more):
    seams = refs[:groups]
    y_ref = refs[groups]
    outs = refs[groups + 1 : groups + 1 + 4 * more]
    tiles, inside, edge_rows, edge_cols, held, left, right, w_cols, sems = refs[
        groups + 1 + 4 * more :
    ]
    faces, rows, cols, ch = x_ref.shape
    me, r, c = lax.axis_index("face"), lax.axis_index("row"), lax.axis_index("col")
    copies = tile_copies(y_in, tiles, sems)
    for k, row in enumerate((0, 1, rows - 2, rows - 1)):
        copies.append(pltpu.make_async_copy(x_ref.at[:, row], inside.at[k], sems.at[2 + k]))
    for k in range(groups):
        copies.append(pltpu.make_async_copy(seams[k], held.at[k], sems.at[6 + k]))
    for copy in copies:
        copy.start()
    for copy in copies:
        copy.wait()

    def oriented(v, flip):
        n = v.shape[0]
        to = lax.broadcasted_iota(jnp.int32, (n, n), 0)
        source = lax.broadcasted_iota(jnp.int32, (n, n), 1)
        order = jnp.where(source == jnp.where(flip == 1, n - 1 - to, to), 1.0, 0.0).astype(BF)
        return jnp.dot(order, v, preferred_element_type=F32)

    even = lax.rem(r, 2) == 0
    outer = (r == 0) | (r == 3)
    w_rows = w_ref[...].reshape(9 * ch, ch)
    for d in range(3):
        for a in range(3):
            w_cols[(3 * d + a) * ch : (3 * d + a + 1) * ch] = w_ref[a, d]
    bias = b_ref[...]

    def holder(n):
        return jnp.minimum(n, FACES - 1) // faces ^ me

    def face(i, carry):
        f = me * faces + i
        edge = 3 - 2 * c
        n = near_ref[f, edge]
        corner = jnp.where(r < 2, c, 3 - c)
        tip_n = near_ref[f, 4 + corner]
        seam_side = oriented(held[holder(n), i, 0:rows], code_ref[f, edge] & 1)
        extra = slice(3 * rows, 3 * rows + EXTRA)
        n_before = jnp.where(r == 0, tip_n, n)
        n_after = jnp.where(r == 3, tip_n, n)
        before = held[holder(n_before), i, extra].astype(F32)[0:1]
        after = held[holder(n_after), i, extra].astype(F32)[1:2]
        before = jnp.where(n_before < FACES, before, 0.0)
        after = jnp.where(n_after < FACES, after, 0.0)
        edge = jnp.where(r < 2, 0, 2)
        n = near_ref[f, edge]
        seam_line = oriented(held[holder(n), i, rows : 3 * rows], code_ref[f, edge] & 1)
        middle = held[holder(n), i, extra].astype(F32)[2:3]

        inner = beside[i, 3].astype(F32)
        block_line = jnp.concatenate([across[i, 1], across[i, 2]], axis=0).astype(F32)
        outward = jnp.where(outer, seam_line, block_line)
        inward = turned[i].astype(F32)
        top = jnp.where(even, outward, inward)
        bottom = jnp.where(even, inward, outward)
        lft = jnp.where(c == 0, seam_side, inner)
        rgt = jnp.where(c == 0, inner, seam_side)
        pair_inner = diagonal[i, 3].astype(F32)
        inward_corner = jnp.where(even, pair_inner[0:1], pair_inner[rows - 1 : rows])
        far_first = far_diagonal[i, 1].astype(F32)[0:1]
        far_last = far_diagonal[i, 2].astype(F32)[rows - 1 : rows]
        outward_corner = jnp.where(outer, middle, jnp.where(c == 0, far_first, far_last))
        inner_top = jnp.where(even, outward_corner, inward_corner)
        inner_bottom = jnp.where(even, inward_corner, outward_corner)
        top_left = jnp.where(c == 0, before, inner_top)
        top_right = jnp.where(c == 0, inner_top, before)
        bottom_left = jnp.where(c == 0, after, inner_bottom)
        bottom_right = jnp.where(c == 0, inner_bottom, after)

        row_0, row_1, row_2, row_3 = (inside[k, i].astype(F32) for k in range(4))
        upper = (
            shifted(top, top_left, top_right)
            + shifted(row_0, lft[0:1], rgt[0:1])
            + shifted(row_1, lft[1:2], rgt[1:2])
        )
        lower = (
            shifted(row_2, lft[rows - 2 : rows - 1], rgt[rows - 2 : rows - 1])
            + shifted(row_3, lft[rows - 1 : rows], rgt[rows - 1 : rows])
            + shifted(bottom, bottom_left, bottom_right)
        )
        both = jnp.concatenate(
            [jnp.concatenate(upper, axis=1), jnp.concatenate(lower, axis=1)], axis=0
        )
        out_rows = gelu(jnp.dot(both, w_rows, preferred_element_type=F32) + bias)
        col_0, col_1, col_2, col_3 = (line_in[i, k].astype(F32) for k in range(4))
        upper = (
            shifted(lft, top_left, bottom_left)
            + shifted(col_0, top[0:1], bottom[0:1])
            + shifted(col_1, top[1:2], bottom[1:2])
        )
        lower = (
            shifted(col_2, top[cols - 2 : cols - 1], bottom[cols - 2 : cols - 1])
            + shifted(col_3, top[cols - 1 : cols], bottom[cols - 1 : cols])
            + shifted(rgt, top_right, bottom_right)
        )
        both = jnp.concatenate(
            [jnp.concatenate(upper, axis=1), jnp.concatenate(lower, axis=1)], axis=0
        )
        out_cols = gelu(jnp.dot(both, w_cols[...], preferred_element_type=F32) + bias)

        edge_rows[0, i] = out_rows[:cols].astype(BF)
        edge_rows[1, i] = out_rows[cols:].astype(BF)
        edge_cols[i] = out_cols
        return carry

    def update(i, carry):
        new_top, new_bottom = edge_rows[0, i].astype(F32), edge_rows[1, i].astype(F32)
        for tile, side, place in ((left, 0, 0), (right, 1, STEP - 1)):
            start = side * (cols - STEP)
            tiles[side, i, 0] = edge_rows[0, i, start : start + STEP]
            tiles[side, i, rows - 1] = edge_rows[1, i, start : start + STEP]
            tile[...] = tiles[side, i].astype(F32).reshape(rows * STEP, ch)
            tile[pl.ds(place, rows, stride=STEP), :] = edge_cols[i, pl.ds(side * rows, rows)]
            tiles[side, i] = tile[...].astype(BF).reshape(rows, STEP, ch)
        if more:
            lines = (
                column(left, 0), column(left, 1),
                column(right, STEP - 2), column(right, STEP - 1),
            )
            put_strips(i, r, c, lines, new_top, new_bottom, *outs)
        return carry

    lax.fori_loop(0, faces, face, 0)
    lax.fori_loop(0, faces, update, 0)
    copies = tile_copies(y_ref, tiles, sems, back=True)
    between = pl.ds(STEP, cols - 2 * STEP)
    if cols > 2 * STEP:
        for k, row in enumerate((0, rows - 1)):
            copies.append(
                pltpu.make_async_copy(
                    edge_rows.at[k, :, between], y_ref.at[:, row, between], sems.at[2 + k]
                )
            )
    for copy in copies:
        copy.start()
    for copy in copies:
        copy.wait()


def ring(neighbour_face, orientation, x, lines, y, parts, weight, bias, seams, more):
    faces, rows, cols, ch = x.shape
    groups = len(seams)
    beside, diagonal, across, far_diagonal, turned = parts
    smem = pl.BlockSpec(memory_space=pltpu.SMEM)
    hbm = pl.BlockSpec(memory_space=pltpu.HBM)
    anywhere = pl.BlockSpec(memory_space=pl.ANY)
    strips = strip_shapes(faces, rows, cols, ch) if more else ()
    x, y = in_hbm(x), in_hbm(y)
    args = (neighbour_face, orientation, x, lines, y, beside, diagonal, across, far_diagonal, turned,
            weight, bias) + tuple(seams)
    in_specs = [smem, smem, hbm, whole(lines.shape), hbm]
    in_specs += [whole(a.shape) for a in args[5:12]] + [anywhere] * groups
    out = pl.pallas_call(
        functools.partial(ring_kernel, groups=groups, more=int(more)),
        grid=(1,),
        in_specs=in_specs,
        out_specs=(hbm,) + tuple(whole(s.shape) for s in strips),
        out_shape=(pltpu.HBM(y.shape, BF),) + tuple(strips),
        scratch_shapes=[
            pltpu.VMEM((2, faces, rows, STEP, ch), BF),
            pltpu.VMEM((4, faces, cols, ch), BF),
            pltpu.VMEM((2, faces, cols, ch), BF),
            pltpu.VMEM((faces, 2 * rows, ch), F32),
            pltpu.VMEM((groups, faces, 3 * rows + EXTRA, ch), BF),
            pltpu.VMEM((rows * STEP, ch), F32),
            pltpu.VMEM((rows * STEP, ch), F32),
            pltpu.VMEM((9 * ch, ch), BF),
            pltpu.SemaphoreType.DMA((6 + groups,)),
        ],
        input_output_aliases={4: 0},
        cost_estimate=pl.CostEstimate(
            flops=faces * (rows + cols) * 36 * ch * ch, bytes_accessed=8 * 2**20, transcendentals=0
        ),
        compiler_params=pltpu.CompilerParams(vmem_limit_bytes=14 * 2**20),
        name="ring",
    )(*args)
    return out


def down_kernel(x_ref, w_ref, b_ref, o_ref, wide):
    rows, cols, ch = x_ref.shape[1:]
    wide[...] = x_ref[0].astype(F32).reshape(rows * cols, ch)
    half = cols // 2
    even = wide[pl.ds(0, rows * half, stride=2), :].astype(BF).reshape(rows // 2, 2, half, ch)
    odd = wide[pl.ds(1, rows * half, stride=2), :].astype(BF).reshape(rows // 2, 2, half, ch)
    taps = jnp.concatenate([even[:, 0], odd[:, 0], even[:, 1], odd[:, 1]], axis=-1)
    taps = taps.reshape(rows // 2 * half, 4 * ch)
    out = jnp.dot(taps, w_ref[...].reshape(4 * ch, -1), preferred_element_type=F32) + b_ref[...]
    o_ref[0] = out.astype(BF).reshape(rows // 2, half, -1)


def downsample(x, weight, bias):
    faces, rows, cols, ch = x.shape
    co = weight.shape[-1]
    return pl.pallas_call(
        down_kernel,
        grid=(faces, rows // STEP),
        in_specs=[
            pl.BlockSpec((1, STEP, cols, ch), lambda f, s: (f, s, 0, 0)),
            whole(weight.shape),
            whole(bias.shape),
        ],
        out_specs=pl.BlockSpec((1, STEP // 2, cols // 2, co), lambda f, s: (f, s, 0, 0)),
        out_shape=jax.ShapeDtypeStruct((faces, rows // 2, cols // 2, co), BF),
        scratch_shapes=[pltpu.VMEM((STEP * cols, ch), F32)],
        cost_estimate=pl.CostEstimate(
            flops=faces * rows * cols * 2 * ch * co,
            bytes_accessed=4 * faces * rows * cols * ch,
            transcendentals=0,
        ),
        compiler_params=pltpu.CompilerParams(vmem_limit_bytes=14 * 2**20),
        name="downsample",
    )(in_hbm(x), weight, bias)


def blocks(change_row, change_col):
    cols = lax.axis_size("col")
    return [
        (r * cols + c, (r ^ change_row) * cols + (c ^ change_col))
        for r in range(lax.axis_size("row"))
        for c in range(cols)
    ]


def swap(v, change_row, change_col):
    return lax.ppermute(v, ("row", "col"), blocks(change_row, change_col))


def exchange(neighbour_face, orientation, strips):
    u, v, turn, _ = strips
    groups = lax.axis_size("face")
    beside = swap(u, 0, 1)
    across = swap(v, 3, 0)
    diagonal = swap(v, 3, 1)
    pair, turned = swap(v, 1, 0), swap(turn, 1, 0)
    pair_beside, pair_across, pair_diagonal = (swap(a, 1, 0) for a in (beside, across, diagonal))
    stores = (v, beside, pair, pair_beside, pair_across, pair_diagonal, across, diagonal)
    picked = select_strips(neighbour_face, orientation, stores, groups)
    seams = (picked[0],) + tuple(
        lax.ppermute(picked[k], "face", [(g, g ^ k) for g in range(groups)])
        for k in range(1, groups)
    )
    return (beside, pair_beside, across, diagonal, turned), seams


def conv_block(x, weight, bias):
    y = None
    for f in range(x.shape[0]):
        y = conv_faces(x, weight, bias, f, 1, y)
    return y


def per_device(
    field, conv1_w, conv1_b, conv2_w, conv2_b, down_w, down_b, neighbour_face, orientation
):
    conv1_b, conv2_b, down_b = conv1_b[None], conv2_b[None], down_b[None]
    tables = (neighbour_face, orientation)
    strips = strips_of(field)
    parts, seams = exchange(*tables, strips)
    hidden = conv_block(field, conv1_w, conv1_b)
    hidden, *strips_2 = ring(
        *tables, field, strips[3], hidden, parts, conv1_w, conv1_b, seams, True
    )
    parts, seams = exchange(*tables, strips_2)
    skip = conv_block(hidden, conv2_w, conv2_b)
    (skip,) = ring(
        *tables, hidden, strips_2[3], skip, parts, conv2_w, conv2_b, seams, False
    )
    return skip, downsample(skip, down_w, down_b)


def solution(mesh):
    groups = mesh.shape["face"]
    fast = mesh.shape["row"] == 4 and mesh.shape["col"] == 2 and groups & (groups - 1) == 0
    return jax.shard_map(
        per_device if fast else general_device,
        mesh=mesh,
        in_specs=(P("face", "row", "col", None), P(), P(), P(), P(), P(), P(), P(), P()),
        out_specs=(P("face", "row", "col", None), P("face", "row", "col", None)),
        check_vma=False,
    )
```

```python
import functools

import jax
import jax.numpy as jnp
import numpy as np
from jax import lax
from jax.experimental import pallas as pl
from jax.experimental.pallas import tpu as pltpu
from jax.sharding import PartitionSpec as P

FACES = 12
BF = jnp.bfloat16
F32 = jnp.float32
STEP = 16
EXTRA = 16

layout = ("NHWC", "HWIO", "NHWC")


def padded_2(block, sides, width):
    for axis, dim in sides:
        count = lax.axis_size(axis)
        forward = [(i, i + 1) for i in range(count - 1)]
        backward = [(target, source) for source, target in forward]
        low = lax.ppermute(
            lax.slice_in_dim(block, block.shape[dim] - width, None, axis=dim), axis, forward
        )
        high = lax.ppermute(lax.slice_in_dim(block, 0, width, axis=dim), axis, backward)
        block = jnp.concatenate([low, block, high], axis=dim)
    return block


def seam_parts(edges, neighbours, codes):
    seam_faces = neighbours[:, :4]
    seam_codes = codes[:, :4]
    seams = edges[seam_faces, seam_codes // 2]
    seams = jnp.where((seam_codes % 2 == 1)[:, :, None, None], seams[:, :, ::-1], seams)
    corner_values = jnp.stack(
        [edges[:, 0, 0], edges[:, 0, -1], edges[:, 2, -1], edges[:, 2, 0]], axis=1
    )
    corner_faces = neighbours[:, 4:]
    picked = corner_values[jnp.minimum(corner_faces, FACES - 1), codes[:, 4:]]
    picked = jnp.where((corner_faces < FACES)[:, :, None], picked, jnp.zeros_like(picked))
    return (seams, picked)


def convolve(padded, weight, bias):
    summed = lax.conv_general_dilated(
        padded,
        weight,
        (1, 1),
        "VALID",
        dimension_numbers=layout,
        preferred_element_type=jnp.float32,
    )
    return jax.nn.gelu(summed + bias, approximate=False).astype(jnp.bfloat16)


def general_layer(block, weight, bias, neighbour_face, orientation):
    face_count, row_size, col_size, channels = block.shape
    row_total = lax.axis_size("row")
    col_total = lax.axis_size("col")
    row_place = lax.axis_index("row")
    col_place = lax.axis_index("col")
    face_side = row_size * row_total
    padded = padded_2(block, (("row", 1), ("col", 2)), 1)
    top_live = row_place == 0
    bottom_live = row_place == row_total - 1
    left_live = col_place == 0
    right_live = col_place == col_total - 1
    empty_line = jnp.zeros((face_count, face_side, channels), jnp.float32)

    def place(strip, offset, live):
        scaled = strip.astype(jnp.float32) * live.astype(jnp.float32)
        return lax.dynamic_update_slice_in_dim(empty_line, scaled, offset, 1)

    lines = jnp.stack(
        [
            place(block[:, 0], col_place * col_size, top_live),
            place(block[:, :, -1], row_place * row_size, right_live),
            place(block[:, -1], col_place * col_size, bottom_live),
            place(block[:, :, 0], row_place * row_size, left_live),
        ],
        axis=1,
    )
    complete = lax.psum(lax.psum(lines.astype(jnp.bfloat16), "col"), "row").astype(jnp.float32)
    every_edge = lax.all_gather(complete.astype(jnp.bfloat16), "face", axis=0, tiled=True)
    first_face = lax.axis_index("face") * face_count
    own_faces = lax.dynamic_slice_in_dim(neighbour_face, first_face, face_count, 0)
    own_codes = lax.dynamic_slice_in_dim(orientation, first_face, face_count, 0)
    seams, corners = seam_parts(every_edge, own_faces, own_codes)
    upper = jnp.concatenate([corners[:, 0:1], seams[:, 0], corners[:, 1:2]], 1)
    lower = jnp.concatenate([corners[:, 3:4], seams[:, 2], corners[:, 2:3]], 1)
    leftward = jnp.concatenate([corners[:, 0:1], seams[:, 3], corners[:, 3:4]], 1)
    rightward = jnp.concatenate([corners[:, 1:2], seams[:, 1], corners[:, 2:3]], 1)
    upper_cut = lax.dynamic_slice_in_dim(upper, col_place * col_size, col_size + 2, 1)
    lower_cut = lax.dynamic_slice_in_dim(lower, col_place * col_size, col_size + 2, 1)
    left_cut = lax.dynamic_slice_in_dim(leftward, row_place * row_size, row_size + 2, 1)
    right_cut = lax.dynamic_slice_in_dim(rightward, row_place * row_size, row_size + 2, 1)
    padded = padded.at[:, 0].set(jnp.where(top_live, upper_cut, padded[:, 0]))
    padded = padded.at[:, -1].set(jnp.where(bottom_live, lower_cut, padded[:, -1]))
    padded = padded.at[:, :, 0].set(jnp.where(left_live, left_cut, padded[:, :, 0]))
    padded = padded.at[:, :, -1].set(jnp.where(right_live, right_cut, padded[:, :, -1]))
    return convolve(padded, weight, bias)


def general_device(
    field, conv1_w, conv1_b, conv2_w, conv2_b, down_w, down_b, neighbour_face, orientation
):
    hidden = general_layer(field, conv1_w, conv1_b, neighbour_face, orientation)
    skip = general_layer(hidden, conv2_w, conv2_b, neighbour_face, orientation)
    summed = lax.conv_general_dilated(
        skip, down_w, (2, 2), "VALID", dimension_numbers=layout, preferred_element_type=jnp.float32
    )
    coarse = (summed + down_b).astype(jnp.bfloat16)
    return (skip, coarse)


def gelu(v):
    return 0.5 * v * (1.0 + lax.erf(v * np.float32(np.sqrt(0.5))))


def shifted(v, before, after):
    n = v.shape[0]
    spot = lax.broadcasted_iota(jnp.int32, (n, 1), 0)
    low = jnp.where(spot == 0, before, pltpu.roll(v, 1, 0))
    high = jnp.where(spot == n - 1, after, pltpu.roll(v, n - 1, 0))
    return low.astype(BF), v.astype(BF), high.astype(BF)


def conv_kernel(first, steps, coarse, x_ref, next_ref, prev_ref, w_ref, b_ref, *refs):
    if coarse:
        dw_ref, db_ref = refs[:2]
        o_ref, c_ref, taps, w_low, w_high, wide = refs[-6:]
    else:
        o_ref, taps, w_low, w_high = refs[-4:]
    rows, cols, ch = x_ref.shape[1:]
    pairs = rows // 2
    start = pl.program_id(0)
    step = lax.rem(first + start, steps)
    zero_row = jnp.zeros((1, ch), F32)
    half = 3 * ch

    def put(v, pair, side):
        low, same, high = shifted(v.astype(F32), zero_row, zero_row)
        place = side * half
        taps[pair, :, place : place + ch] = low
        taps[pair, :, place + ch : place + 2 * ch] = same
        taps[pair, :, place + 2 * ch : place + 3 * ch] = high

    @pl.when(start == 0)
    def _():
        zero = jnp.zeros((ch, ch), BF)
        for d in range(3):
            one = slice(d * ch, (d + 1) * ch)
            two = slice(half + d * ch, half + (d + 1) * ch)
            w_low[one, :ch] = w_ref[0, d]
            w_low[one, ch:] = zero
            w_low[two, :ch] = w_ref[1, d]
            w_low[two, ch:] = w_ref[0, d]
            w_high[one, :ch] = w_ref[2, d]
            w_high[one, ch:] = w_ref[1, d]
            w_high[two, :ch] = zero
            w_high[two, ch:] = w_ref[2, d]

    @pl.when((start == 0) | (step == 0))
    def _():
        inside = (step > 0).astype(F32)
        put(prev_ref[0, 0].astype(F32) * inside, 0, 0)
        put(x_ref[0, 0], 0, 1)

    @pl.when((start > 0) & (step > 0))
    def _():
        taps[0] = taps[pairs]

    for pair in range(1, pairs + 1):
        put(x_ref[0, 2 * pair - 1], pair, 0)
        if pair < pairs:
            put(x_ref[0, 2 * pair], pair, 1)
    inside = (step < steps - 1).astype(F32)
    put(next_ref[0, 0].astype(F32) * inside, pairs, 1)

    lower = taps[pl.ds(0, pairs)].reshape(pairs * cols, 2 * half)
    upper = taps[pl.ds(1, pairs)].reshape(pairs * cols, 2 * half)
    total = jnp.dot(lower, w_low[...], preferred_element_type=F32)
    total += jnp.dot(upper, w_high[...], preferred_element_type=F32)
    total = total.reshape(pairs, cols, 2 * ch)
    bias = b_ref[...]
    for side in range(2):
        out = gelu(total[:, :, side * ch : (side + 1) * ch] + bias[None]).astype(BF)
        for pair in range(pairs):
            o_ref[0, 2 * pair + side] = out[pair]
        if coarse:
            wide[side] = out.astype(F32).reshape(pairs * cols, ch)
    if coarse:
        spots = pairs * cols // 2
        four = [wide[a, pl.ds(d, spots, stride=2), :].astype(BF) for a in range(2) for d in range(2)]
        out = jnp.dot(
            jnp.concatenate(four, axis=1),
            dw_ref[...].reshape(4 * ch, -1),
            preferred_element_type=F32,
        )
        out = (out + db_ref[...]).astype(BF)
        c_ref[0] = out.reshape(pairs, cols // 2, -1)


def in_hbm(x):
    return pltpu.with_memory_space_constraint(x, pltpu.HBM)


def conv_piece(x, weight, bias, first, count, into, down):
    faces, rows, cols, ch = x.shape
    steps = rows // STEP

    def at(i):
        return (first + i) // steps, lax.rem(first + i, steps)

    def block(i):
        face, step = at(i)
        return face, step, 0, 0

    def row_after(i):
        face, step = at(i)
        return face, jnp.minimum((step + 1) * STEP, rows - 1), 0, 0

    def row_before(i):
        face, step = at(i)
        return face, jnp.maximum(step * STEP - 1, 0), 0, 0

    in_specs = [
        pl.BlockSpec((1, STEP, cols, ch), block),
        pl.BlockSpec((1, 1, cols, ch), row_after),
        pl.BlockSpec((1, 1, cols, ch), row_before),
        whole(weight.shape),
        whole(bias.shape),
    ]
    args = [in_hbm(x), in_hbm(x), in_hbm(x), weight, bias]
    out_specs = [pl.BlockSpec((1, STEP, cols, ch), block)]
    out_shape = [pltpu.HBM(x.shape, BF)]
    scratch = [
        pltpu.VMEM((STEP // 2 + 1, cols, 6 * ch), BF),
        pltpu.VMEM((6 * ch, 2 * ch), BF),
        pltpu.VMEM((6 * ch, 2 * ch), BF),
    ]
    flops = 24 * ch * ch
    if down:
        down_w, down_b = down
        co = down_w.shape[-1]
        in_specs += [whole(down_w.shape), whole(down_b.shape)]
        args += [down_w, down_b]
        out_specs.append(pl.BlockSpec((1, STEP // 2, cols // 2, co), block))
        out_shape.append(pltpu.HBM((faces, rows // 2, cols // 2, co), BF))
        scratch.append(pltpu.VMEM((2, STEP // 2 * cols, ch), F32))
        flops += 2 * ch * co
    aliases = {}
    for k, buffer in enumerate(into):
        aliases[len(args)] = k
        in_specs.append(pl.BlockSpec(memory_space=pltpu.HBM))
        args.append(buffer)
    pixels = count * STEP * cols
    return pl.pallas_call(
        functools.partial(conv_kernel, first, steps, bool(down)),
        grid=(count,),
        in_specs=in_specs,
        out_specs=tuple(out_specs),
        out_shape=tuple(out_shape),
        scratch_shapes=scratch,
        input_output_aliases=aliases,
        cost_estimate=pl.CostEstimate(
            flops=pixels * flops, bytes_accessed=4 * pixels * ch, transcendentals=0
        ),
        compiler_params=pltpu.CompilerParams(vmem_limit_bytes=20 * 2**20),
        name="conv_piece",
    )(*args)


def column(tile, place):
    return tile[pl.ds(place, tile.shape[0] // STEP, stride=STEP), :]


def put_strips(i, r, c, lines, top, bottom, u_ref, v_ref, turn_ref, line_ref):
    left, left_in, right_in, right = lines
    size = left.shape[0]
    for place, value in enumerate(lines):
        line_ref[i, place] = value.astype(BF)
    side = jnp.where(c == 0, left, right).astype(BF)
    inner = jnp.where(c == 0, right, left).astype(BF)
    even = lax.rem(r, 2) == 0
    line = jnp.where(even, top, bottom).astype(BF)
    turn_ref[i] = jnp.where(even, bottom, top).astype(BF)
    for ref in (u_ref, v_ref):
        ref[i, 0] = side
        ref[i, 1] = line[:size]
        ref[i, 2] = line[size:]
    u_ref[i, 3] = inner


def strip_shapes(faces, rows, cols, ch):
    return (
        jax.ShapeDtypeStruct((faces, 4, rows, ch), BF),
        jax.ShapeDtypeStruct((faces, 3, rows, ch), BF),
        jax.ShapeDtypeStruct((faces, cols, ch), BF),
        jax.ShapeDtypeStruct((faces, 4, rows, ch), BF),
    )


def whole(shape):
    return pl.BlockSpec(shape, lambda *_: (0,) * len(shape))


def tile_copies(array, tiles, sems, back=False):
    cols = array.shape[2]
    out = []
    for side, start in enumerate((0, cols - STEP)):
        far, near = array.at[:, :, pl.ds(start, STEP), :], tiles.at[side]
        out.append(pltpu.make_async_copy(*((near, far) if back else (far, near)), sems.at[side]))
    return out


def strips_kernel(x_ref, u_ref, v_ref, turn_ref, line_ref, tiles, outer, left, right, sems):
    faces, rows, cols, ch = x_ref.shape
    r, c = lax.axis_index("row"), lax.axis_index("col")
    copies = tile_copies(x_ref, tiles, sems)
    for k, row in enumerate((0, rows - 1)):
        copies.append(pltpu.make_async_copy(x_ref.at[:, row], outer.at[k], sems.at[2 + k]))
    for copy in copies:
        copy.start()
    for copy in copies:
        copy.wait()

    def face(i, carry):
        left[...] = tiles[0, i].astype(F32).reshape(rows * STEP, ch)
        right[...] = tiles[1, i].astype(F32).reshape(rows * STEP, ch)
        lines = (column(left, 0), column(left, 1), column(right, STEP - 2), column(right, STEP - 1))
        put_strips(
            i, r, c, lines, outer[0, i].astype(F32), outer[1, i].astype(F32),
            u_ref, v_ref, turn_ref, line_ref,
        )
        return carry

    lax.fori_loop(0, faces, face, 0)


def strips_of(x):
    faces, rows, cols, ch = x.shape
    shapes = strip_shapes(faces, rows, cols, ch)
    return pl.pallas_call(
        strips_kernel,
        in_specs=[pl.BlockSpec(memory_space=pltpu.HBM)],
        out_specs=(pl.BlockSpec(memory_space=pltpu.VMEM),) * 4,
        out_shape=shapes,
        scratch_shapes=[
            pltpu.VMEM((2, faces, rows, STEP, ch), BF),
            pltpu.VMEM((2, faces, cols, ch), BF),
            pltpu.VMEM((rows * STEP, ch), F32),
            pltpu.VMEM((rows * STEP, ch), F32),
            pltpu.SemaphoreType.DMA((4,)),
        ],
        cost_estimate=pl.CostEstimate(flops=0, bytes_accessed=4 * 2**20, transcendentals=0),
        compiler_params=pltpu.CompilerParams(vmem_limit_bytes=10 * 2**20),
        name="strips_of",
    )(in_hbm(x))


def select_kernel(near_ref, code_ref, *refs):
    stores, outs, held = refs[:8], refs[8:-1], refs[-1]
    faces, _, size, ch = held.shape[1:]
    me, r, c = lax.axis_index("face"), lax.axis_index("row"), lax.axis_index("col")
    for k, store in enumerate(stores):
        for i in range(faces):
            held[k, i] = store[i, 0:3]

    def slot(row, col):
        return ((r ^ row) << 1) | (c ^ col)

    def quarter(edge, q):
        upright = lax.rem(edge, 2) == 1
        row = jnp.where(upright, q, jnp.where(edge == 0, 0, 3))
        col = jnp.where(upright, jnp.where(edge == 3, 0, 1), q >> 1)
        return slot(row, col), jnp.where(upright, 0, 1 + (q & 1))

    def end(n, where, block, last):
        head = held[where, n, block, 0:EXTRA].astype(F32)
        tail = held[where, n, block, size - EXTRA : size].astype(F32)
        return jnp.where(last, tail[EXTRA - 1 : EXTRA], head[0:1])

    spot = lax.broadcasted_iota(jnp.int32, (EXTRA, 1), 0)
    for k, out in enumerate(outs):
        target = me ^ k

        def face(i, carry, out=out, target=target):
            f = target * faces + i
            edge = 3 - 2 * c
            code = code_ref[f, edge]
            far, flip = code >> 1, code & 1
            n = lax.rem(near_ref[f, edge], faces)
            where, block = quarter(far, jnp.where(flip == 1, 3 - r, r))
            out[i, 0:size] = held[where, n, block]
            corner = jnp.where(r < 2, c, 3 - c)
            tip = code_ref[f, 4 + corner]
            tip_n = lax.rem(near_ref[f, 4 + corner], faces)
            tip_row = jnp.where(tip < 2, 0, 3)
            tip_col = jnp.where((tip == 1) | (tip == 2), 1, 0)
            tip_pixel = end(tip_n, slot(tip_row, tip_col), 0, tip_row == 3)
            q = jnp.where(flip == 1, 4 - r, r - 1)
            where, block = quarter(far, jnp.clip(q, 0, 3))
            before = jnp.where(r == 0, tip_pixel, end(n, where, block, flip == 0))
            q = jnp.where(flip == 1, 2 - r, r + 1)
            where, block = quarter(far, jnp.clip(q, 0, 3))
            after = jnp.where(r == 3, tip_pixel, end(n, where, block, flip == 1))

            edge = jnp.where(r < 2, 0, 2)
            code = code_ref[f, edge]
            far, flip = code >> 1, code & 1
            n = lax.rem(near_ref[f, edge], faces)
            part = c ^ flip
            for h in range(2):
                where, block = quarter(far, 2 * part + h)
                out[i, (1 + h) * size : (2 + h) * size] = held[where, n, block]
            where, block = quarter(far, jnp.where(part == 0, 2, 1))
            middle = end(n, where, block, part == 1)
            single = jnp.where(spot == 0, before, jnp.where(spot == 1, after, middle))
            out[i, 3 * size : 3 * size + EXTRA] = single.astype(BF)
            return carry

        lax.fori_loop(0, faces, face, 0)


def select_strips(neighbour_face, orientation, stores, groups):
    faces, _, size, ch = stores[0].shape
    shape = jax.ShapeDtypeStruct((faces, 3 * size + EXTRA, ch), BF)
    smem = pl.BlockSpec(memory_space=pltpu.SMEM)
    return pl.pallas_call(
        select_kernel,
        in_specs=[smem, smem] + [pl.BlockSpec(memory_space=pltpu.VMEM)] * 8,
        out_specs=(pl.BlockSpec(memory_space=pltpu.VMEM),) * groups,
        out_shape=(shape,) * groups,
        scratch_shapes=[pltpu.VMEM((8, faces, 3, size, ch), BF)],
        cost_estimate=pl.CostEstimate(flops=0, bytes_accessed=4 * 2**20, transcendentals=0),
        compiler_params=pltpu.CompilerParams(vmem_limit_bytes=10 * 2**20),
        name="select_strips",
    )(neighbour_face, orientation, *stores)


def ring_kernel(groups, coarse, near_ref, code_ref, x_ref, y_in, line_in, beside, diagonal, across,
                far_diagonal, turned, w_ref, b_ref, *refs):
    seams, refs = refs[:groups], refs[groups:]
    if coarse:
        c_in, dw_ref, db_ref, y_ref, c_ref = refs[:5]
        scratch = refs[5:]
        *scratch, second, c_tiles, c_rows, c_cols, c_left, pair_rows = scratch
    else:
        y_ref, outs, scratch = refs[0], refs[1:5], refs[5:]
    tiles, inside, edge_rows, edge_cols, held, left, right, w_cols, sems = scratch
    faces, rows, cols, ch = x_ref.shape
    me, r, c = lax.axis_index("face"), lax.axis_index("row"), lax.axis_index("col")
    copies = []
    for k, row in enumerate((0, 1, rows - 2, rows - 1)):
        copies.append(pltpu.make_async_copy(x_ref.at[:, row], inside.at[k], sems.at[2 + k]))
    late = tile_copies(y_in, tiles, sems)
    if coarse:
        for k, row in enumerate((1, rows - 2)):
            late.append(pltpu.make_async_copy(y_in.at[:, row], second.at[k], sems.at[6 + k]))
        for side, start in enumerate((0, cols // 2 - STEP)):
            late.append(
                pltpu.make_async_copy(
                    c_in.at[:, :, pl.ds(start, STEP), :], c_tiles.at[side], sems.at[8 + side]
                )
            )
    for copy in copies + late:
        copy.start()
    for k in range(groups):
        held[k] = seams[k][...]

    def oriented(v, flip):
        n = v.shape[0]
        to = lax.broadcasted_iota(jnp.int32, (n, n), 0)
        source = lax.broadcasted_iota(jnp.int32, (n, n), 1)
        order = jnp.where(source == jnp.where(flip == 1, n - 1 - to, to), 1.0, 0.0).astype(BF)
        return jnp.dot(order, v, preferred_element_type=F32)

    even = lax.rem(r, 2) == 0
    outer = (r == 0) | (r == 3)
    w_rows = w_ref[...].reshape(9 * ch, ch)
    for d in range(3):
        for a in range(3):
            w_cols[(3 * d + a) * ch : (3 * d + a + 1) * ch] = w_ref[a, d]
    bias = b_ref[...]

    def holder(n):
        return jnp.minimum(n, FACES - 1) // faces ^ me

    def face(i, carry):
        f = me * faces + i
        edge = 3 - 2 * c
        n = near_ref[f, edge]
        corner = jnp.where(r < 2, c, 3 - c)
        tip_n = near_ref[f, 4 + corner]
        seam_side = oriented(held[holder(n), i, 0:rows], code_ref[f, edge] & 1)
        extra = slice(3 * rows, 3 * rows + EXTRA)
        n_before = jnp.where(r == 0, tip_n, n)
        n_after = jnp.where(r == 3, tip_n, n)
        before = held[holder(n_before), i, extra].astype(F32)[0:1]
        after = held[holder(n_after), i, extra].astype(F32)[1:2]
        before = jnp.where(n_before < FACES, before, 0.0)
        after = jnp.where(n_after < FACES, after, 0.0)
        edge = jnp.where(r < 2, 0, 2)
        n = near_ref[f, edge]
        seam_line = oriented(held[holder(n), i, rows : 3 * rows], code_ref[f, edge] & 1)
        middle = held[holder(n), i, extra].astype(F32)[2:3]

        inner = beside[i, 3].astype(F32)
        block_line = jnp.concatenate([across[i, 1], across[i, 2]], axis=0).astype(F32)
        outward = jnp.where(outer, seam_line, block_line)
        inward = turned[i].astype(F32)
        top = jnp.where(even, outward, inward)
        bottom = jnp.where(even, inward, outward)
        lft = jnp.where(c == 0, seam_side, inner)
        rgt = jnp.where(c == 0, inner, seam_side)
        pair_inner = diagonal[i, 3].astype(F32)
        inward_corner = jnp.where(even, pair_inner[0:1], pair_inner[rows - 1 : rows])
        far_first = far_diagonal[i, 1].astype(F32)[0:1]
        far_last = far_diagonal[i, 2].astype(F32)[rows - 1 : rows]
        outward_corner = jnp.where(outer, middle, jnp.where(c == 0, far_first, far_last))
        inner_top = jnp.where(even, outward_corner, inward_corner)
        inner_bottom = jnp.where(even, inward_corner, outward_corner)
        top_left = jnp.where(c == 0, before, inner_top)
        top_right = jnp.where(c == 0, inner_top, before)
        bottom_left = jnp.where(c == 0, after, inner_bottom)
        bottom_right = jnp.where(c == 0, inner_bottom, after)

        row_0, row_1, row_2, row_3 = (inside[k, i].astype(F32) for k in range(4))
        upper = (
            shifted(top, top_left, top_right)
            + shifted(row_0, lft[0:1], rgt[0:1])
            + shifted(row_1, lft[1:2], rgt[1:2])
        )
        lower = (
            shifted(row_2, lft[rows - 2 : rows - 1], rgt[rows - 2 : rows - 1])
            + shifted(row_3, lft[rows - 1 : rows], rgt[rows - 1 : rows])
            + shifted(bottom, bottom_left, bottom_right)
        )
        both = jnp.concatenate(
            [jnp.concatenate(upper, axis=1), jnp.concatenate(lower, axis=1)], axis=0
        )
        out_rows = gelu(jnp.dot(both, w_rows, preferred_element_type=F32) + bias)
        col_0, col_1, col_2, col_3 = (line_in[i, k].astype(F32) for k in range(4))
        upper = (
            shifted(lft, top_left, bottom_left)
            + shifted(col_0, top[0:1], bottom[0:1])
            + shifted(col_1, top[1:2], bottom[1:2])
        )
        lower = (
            shifted(col_2, top[cols - 2 : cols - 1], bottom[cols - 2 : cols - 1])
            + shifted(col_3, top[cols - 1 : cols], bottom[cols - 1 : cols])
            + shifted(rgt, top_right, bottom_right)
        )
        both = jnp.concatenate(
            [jnp.concatenate(upper, axis=1), jnp.concatenate(lower, axis=1)], axis=0
        )
        out_cols = gelu(jnp.dot(both, w_cols[...], preferred_element_type=F32) + bias)

        edge_rows[0, i] = out_rows[:cols].astype(BF)
        edge_rows[1, i] = out_rows[cols:].astype(BF)
        edge_cols[i] = out_cols
        return carry

    def update(i, carry):
        new_top, new_bottom = edge_rows[0, i].astype(F32), edge_rows[1, i].astype(F32)
        for tile, side, place in ((left, 0, 0), (right, 1, STEP - 1)):
            start = side * (cols - STEP)
            tiles[side, i, 0] = edge_rows[0, i, start : start + STEP]
            tiles[side, i, rows - 1] = edge_rows[1, i, start : start + STEP]
            tile[...] = tiles[side, i].astype(F32).reshape(rows * STEP, ch)
            tile[pl.ds(place, rows, stride=STEP), :] = edge_cols[i, pl.ds(side * rows, rows)]
            tiles[side, i] = tile[...].astype(BF).reshape(rows, STEP, ch)
        if not coarse:
            lines = (
                column(left, 0), column(left, 1),
                column(right, STEP - 2), column(right, STEP - 1),
            )
            put_strips(i, r, c, lines, new_top, new_bottom, *outs)
            return carry
        w_down = dw_ref[...].reshape(4 * ch, -1)
        for k, (own, near) in enumerate(((new_top, 1), (new_bottom, rows - 2))):
            first = edge_cols[i, near : near + 1]
            last = edge_cols[i, rows + near : rows + near + 1]
            spot = lax.broadcasted_iota(jnp.int32, (cols, 1), 0)
            other = second[k, i].astype(F32)
            other = jnp.where(spot == 0, first, jnp.where(spot == cols - 1, last, other))
            pair_rows[k] = own
            pair_rows[1 - k] = other.astype(BF).astype(F32)
            four = [
                pair_rows[a, pl.ds(d, cols // 2, stride=2), :].astype(BF)
                for a in range(2)
                for d in range(2)
            ]
            out = jnp.dot(jnp.concatenate(four, axis=1), w_down, preferred_element_type=F32)
            out = (out + db_ref[...]).astype(BF)
            c_rows[k, i] = out
            for side, start in enumerate((0, cols // 2 - STEP)):
                c_tiles[side, i, k * (rows // 2 - 1)] = out[start : start + STEP]
        for side, (tile, place) in enumerate(((left, 0), (right, STEP - 2))):
            four = [
                tile[pl.ds(a * STEP + place + d, rows // 2, stride=2 * STEP), :].astype(BF)
                for a in range(2)
                for d in range(2)
            ]
            out = jnp.dot(jnp.concatenate(four, axis=1), w_down, preferred_element_type=F32)
            c_cols[...] = (out + db_ref[...])
            for h in range(c_cols.shape[1] // ch):
                lanes = slice(h * ch, (h + 1) * ch)
                c_left[...] = c_tiles[side, i, :, :, lanes].astype(F32).reshape(rows // 2 * STEP, ch)
                c_left[pl.ds(side * (STEP - 1), rows // 2, stride=STEP), :] = c_cols[:, lanes]
                c_tiles[side, i, :, :, lanes] = (
                    c_left[...].astype(BF).reshape(rows // 2, STEP, ch)
                )
        return carry

    for copy in copies:
        copy.wait()
    lax.fori_loop(0, faces, face, 0)
    for copy in late:
        copy.wait()
    lax.fori_loop(0, faces, update, 0)
    copies = tile_copies(y_ref, tiles, sems, back=True)
    between = pl.ds(STEP, cols - 2 * STEP)
    if cols > 2 * STEP:
        for k, row in enumerate((0, rows - 1)):
            copies.append(
                pltpu.make_async_copy(
                    edge_rows.at[k, :, between], y_ref.at[:, row, between], sems.at[2 + k]
                )
            )
    if coarse:
        half = cols // 2
        for side, start in enumerate((0, half - STEP)):
            copies.append(
                pltpu.make_async_copy(
                    c_tiles.at[side], c_ref.at[:, :, pl.ds(start, STEP), :], sems.at[8 + side]
                )
            )
        between = pl.ds(STEP, half - 2 * STEP)
        if half > 2 * STEP:
            for k, row in enumerate((0, rows // 2 - 1)):
                copies.append(
                    pltpu.make_async_copy(
                        c_rows.at[k, :, between], c_ref.at[:, row, between], sems.at[6 + k]
                    )
                )
    for copy in copies:
        copy.start()
    for copy in copies:
        copy.wait()


def ring(neighbour_face, orientation, x, y, lines, parts, weight, bias, seams, down):
    y, *coarse = y
    faces, rows, cols, ch = x.shape
    groups = len(seams)
    smem = pl.BlockSpec(memory_space=pltpu.SMEM)
    hbm = pl.BlockSpec(memory_space=pltpu.HBM)
    vmem = pl.BlockSpec(memory_space=pltpu.VMEM)
    args = [neighbour_face, orientation, in_hbm(x), in_hbm(y), lines, *parts, weight, bias, *seams]
    in_specs = [smem, smem, hbm, hbm] + [vmem] * (len(args) - 4)
    out_shape = [pltpu.HBM(y.shape, BF)]
    out_specs = [hbm]
    aliases = {3: 0}
    scratch = [
        pltpu.VMEM((2, faces, rows, STEP, ch), BF),
        pltpu.VMEM((4, faces, cols, ch), BF),
        pltpu.VMEM((2, faces, cols, ch), BF),
        pltpu.VMEM((faces, 2 * rows, ch), F32),
        pltpu.VMEM((groups, faces, 3 * rows + EXTRA, ch), BF),
        pltpu.VMEM((rows * STEP, ch), F32),
        pltpu.VMEM((rows * STEP, ch), F32),
        pltpu.VMEM((9 * ch, ch), BF),
        pltpu.SemaphoreType.DMA((10,)),
    ]
    if down:
        co = down[0].shape[-1]
        aliases[len(args)] = 1
        args += [in_hbm(coarse[0]), *down]
        in_specs += [hbm, vmem, vmem]
        out_shape.append(pltpu.HBM(coarse[0].shape, BF))
        out_specs.append(hbm)
        scratch += [
            pltpu.VMEM((2, faces, cols, ch), BF),
            pltpu.VMEM((2, faces, rows // 2, STEP, co), BF),
            pltpu.VMEM((2, faces, cols // 2, co), BF),
            pltpu.VMEM((rows // 2, co), F32),
            pltpu.VMEM((rows // 2 * STEP, ch), F32),
            pltpu.VMEM((2, cols, ch), F32),
        ]
    else:
        out_shape += strip_shapes(faces, rows, cols, ch)
        out_specs += [vmem] * 4
    return pl.pallas_call(
        functools.partial(ring_kernel, groups, bool(down)),
        in_specs=in_specs,
        out_specs=tuple(out_specs),
        out_shape=tuple(out_shape),
        scratch_shapes=scratch,
        input_output_aliases=aliases,
        cost_estimate=pl.CostEstimate(
            flops=faces * (rows + cols) * 36 * ch * ch, bytes_accessed=8 * 2**20, transcendentals=0
        ),
        compiler_params=pltpu.CompilerParams(vmem_limit_bytes=24 * 2**20),
        name="ring",
    )(*args)


def blocks(change_row, change_col):
    cols = lax.axis_size("col")
    return [
        (r * cols + c, (r ^ change_row) * cols + (c ^ change_col))
        for r in range(lax.axis_size("row"))
        for c in range(cols)
    ]


def swap(v, change_row, change_col):
    return lax.ppermute(v, ("row", "col"), blocks(change_row, change_col))


def level(neighbour_face, orientation, x, strips, weight, bias, down):
    u, v, turn, lines = strips
    groups = lax.axis_size("face")
    total = x.shape[0] * x.shape[1] // STEP
    early, late = max(total // 3, 1), max(total * 5 // 12, 2)
    piece = functools.partial(conv_piece, x, weight, bias, down=down)
    beside, across, diagonal = swap(u, 0, 1), swap(v, 3, 0), swap(v, 3, 1)
    pair, turned = swap(v, 1, 0), swap(turn, 1, 0)
    y = piece(0, early, ())
    beside, across, diagonal, *y = lax.optimization_barrier((beside, across, diagonal, *y))
    pair_beside, pair_across, pair_diagonal = (swap(a, 1, 0) for a in (beside, across, diagonal))
    y = piece(early, late - early, y)
    stores = (v, beside, pair, pair_beside, pair_across, pair_diagonal, across, diagonal)
    picked = select_strips(neighbour_face, orientation, stores, groups)
    picked, y = lax.optimization_barrier((picked, y))
    seams = [picked[0]]
    for k in range(1, groups):
        seams.append(lax.ppermute(picked[k], "face", [(g, g ^ k) for g in range(groups)]))
    y = piece(late, total - late, y)
    parts = (beside, pair_beside, across, diagonal, turned)
    return ring(neighbour_face, orientation, x, y, lines, parts, weight, bias, seams, down)


def per_device(
    field, conv1_w, conv1_b, conv2_w, conv2_b, down_w, down_b, neighbour_face, orientation
):
    tables = (neighbour_face, orientation)
    hidden, *strips = level(*tables, field, strips_of(field), conv1_w, conv1_b[None], ())
    return level(*tables, hidden, strips, conv2_w, conv2_b[None], (down_w, down_b[None]))


def solution(mesh):
    groups = mesh.shape["face"]
    fast = mesh.shape["row"] == 4 and mesh.shape["col"] == 2 and groups & (groups - 1) == 0
    return jax.shard_map(
        per_device if fast else general_device,
        mesh=mesh,
        in_specs=(P("face", "row", "col", None), P(), P(), P(), P(), P(), P(), P(), P()),
        out_specs=(P("face", "row", "col", None), P("face", "row", "col", None)),
        check_vma=False,
    )
```

```python
import functools

import jax
import jax.numpy as jnp
import numpy as np
from jax import lax
from jax.experimental import pallas as pl
from jax.experimental.pallas import tpu as pltpu
from jax.sharding import PartitionSpec as P

FACES = 12
BF = jnp.bfloat16
F32 = jnp.float32
STEP = 16
EXTRA = 16

layout = ("NHWC", "HWIO", "NHWC")


def padded_2(block, sides, width):
    for axis, dim in sides:
        count = lax.axis_size(axis)
        forward = [(i, i + 1) for i in range(count - 1)]
        backward = [(target, source) for source, target in forward]
        low = lax.ppermute(
            lax.slice_in_dim(block, block.shape[dim] - width, None, axis=dim), axis, forward
        )
        high = lax.ppermute(lax.slice_in_dim(block, 0, width, axis=dim), axis, backward)
        block = jnp.concatenate([low, block, high], axis=dim)
    return block


def seam_parts(edges, neighbours, codes):
    seam_faces = neighbours[:, :4]
    seam_codes = codes[:, :4]
    seams = edges[seam_faces, seam_codes // 2]
    seams = jnp.where((seam_codes % 2 == 1)[:, :, None, None], seams[:, :, ::-1], seams)
    corner_values = jnp.stack(
        [edges[:, 0, 0], edges[:, 0, -1], edges[:, 2, -1], edges[:, 2, 0]], axis=1
    )
    corner_faces = neighbours[:, 4:]
    picked = corner_values[jnp.minimum(corner_faces, FACES - 1), codes[:, 4:]]
    picked = jnp.where((corner_faces < FACES)[:, :, None], picked, jnp.zeros_like(picked))
    return (seams, picked)


def convolve(padded, weight, bias):
    summed = lax.conv_general_dilated(
        padded,
        weight,
        (1, 1),
        "VALID",
        dimension_numbers=layout,
        preferred_element_type=jnp.float32,
    )
    return jax.nn.gelu(summed + bias, approximate=False).astype(jnp.bfloat16)


def general_layer(block, weight, bias, neighbour_face, orientation):
    face_count, row_size, col_size, channels = block.shape
    row_total = lax.axis_size("row")
    col_total = lax.axis_size("col")
    row_place = lax.axis_index("row")
    col_place = lax.axis_index("col")
    face_side = row_size * row_total
    padded = padded_2(block, (("row", 1), ("col", 2)), 1)
    top_live = row_place == 0
    bottom_live = row_place == row_total - 1
    left_live = col_place == 0
    right_live = col_place == col_total - 1
    empty_line = jnp.zeros((face_count, face_side, channels), jnp.float32)

    def place(strip, offset, live):
        scaled = strip.astype(jnp.float32) * live.astype(jnp.float32)
        return lax.dynamic_update_slice_in_dim(empty_line, scaled, offset, 1)

    lines = jnp.stack(
        [
            place(block[:, 0], col_place * col_size, top_live),
            place(block[:, :, -1], row_place * row_size, right_live),
            place(block[:, -1], col_place * col_size, bottom_live),
            place(block[:, :, 0], row_place * row_size, left_live),
        ],
        axis=1,
    )
    complete = lax.psum(lax.psum(lines.astype(jnp.bfloat16), "col"), "row").astype(jnp.float32)
    every_edge = lax.all_gather(complete.astype(jnp.bfloat16), "face", axis=0, tiled=True)
    first_face = lax.axis_index("face") * face_count
    own_faces = lax.dynamic_slice_in_dim(neighbour_face, first_face, face_count, 0)
    own_codes = lax.dynamic_slice_in_dim(orientation, first_face, face_count, 0)
    seams, corners = seam_parts(every_edge, own_faces, own_codes)
    upper = jnp.concatenate([corners[:, 0:1], seams[:, 0], corners[:, 1:2]], 1)
    lower = jnp.concatenate([corners[:, 3:4], seams[:, 2], corners[:, 2:3]], 1)
    leftward = jnp.concatenate([corners[:, 0:1], seams[:, 3], corners[:, 3:4]], 1)
    rightward = jnp.concatenate([corners[:, 1:2], seams[:, 1], corners[:, 2:3]], 1)
    upper_cut = lax.dynamic_slice_in_dim(upper, col_place * col_size, col_size + 2, 1)
    lower_cut = lax.dynamic_slice_in_dim(lower, col_place * col_size, col_size + 2, 1)
    left_cut = lax.dynamic_slice_in_dim(leftward, row_place * row_size, row_size + 2, 1)
    right_cut = lax.dynamic_slice_in_dim(rightward, row_place * row_size, row_size + 2, 1)
    padded = padded.at[:, 0].set(jnp.where(top_live, upper_cut, padded[:, 0]))
    padded = padded.at[:, -1].set(jnp.where(bottom_live, lower_cut, padded[:, -1]))
    padded = padded.at[:, :, 0].set(jnp.where(left_live, left_cut, padded[:, :, 0]))
    padded = padded.at[:, :, -1].set(jnp.where(right_live, right_cut, padded[:, :, -1]))
    return convolve(padded, weight, bias)


def general_device(
    field, conv1_w, conv1_b, conv2_w, conv2_b, down_w, down_b, neighbour_face, orientation
):
    hidden = general_layer(field, conv1_w, conv1_b, neighbour_face, orientation)
    skip = general_layer(hidden, conv2_w, conv2_b, neighbour_face, orientation)
    summed = lax.conv_general_dilated(
        skip, down_w, (2, 2), "VALID", dimension_numbers=layout, preferred_element_type=jnp.float32
    )
    coarse = (summed + down_b).astype(jnp.bfloat16)
    return (skip, coarse)


def gelu(v):
    return 0.5 * v * (1.0 + lax.erf(v * np.float32(np.sqrt(0.5))))


def shifted(v, before, after):
    n = v.shape[0]
    spot = lax.broadcasted_iota(jnp.int32, (n, 1), 0)
    low = jnp.where(spot == 0, before, pltpu.roll(v, 1, 0))
    high = jnp.where(spot == n - 1, after, pltpu.roll(v, n - 1, 0))
    return low.astype(BF), v.astype(BF), high.astype(BF)


def conv_kernel(first, count, build, coarse, x_ref, b_ref, *refs):
    if coarse:
        dw_ref, db_ref, refs = refs[0], refs[1], refs[2:]
        *refs, y_out, c_out, taps_0, taps_1, wide, sems = refs
        if build:
            w_ref, y_ref, c_ref, w_low, w_high = refs[0], *refs[1:]
        else:
            w_low, w_high, y_ref, c_ref = refs[0], refs[1], *refs[6:8]
    else:
        *refs, taps_0, taps_1 = refs
        if build:
            w_ref, y_ref, w_low, w_high = refs
        else:
            w_low, w_high, _, y_ref = refs
    _, size, cols, ch = x_ref.shape
    steps = size // STEP
    pairs = STEP // 2
    zero_row = jnp.zeros((1, ch), F32)
    half = 3 * ch

    if build:
        zero = jnp.zeros((ch, ch), BF)
        for d in range(3):
            one = slice(d * ch, (d + 1) * ch)
            two = slice(half + d * ch, half + (d + 1) * ch)
            w_low[one, :ch] = w_ref[0, d]
            w_low[one, ch:] = zero
            w_low[two, :ch] = w_ref[1, d]
            w_low[two, ch:] = w_ref[0, d]
            w_high[one, :ch] = w_ref[2, d]
            w_high[one, ch:] = w_ref[1, d]
            w_high[two, :ch] = zero
            w_high[two, ch:] = w_ref[2, d]

    def at(t):
        return t // steps, lax.rem(t, steps)

    def fill(taps, t):
        face, step = at(t)
        base = step * STEP

        def put(v, pair, side):
            low, same, high = shifted(v.astype(F32), zero_row, zero_row)
            place = side * half
            taps[pair, :, place : place + ch] = low
            taps[pair, :, place + ch : place + 2 * ch] = same
            taps[pair, :, place + 2 * ch : place + 3 * ch] = high

        inside = (step > 0).astype(F32)
        put(x_ref[face, jnp.maximum(base - 1, 0)].astype(F32) * inside, 0, 0)
        for row in range(STEP):
            put(x_ref[face, base + row], (row + 1) // 2, (row + 1) % 2)
        inside = (step < steps - 1).astype(F32)
        put(x_ref[face, jnp.minimum(base + STEP, size - 1)].astype(F32) * inside, pairs, 1)

    def product(taps, t):
        face, step = at(t)
        base = step * STEP
        lower = taps[pl.ds(0, pairs)].reshape(pairs * cols, 2 * half)
        upper = taps[pl.ds(1, pairs)].reshape(pairs * cols, 2 * half)
        total = jnp.dot(lower, w_low[...], preferred_element_type=F32)
        total += jnp.dot(upper, w_high[...], preferred_element_type=F32)
        total = total.reshape(pairs, cols, 2 * ch)
        bias = b_ref[...]
        for side in range(2):
            out = gelu(total[:, :, side * ch : (side + 1) * ch] + bias[None]).astype(BF)
            for pair in range(pairs):
                y_ref[face, base + 2 * pair + side] = out[pair]
            if coarse:
                wide[side] = out.astype(F32).reshape(pairs * cols, ch)
        if not coarse:
            return
        spots = pairs * cols // 2
        four = [wide[a, pl.ds(d, spots, stride=2), :].astype(BF) for a in range(2) for d in range(2)]
        out = jnp.dot(
            jnp.concatenate(four, axis=1),
            dw_ref[...].reshape(4 * ch, -1),
            preferred_element_type=F32,
        )
        out = (out + db_ref[...]).astype(BF)
        c_ref[face, pl.ds(step * pairs, pairs)] = out.reshape(pairs, cols // 2, -1)

    def copies(t):
        face, step = at(t)
        rows, cells = pl.ds(step * STEP, STEP), pl.ds(step * pairs, pairs)
        return (
            pltpu.make_async_copy(y_ref.at[face, rows], y_out.at[face, rows], sems.at[0]),
            pltpu.make_async_copy(c_ref.at[face, cells], c_out.at[face, cells], sems.at[1]),
        )

    def finish(taps, t):
        product(taps, t)
        if coarse:
            for copy in copies(t):
                copy.start()

    last = first + count - 1
    fill(taps_0, first)

    def double(j, carry):
        t = first + 2 * j
        fill(taps_1, t + 1)
        finish(taps_0, t)
        fill(taps_0, jnp.minimum(t + 2, last))
        finish(taps_1, t + 1)
        return carry

    lax.fori_loop(0, count // 2, double, 0)
    if count % 2:
        finish(taps_0, last)
    if coarse:

        def wait(t, carry):
            for copy in copies(t):
                copy.wait()
            return carry

        lax.fori_loop(first, first + count, wait, 0)


def in_hbm(x):
    return pltpu.with_memory_space_constraint(x, pltpu.HBM)


def conv_piece(x, weight, bias, first, count, state, down):
    faces, rows, cols, ch = x.shape
    vmem = pl.BlockSpec(memory_space=pltpu.VMEM)
    hbm = pl.BlockSpec(memory_space=pltpu.HBM)
    build = state is None
    args = [x, bias] + list(down)
    in_specs = [vmem] * len(args)
    taps = (STEP // 2 + 1, cols, 6 * ch)
    arranged = jax.ShapeDtypeStruct((6 * ch, 2 * ch), BF)
    out_shape = [jax.ShapeDtypeStruct(x.shape, BF)]
    out_specs = [vmem]
    scratch = [pltpu.VMEM(taps, BF), pltpu.VMEM(taps, BF)]
    flops = 24 * ch * ch
    if down:
        co = down[0].shape[-1]
        out_shape.append(jax.ShapeDtypeStruct((faces, rows // 2, cols // 2, co), BF))
        out_specs.append(vmem)
        scratch += [pltpu.VMEM((2, STEP // 2 * cols, ch), F32), pltpu.SemaphoreType.DMA((2,))]
        flops += 2 * ch * co
    aliases = {}
    if build:
        args.append(weight)
        in_specs.append(vmem)
        out_shape += [arranged] * 2
        out_specs += [vmem] * 2
    else:
        weights, buffers, copied = state
        args += list(weights)
        in_specs += [vmem] * 2
        for buffer in buffers:
            aliases[len(args)] = len(aliases)
            args.append(buffer)
            in_specs.append(vmem)
        for buffer in copied:
            aliases[len(args)] = len(aliases)
            args.append(in_hbm(buffer))
            in_specs.append(hbm)
    if down:
        out_shape += [pltpu.HBM(s.shape, BF) for s in out_shape[:2]]
        out_specs += [hbm] * 2
    pixels = count * STEP * cols
    out = pl.pallas_call(
        functools.partial(conv_kernel, first, count, build, bool(down)),
        in_specs=in_specs,
        out_specs=tuple(out_specs),
        out_shape=tuple(out_shape),
        scratch_shapes=scratch,
        input_output_aliases=aliases,
        cost_estimate=pl.CostEstimate(
            flops=pixels * flops, bytes_accessed=4 * pixels * ch, transcendentals=0
        ),
        compiler_params=pltpu.CompilerParams(vmem_limit_bytes=16 * 2**20),
        name="conv_piece",
    )(*args)
    kept = 2 if down else 1
    if build:
        weights = out[kept : kept + 2]
        copied = out[kept + 2 :]
    else:
        copied = out[kept:]
    return tuple(weights), tuple(out[:kept]), tuple(copied)


def column(tile, place):
    return tile[pl.ds(place, tile.shape[0] // STEP, stride=STEP), :]


def put_strips(i, r, c, lines, top, bottom, u_ref, v_ref, turn_ref, line_ref):
    left, left_in, right_in, right = lines
    size = left.shape[0]
    for place, value in enumerate(lines):
        line_ref[i, place] = value.astype(BF)
    side = jnp.where(c == 0, left, right).astype(BF)
    inner = jnp.where(c == 0, right, left).astype(BF)
    even = lax.rem(r, 2) == 0
    line = jnp.where(even, top, bottom).astype(BF)
    turn_ref[i] = jnp.where(even, bottom, top).astype(BF)
    for ref in (u_ref, v_ref):
        ref[i, 0] = side
        ref[i, 1] = line[:size]
        ref[i, 2] = line[size:]
    u_ref[i, 3] = inner


def strip_shapes(faces, rows, cols, ch):
    return (
        jax.ShapeDtypeStruct((faces, 4, rows, ch), BF),
        jax.ShapeDtypeStruct((faces, 3, rows, ch), BF),
        jax.ShapeDtypeStruct((faces, cols, ch), BF),
        jax.ShapeDtypeStruct((faces, 4, rows, ch), BF),
    )


def whole(shape):
    return pl.BlockSpec(shape, lambda *_: (0,) * len(shape))


def tile_copies(array, tiles, sems, back=False):
    cols = array.shape[2]
    out = []
    for side, start in enumerate((0, cols - STEP)):
        far, near = array.at[:, :, pl.ds(start, STEP), :], tiles.at[side]
        out.append(pltpu.make_async_copy(*((near, far) if back else (far, near)), sems.at[side]))
    return out


def strips_kernel(x_ref, u_ref, v_ref, turn_ref, line_ref, tiles, outer, left, right, sems):
    faces, rows, cols, ch = x_ref.shape
    r, c = lax.axis_index("row"), lax.axis_index("col")
    copies = tile_copies(x_ref, tiles, sems)
    for k, row in enumerate((0, rows - 1)):
        copies.append(pltpu.make_async_copy(x_ref.at[:, row], outer.at[k], sems.at[2 + k]))
    for copy in copies:
        copy.start()
    for copy in copies:
        copy.wait()

    def face(i, carry):
        left[...] = tiles[0, i].astype(F32).reshape(rows * STEP, ch)
        right[...] = tiles[1, i].astype(F32).reshape(rows * STEP, ch)
        lines = (column(left, 0), column(left, 1), column(right, STEP - 2), column(right, STEP - 1))
        put_strips(
            i, r, c, lines, outer[0, i].astype(F32), outer[1, i].astype(F32),
            u_ref, v_ref, turn_ref, line_ref,
        )
        return carry

    lax.fori_loop(0, faces, face, 0)


def strips_of(x):
    faces, rows, cols, ch = x.shape
    shapes = strip_shapes(faces, rows, cols, ch)
    return pl.pallas_call(
        strips_kernel,
        in_specs=[pl.BlockSpec(memory_space=pltpu.HBM)],
        out_specs=(pl.BlockSpec(memory_space=pltpu.VMEM),) * 4,
        out_shape=shapes,
        scratch_shapes=[
            pltpu.VMEM((2, faces, rows, STEP, ch), BF),
            pltpu.VMEM((2, faces, cols, ch), BF),
            pltpu.VMEM((rows * STEP, ch), F32),
            pltpu.VMEM((rows * STEP, ch), F32),
            pltpu.SemaphoreType.DMA((4,)),
        ],
        cost_estimate=pl.CostEstimate(flops=0, bytes_accessed=4 * 2**20, transcendentals=0),
        compiler_params=pltpu.CompilerParams(vmem_limit_bytes=10 * 2**20),
        name="strips_of",
    )(in_hbm(x))


def select_kernel(near_ref, code_ref, *refs):
    stores, outs, held = refs[:8], refs[8:-1], refs[-1]
    faces, _, size, ch = held.shape[1:]
    me, r, c = lax.axis_index("face"), lax.axis_index("row"), lax.axis_index("col")
    for k, store in enumerate(stores):
        for i in range(faces):
            held[k, i] = store[i, 0:3]

    def slot(row, col):
        return ((r ^ row) << 1) | (c ^ col)

    def quarter(edge, q):
        upright = lax.rem(edge, 2) == 1
        row = jnp.where(upright, q, jnp.where(edge == 0, 0, 3))
        col = jnp.where(upright, jnp.where(edge == 3, 0, 1), q >> 1)
        return slot(row, col), jnp.where(upright, 0, 1 + (q & 1))

    def end(n, where, block, last):
        head = held[where, n, block, 0:EXTRA].astype(F32)
        tail = held[where, n, block, size - EXTRA : size].astype(F32)
        return jnp.where(last, tail[EXTRA - 1 : EXTRA], head[0:1])

    spot = lax.broadcasted_iota(jnp.int32, (EXTRA, 1), 0)
    for k, out in enumerate(outs):
        target = me ^ k

        def face(i, carry, out=out, target=target):
            f = target * faces + i
            edge = 3 - 2 * c
            code = code_ref[edge, f]
            far, flip = code >> 1, code & 1
            n = lax.rem(near_ref[edge, f], faces)
            where, block = quarter(far, jnp.where(flip == 1, 3 - r, r))
            out[i, 0:size] = held[where, n, block]
            corner = jnp.where(r < 2, c, 3 - c)
            tip = code_ref[4 + corner, f]
            tip_n = lax.rem(near_ref[4 + corner, f], faces)
            tip_row = jnp.where(tip < 2, 0, 3)
            tip_col = jnp.where((tip == 1) | (tip == 2), 1, 0)
            tip_pixel = end(tip_n, slot(tip_row, tip_col), 0, tip_row == 3)
            q = jnp.where(flip == 1, 4 - r, r - 1)
            where, block = quarter(far, jnp.clip(q, 0, 3))
            before = jnp.where(r == 0, tip_pixel, end(n, where, block, flip == 0))
            q = jnp.where(flip == 1, 2 - r, r + 1)
            where, block = quarter(far, jnp.clip(q, 0, 3))
            after = jnp.where(r == 3, tip_pixel, end(n, where, block, flip == 1))

            edge = jnp.where(r < 2, 0, 2)
            code = code_ref[edge, f]
            far, flip = code >> 1, code & 1
            n = lax.rem(near_ref[edge, f], faces)
            part = c ^ flip
            for h in range(2):
                where, block = quarter(far, 2 * part + h)
                out[i, (1 + h) * size : (2 + h) * size] = held[where, n, block]
            where, block = quarter(far, jnp.where(part == 0, 2, 1))
            middle = end(n, where, block, part == 1)
            single = jnp.where(spot == 0, before, jnp.where(spot == 1, after, middle))
            out[i, 3 * size : 3 * size + EXTRA] = single.astype(BF)
            return carry

        lax.fori_loop(0, faces, face, 0)


def select_strips(neighbour_face, orientation, stores, groups):
    faces, _, size, ch = stores[0].shape
    shape = jax.ShapeDtypeStruct((faces, 3 * size + EXTRA, ch), BF)
    smem = pl.BlockSpec(memory_space=pltpu.SMEM)
    return pl.pallas_call(
        select_kernel,
        in_specs=[smem, smem] + [pl.BlockSpec(memory_space=pltpu.VMEM)] * 8,
        out_specs=(pl.BlockSpec(memory_space=pltpu.VMEM),) * groups,
        out_shape=(shape,) * groups,
        scratch_shapes=[pltpu.VMEM((8, faces, 3, size, ch), BF)],
        cost_estimate=pl.CostEstimate(flops=0, bytes_accessed=4 * 2**20, transcendentals=0),
        compiler_params=pltpu.CompilerParams(vmem_limit_bytes=10 * 2**20),
        name="select_strips",
    )(neighbour_face, orientation, *stores)


def ring_kernel(groups, coarse, near_ref, code_ref, x_ref, y_in, line_in, beside, diagonal, across,
                far_diagonal, turned, w_ref, b_ref, *refs):
    seams, refs = refs[:groups], refs[groups:]
    if coarse:
        c_ref, dw_ref, db_ref, _, _, y_out, c_out = refs[:7]
        y_ref = y_in
        scratch = refs[7:]
        *scratch, c_tiles, c_rows, c_cols, c_left, pair_rows, sems = scratch
    else:
        y_ref, outs, scratch = refs[0], refs[1:5], refs[5:]
    tiles, edge_rows, edge_cols, held, left, right, w_cols, across_taps, along_taps = scratch
    faces, rows, cols, ch = x_ref.shape
    me, r, c = lax.axis_index("face"), lax.axis_index("row"), lax.axis_index("col")
    for k in range(groups):
        held[k] = seams[k][...]

    def oriented(v, flip):
        n = v.shape[0]
        to = lax.broadcasted_iota(jnp.int32, (n, n), 0)
        source = lax.broadcasted_iota(jnp.int32, (n, n), 1)
        order = jnp.where(source == jnp.where(flip == 1, n - 1 - to, to), 1.0, 0.0).astype(BF)
        return jnp.dot(order, v, preferred_element_type=F32)

    even = lax.rem(r, 2) == 0
    outer = (r == 0) | (r == 3)
    for d in range(3):
        for a in range(3):
            w_cols[(3 * d + a) * ch : (3 * d + a + 1) * ch] = w_ref[a, d]
    bias = b_ref[...]

    def holder(n):
        return jnp.minimum(n, FACES - 1) // faces ^ me

    def put(taps, place, v, before, after, third):
        for k, part in enumerate(shifted(v, before, after)):
            start = (3 * third + k) * ch
            taps[pl.ds(place, v.shape[0]), start : start + ch] = part

    def face(i):
        f = me * faces + i
        edge = 3 - 2 * c
        n = near_ref[edge, f]
        corner = jnp.where(r < 2, c, 3 - c)
        tip_n = near_ref[4 + corner, f]
        seam_side = oriented(held[holder(n), i, 0:rows], code_ref[edge, f] & 1)
        extra = slice(3 * rows, 3 * rows + EXTRA)
        n_before = jnp.where(r == 0, tip_n, n)
        n_after = jnp.where(r == 3, tip_n, n)
        before = held[holder(n_before), i, extra].astype(F32)[0:1]
        after = held[holder(n_after), i, extra].astype(F32)[1:2]
        before = jnp.where(n_before < FACES, before, 0.0)
        after = jnp.where(n_after < FACES, after, 0.0)
        edge = jnp.where(r < 2, 0, 2)
        n = near_ref[edge, f]
        seam_line = oriented(held[holder(n), i, rows : 3 * rows], code_ref[edge, f] & 1)
        middle = held[holder(n), i, extra].astype(F32)[2:3]

        inner = beside[i, 3].astype(F32)
        block_line = jnp.concatenate([across[i, 1], across[i, 2]], axis=0).astype(F32)
        outward = jnp.where(outer, seam_line, block_line)
        inward = turned[i].astype(F32)
        top = jnp.where(even, outward, inward)
        bottom = jnp.where(even, inward, outward)
        lft = jnp.where(c == 0, seam_side, inner)
        rgt = jnp.where(c == 0, inner, seam_side)
        pair_inner = diagonal[i, 3].astype(F32)
        inward_corner = jnp.where(even, pair_inner[0:1], pair_inner[rows - 1 : rows])
        far_first = far_diagonal[i, 1].astype(F32)[0:1]
        far_last = far_diagonal[i, 2].astype(F32)[rows - 1 : rows]
        outward_corner = jnp.where(outer, middle, jnp.where(c == 0, far_first, far_last))
        inner_top = jnp.where(even, outward_corner, inward_corner)
        inner_bottom = jnp.where(even, inward_corner, outward_corner)
        top_left = jnp.where(c == 0, before, inner_top)
        top_right = jnp.where(c == 0, inner_top, before)
        bottom_left = jnp.where(c == 0, after, inner_bottom)
        bottom_right = jnp.where(c == 0, inner_bottom, after)

        row_0, row_1, row_2, row_3 = (
            x_ref[i, k].astype(F32) for k in (0, 1, rows - 2, rows - 1)
        )
        place = 2 * i * cols
        put(across_taps, place, top, top_left, top_right, 0)
        put(across_taps, place, row_0, lft[0:1], rgt[0:1], 1)
        put(across_taps, place, row_1, lft[1:2], rgt[1:2], 2)
        place += cols
        put(across_taps, place, row_2, lft[rows - 2 : rows - 1], rgt[rows - 2 : rows - 1], 0)
        put(across_taps, place, row_3, lft[rows - 1 : rows], rgt[rows - 1 : rows], 1)
        put(across_taps, place, bottom, bottom_left, bottom_right, 2)
        col_0, col_1, col_2, col_3 = (line_in[i, k].astype(F32) for k in range(4))
        place = 2 * i * rows
        put(along_taps, place, lft, top_left, bottom_left, 0)
        put(along_taps, place, col_0, top[0:1], bottom[0:1], 1)
        put(along_taps, place, col_1, top[1:2], bottom[1:2], 2)
        place += rows
        put(along_taps, place, col_2, top[cols - 2 : cols - 1], bottom[cols - 2 : cols - 1], 0)
        put(along_taps, place, col_3, top[cols - 1 : cols], bottom[cols - 1 : cols], 1)
        put(along_taps, place, rgt, top_right, bottom_right, 2)

    for i in range(faces):
        face(i)
    w_rows = w_ref[...].reshape(9 * ch, ch)
    out = gelu(jnp.dot(across_taps[...], w_rows, preferred_element_type=F32) + bias)
    edge_rows[...] = out.astype(BF).reshape(edge_rows.shape)
    out = gelu(jnp.dot(along_taps[...], w_cols[...], preferred_element_type=F32) + bias)
    edge_cols[...] = out.reshape(edge_cols.shape)
    between = slice(STEP, cols - STEP)

    def update(i, carry):
        new_top, new_bottom = edge_rows[i, 0].astype(F32), edge_rows[i, 1].astype(F32)
        if cols > 2 * STEP:
            y_ref[i, 0, between] = edge_rows[i, 0, between]
            y_ref[i, rows - 1, between] = edge_rows[i, 1, between]
        for tile, side, place in ((left, 0, 0), (right, 1, STEP - 1)):
            start = side * (cols - STEP)
            tiles[side, i] = y_ref[i, :, start : start + STEP]
            tiles[side, i, 0] = edge_rows[i, 0, start : start + STEP]
            tiles[side, i, rows - 1] = edge_rows[i, 1, start : start + STEP]
            tile[...] = tiles[side, i].astype(F32).reshape(rows * STEP, ch)
            tile[pl.ds(place, rows, stride=STEP), :] = edge_cols[i, pl.ds(side * rows, rows)]
            value = tile[...].astype(BF).reshape(rows, STEP, ch)
            if coarse:
                tiles[side, i] = value
            else:
                y_ref[i, :, start : start + STEP] = value
        if not coarse:
            lines = (
                column(left, 0), column(left, 1),
                column(right, STEP - 2), column(right, STEP - 1),
            )
            put_strips(i, r, c, lines, new_top, new_bottom, *outs)
            return carry
        w_down = dw_ref[...].reshape(4 * ch, -1)
        for k, (own, near) in enumerate(((new_top, 1), (new_bottom, rows - 2))):
            first = edge_cols[i, near : near + 1]
            last = edge_cols[i, rows + near : rows + near + 1]
            spot = lax.broadcasted_iota(jnp.int32, (cols, 1), 0)
            other = y_ref[i, near].astype(F32)
            other = jnp.where(spot == 0, first, jnp.where(spot == cols - 1, last, other))
            pair_rows[k] = own
            pair_rows[1 - k] = other.astype(BF).astype(F32)
            four = [
                pair_rows[a, pl.ds(d, cols // 2, stride=2), :].astype(BF)
                for a in range(2)
                for d in range(2)
            ]
            out = jnp.dot(jnp.concatenate(four, axis=1), w_down, preferred_element_type=F32)
            out = (out + db_ref[...]).astype(BF)
            c_rows[k, i] = out
        for side, (tile, place) in enumerate(((left, 0), (right, STEP - 2))):
            start = side * (cols // 2 - STEP)
            c_tiles[side, i] = c_ref[i, :, start : start + STEP]
            for k in range(2):
                c_tiles[side, i, k * (rows // 2 - 1)] = c_rows[k, i, start : start + STEP]
            four = [
                tile[pl.ds(a * STEP + place + d, rows // 2, stride=2 * STEP), :].astype(BF)
                for a in range(2)
                for d in range(2)
            ]
            out = jnp.dot(jnp.concatenate(four, axis=1), w_down, preferred_element_type=F32)
            c_cols[...] = out + db_ref[...]
            for h in range(c_cols.shape[1] // ch):
                lanes = slice(h * ch, (h + 1) * ch)
                c_left[...] = c_tiles[side, i, :, :, lanes].astype(F32).reshape(rows // 2 * STEP, ch)
                c_left[pl.ds(side * (STEP - 1), rows // 2, stride=STEP), :] = c_cols[:, lanes]
                c_tiles[side, i, :, :, lanes] = (
                    c_left[...].astype(BF).reshape(rows // 2, STEP, ch)
                )
        return carry

    lax.fori_loop(0, faces, update, 0)
    if not coarse:
        return
    copies = tile_copies(y_out, tiles, sems, back=True)
    if cols > 2 * STEP:
        between = pl.ds(STEP, cols - 2 * STEP)
        for k, row in enumerate((0, rows - 1)):
            copies.append(
                pltpu.make_async_copy(
                    edge_rows.at[:, k, between], y_out.at[:, row, between], sems.at[2 + k]
                )
            )
    half = cols // 2
    for side, start in enumerate((0, half - STEP)):
        copies.append(
            pltpu.make_async_copy(
                c_tiles.at[side], c_out.at[:, :, pl.ds(start, STEP), :], sems.at[4 + side]
            )
        )
    if half > 2 * STEP:
        between = pl.ds(STEP, half - 2 * STEP)
        for k, row in enumerate((0, rows // 2 - 1)):
            copies.append(
                pltpu.make_async_copy(
                    c_rows.at[k, :, between], c_out.at[:, row, between], sems.at[6 + k]
                )
            )
    for copy in copies:
        copy.start()
    for copy in copies:
        copy.wait()


def ring(neighbour_face, orientation, x, buffers, copied, lines, parts, weight, bias, seams, down):
    y, *coarse = buffers
    faces, rows, cols, ch = x.shape
    groups = len(seams)
    smem = pl.BlockSpec(memory_space=pltpu.SMEM)
    hbm = pl.BlockSpec(memory_space=pltpu.HBM)
    vmem = pl.BlockSpec(memory_space=pltpu.VMEM)
    args = [neighbour_face, orientation, x, y, lines, *parts, weight, bias, *seams]
    in_specs = [smem, smem] + [vmem] * (len(args) - 2)
    scratch = [
        pltpu.VMEM((2, faces, rows, STEP, ch), BF),
        pltpu.VMEM((faces, 2, cols, ch), BF),
        pltpu.VMEM((faces, 2 * rows, ch), F32),
        pltpu.VMEM((groups, faces, 3 * rows + EXTRA, ch), BF),
        pltpu.VMEM((rows * STEP, ch), F32),
        pltpu.VMEM((rows * STEP, ch), F32),
        pltpu.VMEM((9 * ch, ch), BF),
        pltpu.VMEM((2 * faces * cols, 9 * ch), BF),
        pltpu.VMEM((2 * faces * rows, 9 * ch), BF),
    ]
    if down:
        co = down[0].shape[-1]
        args += [coarse[0], *down]
        in_specs += [vmem] * 3
        aliases = {len(args): 0, len(args) + 1: 1}
        args += [in_hbm(buffer) for buffer in copied]
        in_specs += [hbm] * 2
        out_shape = [pltpu.HBM(buffer.shape, BF) for buffer in copied]
        out_specs = [hbm] * 2
        scratch += [
            pltpu.VMEM((2, faces, rows // 2, STEP, co), BF),
            pltpu.VMEM((2, faces, cols // 2, co), BF),
            pltpu.VMEM((rows // 2, co), F32),
            pltpu.VMEM((rows // 2 * STEP, ch), F32),
            pltpu.VMEM((2, cols, ch), F32),
            pltpu.SemaphoreType.DMA((8,)),
        ]
    else:
        aliases = {3: 0}
        out_shape = [jax.ShapeDtypeStruct(y.shape, BF), *strip_shapes(faces, rows, cols, ch)]
        out_specs = [vmem] * 5
    return pl.pallas_call(
        functools.partial(ring_kernel, groups, bool(down)),
        in_specs=in_specs,
        out_specs=tuple(out_specs),
        out_shape=tuple(out_shape),
        scratch_shapes=scratch,
        input_output_aliases=aliases,
        cost_estimate=pl.CostEstimate(
            flops=faces * (rows + cols) * 36 * ch * ch, bytes_accessed=8 * 2**20, transcendentals=0
        ),
        compiler_params=pltpu.CompilerParams(vmem_limit_bytes=20 * 2**20),
        name="ring",
    )(*args)


def blocks(change_row, change_col):
    cols = lax.axis_size("col")
    return [
        (r * cols + c, (r ^ change_row) * cols + (c ^ change_col))
        for r in range(lax.axis_size("row"))
        for c in range(cols)
    ]


def swap(v, change_row, change_col):
    return lax.ppermute(v, ("row", "col"), blocks(change_row, change_col))


def level(neighbour_face, orientation, x, strips, weight, bias, down):
    u, v, turn, lines = strips
    groups = lax.axis_size("face")
    total = x.shape[0] * x.shape[1] // STEP
    early, late = max(total // 3, 1), max(total * 5 // 12, 2)
    piece = functools.partial(conv_piece, x, weight, bias, down=down)
    beside, across, diagonal = swap(u, 0, 1), swap(v, 3, 0), swap(v, 3, 1)
    pair, turned = swap(v, 1, 0), swap(turn, 1, 0)
    state = piece(0, early, None)
    (beside, across, diagonal), state = lax.optimization_barrier(
        ((beside, across, diagonal), state)
    )
    pair_beside, pair_across, pair_diagonal = (swap(a, 1, 0) for a in (beside, across, diagonal))
    state = piece(early, late - early, state)
    stores = (v, beside, pair, pair_beside, pair_across, pair_diagonal, across, diagonal)
    picked = select_strips(neighbour_face, orientation, stores, groups)
    picked, state = lax.optimization_barrier((picked, state))
    seams = [picked[0]]
    for k in range(1, groups):
        seams.append(lax.ppermute(picked[k], "face", [(g, g ^ k) for g in range(groups)]))
    _, buffers, copied = piece(late, total - late, state)
    parts = (beside, pair_beside, across, diagonal, turned)
    return ring(
        neighbour_face, orientation, x, buffers, copied, lines, parts, weight, bias, seams, down
    )


def per_device(
    field, conv1_w, conv1_b, conv2_w, conv2_b, down_w, down_b, neighbour_face, orientation
):
    tables = (neighbour_face.T, orientation.T)
    hidden, *strips = level(*tables, field, strips_of(field), conv1_w, conv1_b[None], ())
    return level(*tables, hidden, strips, conv2_w, conv2_b[None], (down_w, down_b[None]))


def solution(mesh):
    groups = mesh.shape["face"]
    fast = mesh.shape["row"] == 4 and mesh.shape["col"] == 2 and groups & (groups - 1) == 0
    return jax.shard_map(
        per_device if fast else general_device,
        mesh=mesh,
        in_specs=(P("face", "row", "col", None), P(), P(), P(), P(), P(), P(), P(), P()),
        out_specs=(P("face", "row", "col", None), P("face", "row", "col", None)),
        check_vma=False,
    )
```

```python
import functools

import jax
import jax.numpy as jnp
import numpy as np
from jax import lax
from jax.experimental import pallas as pl
from jax.experimental.pallas import tpu as pltpu
from jax.sharding import PartitionSpec as P


FACES = 12
BF = jnp.bfloat16
F32 = jnp.float32
STEP = 16
EXTRA = 16

layout = ("NHWC", "HWIO", "NHWC")


def padded_2(block, sides, width):
    for axis, dim in sides:
        count = lax.axis_size(axis)
        forward = [(i, i + 1) for i in range(count - 1)]
        backward = [(target, source) for source, target in forward]
        low = lax.ppermute(
            lax.slice_in_dim(block, block.shape[dim] - width, None, axis=dim), axis, forward
        )
        high = lax.ppermute(lax.slice_in_dim(block, 0, width, axis=dim), axis, backward)
        block = jnp.concatenate([low, block, high], axis=dim)
    return block


def seam_parts(edges, neighbours, codes):
    seam_faces = neighbours[:, :4]
    seam_codes = codes[:, :4]
    seams = edges[seam_faces, seam_codes // 2]
    seams = jnp.where((seam_codes % 2 == 1)[:, :, None, None], seams[:, :, ::-1], seams)
    corner_values = jnp.stack(
        [edges[:, 0, 0], edges[:, 0, -1], edges[:, 2, -1], edges[:, 2, 0]], axis=1
    )
    corner_faces = neighbours[:, 4:]
    picked = corner_values[jnp.minimum(corner_faces, FACES - 1), codes[:, 4:]]
    picked = jnp.where((corner_faces < FACES)[:, :, None], picked, jnp.zeros_like(picked))
    return (seams, picked)


def convolve(padded, weight, bias):
    summed = lax.conv_general_dilated(
        padded,
        weight,
        (1, 1),
        "VALID",
        dimension_numbers=layout,
        preferred_element_type=jnp.float32,
    )
    return jax.nn.gelu(summed + bias, approximate=False).astype(jnp.bfloat16)


def general_layer(block, weight, bias, neighbour_face, orientation):
    face_count, row_size, col_size, channels = block.shape
    row_total = lax.axis_size("row")
    col_total = lax.axis_size("col")
    row_place = lax.axis_index("row")
    col_place = lax.axis_index("col")
    face_side = row_size * row_total
    padded = padded_2(block, (("row", 1), ("col", 2)), 1)
    top_live = row_place == 0
    bottom_live = row_place == row_total - 1
    left_live = col_place == 0
    right_live = col_place == col_total - 1
    empty_line = jnp.zeros((face_count, face_side, channels), jnp.float32)

    def place(strip, offset, live):
        scaled = strip.astype(jnp.float32) * live.astype(jnp.float32)
        return lax.dynamic_update_slice_in_dim(empty_line, scaled, offset, 1)

    lines = jnp.stack(
        [
            place(block[:, 0], col_place * col_size, top_live),
            place(block[:, :, -1], row_place * row_size, right_live),
            place(block[:, -1], col_place * col_size, bottom_live),
            place(block[:, :, 0], row_place * row_size, left_live),
        ],
        axis=1,
    )
    complete = lax.psum(lax.psum(lines.astype(jnp.bfloat16), "col"), "row").astype(jnp.float32)
    every_edge = lax.all_gather(complete.astype(jnp.bfloat16), "face", axis=0, tiled=True)
    first_face = lax.axis_index("face") * face_count
    own_faces = lax.dynamic_slice_in_dim(neighbour_face, first_face, face_count, 0)
    own_codes = lax.dynamic_slice_in_dim(orientation, first_face, face_count, 0)
    seams, corners = seam_parts(every_edge, own_faces, own_codes)
    upper = jnp.concatenate([corners[:, 0:1], seams[:, 0], corners[:, 1:2]], 1)
    lower = jnp.concatenate([corners[:, 3:4], seams[:, 2], corners[:, 2:3]], 1)
    leftward = jnp.concatenate([corners[:, 0:1], seams[:, 3], corners[:, 3:4]], 1)
    rightward = jnp.concatenate([corners[:, 1:2], seams[:, 1], corners[:, 2:3]], 1)
    upper_cut = lax.dynamic_slice_in_dim(upper, col_place * col_size, col_size + 2, 1)
    lower_cut = lax.dynamic_slice_in_dim(lower, col_place * col_size, col_size + 2, 1)
    left_cut = lax.dynamic_slice_in_dim(leftward, row_place * row_size, row_size + 2, 1)
    right_cut = lax.dynamic_slice_in_dim(rightward, row_place * row_size, row_size + 2, 1)
    padded = padded.at[:, 0].set(jnp.where(top_live, upper_cut, padded[:, 0]))
    padded = padded.at[:, -1].set(jnp.where(bottom_live, lower_cut, padded[:, -1]))
    padded = padded.at[:, :, 0].set(jnp.where(left_live, left_cut, padded[:, :, 0]))
    padded = padded.at[:, :, -1].set(jnp.where(right_live, right_cut, padded[:, :, -1]))
    return convolve(padded, weight, bias)


def general_device(
    field, conv1_w, conv1_b, conv2_w, conv2_b, down_w, down_b, neighbour_face, orientation
):
    hidden = general_layer(field, conv1_w, conv1_b, neighbour_face, orientation)
    skip = general_layer(hidden, conv2_w, conv2_b, neighbour_face, orientation)
    summed = lax.conv_general_dilated(
        skip, down_w, (2, 2), "VALID", dimension_numbers=layout, preferred_element_type=jnp.float32
    )
    coarse = (summed + down_b).astype(jnp.bfloat16)
    return (skip, coarse)


def gelu(v):
    return 0.5 * v * (1.0 + lax.erf(v * np.float32(np.sqrt(0.5))))


def shifted(v, before, after):
    n = v.shape[0]
    spot = lax.broadcasted_iota(jnp.int32, (n, 1), 0)
    low = jnp.where(spot == 0, before, pltpu.roll(v, 1, 0))
    high = jnp.where(spot == n - 1, after, pltpu.roll(v, n - 1, 0))
    return low.astype(BF), v.astype(BF), high.astype(BF)


def parting(n):
    to = lax.broadcasted_iota(jnp.int32, (n, n), 0)
    source = lax.broadcasted_iota(jnp.int32, (n, n), 1)
    half = n // 2
    return jnp.where(source == jnp.where(to < half, 2 * to, 2 * (to - half) + 1), 1.0, 0.0).astype(BF)


def parted(order, v):
    v = jnp.dot(order, v, preferred_element_type=F32).astype(BF)
    half, lanes = v.shape[0] // 2, v.shape[1] // 2
    return v[:half, :lanes], v[:half, lanes:], v[half:, :lanes], v[half:, lanes:]


def conv_kernel(first, count, build, coarse, x_ref, b_ref, *refs):
    if coarse:
        dw_ref, db_ref, refs = refs[0], refs[1], refs[2:]
        *refs, y_out, c_out, taps_0, taps_1, wide, sems = refs
        if build:
            w_ref, y_ref, c_ref, w_low, w_high = refs[0], *refs[1:]
        else:
            w_low, w_high, y_ref, c_ref = refs[0], refs[1], *refs[6:8]
    else:
        *refs, taps_0, taps_1 = refs
        if build:
            w_ref, y_ref, w_low, w_high = refs
        else:
            w_low, w_high, _, y_ref = refs
    _, size, cols, ch = x_ref.shape
    steps = size // STEP
    pairs = STEP // 2
    zero_row = jnp.zeros((1, ch), F32)
    half = 3 * ch

    if build:
        zero = jnp.zeros((ch, ch), BF)
        for d in range(3):
            one = slice(d * ch, (d + 1) * ch)
            two = slice(half + d * ch, half + (d + 1) * ch)
            w_low[one, :ch] = w_ref[0, d]
            w_low[one, ch:] = zero
            w_low[two, :ch] = w_ref[1, d]
            w_low[two, ch:] = w_ref[0, d]
            w_high[one, :ch] = w_ref[2, d]
            w_high[one, ch:] = w_ref[1, d]
            w_high[two, :ch] = zero
            w_high[two, ch:] = w_ref[2, d]

    if coarse:
        order = parting(cols)

    def at(t):
        return t // steps, lax.rem(t, steps)

    def fill(taps, t):
        face, step = at(t)
        base = step * STEP

        def put(v, pair, side):
            low, same, high = shifted(v.astype(F32), zero_row, zero_row)
            place = side * half
            taps[pair, :, place : place + ch] = low
            taps[pair, :, place + ch : place + 2 * ch] = same
            taps[pair, :, place + 2 * ch : place + 3 * ch] = high

        inside = (step > 0).astype(F32)
        put(x_ref[face, jnp.maximum(base - 1, 0)].astype(F32) * inside, 0, 0)
        for row in range(STEP):
            put(x_ref[face, base + row], (row + 1) // 2, (row + 1) % 2)
        inside = (step < steps - 1).astype(F32)
        put(x_ref[face, jnp.minimum(base + STEP, size - 1)].astype(F32) * inside, pairs, 1)

    def product(taps, t):
        face, step = at(t)
        base = step * STEP
        lower = taps[pl.ds(0, pairs)].reshape(pairs * cols, 2 * half)
        upper = taps[pl.ds(1, pairs)].reshape(pairs * cols, 2 * half)
        total = jnp.dot(lower, w_low[...], preferred_element_type=F32)
        total += jnp.dot(upper, w_high[...], preferred_element_type=F32)
        total = total.reshape(pairs, cols, 2 * ch)
        bias = b_ref[...]
        outs = []
        for side in range(2):
            out = gelu(total[:, :, side * ch : (side + 1) * ch] + bias[None]).astype(BF)
            for pair in range(pairs):
                y_ref[face, base + 2 * pair + side] = out[pair]
            outs.append(out)
        if not coarse:
            return
        for pair in range(pairs):
            four = parted(order, jnp.concatenate([out[pair] for out in outs], axis=1))
            wide[pair] = jnp.concatenate([four[k] for k in (0, 2, 1, 3)], axis=1)
        out = jnp.dot(
            wide[...].reshape(pairs * cols // 2, 4 * ch),
            dw_ref[...].reshape(4 * ch, -1),
            preferred_element_type=F32,
        )
        out = (out + db_ref[...]).astype(BF)
        c_ref[face, pl.ds(step * pairs, pairs)] = out.reshape(pairs, cols // 2, -1)

    def copies(t):
        face, step = at(t)
        rows, cells = pl.ds(step * STEP, STEP), pl.ds(step * pairs, pairs)
        return (
            pltpu.make_async_copy(y_ref.at[face, rows], y_out.at[face, rows], sems.at[0]),
            pltpu.make_async_copy(c_ref.at[face, cells], c_out.at[face, cells], sems.at[1]),
        )

    def finish(taps, t):
        product(taps, t)
        if coarse:
            for copy in copies(t):
                copy.start()

    last = first + count - 1
    fill(taps_0, first)

    def double(j, carry):
        t = first + 2 * j
        fill(taps_1, t + 1)
        finish(taps_0, t)
        fill(taps_0, jnp.minimum(t + 2, last))
        finish(taps_1, t + 1)
        return carry

    lax.fori_loop(0, count // 2, double, 0)
    if count % 2:
        finish(taps_0, last)
    if coarse:

        def wait(t, carry):
            for copy in copies(t):
                copy.wait()
            return carry

        lax.fori_loop(first, first + count, wait, 0)


def in_hbm(x):
    return pltpu.with_memory_space_constraint(x, pltpu.HBM)


def conv_piece(x, weight, bias, first, count, state, down):
    faces, rows, cols, ch = x.shape
    vmem = pl.BlockSpec(memory_space=pltpu.VMEM)
    hbm = pl.BlockSpec(memory_space=pltpu.HBM)
    build = state is None
    args = [x, bias] + list(down)
    in_specs = [vmem] * len(args)
    taps = (STEP // 2 + 1, cols, 6 * ch)
    arranged = jax.ShapeDtypeStruct((6 * ch, 2 * ch), BF)
    out_shape = [jax.ShapeDtypeStruct(x.shape, BF)]
    out_specs = [vmem]
    scratch = [pltpu.VMEM(taps, BF), pltpu.VMEM(taps, BF)]
    flops = 24 * ch * ch
    if down:
        co = down[0].shape[-1]
        out_shape.append(jax.ShapeDtypeStruct((faces, rows // 2, cols // 2, co), BF))
        out_specs.append(vmem)
        scratch += [pltpu.VMEM((STEP // 2, cols // 2, 4 * ch), BF), pltpu.SemaphoreType.DMA((2,))]
        flops += 2 * ch * co
    aliases = {}
    if build:
        args.append(weight)
        in_specs.append(vmem)
        out_shape += [arranged] * 2
        out_specs += [vmem] * 2
    else:
        weights, buffers, copied = state
        args += list(weights)
        in_specs += [vmem] * 2
        for buffer in buffers:
            aliases[len(args)] = len(aliases)
            args.append(buffer)
            in_specs.append(vmem)
        for buffer in copied:
            aliases[len(args)] = len(aliases)
            args.append(in_hbm(buffer))
            in_specs.append(hbm)
    if down:
        out_shape += [pltpu.HBM(s.shape, BF) for s in out_shape[:2]]
        out_specs += [hbm] * 2
    pixels = count * STEP * cols
    out = pl.pallas_call(
        functools.partial(conv_kernel, first, count, build, bool(down)),
        in_specs=in_specs,
        out_specs=tuple(out_specs),
        out_shape=tuple(out_shape),
        scratch_shapes=scratch,
        input_output_aliases=aliases,
        cost_estimate=pl.CostEstimate(
            flops=pixels * flops, bytes_accessed=4 * pixels * ch, transcendentals=0
        ),
        compiler_params=pltpu.CompilerParams(vmem_limit_bytes=16 * 2**20),
        name="conv_piece",
    )(*args)
    kept = 2 if down else 1
    if build:
        weights = out[kept : kept + 2]
        copied = out[kept + 2 :]
    else:
        copied = out[kept:]
    return tuple(weights), tuple(out[:kept]), tuple(copied)


def column(tile, place):
    return tile[pl.ds(place, tile.shape[0] // STEP, stride=STEP), :]


def put_strips(i, r, c, lines, top, bottom, u_ref, v_ref, turn_ref, line_ref):
    left, left_in, right_in, right = lines
    size = left.shape[0]
    for place, value in enumerate(lines):
        line_ref[i, place] = value.astype(BF)
    side = jnp.where(c == 0, left, right).astype(BF)
    inner = jnp.where(c == 0, right, left).astype(BF)
    even = lax.rem(r, 2) == 0
    line = jnp.where(even, top, bottom).astype(BF)
    turn_ref[i] = jnp.where(even, bottom, top).astype(BF)
    for ref in (u_ref, v_ref):
        ref[i, 0] = side
        ref[i, 1] = line[:size]
        ref[i, 2] = line[size:]
    u_ref[i, 3] = inner


def strip_shapes(faces, rows, cols, ch):
    return (
        jax.ShapeDtypeStruct((faces, 4, rows, ch), BF),
        jax.ShapeDtypeStruct((faces, 3, rows, ch), BF),
        jax.ShapeDtypeStruct((faces, cols, ch), BF),
        jax.ShapeDtypeStruct((faces, 4, rows, ch), BF),
    )


def whole(shape):
    return pl.BlockSpec(shape, lambda *_: (0,) * len(shape))


def tile_copies(array, tiles, sems, back=False):
    cols = array.shape[2]
    out = []
    for side, start in enumerate((0, cols - STEP)):
        far, near = array.at[:, :, pl.ds(start, STEP), :], tiles.at[side]
        out.append(pltpu.make_async_copy(*((near, far) if back else (far, near)), sems.at[side]))
    return out


def strips_kernel(x_ref, u_ref, v_ref, turn_ref, line_ref, tiles, outer, left, right, sems):
    faces, rows, cols, ch = x_ref.shape
    r, c = lax.axis_index("row"), lax.axis_index("col")
    copies = tile_copies(x_ref, tiles, sems)
    for k, row in enumerate((0, rows - 1)):
        copies.append(pltpu.make_async_copy(x_ref.at[:, row], outer.at[k], sems.at[2 + k]))
    for copy in copies:
        copy.start()
    for copy in copies:
        copy.wait()

    def face(i, carry):
        left[...] = tiles[0, i].astype(F32).reshape(rows * STEP, ch)
        right[...] = tiles[1, i].astype(F32).reshape(rows * STEP, ch)
        lines = (column(left, 0), column(left, 1), column(right, STEP - 2), column(right, STEP - 1))
        put_strips(
            i, r, c, lines, outer[0, i].astype(F32), outer[1, i].astype(F32),
            u_ref, v_ref, turn_ref, line_ref,
        )
        return carry

    lax.fori_loop(0, faces, face, 0)


def strips_of(x):
    faces, rows, cols, ch = x.shape
    shapes = strip_shapes(faces, rows, cols, ch)
    return pl.pallas_call(
        strips_kernel,
        in_specs=[pl.BlockSpec(memory_space=pltpu.HBM)],
        out_specs=(pl.BlockSpec(memory_space=pltpu.VMEM),) * 4,
        out_shape=shapes,
        scratch_shapes=[
            pltpu.VMEM((2, faces, rows, STEP, ch), BF),
            pltpu.VMEM((2, faces, cols, ch), BF),
            pltpu.VMEM((rows * STEP, ch), F32),
            pltpu.VMEM((rows * STEP, ch), F32),
            pltpu.SemaphoreType.DMA((4,)),
        ],
        cost_estimate=pl.CostEstimate(flops=0, bytes_accessed=4 * 2**20, transcendentals=0),
        compiler_params=pltpu.CompilerParams(vmem_limit_bytes=10 * 2**20),
        name="strips_of",
    )(in_hbm(x))


def select_kernel(near_ref, code_ref, *refs):
    stores, held = refs[:8], refs[-1]
    outs = [refs[k : k + 2] for k in range(8, len(refs) - 1, 2)]
    faces, _, size, ch = held.shape[1:]
    me, r, c = lax.axis_index("face"), lax.axis_index("row"), lax.axis_index("col")
    for k, store in enumerate(stores):
        for i in range(faces):
            held[k, i] = store[i, 0:3]

    def slot(row, col):
        return ((r ^ row) << 1) | (c ^ col)

    def quarter(edge, q):
        upright = lax.rem(edge, 2) == 1
        row = jnp.where(upright, q, jnp.where(edge == 0, 0, 3))
        col = jnp.where(upright, jnp.where(edge == 3, 0, 1), q >> 1)
        return slot(row, col), jnp.where(upright, 0, 1 + (q & 1))

    def end(n, where, block, last):
        head = held[where, n, block, 0:EXTRA].astype(F32)
        tail = held[where, n, block, size - EXTRA : size].astype(F32)
        return jnp.where(last, tail[EXTRA - 1 : EXTRA], head[0:1])

    spot = lax.broadcasted_iota(jnp.int32, (EXTRA, 1), 0)
    for k, (out, out_line) in enumerate(outs):
        target = me ^ k

        def face(i, carry, out=out, out_line=out_line, target=target):
            f = target * faces + i
            edge = 3 - 2 * c
            code = code_ref[edge, f]
            far, flip = code >> 1, code & 1
            n = lax.rem(near_ref[edge, f], faces)
            where, block = quarter(far, jnp.where(flip == 1, 3 - r, r))
            out[i, 0:size] = held[where, n, block]
            corner = jnp.where(r < 2, c, 3 - c)
            tip = code_ref[4 + corner, f]
            tip_n = lax.rem(near_ref[4 + corner, f], faces)
            tip_row = jnp.where(tip < 2, 0, 3)
            tip_col = jnp.where((tip == 1) | (tip == 2), 1, 0)
            tip_pixel = end(tip_n, slot(tip_row, tip_col), 0, tip_row == 3)
            q = jnp.where(flip == 1, 4 - r, r - 1)
            where, block = quarter(far, jnp.clip(q, 0, 3))
            before = jnp.where(r == 0, tip_pixel, end(n, where, block, flip == 0))
            q = jnp.where(flip == 1, 2 - r, r + 1)
            where, block = quarter(far, jnp.clip(q, 0, 3))
            after = jnp.where(r == 3, tip_pixel, end(n, where, block, flip == 1))

            edge = jnp.where(r < 2, 0, 2)
            code = code_ref[edge, f]
            far, flip = code >> 1, code & 1
            n = lax.rem(near_ref[edge, f], faces)
            part = c ^ flip
            for h in range(2):
                where, block = quarter(far, 2 * part + h)
                out_line[i, h * size : (h + 1) * size] = held[where, n, block]
            where, block = quarter(far, jnp.where(part == 0, 2, 1))
            middle = end(n, where, block, part == 1)
            single = jnp.where(spot == 0, before, jnp.where(spot == 1, after, middle))
            out[i, size : size + EXTRA] = single.astype(BF)
            return carry

        lax.fori_loop(0, faces, face, 0)


def select_strips(neighbour_face, orientation, stores, groups):
    faces, _, size, ch = stores[0].shape
    shapes = tuple(jax.ShapeDtypeStruct((faces, n, ch), BF) for n in (size + EXTRA, 2 * size))
    smem = pl.BlockSpec(memory_space=pltpu.SMEM)
    return pl.pallas_call(
        select_kernel,
        in_specs=[smem, smem] + [pl.BlockSpec(memory_space=pltpu.VMEM)] * 8,
        out_specs=(pl.BlockSpec(memory_space=pltpu.VMEM),) * (2 * groups),
        out_shape=shapes * groups,
        scratch_shapes=[pltpu.VMEM((8, faces, 3, size, ch), BF)],
        cost_estimate=pl.CostEstimate(flops=0, bytes_accessed=4 * 2**20, transcendentals=0),
        compiler_params=pltpu.CompilerParams(vmem_limit_bytes=10 * 2**20),
        name="select_strips",
    )(neighbour_face, orientation, *stores)


def ring_kernel(groups, coarse, near_ref, code_ref, x_ref, y_in, line_in, beside, diagonal, across,
                far_diagonal, turned, w_ref, b_ref, *refs):
    seams, refs = refs[: 2 * groups], refs[2 * groups :]
    if coarse:
        c_ref, dw_ref, db_ref, _, _, y_out, c_out = refs[:7]
        y_ref = y_in
        scratch = refs[7:]
        *scratch, c_tiles, c_rows, c_cols, c_left, sems = scratch
    else:
        y_ref, outs, scratch = refs[0], refs[1:5], refs[5:]
    tiles, edge_rows, edge_cols, held, held_line, left, right, w_cols, across_taps, along_taps = scratch
    faces, rows, cols, ch = x_ref.shape
    me, r, c = lax.axis_index("face"), lax.axis_index("row"), lax.axis_index("col")
    for k in range(groups):
        held[k] = seams[2 * k][...]
        held_line[k] = seams[2 * k + 1][...]

    def oriented(v, flip):
        n = v.shape[0]
        to = lax.broadcasted_iota(jnp.int32, (n, n), 0)
        source = lax.broadcasted_iota(jnp.int32, (n, n), 1)
        order = jnp.where(source == jnp.where(flip == 1, n - 1 - to, to), 1.0, 0.0).astype(BF)
        return jnp.dot(order, v, preferred_element_type=F32)

    even = lax.rem(r, 2) == 0
    outer = (r == 0) | (r == 3)
    for d in range(3):
        for a in range(3):
            w_cols[(3 * d + a) * ch : (3 * d + a + 1) * ch] = w_ref[a, d]
    bias = b_ref[...]

    def holder(n):
        return jnp.minimum(n, FACES - 1) // faces ^ me

    def put(taps, place, v, before, after, third):
        for k, part in enumerate(shifted(v, before, after)):
            start = (3 * third + k) * ch
            taps[pl.ds(place, v.shape[0]), start : start + ch] = part

    def face(i):
        f = me * faces + i
        edge = 3 - 2 * c
        n = near_ref[edge, f]
        corner = jnp.where(r < 2, c, 3 - c)
        tip_n = near_ref[4 + corner, f]
        seam_side = oriented(held[holder(n), i, 0:rows], code_ref[edge, f] & 1)
        extra = slice(rows, rows + EXTRA)
        n_before = jnp.where(r == 0, tip_n, n)
        n_after = jnp.where(r == 3, tip_n, n)
        before = held[holder(n_before), i, extra].astype(F32)[0:1]
        after = held[holder(n_after), i, extra].astype(F32)[1:2]
        before = jnp.where(n_before < FACES, before, 0.0)
        after = jnp.where(n_after < FACES, after, 0.0)
        edge = jnp.where(r < 2, 0, 2)
        n = near_ref[edge, f]
        seam_line = oriented(held_line[holder(n), i], code_ref[edge, f] & 1)
        middle = held[holder(n), i, extra].astype(F32)[2:3]

        inner = beside[i, 3].astype(F32)
        block_line = jnp.concatenate([across[i, 1], across[i, 2]], axis=0).astype(F32)
        outward = jnp.where(outer, seam_line, block_line)
        inward = turned[i].astype(F32)
        top = jnp.where(even, outward, inward)
        bottom = jnp.where(even, inward, outward)
        lft = jnp.where(c == 0, seam_side, inner)
        rgt = jnp.where(c == 0, inner, seam_side)
        pair_inner = diagonal[i, 3].astype(F32)
        inward_corner = jnp.where(even, pair_inner[0:1], pair_inner[rows - 1 : rows])
        far_first = far_diagonal[i, 1].astype(F32)[0:1]
        far_last = far_diagonal[i, 2].astype(F32)[rows - 1 : rows]
        outward_corner = jnp.where(outer, middle, jnp.where(c == 0, far_first, far_last))
        inner_top = jnp.where(even, outward_corner, inward_corner)
        inner_bottom = jnp.where(even, inward_corner, outward_corner)
        top_left = jnp.where(c == 0, before, inner_top)
        top_right = jnp.where(c == 0, inner_top, before)
        bottom_left = jnp.where(c == 0, after, inner_bottom)
        bottom_right = jnp.where(c == 0, inner_bottom, after)

        row_0, row_1, row_2, row_3 = (
            x_ref[i, k].astype(F32) for k in (0, 1, rows - 2, rows - 1)
        )
        place = 2 * i * cols
        put(across_taps, place, top, top_left, top_right, 0)
        put(across_taps, place, row_0, lft[0:1], rgt[0:1], 1)
        put(across_taps, place, row_1, lft[1:2], rgt[1:2], 2)
        place += cols
        put(across_taps, place, row_2, lft[rows - 2 : rows - 1], rgt[rows - 2 : rows - 1], 0)
        put(across_taps, place, row_3, lft[rows - 1 : rows], rgt[rows - 1 : rows], 1)
        put(across_taps, place, bottom, bottom_left, bottom_right, 2)
        col_0, col_1, col_2, col_3 = (line_in[i, k].astype(F32) for k in range(4))
        place = 2 * i * rows
        put(along_taps, place, lft, top_left, bottom_left, 0)
        put(along_taps, place, col_0, top[0:1], bottom[0:1], 1)
        put(along_taps, place, col_1, top[1:2], bottom[1:2], 2)
        place += rows
        put(along_taps, place, col_2, top[cols - 2 : cols - 1], bottom[cols - 2 : cols - 1], 0)
        put(along_taps, place, col_3, top[cols - 1 : cols], bottom[cols - 1 : cols], 1)
        put(along_taps, place, rgt, top_right, bottom_right, 2)

    for i in range(faces):
        face(i)
    w_rows = w_ref[...].reshape(9 * ch, ch)
    out = gelu(jnp.dot(across_taps[...], w_rows, preferred_element_type=F32) + bias)
    edge_rows[...] = out.astype(BF).reshape(edge_rows.shape)
    out = gelu(jnp.dot(along_taps[...], w_cols[...], preferred_element_type=F32) + bias)
    edge_cols[...] = out.reshape(edge_cols.shape)
    between = slice(STEP, cols - STEP)
    if coarse:
        order_cols, order_rows = parting(cols), parting(rows)

    def update(i, carry):
        new_top, new_bottom = edge_rows[i, 0].astype(F32), edge_rows[i, 1].astype(F32)
        if cols > 2 * STEP:
            y_ref[i, 0, between] = edge_rows[i, 0, between]
            y_ref[i, rows - 1, between] = edge_rows[i, 1, between]
        for tile, side, place in ((left, 0, 0), (right, 1, STEP - 1)):
            start = side * (cols - STEP)
            tiles[side, i] = y_ref[i, :, start : start + STEP]
            tiles[side, i, 0] = edge_rows[i, 0, start : start + STEP]
            tiles[side, i, rows - 1] = edge_rows[i, 1, start : start + STEP]
            tile[...] = tiles[side, i].astype(F32).reshape(rows * STEP, ch)
            tile[pl.ds(place, rows, stride=STEP), :] = edge_cols[i, pl.ds(side * rows, rows)]
            value = tile[...].astype(BF).reshape(rows, STEP, ch)
            if coarse:
                tiles[side, i] = value
            else:
                y_ref[i, :, start : start + STEP] = value
        if not coarse:
            lines = (
                column(left, 0), column(left, 1),
                column(right, STEP - 2), column(right, STEP - 1),
            )
            put_strips(i, r, c, lines, new_top, new_bottom, *outs)
            return carry
        w_down = dw_ref[...].reshape(4 * ch, -1)
        for k, (own, near) in enumerate(((new_top, 1), (new_bottom, rows - 2))):
            first = edge_cols[i, near : near + 1]
            last = edge_cols[i, rows + near : rows + near + 1]
            spot = lax.broadcasted_iota(jnp.int32, (cols, 1), 0)
            other = y_ref[i, near].astype(F32)
            other = jnp.where(spot == 0, first, jnp.where(spot == cols - 1, last, other))
            both = (own, other) if k == 0 else (other, own)
            both = jnp.concatenate([v.astype(BF) for v in both], axis=1)
            four = parted(order_cols, both)
            four = jnp.concatenate([four[j] for j in (0, 2, 1, 3)], axis=1)
            out = jnp.dot(four, w_down, preferred_element_type=F32)
            out = (out + db_ref[...]).astype(BF)
            c_rows[k, i] = out
        for side, (tile, place) in enumerate(((left, 0), (right, STEP - 2))):
            start = side * (cols // 2 - STEP)
            c_tiles[side, i] = c_ref[i, :, start : start + STEP]
            for k in range(2):
                c_tiles[side, i, k * (rows // 2 - 1)] = c_rows[k, i, start : start + STEP]
            both = [column(tile, place + d).astype(BF) for d in range(2)]
            four = parted(order_rows, jnp.concatenate(both, axis=1))
            out = jnp.dot(jnp.concatenate(four, axis=1), w_down, preferred_element_type=F32)
            c_cols[...] = out + db_ref[...]
            for h in range(c_cols.shape[1] // ch):
                lanes = slice(h * ch, (h + 1) * ch)
                c_left[...] = c_tiles[side, i, :, :, lanes].astype(F32).reshape(rows // 2 * STEP, ch)
                c_left[pl.ds(side * (STEP - 1), rows // 2, stride=STEP), :] = c_cols[:, lanes]
                c_tiles[side, i, :, :, lanes] = (
                    c_left[...].astype(BF).reshape(rows // 2, STEP, ch)
                )
        return carry

    lax.fori_loop(0, faces, update, 0)
    if not coarse:
        return
    copies = tile_copies(y_out, tiles, sems, back=True)
    if cols > 2 * STEP:
        between = pl.ds(STEP, cols - 2 * STEP)
        for k, row in enumerate((0, rows - 1)):
            copies.append(
                pltpu.make_async_copy(
                    edge_rows.at[:, k, between], y_out.at[:, row, between], sems.at[2 + k]
                )
            )
    half = cols // 2
    for side, start in enumerate((0, half - STEP)):
        copies.append(
            pltpu.make_async_copy(
                c_tiles.at[side], c_out.at[:, :, pl.ds(start, STEP), :], sems.at[4 + side]
            )
        )
    if half > 2 * STEP:
        between = pl.ds(STEP, half - 2 * STEP)
        for k, row in enumerate((0, rows // 2 - 1)):
            copies.append(
                pltpu.make_async_copy(
                    c_rows.at[k, :, between], c_out.at[:, row, between], sems.at[6 + k]
                )
            )
    for copy in copies:
        copy.start()
    for copy in copies:
        copy.wait()


def ring(neighbour_face, orientation, x, buffers, copied, lines, parts, weight, bias, seams, down):
    y, *coarse = buffers
    faces, rows, cols, ch = x.shape
    groups = len(seams) // 2
    smem = pl.BlockSpec(memory_space=pltpu.SMEM)
    hbm = pl.BlockSpec(memory_space=pltpu.HBM)
    vmem = pl.BlockSpec(memory_space=pltpu.VMEM)
    args = [neighbour_face, orientation, x, y, lines, *parts, weight, bias, *seams]
    in_specs = [smem, smem] + [vmem] * (len(args) - 2)
    scratch = [
        pltpu.VMEM((2, faces, rows, STEP, ch), BF),
        pltpu.VMEM((faces, 2, cols, ch), BF),
        pltpu.VMEM((faces, 2 * rows, ch), F32),
        pltpu.VMEM((groups, faces, rows + EXTRA, ch), BF),
        pltpu.VMEM((groups, faces, cols, ch), BF),
        pltpu.VMEM((rows * STEP, ch), F32),
        pltpu.VMEM((rows * STEP, ch), F32),
        pltpu.VMEM((9 * ch, ch), BF),
        pltpu.VMEM((2 * faces * cols, 9 * ch), BF),
        pltpu.VMEM((2 * faces * rows, 9 * ch), BF),
    ]
    if down:
        co = down[0].shape[-1]
        args += [coarse[0], *down]
        in_specs += [vmem] * 3
        aliases = {len(args): 0, len(args) + 1: 1}
        args += [in_hbm(buffer) for buffer in copied]
        in_specs += [hbm] * 2
        out_shape = [pltpu.HBM(buffer.shape, BF) for buffer in copied]
        out_specs = [hbm] * 2
        scratch += [
            pltpu.VMEM((2, faces, rows // 2, STEP, co), BF),
            pltpu.VMEM((2, faces, cols // 2, co), BF),
            pltpu.VMEM((rows // 2, co), F32),
            pltpu.VMEM((rows // 2 * STEP, ch), F32),
            pltpu.SemaphoreType.DMA((8,)),
        ]
    else:
        aliases = {3: 0}
        out_shape = [jax.ShapeDtypeStruct(y.shape, BF), *strip_shapes(faces, rows, cols, ch)]
        out_specs = [vmem] * 5
    return pl.pallas_call(
        functools.partial(ring_kernel, groups, bool(down)),
        in_specs=in_specs,
        out_specs=tuple(out_specs),
        out_shape=tuple(out_shape),
        scratch_shapes=scratch,
        input_output_aliases=aliases,
        cost_estimate=pl.CostEstimate(
            flops=faces * (rows + cols) * 36 * ch * ch, bytes_accessed=8 * 2**20, transcendentals=0
        ),
        compiler_params=pltpu.CompilerParams(vmem_limit_bytes=20 * 2**20),
        name="ring",
    )(*args)


def blocks(change_row, change_col):
    cols = lax.axis_size("col")
    return [
        (r * cols + c, (r ^ change_row) * cols + (c ^ change_col))
        for r in range(lax.axis_size("row"))
        for c in range(cols)
    ]


def swap(v, change_row, change_col):
    return lax.ppermute(v, ("row", "col"), blocks(change_row, change_col))


def between_faces(v, change, rows):
    row_total, cols = lax.axis_size("row"), lax.axis_size("col")
    place = lambda g, r, c: (g * row_total + r) * cols + c
    pairs = [
        (place(g, r, c), place(g ^ change, r, c))
        for g in range(lax.axis_size("face"))
        for r in rows
        for c in range(cols)
    ]
    return lax.ppermute(v, ("face", "row", "col"), pairs)


def level(neighbour_face, orientation, x, strips, weight, bias, down):
    u, v, turn, lines = strips
    groups = lax.axis_size("face")
    total = x.shape[0] * x.shape[1] // STEP
    early, late = max(total * 5 // 12, 1), max(total // 2, 2)
    piece = functools.partial(conv_piece, x, weight, bias, down=down)
    beside, across, diagonal = swap(u, 0, 1), swap(v, 3, 0), swap(v, 3, 1)
    pair, turned = swap(v, 1, 0), swap(turn, 1, 0)
    state = piece(0, early, None)
    (beside, across, diagonal), state = lax.optimization_barrier(
        ((beside, across, diagonal), state)
    )
    pair_beside, pair_across, pair_diagonal = (swap(a, 1, 0) for a in (beside, across, diagonal))
    state = piece(early, late - early, state)
    stores = (v, beside, pair, pair_beside, pair_across, pair_diagonal, across, diagonal)
    picked = select_strips(neighbour_face, orientation, stores, groups)
    picked, state = lax.optimization_barrier((picked, state))
    seams = list(picked)
    for k in range(groups - 1, 0, -1):
        seams[2 * k] = between_faces(picked[2 * k], k, range(lax.axis_size("row")))
        seams[2 * k + 1] = between_faces(picked[2 * k + 1], k, (0, 3))
    _, buffers, copied = piece(late, total - late, state)
    parts = (beside, pair_beside, across, diagonal, turned)
    return ring(
        neighbour_face, orientation, x, buffers, copied, lines, parts, weight, bias, seams, down
    )


def per_device(
    field, conv1_w, conv1_b, conv2_w, conv2_b, down_w, down_b, neighbour_face, orientation
):
    tables = (neighbour_face.T, orientation.T)
    hidden, *strips = level(*tables, field, strips_of(field), conv1_w, conv1_b[None], ())
    return level(*tables, hidden, strips, conv2_w, conv2_b[None], (down_w, down_b[None]))


def solution(mesh):
    groups = mesh.shape["face"]
    fast = mesh.shape["row"] == 4 and mesh.shape["col"] == 2 and groups & (groups - 1) == 0
    return jax.shard_map(
        per_device if fast else general_device,
        mesh=mesh,
        in_specs=(P("face", "row", "col", None), P(), P(), P(), P(), P(), P(), P(), P()),
        out_specs=(P("face", "row", "col", None), P("face", "row", "col", None)),
        check_vma=False,
    )
```

```python
import functools

import jax
import jax.numpy as jnp
import numpy as np
from jax import lax
from jax.experimental import pallas as pl
from jax.experimental.pallas import tpu as pltpu
from jax.sharding import PartitionSpec as P


FACES = 12
BF = jnp.bfloat16
F32 = jnp.float32
STEP = 16
EXTRA = 16

layout = ("NHWC", "HWIO", "NHWC")


def padded_2(block, sides, width):
    for axis, dim in sides:
        count = lax.axis_size(axis)
        forward = [(i, i + 1) for i in range(count - 1)]
        backward = [(target, source) for source, target in forward]
        low = lax.ppermute(
            lax.slice_in_dim(block, block.shape[dim] - width, None, axis=dim), axis, forward
        )
        high = lax.ppermute(lax.slice_in_dim(block, 0, width, axis=dim), axis, backward)
        block = jnp.concatenate([low, block, high], axis=dim)
    return block


def seam_parts(edges, neighbours, codes):
    seam_faces = neighbours[:, :4]
    seam_codes = codes[:, :4]
    seams = edges[seam_faces, seam_codes // 2]
    seams = jnp.where((seam_codes % 2 == 1)[:, :, None, None], seams[:, :, ::-1], seams)
    corner_values = jnp.stack(
        [edges[:, 0, 0], edges[:, 0, -1], edges[:, 2, -1], edges[:, 2, 0]], axis=1
    )
    corner_faces = neighbours[:, 4:]
    picked = corner_values[jnp.minimum(corner_faces, FACES - 1), codes[:, 4:]]
    picked = jnp.where((corner_faces < FACES)[:, :, None], picked, jnp.zeros_like(picked))
    return (seams, picked)


def convolve(padded, weight, bias):
    summed = lax.conv_general_dilated(
        padded,
        weight,
        (1, 1),
        "VALID",
        dimension_numbers=layout,
        preferred_element_type=jnp.float32,
    )
    return jax.nn.gelu(summed + bias, approximate=False).astype(jnp.bfloat16)


def general_layer(block, weight, bias, neighbour_face, orientation):
    face_count, row_size, col_size, channels = block.shape
    row_total = lax.axis_size("row")
    col_total = lax.axis_size("col")
    row_place = lax.axis_index("row")
    col_place = lax.axis_index("col")
    face_side = row_size * row_total
    padded = padded_2(block, (("row", 1), ("col", 2)), 1)
    top_live = row_place == 0
    bottom_live = row_place == row_total - 1
    left_live = col_place == 0
    right_live = col_place == col_total - 1
    empty_line = jnp.zeros((face_count, face_side, channels), jnp.float32)

    def place(strip, offset, live):
        scaled = strip.astype(jnp.float32) * live.astype(jnp.float32)
        return lax.dynamic_update_slice_in_dim(empty_line, scaled, offset, 1)

    lines = jnp.stack(
        [
            place(block[:, 0], col_place * col_size, top_live),
            place(block[:, :, -1], row_place * row_size, right_live),
            place(block[:, -1], col_place * col_size, bottom_live),
            place(block[:, :, 0], row_place * row_size, left_live),
        ],
        axis=1,
    )
    complete = lax.psum(lax.psum(lines.astype(jnp.bfloat16), "col"), "row").astype(jnp.float32)
    every_edge = lax.all_gather(complete.astype(jnp.bfloat16), "face", axis=0, tiled=True)
    first_face = lax.axis_index("face") * face_count
    own_faces = lax.dynamic_slice_in_dim(neighbour_face, first_face, face_count, 0)
    own_codes = lax.dynamic_slice_in_dim(orientation, first_face, face_count, 0)
    seams, corners = seam_parts(every_edge, own_faces, own_codes)
    upper = jnp.concatenate([corners[:, 0:1], seams[:, 0], corners[:, 1:2]], 1)
    lower = jnp.concatenate([corners[:, 3:4], seams[:, 2], corners[:, 2:3]], 1)
    leftward = jnp.concatenate([corners[:, 0:1], seams[:, 3], corners[:, 3:4]], 1)
    rightward = jnp.concatenate([corners[:, 1:2], seams[:, 1], corners[:, 2:3]], 1)
    upper_cut = lax.dynamic_slice_in_dim(upper, col_place * col_size, col_size + 2, 1)
    lower_cut = lax.dynamic_slice_in_dim(lower, col_place * col_size, col_size + 2, 1)
    left_cut = lax.dynamic_slice_in_dim(leftward, row_place * row_size, row_size + 2, 1)
    right_cut = lax.dynamic_slice_in_dim(rightward, row_place * row_size, row_size + 2, 1)
    padded = padded.at[:, 0].set(jnp.where(top_live, upper_cut, padded[:, 0]))
    padded = padded.at[:, -1].set(jnp.where(bottom_live, lower_cut, padded[:, -1]))
    padded = padded.at[:, :, 0].set(jnp.where(left_live, left_cut, padded[:, :, 0]))
    padded = padded.at[:, :, -1].set(jnp.where(right_live, right_cut, padded[:, :, -1]))
    return convolve(padded, weight, bias)


def general_device(
    field, conv1_w, conv1_b, conv2_w, conv2_b, down_w, down_b, neighbour_face, orientation
):
    hidden = general_layer(field, conv1_w, conv1_b, neighbour_face, orientation)
    skip = general_layer(hidden, conv2_w, conv2_b, neighbour_face, orientation)
    summed = lax.conv_general_dilated(
        skip, down_w, (2, 2), "VALID", dimension_numbers=layout, preferred_element_type=jnp.float32
    )
    coarse = (summed + down_b).astype(jnp.bfloat16)
    return (skip, coarse)


def gelu(v):
    return 0.5 * v * (1.0 + lax.erf(v * np.float32(np.sqrt(0.5))))


def shifted(v, before, after):
    n = v.shape[0]
    spot = lax.broadcasted_iota(jnp.int32, (n, 1), 0)
    low = jnp.where(spot == 0, before, pltpu.roll(v, 1, 0))
    high = jnp.where(spot == n - 1, after, pltpu.roll(v, n - 1, 0))
    return low.astype(BF), v.astype(BF), high.astype(BF)


def parting(n):
    to = lax.broadcasted_iota(jnp.int32, (n, n), 0)
    source = lax.broadcasted_iota(jnp.int32, (n, n), 1)
    half = n // 2
    return jnp.where(source == jnp.where(to < half, 2 * to, 2 * (to - half) + 1), 1.0, 0.0).astype(BF)


def parted(order, v):
    v = jnp.dot(order, v, preferred_element_type=F32).astype(BF)
    half, lanes = v.shape[0] // 2, v.shape[1] // 2
    return v[:half, :lanes], v[:half, lanes:], v[half:, :lanes], v[half:, lanes:]


def conv_kernel(first, count, build, x_ref, b_ref, *refs):
    *refs, taps_0, taps_1 = refs
    if build:
        w_ref, y_ref, w_low, w_high = refs
    else:
        w_low, w_high, _, y_ref = refs
    _, size, cols, ch = x_ref.shape
    steps = size // STEP
    pairs = STEP // 2
    zero_row = jnp.zeros((1, ch), F32)
    half = 3 * ch

    if build:
        zero = jnp.zeros((ch, ch), BF)
        for d in range(3):
            one = slice(d * ch, (d + 1) * ch)
            two = slice(half + d * ch, half + (d + 1) * ch)
            w_low[one, :ch] = w_ref[0, d]
            w_low[one, ch:] = zero
            w_low[two, :ch] = w_ref[1, d]
            w_low[two, ch:] = w_ref[0, d]
            w_high[one, :ch] = w_ref[2, d]
            w_high[one, ch:] = w_ref[1, d]
            w_high[two, :ch] = zero
            w_high[two, ch:] = w_ref[2, d]

    def at(t):
        return t // steps, lax.rem(t, steps)

    def fill(taps, t):
        face, step = at(t)
        base = step * STEP

        def put(v, pair, side):
            low, same, high = shifted(v.astype(F32), zero_row, zero_row)
            place = side * half
            taps[pair, :, place : place + ch] = low
            taps[pair, :, place + ch : place + 2 * ch] = same
            taps[pair, :, place + 2 * ch : place + 3 * ch] = high

        inside = (step > 0).astype(F32)
        put(x_ref[face, jnp.maximum(base - 1, 0)].astype(F32) * inside, 0, 0)
        for row in range(STEP):
            put(x_ref[face, base + row], (row + 1) // 2, (row + 1) % 2)
        inside = (step < steps - 1).astype(F32)
        put(x_ref[face, jnp.minimum(base + STEP, size - 1)].astype(F32) * inside, pairs, 1)

    def product(taps, t):
        face, step = at(t)
        base = step * STEP
        lower = taps[pl.ds(0, pairs)].reshape(pairs * cols, 2 * half)
        upper = taps[pl.ds(1, pairs)].reshape(pairs * cols, 2 * half)
        total = jnp.dot(lower, w_low[...], preferred_element_type=F32)
        total += jnp.dot(upper, w_high[...], preferred_element_type=F32)
        total = total.reshape(pairs, cols, 2 * ch)
        bias = b_ref[...]
        for side in range(2):
            out = gelu(total[:, :, side * ch : (side + 1) * ch] + bias[None]).astype(BF)
            for pair in range(pairs):
                y_ref[face, base + 2 * pair + side] = out[pair]
    last = first + count - 1
    fill(taps_0, first)

    def double(j, carry):
        t = first + 2 * j
        fill(taps_1, t + 1)
        product(taps_0, t)
        fill(taps_0, jnp.minimum(t + 2, last))
        product(taps_1, t + 1)
        return carry

    lax.fori_loop(0, count // 2, double, 0)
    if count % 2:
        product(taps_0, last)


def in_hbm(x):
    return pltpu.with_memory_space_constraint(x, pltpu.HBM)


def conv_piece(x, weight, bias, first, count, state):
    faces, rows, cols, ch = x.shape
    vmem = pl.BlockSpec(memory_space=pltpu.VMEM)
    build = state is None
    taps = (STEP // 2 + 1, cols, 6 * ch)
    arranged = jax.ShapeDtypeStruct((6 * ch, 2 * ch), BF)
    args = [x, bias, weight] if build else [x, bias, *state]
    out_shape = [jax.ShapeDtypeStruct(x.shape, BF)] + [arranged] * (2 if build else 0)
    pixels = count * STEP * cols
    out = pl.pallas_call(
        functools.partial(conv_kernel, first, count, build),
        in_specs=[vmem] * len(args),
        out_specs=tuple([vmem] * len(out_shape)),
        out_shape=tuple(out_shape),
        scratch_shapes=[pltpu.VMEM(taps, BF), pltpu.VMEM(taps, BF)],
        input_output_aliases={} if build else {4: 0},
        cost_estimate=pl.CostEstimate(
            flops=pixels * 24 * ch * ch, bytes_accessed=4 * pixels * ch, transcendentals=0
        ),
        compiler_params=pltpu.CompilerParams(vmem_limit_bytes=16 * 2**20),
        name="conv_piece",
    )(*args)
    return (out[1], out[2], out[0]) if build else (state[0], state[1], out[0])


def down_kernel(y_ref, w_ref, b_ref, c_ref, y_out, c_out, taps_0, taps_1, sems):
    faces, rows, cols, ch = y_ref.shape
    steps, pairs = rows // STEP, STEP // 2
    count = faces * steps
    order = parting(cols)

    def copies(t):
        face, step = t // steps, lax.rem(t, steps)
        some, cells = pl.ds(step * STEP, STEP), pl.ds(step * pairs, pairs)
        return (
            pltpu.make_async_copy(y_ref.at[face, some], y_out.at[face, some], sems.at[0]),
            pltpu.make_async_copy(c_ref.at[face, cells], c_out.at[face, cells], sems.at[1]),
        )

    def fill(taps, t):
        face, step = t // steps, lax.rem(t, steps)
        for pair in range(pairs):
            row = step * STEP + 2 * pair
            both = jnp.concatenate([y_ref[face, row], y_ref[face, row + 1]], axis=1)
            four = parted(order, both)
            taps[pair] = jnp.concatenate([four[k] for k in (0, 2, 1, 3)], axis=1)

    def product(taps, t):
        face, step = t // steps, lax.rem(t, steps)
        out = jnp.dot(
            taps[...].reshape(pairs * cols // 2, 4 * ch),
            w_ref[...].reshape(4 * ch, -1),
            preferred_element_type=F32,
        )
        out = (out + b_ref[...]).astype(BF)
        c_ref[face, pl.ds(step * pairs, pairs)] = out.reshape(pairs, cols // 2, -1)
        copies(t)[1].start()

    def send(t, carry):
        copies(t)[0].start()
        return carry

    def wait(t, carry):
        for copy in copies(t):
            copy.wait()
        return carry

    lax.fori_loop(0, count, send, 0)
    fill(taps_0, 0)

    def double(j, carry):
        fill(taps_1, 2 * j + 1)
        product(taps_0, 2 * j)
        fill(taps_0, jnp.minimum(2 * j + 2, count - 1))
        product(taps_1, 2 * j + 1)
        return carry

    lax.fori_loop(0, count // 2, double, 0)
    if count % 2:
        product(taps_0, count - 1)
    lax.fori_loop(0, count, wait, 0)


def downsample(y, weight, bias):
    faces, rows, cols, ch = y.shape
    shape = (faces, rows // 2, cols // 2, weight.shape[-1])
    vmem = pl.BlockSpec(memory_space=pltpu.VMEM)
    hbm = pl.BlockSpec(memory_space=pltpu.HBM)
    taps = (STEP // 2, cols // 2, 4 * ch)
    return pl.pallas_call(
        down_kernel,
        in_specs=[vmem] * 3,
        out_specs=(vmem, hbm, hbm),
        out_shape=(jax.ShapeDtypeStruct(shape, BF), pltpu.HBM(y.shape, BF), pltpu.HBM(shape, BF)),
        scratch_shapes=[pltpu.VMEM(taps, BF), pltpu.VMEM(taps, BF), pltpu.SemaphoreType.DMA((2,))],
        cost_estimate=pl.CostEstimate(
            flops=faces * rows * cols * 2 * ch * shape[-1],
            bytes_accessed=4 * faces * rows * cols * ch,
            transcendentals=0,
        ),
        compiler_params=pltpu.CompilerParams(vmem_limit_bytes=16 * 2**20),
        name="downsample",
    )(y, weight, bias)


def column(tile, place):
    return tile[pl.ds(place, tile.shape[0] // STEP, stride=STEP), :]


def put_strips(i, r, c, lines, top, bottom, u_ref, v_ref, turn_ref, line_ref):
    left, left_in, right_in, right = lines
    size = left.shape[0]
    for place, value in enumerate(lines):
        line_ref[i, place] = value.astype(BF)
    side = jnp.where(c == 0, left, right).astype(BF)
    inner = jnp.where(c == 0, right, left).astype(BF)
    even = lax.rem(r, 2) == 0
    line = jnp.where(even, top, bottom).astype(BF)
    turn_ref[i] = jnp.where(even, bottom, top).astype(BF)
    for ref in (u_ref, v_ref):
        ref[i, 0] = side
        ref[i, 1] = line[:size]
        ref[i, 2] = line[size:]
    u_ref[i, 3] = inner


def strip_shapes(faces, rows, cols, ch):
    return (
        jax.ShapeDtypeStruct((faces, 4, rows, ch), BF),
        jax.ShapeDtypeStruct((faces, 3, rows, ch), BF),
        jax.ShapeDtypeStruct((faces, cols, ch), BF),
        jax.ShapeDtypeStruct((faces, 4, rows, ch), BF),
    )


def whole(shape):
    return pl.BlockSpec(shape, lambda *_: (0,) * len(shape))


def tile_copies(array, tiles, sems, back=False):
    cols = array.shape[2]
    out = []
    for side, start in enumerate((0, cols - STEP)):
        far, near = array.at[:, :, pl.ds(start, STEP), :], tiles.at[side]
        out.append(pltpu.make_async_copy(*((near, far) if back else (far, near)), sems.at[side]))
    return out


def strips_kernel(x_ref, u_ref, v_ref, turn_ref, line_ref, tiles, outer, left, right, sems):
    faces, rows, cols, ch = x_ref.shape
    r, c = lax.axis_index("row"), lax.axis_index("col")
    copies = tile_copies(x_ref, tiles, sems)
    for k, row in enumerate((0, rows - 1)):
        copies.append(pltpu.make_async_copy(x_ref.at[:, row], outer.at[k], sems.at[2 + k]))
    for copy in copies:
        copy.start()
    for copy in copies:
        copy.wait()

    def face(i, carry):
        left[...] = tiles[0, i].astype(F32).reshape(rows * STEP, ch)
        right[...] = tiles[1, i].astype(F32).reshape(rows * STEP, ch)
        lines = (column(left, 0), column(left, 1), column(right, STEP - 2), column(right, STEP - 1))
        put_strips(
            i, r, c, lines, outer[0, i].astype(F32), outer[1, i].astype(F32),
            u_ref, v_ref, turn_ref, line_ref,
        )
        return carry

    lax.fori_loop(0, faces, face, 0)


def strips_of(x):
    faces, rows, cols, ch = x.shape
    shapes = strip_shapes(faces, rows, cols, ch)
    return pl.pallas_call(
        strips_kernel,
        in_specs=[pl.BlockSpec(memory_space=pltpu.HBM)],
        out_specs=(pl.BlockSpec(memory_space=pltpu.VMEM),) * 4,
        out_shape=shapes,
        scratch_shapes=[
            pltpu.VMEM((2, faces, rows, STEP, ch), BF),
            pltpu.VMEM((2, faces, cols, ch), BF),
            pltpu.VMEM((rows * STEP, ch), F32),
            pltpu.VMEM((rows * STEP, ch), F32),
            pltpu.SemaphoreType.DMA((4,)),
        ],
        cost_estimate=pl.CostEstimate(flops=0, bytes_accessed=4 * 2**20, transcendentals=0),
        compiler_params=pltpu.CompilerParams(vmem_limit_bytes=10 * 2**20),
        name="strips_of",
    )(in_hbm(x))


def select_kernel(near_ref, code_ref, *refs):
    stores, outs, held = refs[:8], refs[8:-1], refs[-1]
    faces, _, size, ch = held.shape[1:]
    me, r, c = lax.axis_index("face"), lax.axis_index("row"), lax.axis_index("col")
    for k, store in enumerate(stores):
        for i in range(faces):
            held[k, i] = store[i, 0:3]

    def slot(row, col):
        return ((r ^ row) << 1) | (c ^ col)

    def quarter(edge, q):
        upright = lax.rem(edge, 2) == 1
        row = jnp.where(upright, q, jnp.where(edge == 0, 0, 3))
        col = jnp.where(upright, jnp.where(edge == 3, 0, 1), q >> 1)
        return slot(row, col), jnp.where(upright, 0, 1 + (q & 1))

    def end(n, where, block, last):
        head = held[where, n, block, 0:EXTRA].astype(F32)
        tail = held[where, n, block, size - EXTRA : size].astype(F32)
        return jnp.where(last, tail[EXTRA - 1 : EXTRA], head[0:1])

    spot = lax.broadcasted_iota(jnp.int32, (EXTRA, 1), 0)
    for k, out in enumerate(outs):
        target = me ^ k

        def face(i, carry, out=out, target=target):
            f = target * faces + i
            edge = 3 - 2 * c
            code = code_ref[edge, f]
            far, flip = code >> 1, code & 1
            n = lax.rem(near_ref[edge, f], faces)
            where, block = quarter(far, jnp.where(flip == 1, 3 - r, r))
            out[i, 0:size] = held[where, n, block]
            corner = jnp.where(r < 2, c, 3 - c)
            tip = code_ref[4 + corner, f]
            tip_n = lax.rem(near_ref[4 + corner, f], faces)
            tip_row = jnp.where(tip < 2, 0, 3)
            tip_col = jnp.where((tip == 1) | (tip == 2), 1, 0)
            tip_pixel = end(tip_n, slot(tip_row, tip_col), 0, tip_row == 3)
            q = jnp.where(flip == 1, 4 - r, r - 1)
            where, block = quarter(far, jnp.clip(q, 0, 3))
            before = jnp.where(r == 0, tip_pixel, end(n, where, block, flip == 0))
            q = jnp.where(flip == 1, 2 - r, r + 1)
            where, block = quarter(far, jnp.clip(q, 0, 3))
            after = jnp.where(r == 3, tip_pixel, end(n, where, block, flip == 1))

            edge = jnp.where(r < 2, 0, 2)
            code = code_ref[edge, f]
            far, flip = code >> 1, code & 1
            n = lax.rem(near_ref[edge, f], faces)
            part = c ^ flip
            for h in range(2):
                where, block = quarter(far, 2 * part + h)
                out[i, (1 + h) * size : (2 + h) * size] = held[where, n, block]
            where, block = quarter(far, jnp.where(part == 0, 2, 1))
            middle = end(n, where, block, part == 1)
            single = jnp.where(spot == 0, before, jnp.where(spot == 1, after, middle))
            out[i, 3 * size : 3 * size + EXTRA] = single.astype(BF)
            return carry

        lax.fori_loop(0, faces, face, 0)


def select_strips(neighbour_face, orientation, stores, groups):
    faces, _, size, ch = stores[0].shape
    shape = jax.ShapeDtypeStruct((faces, 3 * size + EXTRA, ch), BF)
    smem = pl.BlockSpec(memory_space=pltpu.SMEM)
    return pl.pallas_call(
        select_kernel,
        in_specs=[smem, smem] + [pl.BlockSpec(memory_space=pltpu.VMEM)] * 8,
        out_specs=(pl.BlockSpec(memory_space=pltpu.VMEM),) * groups,
        out_shape=(shape,) * groups,
        scratch_shapes=[pltpu.VMEM((8, faces, 3, size, ch), BF)],
        cost_estimate=pl.CostEstimate(flops=0, bytes_accessed=4 * 2**20, transcendentals=0),
        compiler_params=pltpu.CompilerParams(vmem_limit_bytes=10 * 2**20),
        name="select_strips",
    )(neighbour_face, orientation, *stores)


def ring_kernel(groups, coarse, near_ref, code_ref, x_ref, y_in, line_in, beside, diagonal, across,
                far_diagonal, turned, w_ref, b_ref, *refs):
    seams, refs = refs[:groups], refs[groups:]
    if coarse:
        c_ref, dw_ref, db_ref, _, _, y_out, c_out = refs[:7]
        y_ref = y_in
        scratch = refs[7:]
        *scratch, c_tiles, c_rows, c_cols, c_left, sems = scratch
    else:
        y_ref, outs, scratch = refs[0], refs[1:5], refs[5:]
    tiles, edge_rows, edge_cols, held, left, right, w_cols, across_taps, along_taps = scratch
    faces, rows, cols, ch = x_ref.shape
    me, r, c = lax.axis_index("face"), lax.axis_index("row"), lax.axis_index("col")
    for k in range(groups):
        held[k] = seams[k][...]

    def oriented(v, flip):
        n = v.shape[0]
        to = lax.broadcasted_iota(jnp.int32, (n, n), 0)
        source = lax.broadcasted_iota(jnp.int32, (n, n), 1)
        order = jnp.where(source == jnp.where(flip == 1, n - 1 - to, to), 1.0, 0.0).astype(BF)
        return jnp.dot(order, v, preferred_element_type=F32)

    even = lax.rem(r, 2) == 0
    outer = (r == 0) | (r == 3)
    for d in range(3):
        for a in range(3):
            w_cols[(3 * d + a) * ch : (3 * d + a + 1) * ch] = w_ref[a, d]
    bias = b_ref[...]

    def holder(n):
        return jnp.minimum(n, FACES - 1) // faces ^ me

    def put(taps, place, v, before, after, third):
        for k, part in enumerate(shifted(v, before, after)):
            start = (3 * third + k) * ch
            taps[pl.ds(place, v.shape[0]), start : start + ch] = part

    def face(i):
        f = me * faces + i
        edge = 3 - 2 * c
        n = near_ref[edge, f]
        corner = jnp.where(r < 2, c, 3 - c)
        tip_n = near_ref[4 + corner, f]
        seam_side = oriented(held[holder(n), i, 0:rows], code_ref[edge, f] & 1)
        extra = slice(3 * rows, 3 * rows + EXTRA)
        n_before = jnp.where(r == 0, tip_n, n)
        n_after = jnp.where(r == 3, tip_n, n)
        before = held[holder(n_before), i, extra].astype(F32)[0:1]
        after = held[holder(n_after), i, extra].astype(F32)[1:2]
        before = jnp.where(n_before < FACES, before, 0.0)
        after = jnp.where(n_after < FACES, after, 0.0)
        edge = jnp.where(r < 2, 0, 2)
        n = near_ref[edge, f]
        seam_line = oriented(held[holder(n), i, rows : 3 * rows], code_ref[edge, f] & 1)
        middle = held[holder(n), i, extra].astype(F32)[2:3]

        inner = beside[i, 3].astype(F32)
        block_line = jnp.concatenate([across[i, 1], across[i, 2]], axis=0).astype(F32)
        outward = jnp.where(outer, seam_line, block_line)
        inward = turned[i].astype(F32)
        top = jnp.where(even, outward, inward)
        bottom = jnp.where(even, inward, outward)
        lft = jnp.where(c == 0, seam_side, inner)
        rgt = jnp.where(c == 0, inner, seam_side)
        pair_inner = diagonal[i, 3].astype(F32)
        inward_corner = jnp.where(even, pair_inner[0:1], pair_inner[rows - 1 : rows])
        far_first = far_diagonal[i, 1].astype(F32)[0:1]
        far_last = far_diagonal[i, 2].astype(F32)[rows - 1 : rows]
        outward_corner = jnp.where(outer, middle, jnp.where(c == 0, far_first, far_last))
        inner_top = jnp.where(even, outward_corner, inward_corner)
        inner_bottom = jnp.where(even, inward_corner, outward_corner)
        top_left = jnp.where(c == 0, before, inner_top)
        top_right = jnp.where(c == 0, inner_top, before)
        bottom_left = jnp.where(c == 0, after, inner_bottom)
        bottom_right = jnp.where(c == 0, inner_bottom, after)

        row_0, row_1, row_2, row_3 = (
            x_ref[i, k].astype(F32) for k in (0, 1, rows - 2, rows - 1)
        )
        place = 2 * i * cols
        put(across_taps, place, top, top_left, top_right, 0)
        put(across_taps, place, row_0, lft[0:1], rgt[0:1], 1)
        put(across_taps, place, row_1, lft[1:2], rgt[1:2], 2)
        place += cols
        put(across_taps, place, row_2, lft[rows - 2 : rows - 1], rgt[rows - 2 : rows - 1], 0)
        put(across_taps, place, row_3, lft[rows - 1 : rows], rgt[rows - 1 : rows], 1)
        put(across_taps, place, bottom, bottom_left, bottom_right, 2)
        col_0, col_1, col_2, col_3 = (line_in[i, k].astype(F32) for k in range(4))
        place = 2 * i * rows
        put(along_taps, place, lft, top_left, bottom_left, 0)
        put(along_taps, place, col_0, top[0:1], bottom[0:1], 1)
        put(along_taps, place, col_1, top[1:2], bottom[1:2], 2)
        place += rows
        put(along_taps, place, col_2, top[cols - 2 : cols - 1], bottom[cols - 2 : cols - 1], 0)
        put(along_taps, place, col_3, top[cols - 1 : cols], bottom[cols - 1 : cols], 1)
        put(along_taps, place, rgt, top_right, bottom_right, 2)

    for i in range(faces):
        face(i)
    w_rows = w_ref[...].reshape(9 * ch, ch)
    out = gelu(jnp.dot(across_taps[...], w_rows, preferred_element_type=F32) + bias)
    edge_rows[...] = out.astype(BF).reshape(edge_rows.shape)
    out = gelu(jnp.dot(along_taps[...], w_cols[...], preferred_element_type=F32) + bias)
    edge_cols[...] = out.reshape(edge_cols.shape)
    between = slice(STEP, cols - STEP)
    if coarse:
        order_cols, order_rows = parting(cols), parting(rows)

    def update(i, carry):
        new_top, new_bottom = edge_rows[i, 0].astype(F32), edge_rows[i, 1].astype(F32)
        if cols > 2 * STEP and not coarse:
            y_ref[i, 0, between] = edge_rows[i, 0, between]
            y_ref[i, rows - 1, between] = edge_rows[i, 1, between]
        for tile, side, place in ((left, 0, 0), (right, 1, STEP - 1)):
            start = side * (cols - STEP)
            tiles[side, i] = y_ref[i, :, start : start + STEP]
            tiles[side, i, 0] = edge_rows[i, 0, start : start + STEP]
            tiles[side, i, rows - 1] = edge_rows[i, 1, start : start + STEP]
            tile[...] = tiles[side, i].astype(F32).reshape(rows * STEP, ch)
            tile[pl.ds(place, rows, stride=STEP), :] = edge_cols[i, pl.ds(side * rows, rows)]
            value = tile[...].astype(BF).reshape(rows, STEP, ch)
            if coarse:
                tiles[side, i] = value
            else:
                y_ref[i, :, start : start + STEP] = value
        if not coarse:
            lines = (
                column(left, 0), column(left, 1),
                column(right, STEP - 2), column(right, STEP - 1),
            )
            put_strips(i, r, c, lines, new_top, new_bottom, *outs)
            return carry
        w_down = dw_ref[...].reshape(4 * ch, -1)
        for k, (own, near) in enumerate(((new_top, 1), (new_bottom, rows - 2))):
            first = edge_cols[i, near : near + 1]
            last = edge_cols[i, rows + near : rows + near + 1]
            spot = lax.broadcasted_iota(jnp.int32, (cols, 1), 0)
            other = y_ref[i, near].astype(F32)
            other = jnp.where(spot == 0, first, jnp.where(spot == cols - 1, last, other))
            both = (own, other) if k == 0 else (other, own)
            both = jnp.concatenate([v.astype(BF) for v in both], axis=1)
            four = parted(order_cols, both)
            four = jnp.concatenate([four[j] for j in (0, 2, 1, 3)], axis=1)
            out = jnp.dot(four, w_down, preferred_element_type=F32)
            out = (out + db_ref[...]).astype(BF)
            c_rows[k, i] = out
        for side, (tile, place) in enumerate(((left, 0), (right, STEP - 2))):
            start = side * (cols // 2 - STEP)
            c_tiles[side, i] = c_ref[i, :, start : start + STEP]
            for k in range(2):
                c_tiles[side, i, k * (rows // 2 - 1)] = c_rows[k, i, start : start + STEP]
            both = [column(tile, place + d).astype(BF) for d in range(2)]
            four = parted(order_rows, jnp.concatenate(both, axis=1))
            out = jnp.dot(jnp.concatenate(four, axis=1), w_down, preferred_element_type=F32)
            c_cols[...] = out + db_ref[...]
            for h in range(c_cols.shape[1] // ch):
                lanes = slice(h * ch, (h + 1) * ch)
                c_left[...] = c_tiles[side, i, :, :, lanes].astype(F32).reshape(rows // 2 * STEP, ch)
                c_left[pl.ds(side * (STEP - 1), rows // 2, stride=STEP), :] = c_cols[:, lanes]
                c_tiles[side, i, :, :, lanes] = (
                    c_left[...].astype(BF).reshape(rows // 2, STEP, ch)
                )
        return carry

    lax.fori_loop(0, faces, update, 0)
    if not coarse:
        return
    copies = tile_copies(y_out, tiles, sems, back=True)
    if cols > 2 * STEP:
        between = pl.ds(STEP, cols - 2 * STEP)
        for k, row in enumerate((0, rows - 1)):
            copies.append(
                pltpu.make_async_copy(
                    edge_rows.at[:, k, between], y_out.at[:, row, between], sems.at[2 + k]
                )
            )
    half = cols // 2
    for side, start in enumerate((0, half - STEP)):
        copies.append(
            pltpu.make_async_copy(
                c_tiles.at[side], c_out.at[:, :, pl.ds(start, STEP), :], sems.at[4 + side]
            )
        )
    if half > 2 * STEP:
        between = pl.ds(STEP, half - 2 * STEP)
        for k, row in enumerate((0, rows // 2 - 1)):
            copies.append(
                pltpu.make_async_copy(
                    c_rows.at[k, :, between], c_out.at[:, row, between], sems.at[6 + k]
                )
            )
    for copy in copies:
        copy.start()
    for copy in copies:
        copy.wait()


def ring(neighbour_face, orientation, x, buffers, copied, lines, parts, weight, bias, seams, down):
    y, *coarse = buffers
    faces, rows, cols, ch = x.shape
    groups = len(seams)
    smem = pl.BlockSpec(memory_space=pltpu.SMEM)
    hbm = pl.BlockSpec(memory_space=pltpu.HBM)
    vmem = pl.BlockSpec(memory_space=pltpu.VMEM)
    args = [neighbour_face, orientation, x, y, lines, *parts, weight, bias, *seams]
    in_specs = [smem, smem] + [vmem] * (len(args) - 2)
    scratch = [
        pltpu.VMEM((2, faces, rows, STEP, ch), BF),
        pltpu.VMEM((faces, 2, cols, ch), BF),
        pltpu.VMEM((faces, 2 * rows, ch), F32),
        pltpu.VMEM((groups, faces, 3 * rows + EXTRA, ch), BF),
        pltpu.VMEM((rows * STEP, ch), F32),
        pltpu.VMEM((rows * STEP, ch), F32),
        pltpu.VMEM((9 * ch, ch), BF),
        pltpu.VMEM((2 * faces * cols, 9 * ch), BF),
        pltpu.VMEM((2 * faces * rows, 9 * ch), BF),
    ]
    if down:
        co = down[0].shape[-1]
        args += [coarse[0], *down]
        in_specs += [vmem] * 3
        aliases = {len(args): 0, len(args) + 1: 1}
        args += [in_hbm(buffer) for buffer in copied]
        in_specs += [hbm] * 2
        out_shape = [pltpu.HBM(buffer.shape, BF) for buffer in copied]
        out_specs = [hbm] * 2
        scratch += [
            pltpu.VMEM((2, faces, rows // 2, STEP, co), BF),
            pltpu.VMEM((2, faces, cols // 2, co), BF),
            pltpu.VMEM((rows // 2, co), F32),
            pltpu.VMEM((rows // 2 * STEP, ch), F32),
            pltpu.SemaphoreType.DMA((8,)),
        ]
    else:
        aliases = {3: 0}
        out_shape = [jax.ShapeDtypeStruct(y.shape, BF), *strip_shapes(faces, rows, cols, ch)]
        out_specs = [vmem] * 5
    return pl.pallas_call(
        functools.partial(ring_kernel, groups, bool(down)),
        in_specs=in_specs,
        out_specs=tuple(out_specs),
        out_shape=tuple(out_shape),
        scratch_shapes=scratch,
        input_output_aliases=aliases,
        cost_estimate=pl.CostEstimate(
            flops=faces * (rows + cols) * 36 * ch * ch, bytes_accessed=8 * 2**20, transcendentals=0
        ),
        compiler_params=pltpu.CompilerParams(vmem_limit_bytes=20 * 2**20),
        name="ring",
    )(*args)


def blocks(change_row, change_col):
    cols = lax.axis_size("col")
    return [
        (r * cols + c, (r ^ change_row) * cols + (c ^ change_col))
        for r in range(lax.axis_size("row"))
        for c in range(cols)
    ]


def swap(v, change_row, change_col):
    return lax.ppermute(v, ("row", "col"), blocks(change_row, change_col))


def level(neighbour_face, orientation, x, strips, weight, bias, down):
    u, v, turn, lines = strips
    groups = lax.axis_size("face")
    total = x.shape[0] * x.shape[1] // STEP
    early, late = max(total * 5 // 12, 1), max(total // 2, 2)
    piece = functools.partial(conv_piece, x, weight, bias)
    beside, across, diagonal = swap(u, 0, 1), swap(v, 3, 0), swap(v, 3, 1)
    pair, turned = swap(v, 1, 0), swap(turn, 1, 0)
    state = piece(0, early, None)
    (beside, across, diagonal), state = lax.optimization_barrier(
        ((beside, across, diagonal), state)
    )
    pair_beside, pair_across, pair_diagonal = (swap(a, 1, 0) for a in (beside, across, diagonal))
    state = piece(early, late - early, state)
    stores = (v, beside, pair, pair_beside, pair_across, pair_diagonal, across, diagonal)
    picked = select_strips(neighbour_face, orientation, stores, groups)
    picked, state = lax.optimization_barrier((picked, state))
    seams = list(picked)
    for k in range(1, groups):
        pairs = [(g, g ^ k) for g in range(groups)]
        seams[k] = lax.ppermute(picked[k], "face", pairs)
    buffers, copied = piece(late, total - late, state)[2:], ()
    if down:
        coarse, *copied = downsample(buffers[0], *down)
        buffers += (coarse,)
    parts = (beside, pair_beside, across, diagonal, turned)
    return ring(
        neighbour_face, orientation, x, buffers, copied, lines, parts, weight, bias, seams, down
    )


def per_device(
    field, conv1_w, conv1_b, conv2_w, conv2_b, down_w, down_b, neighbour_face, orientation
):
    tables = (neighbour_face.T, orientation.T)
    hidden, *strips = level(*tables, field, strips_of(field), conv1_w, conv1_b[None], ())
    return level(*tables, hidden, strips, conv2_w, conv2_b[None], (down_w, down_b[None]))


def solution(mesh):
    groups = mesh.shape["face"]
    fast = mesh.shape["row"] == 4 and mesh.shape["col"] == 2 and groups & (groups - 1) == 0
    return jax.shard_map(
        per_device if fast else general_device,
        mesh=mesh,
        in_specs=(P("face", "row", "col", None), P(), P(), P(), P(), P(), P(), P(), P()),
        out_specs=(P("face", "row", "col", None), P("face", "row", "col", None)),
        check_vma=False,
    )
```

```python
import functools

import jax
import jax.numpy as jnp
import numpy as np
from jax import lax
from jax.experimental import pallas as pl
from jax.experimental.pallas import tpu as pltpu
from jax.sharding import PartitionSpec as P


FACES = 12
BF = jnp.bfloat16
F32 = jnp.float32
STEP = 16
EXTRA = 16

layout = ("NHWC", "HWIO", "NHWC")


def padded_2(block, sides, width):
    for axis, dim in sides:
        count = lax.axis_size(axis)
        forward = [(i, i + 1) for i in range(count - 1)]
        backward = [(target, source) for source, target in forward]
        low = lax.ppermute(
            lax.slice_in_dim(block, block.shape[dim] - width, None, axis=dim), axis, forward
        )
        high = lax.ppermute(lax.slice_in_dim(block, 0, width, axis=dim), axis, backward)
        block = jnp.concatenate([low, block, high], axis=dim)
    return block


def seam_parts(edges, neighbours, codes):
    seam_faces = neighbours[:, :4]
    seam_codes = codes[:, :4]
    seams = edges[seam_faces, seam_codes // 2]
    seams = jnp.where((seam_codes % 2 == 1)[:, :, None, None], seams[:, :, ::-1], seams)
    corner_values = jnp.stack(
        [edges[:, 0, 0], edges[:, 0, -1], edges[:, 2, -1], edges[:, 2, 0]], axis=1
    )
    corner_faces = neighbours[:, 4:]
    picked = corner_values[jnp.minimum(corner_faces, FACES - 1), codes[:, 4:]]
    picked = jnp.where((corner_faces < FACES)[:, :, None], picked, jnp.zeros_like(picked))
    return (seams, picked)


def convolve(padded, weight, bias):
    summed = lax.conv_general_dilated(
        padded,
        weight,
        (1, 1),
        "VALID",
        dimension_numbers=layout,
        preferred_element_type=jnp.float32,
    )
    return jax.nn.gelu(summed + bias, approximate=False).astype(jnp.bfloat16)


def general_layer(block, weight, bias, neighbour_face, orientation):
    face_count, row_size, col_size, channels = block.shape
    row_total = lax.axis_size("row")
    col_total = lax.axis_size("col")
    row_place = lax.axis_index("row")
    col_place = lax.axis_index("col")
    face_side = row_size * row_total
    padded = padded_2(block, (("row", 1), ("col", 2)), 1)
    top_live = row_place == 0
    bottom_live = row_place == row_total - 1
    left_live = col_place == 0
    right_live = col_place == col_total - 1
    empty_line = jnp.zeros((face_count, face_side, channels), jnp.float32)

    def place(strip, offset, live):
        scaled = strip.astype(jnp.float32) * live.astype(jnp.float32)
        return lax.dynamic_update_slice_in_dim(empty_line, scaled, offset, 1)

    lines = jnp.stack(
        [
            place(block[:, 0], col_place * col_size, top_live),
            place(block[:, :, -1], row_place * row_size, right_live),
            place(block[:, -1], col_place * col_size, bottom_live),
            place(block[:, :, 0], row_place * row_size, left_live),
        ],
        axis=1,
    )
    complete = lax.psum(lax.psum(lines.astype(jnp.bfloat16), "col"), "row").astype(jnp.float32)
    every_edge = lax.all_gather(complete.astype(jnp.bfloat16), "face", axis=0, tiled=True)
    first_face = lax.axis_index("face") * face_count
    own_faces = lax.dynamic_slice_in_dim(neighbour_face, first_face, face_count, 0)
    own_codes = lax.dynamic_slice_in_dim(orientation, first_face, face_count, 0)
    seams, corners = seam_parts(every_edge, own_faces, own_codes)
    upper = jnp.concatenate([corners[:, 0:1], seams[:, 0], corners[:, 1:2]], 1)
    lower = jnp.concatenate([corners[:, 3:4], seams[:, 2], corners[:, 2:3]], 1)
    leftward = jnp.concatenate([corners[:, 0:1], seams[:, 3], corners[:, 3:4]], 1)
    rightward = jnp.concatenate([corners[:, 1:2], seams[:, 1], corners[:, 2:3]], 1)
    upper_cut = lax.dynamic_slice_in_dim(upper, col_place * col_size, col_size + 2, 1)
    lower_cut = lax.dynamic_slice_in_dim(lower, col_place * col_size, col_size + 2, 1)
    left_cut = lax.dynamic_slice_in_dim(leftward, row_place * row_size, row_size + 2, 1)
    right_cut = lax.dynamic_slice_in_dim(rightward, row_place * row_size, row_size + 2, 1)
    padded = padded.at[:, 0].set(jnp.where(top_live, upper_cut, padded[:, 0]))
    padded = padded.at[:, -1].set(jnp.where(bottom_live, lower_cut, padded[:, -1]))
    padded = padded.at[:, :, 0].set(jnp.where(left_live, left_cut, padded[:, :, 0]))
    padded = padded.at[:, :, -1].set(jnp.where(right_live, right_cut, padded[:, :, -1]))
    return convolve(padded, weight, bias)


def general_device(
    field, conv1_w, conv1_b, conv2_w, conv2_b, down_w, down_b, neighbour_face, orientation
):
    hidden = general_layer(field, conv1_w, conv1_b, neighbour_face, orientation)
    skip = general_layer(hidden, conv2_w, conv2_b, neighbour_face, orientation)
    summed = lax.conv_general_dilated(
        skip, down_w, (2, 2), "VALID", dimension_numbers=layout, preferred_element_type=jnp.float32
    )
    coarse = (summed + down_b).astype(jnp.bfloat16)
    return (skip, coarse)


def gelu(v):
    return 0.5 * v * (1.0 + lax.erf(v * np.float32(np.sqrt(0.5))))


def shifted(v, before, after):
    n = v.shape[0]
    spot = lax.broadcasted_iota(jnp.int32, (n, 1), 0)
    low = jnp.where(spot == 0, before, pltpu.roll(v, 1, 0))
    high = jnp.where(spot == n - 1, after, pltpu.roll(v, n - 1, 0))
    return low.astype(BF), v.astype(BF), high.astype(BF)


def parting(n):
    to = lax.broadcasted_iota(jnp.int32, (n, n), 0)
    source = lax.broadcasted_iota(jnp.int32, (n, n), 1)
    half = n // 2
    return jnp.where(source == jnp.where(to < half, 2 * to, 2 * (to - half) + 1), 1.0, 0.0).astype(BF)


def parted(order, v):
    v = jnp.dot(order, v, preferred_element_type=F32).astype(BF)
    half, lanes = v.shape[0] // 2, v.shape[1] // 2
    return v[:half, :lanes], v[:half, lanes:], v[half:, :lanes], v[half:, lanes:]


def conv_kernel(first, count, build, x_ref, b_ref, *refs):
    *refs, taps_0, taps_1 = refs
    if build:
        w_ref, y_ref, w_low, w_high = refs
    else:
        w_low, w_high, _, y_ref = refs
    _, size, cols, ch = x_ref.shape
    steps = size // STEP
    pairs = STEP // 2
    zero_row = jnp.zeros((1, ch), F32)
    half = 3 * ch

    if build:
        zero = jnp.zeros((ch, ch), BF)
        for d in range(3):
            one = slice(d * ch, (d + 1) * ch)
            two = slice(half + d * ch, half + (d + 1) * ch)
            w_low[one, :ch] = w_ref[0, d]
            w_low[one, ch:] = zero
            w_low[two, :ch] = w_ref[1, d]
            w_low[two, ch:] = w_ref[0, d]
            w_high[one, :ch] = w_ref[2, d]
            w_high[one, ch:] = w_ref[1, d]
            w_high[two, :ch] = zero
            w_high[two, ch:] = w_ref[2, d]

    def at(t):
        return t // steps, lax.rem(t, steps)

    def fill(taps, t):
        face, step = at(t)
        base = step * STEP

        def put(v, pair, side):
            low, same, high = shifted(v.astype(F32), zero_row, zero_row)
            place = side * half
            taps[pair, :, place : place + ch] = low
            taps[pair, :, place + ch : place + 2 * ch] = same
            taps[pair, :, place + 2 * ch : place + 3 * ch] = high

        inside = (step > 0).astype(F32)
        put(x_ref[face, jnp.maximum(base - 1, 0)].astype(F32) * inside, 0, 0)
        for row in range(STEP):
            put(x_ref[face, base + row], (row + 1) // 2, (row + 1) % 2)
        inside = (step < steps - 1).astype(F32)
        put(x_ref[face, jnp.minimum(base + STEP, size - 1)].astype(F32) * inside, pairs, 1)

    def product(taps, t):
        face, step = at(t)
        base = step * STEP
        lower = taps[pl.ds(0, pairs)].reshape(pairs * cols, 2 * half)
        upper = taps[pl.ds(1, pairs)].reshape(pairs * cols, 2 * half)
        total = jnp.dot(lower, w_low[...], preferred_element_type=F32)
        total += jnp.dot(upper, w_high[...], preferred_element_type=F32)
        total = total.reshape(pairs, cols, 2 * ch)
        bias = b_ref[...]
        for side in range(2):
            out = gelu(total[:, :, side * ch : (side + 1) * ch] + bias[None]).astype(BF)
            for pair in range(pairs):
                y_ref[face, base + 2 * pair + side] = out[pair]
    last = first + count - 1
    fill(taps_0, first)

    def double(j, carry):
        t = first + 2 * j
        fill(taps_1, t + 1)
        product(taps_0, t)
        fill(taps_0, jnp.minimum(t + 2, last))
        product(taps_1, t + 1)
        return carry

    lax.fori_loop(0, count // 2, double, 0)
    if count % 2:
        product(taps_0, last)


def in_hbm(x):
    return pltpu.with_memory_space_constraint(x, pltpu.HBM)


def conv_piece(x, weight, bias, first, count, state):
    faces, rows, cols, ch = x.shape
    vmem = pl.BlockSpec(memory_space=pltpu.VMEM)
    build = state is None
    taps = (STEP // 2 + 1, cols, 6 * ch)
    arranged = jax.ShapeDtypeStruct((6 * ch, 2 * ch), BF)
    args = [x, bias, weight] if build else [x, bias, *state]
    out_shape = [jax.ShapeDtypeStruct(x.shape, BF)] + [arranged] * (2 if build else 0)
    pixels = count * STEP * cols
    out = pl.pallas_call(
        functools.partial(conv_kernel, first, count, build),
        in_specs=[vmem] * len(args),
        out_specs=tuple([vmem] * len(out_shape)),
        out_shape=tuple(out_shape),
        scratch_shapes=[pltpu.VMEM(taps, BF), pltpu.VMEM(taps, BF)],
        input_output_aliases={} if build else {4: 0},
        cost_estimate=pl.CostEstimate(
            flops=pixels * 24 * ch * ch, bytes_accessed=4 * pixels * ch, transcendentals=0
        ),
        compiler_params=pltpu.CompilerParams(vmem_limit_bytes=16 * 2**20),
        name="conv_piece",
    )(*args)
    return (out[1], out[2], out[0]) if build else (state[0], state[1], out[0])


def down_kernel(y_ref, w_ref, b_ref, c_ref, y_out, c_out, taps_0, taps_1, sems):
    faces, rows, cols, ch = y_ref.shape
    steps, pairs = rows // STEP, STEP // 2
    count = faces * steps
    order = parting(cols)

    def copies(t):
        face, step = t // steps, lax.rem(t, steps)
        some, cells = pl.ds(step * STEP, STEP), pl.ds(step * pairs, pairs)
        return (
            pltpu.make_async_copy(y_ref.at[face, some], y_out.at[face, some], sems.at[0]),
            pltpu.make_async_copy(c_ref.at[face, cells], c_out.at[face, cells], sems.at[1]),
        )

    def fill(taps, t):
        face, step = t // steps, lax.rem(t, steps)
        for pair in range(pairs):
            row = step * STEP + 2 * pair
            both = jnp.concatenate([y_ref[face, row], y_ref[face, row + 1]], axis=1)
            four = parted(order, both)
            taps[pair] = jnp.concatenate([four[k] for k in (0, 2, 1, 3)], axis=1)

    def product(taps, t):
        face, step = t // steps, lax.rem(t, steps)
        out = jnp.dot(
            taps[...].reshape(pairs * cols // 2, 4 * ch),
            w_ref[...].reshape(4 * ch, -1),
            preferred_element_type=F32,
        )
        out = (out + b_ref[...]).astype(BF)
        c_ref[face, pl.ds(step * pairs, pairs)] = out.reshape(pairs, cols // 2, -1)
        copies(t)[1].start()

    def send(t, carry):
        copies(t)[0].start()
        return carry

    def wait(t, carry):
        for copy in copies(t):
            copy.wait()
        return carry

    lax.fori_loop(0, count, send, 0)
    fill(taps_0, 0)

    def double(j, carry):
        fill(taps_1, 2 * j + 1)
        product(taps_0, 2 * j)
        fill(taps_0, jnp.minimum(2 * j + 2, count - 1))
        product(taps_1, 2 * j + 1)
        return carry

    lax.fori_loop(0, count // 2, double, 0)
    if count % 2:
        product(taps_0, count - 1)
    lax.fori_loop(0, count, wait, 0)


def downsample(y, weight, bias):
    faces, rows, cols, ch = y.shape
    shape = (faces, rows // 2, cols // 2, weight.shape[-1])
    vmem = pl.BlockSpec(memory_space=pltpu.VMEM)
    hbm = pl.BlockSpec(memory_space=pltpu.HBM)
    taps = (STEP // 2, cols // 2, 4 * ch)
    return pl.pallas_call(
        down_kernel,
        in_specs=[vmem] * 3,
        out_specs=(vmem, hbm, hbm),
        out_shape=(jax.ShapeDtypeStruct(shape, BF), pltpu.HBM(y.shape, BF), pltpu.HBM(shape, BF)),
        scratch_shapes=[pltpu.VMEM(taps, BF), pltpu.VMEM(taps, BF), pltpu.SemaphoreType.DMA((2,))],
        cost_estimate=pl.CostEstimate(
            flops=faces * rows * cols * 2 * ch * shape[-1],
            bytes_accessed=4 * faces * rows * cols * ch,
            transcendentals=0,
        ),
        compiler_params=pltpu.CompilerParams(vmem_limit_bytes=16 * 2**20),
        name="downsample",
    )(y, weight, bias)


def column(tile, place):
    return tile[pl.ds(place, tile.shape[0] // STEP, stride=STEP), :]


def put_strips(i, r, c, lines, top, bottom, u_ref, v_ref, turn_ref, line_ref):
    left, left_in, right_in, right = lines
    size = left.shape[0]
    for place, value in enumerate(lines):
        line_ref[i, place] = value.astype(BF)
    side = jnp.where(c == 0, left, right).astype(BF)
    inner = jnp.where(c == 0, right, left).astype(BF)
    even = lax.rem(r, 2) == 0
    line = jnp.where(even, top, bottom).astype(BF)
    turn_ref[i] = jnp.where(even, bottom, top).astype(BF)
    for ref in (u_ref, v_ref):
        ref[i, 0] = side
        ref[i, 1] = line[:size]
        ref[i, 2] = line[size:]
    u_ref[i, 3] = inner


def strip_shapes(faces, rows, cols, ch):
    return (
        jax.ShapeDtypeStruct((faces, 4, rows, ch), BF),
        jax.ShapeDtypeStruct((faces, 3, rows, ch), BF),
        jax.ShapeDtypeStruct((faces, cols, ch), BF),
        jax.ShapeDtypeStruct((faces, 4, rows, ch), BF),
    )


def whole(shape):
    return pl.BlockSpec(shape, lambda *_: (0,) * len(shape))


def tile_copies(array, tiles, sems, back=False):
    cols = array.shape[2]
    out = []
    for side, start in enumerate((0, cols - STEP)):
        far, near = array.at[:, :, pl.ds(start, STEP), :], tiles.at[side]
        out.append(pltpu.make_async_copy(*((near, far) if back else (far, near)), sems.at[side]))
    return out


def strips_kernel(x_ref, u_ref, v_ref, turn_ref, line_ref, tiles, outer, left, right, sems):
    faces, rows, cols, ch = x_ref.shape
    r, c = lax.axis_index("row"), lax.axis_index("col")
    copies = tile_copies(x_ref, tiles, sems)
    for k, row in enumerate((0, rows - 1)):
        copies.append(pltpu.make_async_copy(x_ref.at[:, row], outer.at[k], sems.at[2 + k]))
    for copy in copies:
        copy.start()
    for copy in copies:
        copy.wait()

    def face(i, carry):
        left[...] = tiles[0, i].astype(F32).reshape(rows * STEP, ch)
        right[...] = tiles[1, i].astype(F32).reshape(rows * STEP, ch)
        lines = (column(left, 0), column(left, 1), column(right, STEP - 2), column(right, STEP - 1))
        put_strips(
            i, r, c, lines, outer[0, i].astype(F32), outer[1, i].astype(F32),
            u_ref, v_ref, turn_ref, line_ref,
        )
        return carry

    lax.fori_loop(0, faces, face, 0)


def strips_of(x):
    faces, rows, cols, ch = x.shape
    shapes = strip_shapes(faces, rows, cols, ch)
    return pl.pallas_call(
        strips_kernel,
        in_specs=[pl.BlockSpec(memory_space=pltpu.HBM)],
        out_specs=(pl.BlockSpec(memory_space=pltpu.VMEM),) * 4,
        out_shape=shapes,
        scratch_shapes=[
            pltpu.VMEM((2, faces, rows, STEP, ch), BF),
            pltpu.VMEM((2, faces, cols, ch), BF),
            pltpu.VMEM((rows * STEP, ch), F32),
            pltpu.VMEM((rows * STEP, ch), F32),
            pltpu.SemaphoreType.DMA((4,)),
        ],
        cost_estimate=pl.CostEstimate(flops=0, bytes_accessed=4 * 2**20, transcendentals=0),
        compiler_params=pltpu.CompilerParams(vmem_limit_bytes=10 * 2**20),
        name="strips_of",
    )(in_hbm(x))


def select_kernel(near_ref, code_ref, *refs):
    stores, outs, held = refs[:8], refs[8:-1], refs[-1]
    faces, _, size, ch = held.shape[1:]
    me, r, c = lax.axis_index("face"), lax.axis_index("row"), lax.axis_index("col")
    for k, store in enumerate(stores):
        for i in range(faces):
            held[k, i] = store[i, 0:3]

    def slot(row, col):
        return ((r ^ row) << 1) | (c ^ col)

    def quarter(edge, q):
        upright = lax.rem(edge, 2) == 1
        row = jnp.where(upright, q, jnp.where(edge == 0, 0, 3))
        col = jnp.where(upright, jnp.where(edge == 3, 0, 1), q >> 1)
        return slot(row, col), jnp.where(upright, 0, 1 + (q & 1))

    def end(n, where, block, last):
        head = held[where, n, block, 0:EXTRA].astype(F32)
        tail = held[where, n, block, size - EXTRA : size].astype(F32)
        return jnp.where(last, tail[EXTRA - 1 : EXTRA], head[0:1])

    spot = lax.broadcasted_iota(jnp.int32, (EXTRA, 1), 0)
    for k, out in enumerate(outs):
        target = me ^ k

        def face(i, carry, k=k, out=out, target=target):
            f = target * faces + i
            edge = 3 - 2 * c
            code = code_ref[edge, f]
            far, flip = code >> 1, code & 1
            n = lax.rem(near_ref[edge, f], faces)
            where, block = quarter(far, jnp.where(flip == 1, 3 - r, r))
            out[i, 0:size] = held[where, n, block]
            corner = jnp.where(r < 2, c, 3 - c)
            tip = code_ref[4 + corner, f]
            tip_n = lax.rem(near_ref[4 + corner, f], faces)
            tip_row = jnp.where(tip < 2, 0, 3)
            tip_col = jnp.where((tip == 1) | (tip == 2), 1, 0)
            tip_pixel = end(tip_n, slot(tip_row, tip_col), 0, tip_row == 3)
            q = jnp.where(flip == 1, 4 - r, r - 1)
            where, block = quarter(far, jnp.clip(q, 0, 3))
            before = jnp.where(r == 0, tip_pixel, end(n, where, block, flip == 0))
            q = jnp.where(flip == 1, 2 - r, r + 1)
            where, block = quarter(far, jnp.clip(q, 0, 3))
            after = jnp.where(r == 3, tip_pixel, end(n, where, block, flip == 1))

            edge = jnp.where(r < 2, 0, 2)
            code = code_ref[edge, f]
            far, flip = code >> 1, code & 1
            n = lax.rem(near_ref[edge, f], faces)
            part = c ^ flip
            for h in range(out.shape[1] // size - 1):
                own = jnp.where((r == 0) | (r == 3), 0, 1) if k else h
                where, block = quarter(far, 2 * part + own)
                out[i, (1 + h) * size : (2 + h) * size] = held[where, n, block]
            where, block = quarter(far, jnp.where(part == 0, 2, 1))
            middle = end(n, where, block, part == 1)
            single = jnp.where(spot == 0, before, jnp.where(spot == 1, after, middle))
            out[i, out.shape[1] - EXTRA :] = single.astype(BF)
            return carry

        lax.fori_loop(0, faces, face, 0)


def select_strips(neighbour_face, orientation, stores, groups):
    faces, _, size, ch = stores[0].shape
    shapes = [
        jax.ShapeDtypeStruct((faces, (2 if k else 3) * size + EXTRA, ch), BF) for k in range(groups)
    ]
    smem = pl.BlockSpec(memory_space=pltpu.SMEM)
    return pl.pallas_call(
        select_kernel,
        in_specs=[smem, smem] + [pl.BlockSpec(memory_space=pltpu.VMEM)] * 8,
        out_specs=(pl.BlockSpec(memory_space=pltpu.VMEM),) * groups,
        out_shape=tuple(shapes),
        scratch_shapes=[pltpu.VMEM((8, faces, 3, size, ch), BF)],
        cost_estimate=pl.CostEstimate(flops=0, bytes_accessed=4 * 2**20, transcendentals=0),
        compiler_params=pltpu.CompilerParams(vmem_limit_bytes=10 * 2**20),
        name="select_strips",
    )(neighbour_face, orientation, *stores)


def ring_kernel(groups, coarse, near_ref, code_ref, x_ref, y_in, line_in, beside, diagonal, across,
                far_diagonal, turned, w_ref, b_ref, *refs):
    seams, seconds, refs = refs[:groups], refs[groups : 2 * groups - 1], refs[2 * groups - 1 :]
    if coarse:
        c_ref, dw_ref, db_ref, _, _, y_out, c_out = refs[:7]
        y_ref = y_in
        scratch = refs[7:]
        *scratch, c_taps, c_tiles, c_rows, c_cols, c_left, sems = scratch
    else:
        y_ref, outs, scratch = refs[0], refs[1:5], refs[5:]
    tiles, edge_rows, edge_cols, held, left, right, w_cols, across_taps, along_taps = scratch
    faces, rows, cols, ch = x_ref.shape
    me, r, c = lax.axis_index("face"), lax.axis_index("row"), lax.axis_index("col")
    for k in range(groups):
        seam = seams[k]
        extras = slice(seam.shape[1] - EXTRA, seam.shape[1])
        held[k, :, : 2 * rows] = seam[:, : 2 * rows]
        held[k, :, 2 * rows : 3 * rows] = (
            seconds[k - 1][:, rows : 2 * rows] if k else seam[:, 2 * rows : 3 * rows]
        )
        held[k, :, 3 * rows :] = seam[:, extras]

    def oriented(v, flip):
        n = v.shape[0]
        to = lax.broadcasted_iota(jnp.int32, (n, n), 0)
        source = lax.broadcasted_iota(jnp.int32, (n, n), 1)
        order = jnp.where(source == jnp.where(flip == 1, n - 1 - to, to), 1.0, 0.0).astype(BF)
        return jnp.dot(order, v, preferred_element_type=F32)

    even = lax.rem(r, 2) == 0
    outer = (r == 0) | (r == 3)
    for d in range(3):
        for a in range(3):
            w_cols[(3 * d + a) * ch : (3 * d + a + 1) * ch] = w_ref[a, d]
    bias = b_ref[...]

    def holder(n):
        return jnp.minimum(n, FACES - 1) // faces ^ me

    def put(taps, place, v, before, after, third):
        for k, part in enumerate(shifted(v, before, after)):
            start = (3 * third + k) * ch
            taps[pl.ds(place, v.shape[0]), start : start + ch] = part

    def face(i):
        f = me * faces + i
        edge = 3 - 2 * c
        n = near_ref[edge, f]
        corner = jnp.where(r < 2, c, 3 - c)
        tip_n = near_ref[4 + corner, f]
        seam_side = oriented(held[holder(n), i, 0:rows], code_ref[edge, f] & 1)
        extra = slice(3 * rows, 3 * rows + EXTRA)
        n_before = jnp.where(r == 0, tip_n, n)
        n_after = jnp.where(r == 3, tip_n, n)
        before = held[holder(n_before), i, extra].astype(F32)[0:1]
        after = held[holder(n_after), i, extra].astype(F32)[1:2]
        before = jnp.where(n_before < FACES, before, 0.0)
        after = jnp.where(n_after < FACES, after, 0.0)
        edge = jnp.where(r < 2, 0, 2)
        n = near_ref[edge, f]
        seam_line = oriented(held[holder(n), i, rows : 3 * rows], code_ref[edge, f] & 1)
        middle = held[holder(n), i, extra].astype(F32)[2:3]

        inner = beside[i, 3].astype(F32)
        block_line = jnp.concatenate([across[i, 1], across[i, 2]], axis=0).astype(F32)
        outward = jnp.where(outer, seam_line, block_line)
        inward = turned[i].astype(F32)
        top = jnp.where(even, outward, inward)
        bottom = jnp.where(even, inward, outward)
        lft = jnp.where(c == 0, seam_side, inner)
        rgt = jnp.where(c == 0, inner, seam_side)
        pair_inner = diagonal[i, 3].astype(F32)
        inward_corner = jnp.where(even, pair_inner[0:1], pair_inner[rows - 1 : rows])
        far_first = far_diagonal[i, 1].astype(F32)[0:1]
        far_last = far_diagonal[i, 2].astype(F32)[rows - 1 : rows]
        outward_corner = jnp.where(outer, middle, jnp.where(c == 0, far_first, far_last))
        inner_top = jnp.where(even, outward_corner, inward_corner)
        inner_bottom = jnp.where(even, inward_corner, outward_corner)
        top_left = jnp.where(c == 0, before, inner_top)
        top_right = jnp.where(c == 0, inner_top, before)
        bottom_left = jnp.where(c == 0, after, inner_bottom)
        bottom_right = jnp.where(c == 0, inner_bottom, after)

        row_0, row_1, row_2, row_3 = (
            x_ref[i, k].astype(F32) for k in (0, 1, rows - 2, rows - 1)
        )
        place = 2 * i * cols
        put(across_taps, place, top, top_left, top_right, 0)
        put(across_taps, place, row_0, lft[0:1], rgt[0:1], 1)
        put(across_taps, place, row_1, lft[1:2], rgt[1:2], 2)
        place += cols
        put(across_taps, place, row_2, lft[rows - 2 : rows - 1], rgt[rows - 2 : rows - 1], 0)
        put(across_taps, place, row_3, lft[rows - 1 : rows], rgt[rows - 1 : rows], 1)
        put(across_taps, place, bottom, bottom_left, bottom_right, 2)
        col_0, col_1, col_2, col_3 = (line_in[i, k].astype(F32) for k in range(4))
        place = 2 * i * rows
        put(along_taps, place, lft, top_left, bottom_left, 0)
        put(along_taps, place, col_0, top[0:1], bottom[0:1], 1)
        put(along_taps, place, col_1, top[1:2], bottom[1:2], 2)
        place += rows
        put(along_taps, place, col_2, top[cols - 2 : cols - 1], bottom[cols - 2 : cols - 1], 0)
        put(along_taps, place, col_3, top[cols - 1 : cols], bottom[cols - 1 : cols], 1)
        put(along_taps, place, rgt, top_right, bottom_right, 2)

    for i in range(faces):
        face(i)
    w_rows = w_ref[...].reshape(9 * ch, ch)
    out = gelu(jnp.dot(across_taps[...], w_rows, preferred_element_type=F32) + bias)
    edge_rows[...] = out.astype(BF).reshape(edge_rows.shape)
    out = gelu(jnp.dot(along_taps[...], w_cols[...], preferred_element_type=F32) + bias)
    edge_cols[...] = out.reshape(edge_cols.shape)
    between = slice(STEP, cols - STEP)
    if coarse:
        order_cols, order_rows = parting(cols), parting(rows)

    def update(i, carry):
        new_top, new_bottom = edge_rows[i, 0].astype(F32), edge_rows[i, 1].astype(F32)
        if cols > 2 * STEP and not coarse:
            y_ref[i, 0, between] = edge_rows[i, 0, between]
            y_ref[i, rows - 1, between] = edge_rows[i, 1, between]
        for tile, side, place in ((left, 0, 0), (right, 1, STEP - 1)):
            start = side * (cols - STEP)
            tiles[side, i] = y_ref[i, :, start : start + STEP]
            tiles[side, i, 0] = edge_rows[i, 0, start : start + STEP]
            tiles[side, i, rows - 1] = edge_rows[i, 1, start : start + STEP]
            tile[...] = tiles[side, i].astype(F32).reshape(rows * STEP, ch)
            tile[pl.ds(place, rows, stride=STEP), :] = edge_cols[i, pl.ds(side * rows, rows)]
            value = tile[...].astype(BF).reshape(rows, STEP, ch)
            if coarse:
                tiles[side, i] = value
            else:
                y_ref[i, :, start : start + STEP] = value
        lines = (
            column(left, 0), column(left, 1), column(right, STEP - 2), column(right, STEP - 1)
        )
        if not coarse:
            put_strips(i, r, c, lines, new_top, new_bottom, *outs)
            return carry
        spot = lax.broadcasted_iota(jnp.int32, (cols, 1), 0)
        half = cols // 2
        for k, (own, near) in enumerate(((new_top, 1), (new_bottom, rows - 2))):
            first = edge_cols[i, near : near + 1]
            last = edge_cols[i, rows + near : rows + near + 1]
            other = y_ref[i, near].astype(F32)
            other = jnp.where(spot == 0, first, jnp.where(spot == cols - 1, last, other))
            both = (own, other) if k == 0 else (other, own)
            four = parted(order_cols, jnp.concatenate([v.astype(BF) for v in both], axis=1))
            four = jnp.concatenate([four[j] for j in (0, 2, 1, 3)], axis=1)
            c_taps[pl.ds((2 * i + k) * half, half)] = four
        for k, both in enumerate((lines[:2], lines[2:])):
            four = parted(order_rows, jnp.concatenate([v.astype(BF) for v in both], axis=1))
            place = 2 * faces * half + (2 * i + k) * (rows // 2)
            c_taps[pl.ds(place, rows // 2)] = jnp.concatenate(four, axis=1)
        return carry

    lax.fori_loop(0, faces, update, 0, unroll=True)
    if not coarse:
        return
    copies = tile_copies(y_out, tiles, sems, back=True)
    if cols > 2 * STEP:
        between = pl.ds(STEP, cols - 2 * STEP)
        for k, row in enumerate((0, rows - 1)):
            copies.append(
                pltpu.make_async_copy(
                    edge_rows.at[:, k, between], y_out.at[:, row, between], sems.at[2 + k]
                )
            )
    for copy in copies:
        copy.start()
    half = cols // 2
    out = jnp.dot(
        c_taps[...], dw_ref[...].reshape(4 * ch, -1), preferred_element_type=F32
    ) + db_ref[...]
    across_cells = 2 * faces * half
    c_rows[...] = out[:across_cells].astype(BF).reshape(c_rows.shape)
    c_cols[...] = out[across_cells:].reshape(c_cols.shape)

    def cells(i, carry):
        for side in range(2):
            start = side * (half - STEP)
            c_tiles[side, i] = c_ref[i, :, start : start + STEP]
            for k in range(2):
                c_tiles[side, i, k * (rows // 2 - 1)] = c_rows[i, k, start : start + STEP]
            for h in range(c_cols.shape[-1] // ch):
                lanes = slice(h * ch, (h + 1) * ch)
                c_left[...] = c_tiles[side, i, :, :, lanes].astype(F32).reshape(rows // 2 * STEP, ch)
                c_left[pl.ds(side * (STEP - 1), rows // 2, stride=STEP), :] = c_cols[i, side, :, lanes]
                c_tiles[side, i, :, :, lanes] = (
                    c_left[...].astype(BF).reshape(rows // 2, STEP, ch)
                )
        return carry

    lax.fori_loop(0, faces, cells, 0)
    more = []
    for side, start in enumerate((0, half - STEP)):
        more.append(
            pltpu.make_async_copy(
                c_tiles.at[side], c_out.at[:, :, pl.ds(start, STEP), :], sems.at[4 + side]
            )
        )
    if half > 2 * STEP:
        between = pl.ds(STEP, half - 2 * STEP)
        for k, row in enumerate((0, rows // 2 - 1)):
            more.append(
                pltpu.make_async_copy(
                    c_rows.at[:, k, between], c_out.at[:, row, between], sems.at[6 + k]
                )
            )
    for copy in more:
        copy.start()
    for copy in copies + more:
        copy.wait()


def ring(
    neighbour_face, orientation, x, buffers, copied, lines, parts, weight, bias, seams, seconds, down
):
    y, *coarse = buffers
    faces, rows, cols, ch = x.shape
    groups = len(seams)
    smem = pl.BlockSpec(memory_space=pltpu.SMEM)
    hbm = pl.BlockSpec(memory_space=pltpu.HBM)
    vmem = pl.BlockSpec(memory_space=pltpu.VMEM)
    args = [neighbour_face, orientation, x, y, lines, *parts, weight, bias, *seams, *seconds]
    in_specs = [smem, smem] + [vmem] * (len(args) - 2)
    scratch = [
        pltpu.VMEM((2, faces, rows, STEP, ch), BF),
        pltpu.VMEM((faces, 2, cols, ch), BF),
        pltpu.VMEM((faces, 2 * rows, ch), F32),
        pltpu.VMEM((groups, faces, 3 * rows + EXTRA, ch), BF),
        pltpu.VMEM((rows * STEP, ch), F32),
        pltpu.VMEM((rows * STEP, ch), F32),
        pltpu.VMEM((9 * ch, ch), BF),
        pltpu.VMEM((2 * faces * cols, 9 * ch), BF),
        pltpu.VMEM((2 * faces * rows, 9 * ch), BF),
    ]
    if down:
        co = down[0].shape[-1]
        args += [coarse[0], *down]
        in_specs += [vmem] * 3
        aliases = {len(args): 0, len(args) + 1: 1}
        args += [in_hbm(buffer) for buffer in copied]
        in_specs += [hbm] * 2
        out_shape = [pltpu.HBM(buffer.shape, BF) for buffer in copied]
        out_specs = [hbm] * 2
        scratch += [
            pltpu.VMEM((faces * (rows + cols), 4 * ch), BF),
            pltpu.VMEM((2, faces, rows // 2, STEP, co), BF),
            pltpu.VMEM((faces, 2, cols // 2, co), BF),
            pltpu.VMEM((faces, 2, rows // 2, co), F32),
            pltpu.VMEM((rows // 2 * STEP, ch), F32),
            pltpu.SemaphoreType.DMA((8,)),
        ]
    else:
        aliases = {3: 0}
        out_shape = [jax.ShapeDtypeStruct(y.shape, BF), *strip_shapes(faces, rows, cols, ch)]
        out_specs = [vmem] * 5
    return pl.pallas_call(
        functools.partial(ring_kernel, groups, bool(down)),
        in_specs=in_specs,
        out_specs=tuple(out_specs),
        out_shape=tuple(out_shape),
        scratch_shapes=scratch,
        input_output_aliases=aliases,
        cost_estimate=pl.CostEstimate(
            flops=faces * (rows + cols) * 36 * ch * ch, bytes_accessed=8 * 2**20, transcendentals=0
        ),
        compiler_params=pltpu.CompilerParams(vmem_limit_bytes=20 * 2**20),
        name="ring",
    )(*args)


def blocks(change_row, change_col):
    cols = lax.axis_size("col")
    return [
        (r * cols + c, (r ^ change_row) * cols + (c ^ change_col))
        for r in range(lax.axis_size("row"))
        for c in range(cols)
    ]


def swap(v, change_row, change_col):
    return lax.ppermute(v, ("row", "col"), blocks(change_row, change_col))


def level(neighbour_face, orientation, x, strips, weight, bias, down):
    u, v, turn, lines = strips
    groups = lax.axis_size("face")
    total = x.shape[0] * x.shape[1] // STEP
    early = max(total * 5 // 12, 1)
    piece = functools.partial(conv_piece, x, weight, bias)
    beside, across, diagonal = swap(u, 0, 1), swap(v, 3, 0), swap(v, 3, 1)
    pair, turned = swap(v, 1, 0), swap(turn, 1, 0)
    state = piece(0, early, None)
    (beside, across, diagonal), state = lax.optimization_barrier(
        ((beside, across, diagonal), state)
    )
    pair_beside, pair_across, pair_diagonal = (swap(a, 1, 0) for a in (beside, across, diagonal))
    stores = (v, beside, pair, pair_beside, pair_across, pair_diagonal, across, diagonal)
    picked = select_strips(neighbour_face, orientation, stores, groups)
    picked, state = lax.optimization_barrier((picked, state))
    seams = list(picked)
    for k in sorted(range(1, groups), key=lambda k: -(k.bit_length())):
        pairs = [(g, g ^ k) for g in range(groups)]
        seams[k] = lax.ppermute(picked[k], "face", pairs)
    buffers, copied = piece(early, total - early, state)[2:], ()
    if down:
        coarse, *copied = downsample(buffers[0], *down)
        buffers += (coarse,)
    parts = (beside, pair_beside, across, diagonal, turned)
    seams[1:], buffers = lax.optimization_barrier((seams[1:], buffers))
    seconds = [swap(seam, 1, 0) for seam in seams[1:]]
    return ring(
        *(neighbour_face, orientation, x, buffers, copied, lines, parts, weight, bias),
        *(seams, seconds, down),
    )


def per_device(
    field, conv1_w, conv1_b, conv2_w, conv2_b, down_w, down_b, neighbour_face, orientation
):
    tables = (neighbour_face.T, orientation.T)
    hidden, *strips = level(*tables, field, strips_of(field), conv1_w, conv1_b[None], ())
    return level(*tables, hidden, strips, conv2_w, conv2_b[None], (down_w, down_b[None]))


def solution(mesh):
    groups = mesh.shape["face"]
    fast = mesh.shape["row"] == 4 and mesh.shape["col"] == 2 and groups & (groups - 1) == 0
    return jax.shard_map(
        per_device if fast else general_device,
        mesh=mesh,
        in_specs=(P("face", "row", "col", None), P(), P(), P(), P(), P(), P(), P(), P()),
        out_specs=(P("face", "row", "col", None), P("face", "row", "col", None)),
        check_vma=False,
    )
```

```python
import functools

import jax
import jax.numpy as jnp
import numpy as np
from jax import lax
from jax.experimental import pallas as pl
from jax.experimental.pallas import tpu as pltpu
from jax.sharding import PartitionSpec as P


FACES = 12
BF = jnp.bfloat16
F32 = jnp.float32
STEP = 16
EXTRA = 16

layout = ("NHWC", "HWIO", "NHWC")


def padded_2(block, sides, width):
    for axis, dim in sides:
        count = lax.axis_size(axis)
        forward = [(i, i + 1) for i in range(count - 1)]
        backward = [(target, source) for source, target in forward]
        low = lax.ppermute(
            lax.slice_in_dim(block, block.shape[dim] - width, None, axis=dim), axis, forward
        )
        high = lax.ppermute(lax.slice_in_dim(block, 0, width, axis=dim), axis, backward)
        block = jnp.concatenate([low, block, high], axis=dim)
    return block


def seam_parts(edges, neighbours, codes):
    seam_faces = neighbours[:, :4]
    seam_codes = codes[:, :4]
    seams = edges[seam_faces, seam_codes // 2]
    seams = jnp.where((seam_codes % 2 == 1)[:, :, None, None], seams[:, :, ::-1], seams)
    corner_values = jnp.stack(
        [edges[:, 0, 0], edges[:, 0, -1], edges[:, 2, -1], edges[:, 2, 0]], axis=1
    )
    corner_faces = neighbours[:, 4:]
    picked = corner_values[jnp.minimum(corner_faces, FACES - 1), codes[:, 4:]]
    picked = jnp.where((corner_faces < FACES)[:, :, None], picked, jnp.zeros_like(picked))
    return (seams, picked)


def convolve(padded, weight, bias):
    summed = lax.conv_general_dilated(
        padded,
        weight,
        (1, 1),
        "VALID",
        dimension_numbers=layout,
        preferred_element_type=jnp.float32,
    )
    return jax.nn.gelu(summed + bias, approximate=False).astype(jnp.bfloat16)


def general_layer(block, weight, bias, neighbour_face, orientation):
    face_count, row_size, col_size, channels = block.shape
    row_total = lax.axis_size("row")
    col_total = lax.axis_size("col")
    row_place = lax.axis_index("row")
    col_place = lax.axis_index("col")
    face_side = row_size * row_total
    padded = padded_2(block, (("row", 1), ("col", 2)), 1)
    top_live = row_place == 0
    bottom_live = row_place == row_total - 1
    left_live = col_place == 0
    right_live = col_place == col_total - 1
    empty_line = jnp.zeros((face_count, face_side, channels), jnp.float32)

    def place(strip, offset, live):
        scaled = strip.astype(jnp.float32) * live.astype(jnp.float32)
        return lax.dynamic_update_slice_in_dim(empty_line, scaled, offset, 1)

    lines = jnp.stack(
        [
            place(block[:, 0], col_place * col_size, top_live),
            place(block[:, :, -1], row_place * row_size, right_live),
            place(block[:, -1], col_place * col_size, bottom_live),
            place(block[:, :, 0], row_place * row_size, left_live),
        ],
        axis=1,
    )
    complete = lax.psum(lax.psum(lines.astype(jnp.bfloat16), "col"), "row").astype(jnp.float32)
    every_edge = lax.all_gather(complete.astype(jnp.bfloat16), "face", axis=0, tiled=True)
    first_face = lax.axis_index("face") * face_count
    own_faces = lax.dynamic_slice_in_dim(neighbour_face, first_face, face_count, 0)
    own_codes = lax.dynamic_slice_in_dim(orientation, first_face, face_count, 0)
    seams, corners = seam_parts(every_edge, own_faces, own_codes)
    upper = jnp.concatenate([corners[:, 0:1], seams[:, 0], corners[:, 1:2]], 1)
    lower = jnp.concatenate([corners[:, 3:4], seams[:, 2], corners[:, 2:3]], 1)
    leftward = jnp.concatenate([corners[:, 0:1], seams[:, 3], corners[:, 3:4]], 1)
    rightward = jnp.concatenate([corners[:, 1:2], seams[:, 1], corners[:, 2:3]], 1)
    upper_cut = lax.dynamic_slice_in_dim(upper, col_place * col_size, col_size + 2, 1)
    lower_cut = lax.dynamic_slice_in_dim(lower, col_place * col_size, col_size + 2, 1)
    left_cut = lax.dynamic_slice_in_dim(leftward, row_place * row_size, row_size + 2, 1)
    right_cut = lax.dynamic_slice_in_dim(rightward, row_place * row_size, row_size + 2, 1)
    padded = padded.at[:, 0].set(jnp.where(top_live, upper_cut, padded[:, 0]))
    padded = padded.at[:, -1].set(jnp.where(bottom_live, lower_cut, padded[:, -1]))
    padded = padded.at[:, :, 0].set(jnp.where(left_live, left_cut, padded[:, :, 0]))
    padded = padded.at[:, :, -1].set(jnp.where(right_live, right_cut, padded[:, :, -1]))
    return convolve(padded, weight, bias)


def general_device(
    field, conv1_w, conv1_b, conv2_w, conv2_b, down_w, down_b, neighbour_face, orientation
):
    hidden = general_layer(field, conv1_w, conv1_b, neighbour_face, orientation)
    skip = general_layer(hidden, conv2_w, conv2_b, neighbour_face, orientation)
    summed = lax.conv_general_dilated(
        skip, down_w, (2, 2), "VALID", dimension_numbers=layout, preferred_element_type=jnp.float32
    )
    coarse = (summed + down_b).astype(jnp.bfloat16)
    return (skip, coarse)


def gelu(v):
    return 0.5 * v * (1.0 + lax.erf(v * np.float32(np.sqrt(0.5))))


def shifted(v, before, after):
    n = v.shape[0]
    spot = lax.broadcasted_iota(jnp.int32, (n, 1), 0)
    low = jnp.where(spot == 0, before, pltpu.roll(v, 1, 0))
    high = jnp.where(spot == n - 1, after, pltpu.roll(v, n - 1, 0))
    return low.astype(BF), v.astype(BF), high.astype(BF)


def parting(n):
    to = lax.broadcasted_iota(jnp.int32, (n, n), 0)
    source = lax.broadcasted_iota(jnp.int32, (n, n), 1)
    half = n // 2
    return jnp.where(source == jnp.where(to < half, 2 * to, 2 * (to - half) + 1), 1.0, 0.0).astype(BF)


def parted(order, v):
    v = jnp.dot(order, v, preferred_element_type=F32).astype(BF)
    half, lanes = v.shape[0] // 2, v.shape[1] // 2
    return v[:half, :lanes], v[:half, lanes:], v[half:, :lanes], v[half:, lanes:]


def conv_kernel(first, count, build, x_ref, b_ref, *refs):
    *refs, taps_0, taps_1 = refs
    if build:
        w_ref, y_ref, w_low, w_high = refs
    else:
        w_low, w_high, _, y_ref = refs
    _, size, cols, ch = x_ref.shape
    steps = size // STEP
    pairs = STEP // 2
    zero_row = jnp.zeros((1, ch), F32)
    half = 3 * ch

    if build:
        zero = jnp.zeros((ch, ch), BF)
        for d in range(3):
            one = slice(d * ch, (d + 1) * ch)
            two = slice(half + d * ch, half + (d + 1) * ch)
            w_low[one, :ch] = w_ref[0, d]
            w_low[one, ch:] = zero
            w_low[two, :ch] = w_ref[1, d]
            w_low[two, ch:] = w_ref[0, d]
            w_high[one, :ch] = w_ref[2, d]
            w_high[one, ch:] = w_ref[1, d]
            w_high[two, :ch] = zero
            w_high[two, ch:] = w_ref[2, d]

    def at(t):
        return t // steps, lax.rem(t, steps)

    def fill(taps, t):
        face, step = at(t)
        base = step * STEP

        def put(v, pair, side):
            low, same, high = shifted(v.astype(F32), zero_row, zero_row)
            place = side * half
            taps[pair, :, place : place + ch] = low
            taps[pair, :, place + ch : place + 2 * ch] = same
            taps[pair, :, place + 2 * ch : place + 3 * ch] = high

        inside = (step > 0).astype(F32)
        put(x_ref[face, jnp.maximum(base - 1, 0)].astype(F32) * inside, 0, 0)
        for row in range(STEP):
            put(x_ref[face, base + row], (row + 1) // 2, (row + 1) % 2)
        inside = (step < steps - 1).astype(F32)
        put(x_ref[face, jnp.minimum(base + STEP, size - 1)].astype(F32) * inside, pairs, 1)

    def product(taps, t):
        face, step = at(t)
        base = step * STEP
        lower = taps[pl.ds(0, pairs)].reshape(pairs * cols, 2 * half)
        upper = taps[pl.ds(1, pairs)].reshape(pairs * cols, 2 * half)
        total = jnp.dot(lower, w_low[...], preferred_element_type=F32)
        total += jnp.dot(upper, w_high[...], preferred_element_type=F32)
        total = total.reshape(pairs, cols, 2 * ch)
        bias = b_ref[...]
        for side in range(2):
            out = gelu(total[:, :, side * ch : (side + 1) * ch] + bias[None]).astype(BF)
            for pair in range(pairs):
                y_ref[face, base + 2 * pair + side] = out[pair]
    last = first + count - 1
    fill(taps_0, first)

    def double(j, carry):
        t = first + 2 * j
        fill(taps_1, t + 1)
        product(taps_0, t)
        fill(taps_0, jnp.minimum(t + 2, last))
        product(taps_1, t + 1)
        return carry

    lax.fori_loop(0, count // 2, double, 0)
    if count % 2:
        product(taps_0, last)


def in_hbm(x):
    return pltpu.with_memory_space_constraint(x, pltpu.HBM)


def conv_piece(x, weight, bias, first, count, state):
    faces, rows, cols, ch = x.shape
    vmem = pl.BlockSpec(memory_space=pltpu.VMEM)
    build = state is None
    taps = (STEP // 2 + 1, cols, 6 * ch)
    arranged = jax.ShapeDtypeStruct((6 * ch, 2 * ch), BF)
    args = [x, bias, weight] if build else [x, bias, *state]
    out_shape = [jax.ShapeDtypeStruct(x.shape, BF)] + [arranged] * (2 if build else 0)
    pixels = count * STEP * cols
    out = pl.pallas_call(
        functools.partial(conv_kernel, first, count, build),
        in_specs=[vmem] * len(args),
        out_specs=tuple([vmem] * len(out_shape)),
        out_shape=tuple(out_shape),
        scratch_shapes=[pltpu.VMEM(taps, BF), pltpu.VMEM(taps, BF)],
        input_output_aliases={} if build else {4: 0},
        cost_estimate=pl.CostEstimate(
            flops=pixels * 24 * ch * ch, bytes_accessed=4 * pixels * ch, transcendentals=0
        ),
        compiler_params=pltpu.CompilerParams(vmem_limit_bytes=16 * 2**20),
        name="conv_piece",
    )(*args)
    return (out[1], out[2], out[0]) if build else (state[0], state[1], out[0])


def down_kernel(y_ref, w_ref, b_ref, c_ref, y_out, c_out, taps_0, taps_1, sems):
    faces, rows, cols, ch = y_ref.shape
    steps, pairs = rows // STEP, STEP // 2
    count = faces * steps
    order = parting(cols)

    def copies(t):
        face, step = t // steps, lax.rem(t, steps)
        some, cells = pl.ds(step * STEP, STEP), pl.ds(step * pairs, pairs)
        return (
            pltpu.make_async_copy(y_ref.at[face, some], y_out.at[face, some], sems.at[0]),
            pltpu.make_async_copy(c_ref.at[face, cells], c_out.at[face, cells], sems.at[1]),
        )

    def fill(taps, t):
        face, step = t // steps, lax.rem(t, steps)
        for pair in range(pairs):
            row = step * STEP + 2 * pair
            both = jnp.concatenate([y_ref[face, row], y_ref[face, row + 1]], axis=1)
            four = parted(order, both)
            taps[pair] = jnp.concatenate([four[k] for k in (0, 2, 1, 3)], axis=1)

    def product(taps, t):
        face, step = t // steps, lax.rem(t, steps)
        out = jnp.dot(
            taps[...].reshape(pairs * cols // 2, 4 * ch),
            w_ref[...].reshape(4 * ch, -1),
            preferred_element_type=F32,
        )
        out = (out + b_ref[...]).astype(BF)
        c_ref[face, pl.ds(step * pairs, pairs)] = out.reshape(pairs, cols // 2, -1)
        copies(t)[1].start()

    def send(t, carry):
        copies(t)[0].start()
        return carry

    def wait(t, carry):
        for copy in copies(t):
            copy.wait()
        return carry

    lax.fori_loop(0, count, send, 0)
    fill(taps_0, 0)

    def double(j, carry):
        fill(taps_1, 2 * j + 1)
        product(taps_0, 2 * j)
        fill(taps_0, jnp.minimum(2 * j + 2, count - 1))
        product(taps_1, 2 * j + 1)
        return carry

    lax.fori_loop(0, count // 2, double, 0, unroll=True)
    if count % 2:
        product(taps_0, count - 1)
    lax.fori_loop(0, count, wait, 0)


def downsample(y, weight, bias):
    faces, rows, cols, ch = y.shape
    shape = (faces, rows // 2, cols // 2, weight.shape[-1])
    vmem = pl.BlockSpec(memory_space=pltpu.VMEM)
    hbm = pl.BlockSpec(memory_space=pltpu.HBM)
    taps = (STEP // 2, cols // 2, 4 * ch)
    return pl.pallas_call(
        down_kernel,
        in_specs=[vmem] * 3,
        out_specs=(vmem, hbm, hbm),
        out_shape=(jax.ShapeDtypeStruct(shape, BF), pltpu.HBM(y.shape, BF), pltpu.HBM(shape, BF)),
        scratch_shapes=[pltpu.VMEM(taps, BF), pltpu.VMEM(taps, BF), pltpu.SemaphoreType.DMA((2,))],
        cost_estimate=pl.CostEstimate(
            flops=faces * rows * cols * 2 * ch * shape[-1],
            bytes_accessed=4 * faces * rows * cols * ch,
            transcendentals=0,
        ),
        compiler_params=pltpu.CompilerParams(vmem_limit_bytes=16 * 2**20),
        name="downsample",
    )(y, weight, bias)


def column(tile, place):
    return tile[pl.ds(place, tile.shape[0] // STEP, stride=STEP), :]


def put_strips(i, r, c, lines, top, bottom, u_ref, v_ref, turn_ref, line_ref):
    left, left_in, right_in, right = lines
    size = left.shape[0]
    for place, value in enumerate(lines):
        line_ref[i, place] = value.astype(BF)
    side = jnp.where(c == 0, left, right).astype(BF)
    inner = jnp.where(c == 0, right, left).astype(BF)
    even = lax.rem(r, 2) == 0
    line = jnp.where(even, top, bottom).astype(BF)
    turn_ref[i] = jnp.where(even, bottom, top).astype(BF)
    for ref in (u_ref, v_ref):
        ref[i, 0] = side
        ref[i, 1] = line[:size]
        ref[i, 2] = line[size:]
    u_ref[i, 3] = inner


def strip_shapes(faces, rows, cols, ch):
    return (
        jax.ShapeDtypeStruct((faces, 4, rows, ch), BF),
        jax.ShapeDtypeStruct((faces, 3, rows, ch), BF),
        jax.ShapeDtypeStruct((faces, cols, ch), BF),
        jax.ShapeDtypeStruct((faces, 4, rows, ch), BF),
    )


def whole(shape):
    return pl.BlockSpec(shape, lambda *_: (0,) * len(shape))


def tile_copies(array, tiles, sems, back=False):
    cols = array.shape[2]
    out = []
    for side, start in enumerate((0, cols - STEP)):
        far, near = array.at[:, :, pl.ds(start, STEP), :], tiles.at[side]
        out.append(pltpu.make_async_copy(*((near, far) if back else (far, near)), sems.at[side]))
    return out


def strips_kernel(x_ref, u_ref, v_ref, turn_ref, line_ref, tiles, outer, left, right, sems):
    faces, rows, cols, ch = x_ref.shape
    r, c = lax.axis_index("row"), lax.axis_index("col")
    copies = tile_copies(x_ref, tiles, sems)
    for k, row in enumerate((0, rows - 1)):
        copies.append(pltpu.make_async_copy(x_ref.at[:, row], outer.at[k], sems.at[2 + k]))
    for copy in copies:
        copy.start()
    for copy in copies:
        copy.wait()

    def face(i, carry):
        left[...] = tiles[0, i].astype(F32).reshape(rows * STEP, ch)
        right[...] = tiles[1, i].astype(F32).reshape(rows * STEP, ch)
        lines = (column(left, 0), column(left, 1), column(right, STEP - 2), column(right, STEP - 1))
        put_strips(
            i, r, c, lines, outer[0, i].astype(F32), outer[1, i].astype(F32),
            u_ref, v_ref, turn_ref, line_ref,
        )
        return carry

    lax.fori_loop(0, faces, face, 0, unroll=True)


def strips_of(x):
    faces, rows, cols, ch = x.shape
    shapes = strip_shapes(faces, rows, cols, ch)
    return pl.pallas_call(
        strips_kernel,
        in_specs=[pl.BlockSpec(memory_space=pltpu.HBM)],
        out_specs=(pl.BlockSpec(memory_space=pltpu.VMEM),) * 4,
        out_shape=shapes,
        scratch_shapes=[
            pltpu.VMEM((2, faces, rows, STEP, ch), BF),
            pltpu.VMEM((2, faces, cols, ch), BF),
            pltpu.VMEM((rows * STEP, ch), F32),
            pltpu.VMEM((rows * STEP, ch), F32),
            pltpu.SemaphoreType.DMA((4,)),
        ],
        cost_estimate=pl.CostEstimate(flops=0, bytes_accessed=4 * 2**20, transcendentals=0),
        compiler_params=pltpu.CompilerParams(vmem_limit_bytes=10 * 2**20),
        name="strips_of",
    )(in_hbm(x))


def select_kernel(near_ref, code_ref, *refs):
    stores, outs, held = refs[:8], refs[8:-1], refs[-1]
    faces, _, size, ch = held.shape[1:]
    me, r, c = lax.axis_index("face"), lax.axis_index("row"), lax.axis_index("col")
    for k, store in enumerate(stores):
        for i in range(faces):
            held[k, i] = store[i, 0:3]

    def slot(row, col):
        return ((r ^ row) << 1) | (c ^ col)

    def quarter(edge, q):
        upright = lax.rem(edge, 2) == 1
        row = jnp.where(upright, q, jnp.where(edge == 0, 0, 3))
        col = jnp.where(upright, jnp.where(edge == 3, 0, 1), q >> 1)
        return slot(row, col), jnp.where(upright, 0, 1 + (q & 1))

    def end(n, where, block, last):
        head = held[where, n, block, 0:EXTRA].astype(F32)
        tail = held[where, n, block, size - EXTRA : size].astype(F32)
        return jnp.where(last, tail[EXTRA - 1 : EXTRA], head[0:1])

    spot = lax.broadcasted_iota(jnp.int32, (EXTRA, 1), 0)
    for k, out in enumerate(outs):
        target = me ^ k

        def face(i, carry, k=k, out=out, target=target):
            f = target * faces + i
            edge = 3 - 2 * c
            code = code_ref[edge, f]
            far, flip = code >> 1, code & 1
            n = lax.rem(near_ref[edge, f], faces)
            where, block = quarter(far, jnp.where(flip == 1, 3 - r, r))
            out[i, 0:size] = held[where, n, block]
            corner = jnp.where(r < 2, c, 3 - c)
            tip = code_ref[4 + corner, f]
            tip_n = lax.rem(near_ref[4 + corner, f], faces)
            tip_row = jnp.where(tip < 2, 0, 3)
            tip_col = jnp.where((tip == 1) | (tip == 2), 1, 0)
            tip_pixel = end(tip_n, slot(tip_row, tip_col), 0, tip_row == 3)
            q = jnp.where(flip == 1, 4 - r, r - 1)
            where, block = quarter(far, jnp.clip(q, 0, 3))
            before = jnp.where(r == 0, tip_pixel, end(n, where, block, flip == 0))
            q = jnp.where(flip == 1, 2 - r, r + 1)
            where, block = quarter(far, jnp.clip(q, 0, 3))
            after = jnp.where(r == 3, tip_pixel, end(n, where, block, flip == 1))

            edge = jnp.where(r < 2, 0, 2)
            code = code_ref[edge, f]
            far, flip = code >> 1, code & 1
            n = lax.rem(near_ref[edge, f], faces)
            part = c ^ flip
            for h in range(out.shape[1] // size - 1):
                own = jnp.where((r == 0) | (r == 3), 0, 1) if k else h
                where, block = quarter(far, 2 * part + own)
                out[i, (1 + h) * size : (2 + h) * size] = held[where, n, block]
            where, block = quarter(far, jnp.where(part == 0, 2, 1))
            middle = end(n, where, block, part == 1)
            single = jnp.where(spot == 0, before, jnp.where(spot == 1, after, middle))
            out[i, out.shape[1] - EXTRA :] = single.astype(BF)
            return carry

        lax.fori_loop(0, faces, face, 0, unroll=True)


def select_strips(neighbour_face, orientation, stores, groups):
    faces, _, size, ch = stores[0].shape
    shapes = [
        jax.ShapeDtypeStruct((faces, (2 if k else 3) * size + EXTRA, ch), BF) for k in range(groups)
    ]
    smem = pl.BlockSpec(memory_space=pltpu.SMEM)
    return pl.pallas_call(
        select_kernel,
        in_specs=[smem, smem] + [pl.BlockSpec(memory_space=pltpu.VMEM)] * 8,
        out_specs=(pl.BlockSpec(memory_space=pltpu.VMEM),) * groups,
        out_shape=tuple(shapes),
        scratch_shapes=[pltpu.VMEM((8, faces, 3, size, ch), BF)],
        cost_estimate=pl.CostEstimate(flops=0, bytes_accessed=4 * 2**20, transcendentals=0),
        compiler_params=pltpu.CompilerParams(vmem_limit_bytes=10 * 2**20),
        name="select_strips",
    )(neighbour_face, orientation, *stores)


def ring_kernel(groups, coarse, near_ref, code_ref, x_ref, y_in, line_in, beside, diagonal, across,
                far_diagonal, turned, w_ref, b_ref, *refs):
    seams, seconds, refs = refs[:groups], refs[groups : 2 * groups - 1], refs[2 * groups - 1 :]
    if coarse:
        c_ref, dw_ref, db_ref, _, _, y_out, c_out = refs[:7]
        y_ref = y_in
        scratch = refs[7:]
        *scratch, c_taps, c_tiles, c_rows, c_cols, sems = scratch
    else:
        y_ref, outs, scratch = refs[0], refs[1:5], refs[5:]
    tiles, edge_rows, edge_cols, held, left, right, w_cols, across_taps, along_taps = scratch
    faces, rows, cols, ch = x_ref.shape
    me, r, c = lax.axis_index("face"), lax.axis_index("row"), lax.axis_index("col")
    for k in range(groups):
        seam = seams[k]
        extras = slice(seam.shape[1] - EXTRA, seam.shape[1])
        held[k, :, : 2 * rows] = seam[:, : 2 * rows]
        held[k, :, 2 * rows : 3 * rows] = (
            seconds[k - 1][:, rows : 2 * rows] if k else seam[:, 2 * rows : 3 * rows]
        )
        held[k, :, 3 * rows :] = seam[:, extras]

    def oriented(v, flip):
        n = v.shape[0]
        to = lax.broadcasted_iota(jnp.int32, (n, n), 0)
        source = lax.broadcasted_iota(jnp.int32, (n, n), 1)
        order = jnp.where(source == jnp.where(flip == 1, n - 1 - to, to), 1.0, 0.0).astype(BF)
        return jnp.dot(order, v, preferred_element_type=F32)

    even = lax.rem(r, 2) == 0
    outer = (r == 0) | (r == 3)
    for d in range(3):
        for a in range(3):
            w_cols[(3 * d + a) * ch : (3 * d + a + 1) * ch] = w_ref[a, d]
    bias = b_ref[...]

    def holder(n):
        return jnp.minimum(n, FACES - 1) // faces ^ me

    def put(taps, place, v, before, after, third):
        for k, part in enumerate(shifted(v, before, after)):
            start = (3 * third + k) * ch
            taps[pl.ds(place, v.shape[0]), start : start + ch] = part

    def face(i):
        f = me * faces + i
        edge = 3 - 2 * c
        n = near_ref[edge, f]
        corner = jnp.where(r < 2, c, 3 - c)
        tip_n = near_ref[4 + corner, f]
        seam_side = oriented(held[holder(n), i, 0:rows], code_ref[edge, f] & 1)
        extra = slice(3 * rows, 3 * rows + EXTRA)
        n_before = jnp.where(r == 0, tip_n, n)
        n_after = jnp.where(r == 3, tip_n, n)
        before = held[holder(n_before), i, extra].astype(F32)[0:1]
        after = held[holder(n_after), i, extra].astype(F32)[1:2]
        before = jnp.where(n_before < FACES, before, 0.0)
        after = jnp.where(n_after < FACES, after, 0.0)
        edge = jnp.where(r < 2, 0, 2)
        n = near_ref[edge, f]
        seam_line = oriented(held[holder(n), i, rows : 3 * rows], code_ref[edge, f] & 1)
        middle = held[holder(n), i, extra].astype(F32)[2:3]

        inner = beside[i, 3].astype(F32)
        block_line = jnp.concatenate([across[i, 1], across[i, 2]], axis=0).astype(F32)
        outward = jnp.where(outer, seam_line, block_line)
        inward = turned[i].astype(F32)
        top = jnp.where(even, outward, inward)
        bottom = jnp.where(even, inward, outward)
        lft = jnp.where(c == 0, seam_side, inner)
        rgt = jnp.where(c == 0, inner, seam_side)
        pair_inner = diagonal[i, 3].astype(F32)
        inward_corner = jnp.where(even, pair_inner[0:1], pair_inner[rows - 1 : rows])
        far_first = far_diagonal[i, 1].astype(F32)[0:1]
        far_last = far_diagonal[i, 2].astype(F32)[rows - 1 : rows]
        outward_corner = jnp.where(outer, middle, jnp.where(c == 0, far_first, far_last))
        inner_top = jnp.where(even, outward_corner, inward_corner)
        inner_bottom = jnp.where(even, inward_corner, outward_corner)
        top_left = jnp.where(c == 0, before, inner_top)
        top_right = jnp.where(c == 0, inner_top, before)
        bottom_left = jnp.where(c == 0, after, inner_bottom)
        bottom_right = jnp.where(c == 0, inner_bottom, after)

        row_0, row_1, row_2, row_3 = (
            x_ref[i, k].astype(F32) for k in (0, 1, rows - 2, rows - 1)
        )
        place = 2 * i * cols
        put(across_taps, place, top, top_left, top_right, 0)
        put(across_taps, place, row_0, lft[0:1], rgt[0:1], 1)
        put(across_taps, place, row_1, lft[1:2], rgt[1:2], 2)
        place += cols
        put(across_taps, place, row_2, lft[rows - 2 : rows - 1], rgt[rows - 2 : rows - 1], 0)
        put(across_taps, place, row_3, lft[rows - 1 : rows], rgt[rows - 1 : rows], 1)
        put(across_taps, place, bottom, bottom_left, bottom_right, 2)
        col_0, col_1, col_2, col_3 = (line_in[i, k].astype(F32) for k in range(4))
        place = 2 * i * rows
        put(along_taps, place, lft, top_left, bottom_left, 0)
        put(along_taps, place, col_0, top[0:1], bottom[0:1], 1)
        put(along_taps, place, col_1, top[1:2], bottom[1:2], 2)
        place += rows
        put(along_taps, place, col_2, top[cols - 2 : cols - 1], bottom[cols - 2 : cols - 1], 0)
        put(along_taps, place, col_3, top[cols - 1 : cols], bottom[cols - 1 : cols], 1)
        put(along_taps, place, rgt, top_right, bottom_right, 2)

    for i in range(faces):
        face(i)
    w_rows = w_ref[...].reshape(9 * ch, ch)
    out = gelu(jnp.dot(across_taps[...], w_rows, preferred_element_type=F32) + bias)
    edge_rows[...] = out.astype(BF).reshape(edge_rows.shape)
    out = gelu(jnp.dot(along_taps[...], w_cols[...], preferred_element_type=F32) + bias)
    edge_cols[...] = out.reshape(edge_cols.shape)
    if coarse:
        order_cols, order_rows = parting(cols), parting(rows)

    def with_column(tile, place, value):
        spots = lax.broadcasted_iota(jnp.int32, tile.shape, 1)
        return jnp.where(spots == place, value[:, None, :], tile)

    def update(i, carry):
        new_top, new_bottom = edge_rows[i, 0].astype(F32), edge_rows[i, 1].astype(F32)
        end = (rows - 1) * STEP
        for tile, side, place in ((left, 0, 0), (right, 1, STEP - 1)):
            start = side * (cols - STEP)
            value = y_ref[i, :, start : start + STEP].astype(F32)
            value = with_column(value, place, edge_cols[i, side * rows : (side + 1) * rows])
            tile[...] = value.reshape(rows * STEP, ch)
            tile[0:STEP] = new_top[start : start + STEP]
            tile[end : end + STEP] = new_bottom[start : start + STEP]
            if coarse:
                tiles[side, i] = value.astype(BF)
                tiles[side, i, 0] = edge_rows[i, 0, start : start + STEP]
                tiles[side, i, rows - 1] = edge_rows[i, 1, start : start + STEP]
            else:
                y_ref[i, :, start : start + STEP] = value.astype(BF)
        if not coarse:
            y_ref[i, 0] = edge_rows[i, 0]
            y_ref[i, rows - 1] = edge_rows[i, 1]
        lines = (
            column(left, 0), column(left, 1), column(right, STEP - 2), column(right, STEP - 1)
        )
        if not coarse:
            put_strips(i, r, c, lines, new_top, new_bottom, *outs)
            return carry
        spot = lax.broadcasted_iota(jnp.int32, (cols, 1), 0)
        half = cols // 2
        for k, (own, near) in enumerate(((new_top, 1), (new_bottom, rows - 2))):
            first = edge_cols[i, near : near + 1]
            last = edge_cols[i, rows + near : rows + near + 1]
            other = y_ref[i, near].astype(F32)
            other = jnp.where(spot == 0, first, jnp.where(spot == cols - 1, last, other))
            both = (own, other) if k == 0 else (other, own)
            four = parted(order_cols, jnp.concatenate([v.astype(BF) for v in both], axis=1))
            four = jnp.concatenate([four[j] for j in (0, 2, 1, 3)], axis=1)
            c_taps[pl.ds((2 * i + k) * half, half)] = four
        for k, both in enumerate((lines[:2], lines[2:])):
            four = parted(order_rows, jnp.concatenate([v.astype(BF) for v in both], axis=1))
            place = 2 * faces * half + (2 * i + k) * (rows // 2)
            c_taps[pl.ds(place, rows // 2)] = jnp.concatenate(four, axis=1)
        return carry

    lax.fori_loop(0, faces, update, 0, unroll=True)
    if not coarse:
        return
    copies = tile_copies(y_out, tiles, sems, back=True)
    if cols > 2 * STEP:
        between = pl.ds(STEP, cols - 2 * STEP)
        for k, row in enumerate((0, rows - 1)):
            copies.append(
                pltpu.make_async_copy(
                    edge_rows.at[:, k, between], y_out.at[:, row, between], sems.at[2 + k]
                )
            )
    for copy in copies:
        copy.start()
    half = cols // 2
    out = jnp.dot(
        c_taps[...], dw_ref[...].reshape(4 * ch, -1), preferred_element_type=F32
    ) + db_ref[...]
    across_cells = 2 * faces * half
    c_rows[...] = out[:across_cells].astype(BF).reshape(c_rows.shape)
    c_cols[...] = out[across_cells:].reshape(c_cols.shape)

    def cells(i, carry):
        for side in range(2):
            start = side * (half - STEP)
            value = c_ref[i, :, start : start + STEP].astype(F32)
            value = with_column(value, side * (STEP - 1), c_cols[i, side])
            c_tiles[side, i] = value.astype(BF)
            for k in range(2):
                c_tiles[side, i, k * (rows // 2 - 1)] = c_rows[i, k, start : start + STEP]
        return carry

    lax.fori_loop(0, faces, cells, 0, unroll=True)
    more = []
    for side, start in enumerate((0, half - STEP)):
        more.append(
            pltpu.make_async_copy(
                c_tiles.at[side], c_out.at[:, :, pl.ds(start, STEP), :], sems.at[4 + side]
            )
        )
    if half > 2 * STEP:
        between = pl.ds(STEP, half - 2 * STEP)
        for k, row in enumerate((0, rows // 2 - 1)):
            more.append(
                pltpu.make_async_copy(
                    c_rows.at[:, k, between], c_out.at[:, row, between], sems.at[6 + k]
                )
            )
    for copy in more:
        copy.start()
    for copy in copies + more:
        copy.wait()


def ring(
    neighbour_face, orientation, x, buffers, copied, lines, parts, weight, bias, seams, seconds, down
):
    y, *coarse = buffers
    faces, rows, cols, ch = x.shape
    groups = len(seams)
    smem = pl.BlockSpec(memory_space=pltpu.SMEM)
    hbm = pl.BlockSpec(memory_space=pltpu.HBM)
    vmem = pl.BlockSpec(memory_space=pltpu.VMEM)
    args = [neighbour_face, orientation, x, y, lines, *parts, weight, bias, *seams, *seconds]
    in_specs = [smem, smem] + [vmem] * (len(args) - 2)
    scratch = [
        pltpu.VMEM((2, faces, rows, STEP, ch), BF),
        pltpu.VMEM((faces, 2, cols, ch), BF),
        pltpu.VMEM((faces, 2 * rows, ch), F32),
        pltpu.VMEM((groups, faces, 3 * rows + EXTRA, ch), BF),
        pltpu.VMEM((rows * STEP, ch), F32),
        pltpu.VMEM((rows * STEP, ch), F32),
        pltpu.VMEM((9 * ch, ch), BF),
        pltpu.VMEM((2 * faces * cols, 9 * ch), BF),
        pltpu.VMEM((2 * faces * rows, 9 * ch), BF),
    ]
    if down:
        co = down[0].shape[-1]
        args += [coarse[0], *down]
        in_specs += [vmem] * 3
        aliases = {len(args): 0, len(args) + 1: 1}
        args += [in_hbm(buffer) for buffer in copied]
        in_specs += [hbm] * 2
        out_shape = [pltpu.HBM(buffer.shape, BF) for buffer in copied]
        out_specs = [hbm] * 2
        scratch += [
            pltpu.VMEM((faces * (rows + cols), 4 * ch), BF),
            pltpu.VMEM((2, faces, rows // 2, STEP, co), BF),
            pltpu.VMEM((faces, 2, cols // 2, co), BF),
            pltpu.VMEM((faces, 2, rows // 2, co), F32),
            pltpu.SemaphoreType.DMA((8,)),
        ]
    else:
        aliases = {3: 0}
        out_shape = [jax.ShapeDtypeStruct(y.shape, BF), *strip_shapes(faces, rows, cols, ch)]
        out_specs = [vmem] * 5
    return pl.pallas_call(
        functools.partial(ring_kernel, groups, bool(down)),
        in_specs=in_specs,
        out_specs=tuple(out_specs),
        out_shape=tuple(out_shape),
        scratch_shapes=scratch,
        input_output_aliases=aliases,
        cost_estimate=pl.CostEstimate(
            flops=faces * (rows + cols) * 36 * ch * ch, bytes_accessed=8 * 2**20, transcendentals=0
        ),
        compiler_params=pltpu.CompilerParams(vmem_limit_bytes=20 * 2**20),
        name="ring",
    )(*args)


def blocks(change_row, change_col):
    cols = lax.axis_size("col")
    return [
        (r * cols + c, (r ^ change_row) * cols + (c ^ change_col))
        for r in range(lax.axis_size("row"))
        for c in range(cols)
    ]


def swap(v, change_row, change_col):
    return lax.ppermute(v, ("row", "col"), blocks(change_row, change_col))


def level(neighbour_face, orientation, x, strips, weight, bias, down):
    u, v, turn, lines = strips
    groups = lax.axis_size("face")
    total = x.shape[0] * x.shape[1] // STEP
    early = max(total * (6 if down else 5) // 12, 1)
    late = early + max(total // 12, 1)
    piece = functools.partial(conv_piece, x, weight, bias)
    beside, across, diagonal = swap(u, 0, 1), swap(v, 3, 0), swap(v, 3, 1)
    pair, turned = swap(v, 1, 0), swap(turn, 1, 0)
    state = piece(0, early, None)
    (beside, across, diagonal, turned), state = lax.optimization_barrier(
        ((beside, across, diagonal, turned), state)
    )
    pair_beside, pair_across, pair_diagonal = (swap(a, 1, 0) for a in (beside, across, diagonal))
    state = piece(early, late - early, state)
    stores = (v, beside, pair, pair_beside, pair_across, pair_diagonal, across, diagonal)
    picked = select_strips(neighbour_face, orientation, stores, groups)
    picked, state = lax.optimization_barrier((picked, state))
    seams = list(picked)
    for k in sorted(range(1, groups), key=lambda k: -(k.bit_length())):
        pairs = [(g, g ^ k) for g in range(groups)]
        seams[k] = lax.ppermute(picked[k], "face", pairs)
    buffers, copied = piece(late, total - late, state)[2:], ()
    if down:
        coarse, *copied = downsample(buffers[0], *down)
        buffers += (coarse,)
    parts = (beside, pair_beside, across, diagonal, turned)
    seams[1:], buffers = lax.optimization_barrier((seams[1:], buffers))
    seconds = [swap(seam, 1, 0) for seam in seams[1:]]
    return ring(
        *(neighbour_face, orientation, x, buffers, copied, lines, parts, weight, bias),
        *(seams, seconds, down),
    )


def per_device(
    field, conv1_w, conv1_b, conv2_w, conv2_b, down_w, down_b, neighbour_face, orientation
):
    tables = (neighbour_face.T, orientation.T)
    hidden, *strips = level(*tables, field, strips_of(field), conv1_w, conv1_b[None], ())
    return level(*tables, hidden, strips, conv2_w, conv2_b[None], (down_w, down_b[None]))


def solution(mesh):
    groups = mesh.shape["face"]
    fast = mesh.shape["row"] == 4 and mesh.shape["col"] == 2 and groups & (groups - 1) == 0
    return jax.shard_map(
        per_device if fast else general_device,
        mesh=mesh,
        in_specs=(P("face", "row", "col", None), P(), P(), P(), P(), P(), P(), P(), P()),
        out_specs=(P("face", "row", "col", None), P("face", "row", "col", None)),
        check_vma=False,
    )
```

```python
import functools

import jax
import jax.numpy as jnp
import numpy as np
from jax import lax
from jax.experimental import pallas as pl
from jax.experimental.pallas import tpu as pltpu
from jax.sharding import PartitionSpec as P


FACES = 12
BF = jnp.bfloat16
F32 = jnp.float32
STEP = 16
EDGE = 8
EXTRA = 16

layout = ("NHWC", "HWIO", "NHWC")


def padded_2(block, sides, width):
    for axis, dim in sides:
        count = lax.axis_size(axis)
        forward = [(i, i + 1) for i in range(count - 1)]
        backward = [(target, source) for source, target in forward]
        low = lax.ppermute(
            lax.slice_in_dim(block, block.shape[dim] - width, None, axis=dim), axis, forward
        )
        high = lax.ppermute(lax.slice_in_dim(block, 0, width, axis=dim), axis, backward)
        block = jnp.concatenate([low, block, high], axis=dim)
    return block


def seam_parts(edges, neighbours, codes):
    seam_faces = neighbours[:, :4]
    seam_codes = codes[:, :4]
    seams = edges[seam_faces, seam_codes // 2]
    seams = jnp.where((seam_codes % 2 == 1)[:, :, None, None], seams[:, :, ::-1], seams)
    corner_values = jnp.stack(
        [edges[:, 0, 0], edges[:, 0, -1], edges[:, 2, -1], edges[:, 2, 0]], axis=1
    )
    corner_faces = neighbours[:, 4:]
    picked = corner_values[jnp.minimum(corner_faces, FACES - 1), codes[:, 4:]]
    picked = jnp.where((corner_faces < FACES)[:, :, None], picked, jnp.zeros_like(picked))
    return (seams, picked)


def convolve(padded, weight, bias):
    summed = lax.conv_general_dilated(
        padded,
        weight,
        (1, 1),
        "VALID",
        dimension_numbers=layout,
        preferred_element_type=jnp.float32,
    )
    return jax.nn.gelu(summed + bias, approximate=False).astype(jnp.bfloat16)


def general_layer(block, weight, bias, neighbour_face, orientation):
    face_count, row_size, col_size, channels = block.shape
    row_total = lax.axis_size("row")
    col_total = lax.axis_size("col")
    row_place = lax.axis_index("row")
    col_place = lax.axis_index("col")
    face_side = row_size * row_total
    padded = padded_2(block, (("row", 1), ("col", 2)), 1)
    top_live = row_place == 0
    bottom_live = row_place == row_total - 1
    left_live = col_place == 0
    right_live = col_place == col_total - 1
    empty_line = jnp.zeros((face_count, face_side, channels), jnp.float32)

    def place(strip, offset, live):
        scaled = strip.astype(jnp.float32) * live.astype(jnp.float32)
        return lax.dynamic_update_slice_in_dim(empty_line, scaled, offset, 1)

    lines = jnp.stack(
        [
            place(block[:, 0], col_place * col_size, top_live),
            place(block[:, :, -1], row_place * row_size, right_live),
            place(block[:, -1], col_place * col_size, bottom_live),
            place(block[:, :, 0], row_place * row_size, left_live),
        ],
        axis=1,
    )
    complete = lax.psum(lax.psum(lines.astype(jnp.bfloat16), "col"), "row").astype(jnp.float32)
    every_edge = lax.all_gather(complete.astype(jnp.bfloat16), "face", axis=0, tiled=True)
    first_face = lax.axis_index("face") * face_count
    own_faces = lax.dynamic_slice_in_dim(neighbour_face, first_face, face_count, 0)
    own_codes = lax.dynamic_slice_in_dim(orientation, first_face, face_count, 0)
    seams, corners = seam_parts(every_edge, own_faces, own_codes)
    upper = jnp.concatenate([corners[:, 0:1], seams[:, 0], corners[:, 1:2]], 1)
    lower = jnp.concatenate([corners[:, 3:4], seams[:, 2], corners[:, 2:3]], 1)
    leftward = jnp.concatenate([corners[:, 0:1], seams[:, 3], corners[:, 3:4]], 1)
    rightward = jnp.concatenate([corners[:, 1:2], seams[:, 1], corners[:, 2:3]], 1)
    upper_cut = lax.dynamic_slice_in_dim(upper, col_place * col_size, col_size + 2, 1)
    lower_cut = lax.dynamic_slice_in_dim(lower, col_place * col_size, col_size + 2, 1)
    left_cut = lax.dynamic_slice_in_dim(leftward, row_place * row_size, row_size + 2, 1)
    right_cut = lax.dynamic_slice_in_dim(rightward, row_place * row_size, row_size + 2, 1)
    padded = padded.at[:, 0].set(jnp.where(top_live, upper_cut, padded[:, 0]))
    padded = padded.at[:, -1].set(jnp.where(bottom_live, lower_cut, padded[:, -1]))
    padded = padded.at[:, :, 0].set(jnp.where(left_live, left_cut, padded[:, :, 0]))
    padded = padded.at[:, :, -1].set(jnp.where(right_live, right_cut, padded[:, :, -1]))
    return convolve(padded, weight, bias)


def general_device(
    field, conv1_w, conv1_b, conv2_w, conv2_b, down_w, down_b, neighbour_face, orientation
):
    hidden = general_layer(field, conv1_w, conv1_b, neighbour_face, orientation)
    skip = general_layer(hidden, conv2_w, conv2_b, neighbour_face, orientation)
    summed = lax.conv_general_dilated(
        skip, down_w, (2, 2), "VALID", dimension_numbers=layout, preferred_element_type=jnp.float32
    )
    coarse = (summed + down_b).astype(jnp.bfloat16)
    return (skip, coarse)


def gelu(v):
    return 0.5 * v * (1.0 + lax.erf(v * np.float32(np.sqrt(0.5))))


def shifted(v, before, after):
    n = v.shape[0]
    spot = lax.broadcasted_iota(jnp.int32, (n, 1), 0)
    low = jnp.where(spot == 0, before, pltpu.roll(v, 1, 0))
    high = jnp.where(spot == n - 1, after, pltpu.roll(v, n - 1, 0))
    return low.astype(BF), v.astype(BF), high.astype(BF)


def parting(n):
    to = lax.broadcasted_iota(jnp.int32, (n, n), 0)
    source = lax.broadcasted_iota(jnp.int32, (n, n), 1)
    half = n // 2
    return jnp.where(source == jnp.where(to < half, 2 * to, 2 * (to - half) + 1), 1.0, 0.0).astype(BF)


def parted(order, v):
    v = jnp.dot(order, v, preferred_element_type=F32).astype(BF)
    half, lanes = v.shape[0] // 2, v.shape[1] // 2
    return v[:half, :lanes], v[:half, lanes:], v[half:, :lanes], v[half:, lanes:]


def conv_kernel(first, count, build, x_ref, b_ref, *refs):
    *refs, taps_0, taps_1 = refs
    if build:
        w_ref, y_ref, w_low, w_high = refs
    else:
        w_low, w_high, _, y_ref = refs
    _, size, cols, ch = x_ref.shape
    steps = size // STEP
    pairs = STEP // 2
    zero_row = jnp.zeros((1, ch), F32)
    half = 3 * ch

    if build:
        zero = jnp.zeros((ch, ch), BF)
        for d in range(3):
            one = slice(d * ch, (d + 1) * ch)
            two = slice(half + d * ch, half + (d + 1) * ch)
            w_low[one, :ch] = w_ref[0, d]
            w_low[one, ch:] = zero
            w_low[two, :ch] = w_ref[1, d]
            w_low[two, ch:] = w_ref[0, d]
            w_high[one, :ch] = w_ref[2, d]
            w_high[one, ch:] = w_ref[1, d]
            w_high[two, :ch] = zero
            w_high[two, ch:] = w_ref[2, d]

    def at(t):
        return t // steps, lax.rem(t, steps)

    def fill(taps, t):
        face, step = at(t)
        base = step * STEP

        def put(v, pair, side):
            low, same, high = shifted(v.astype(F32), zero_row, zero_row)
            place = side * half
            taps[pair, :, place : place + ch] = low
            taps[pair, :, place + ch : place + 2 * ch] = same
            taps[pair, :, place + 2 * ch : place + 3 * ch] = high

        inside = (step > 0).astype(F32)
        put(x_ref[face, jnp.maximum(base - 1, 0)].astype(F32) * inside, 0, 0)
        for row in range(STEP):
            put(x_ref[face, base + row], (row + 1) // 2, (row + 1) % 2)
        inside = (step < steps - 1).astype(F32)
        put(x_ref[face, jnp.minimum(base + STEP, size - 1)].astype(F32) * inside, pairs, 1)

    def product(taps, t):
        face, step = at(t)
        base = step * STEP
        lower = taps[pl.ds(0, pairs)].reshape(pairs * cols, 2 * half)
        upper = taps[pl.ds(1, pairs)].reshape(pairs * cols, 2 * half)
        total = jnp.dot(lower, w_low[...], preferred_element_type=F32)
        total += jnp.dot(upper, w_high[...], preferred_element_type=F32)
        total = total.reshape(pairs, cols, 2 * ch)
        bias = b_ref[...]
        for side in range(2):
            out = gelu(total[:, :, side * ch : (side + 1) * ch] + bias[None]).astype(BF)
            for pair in range(pairs):
                y_ref[face, base + 2 * pair + side] = out[pair]
    last = first + count - 1
    fill(taps_0, first)

    def double(j, carry):
        t = first + 2 * j
        fill(taps_1, t + 1)
        product(taps_0, t)
        fill(taps_0, jnp.minimum(t + 2, last))
        product(taps_1, t + 1)
        return carry

    lax.fori_loop(0, count // 2, double, 0)
    if count % 2:
        product(taps_0, last)


def in_hbm(x):
    return pltpu.with_memory_space_constraint(x, pltpu.HBM)


def conv_piece(x, weight, bias, first, count, state):
    faces, rows, cols, ch = x.shape
    vmem = pl.BlockSpec(memory_space=pltpu.VMEM)
    build = state is None
    taps = (STEP // 2 + 1, cols, 6 * ch)
    arranged = jax.ShapeDtypeStruct((6 * ch, 2 * ch), BF)
    args = [x, bias, weight] if build else [x, bias, *state]
    out_shape = [jax.ShapeDtypeStruct(x.shape, BF)] + [arranged] * (2 if build else 0)
    pixels = count * STEP * cols
    out = pl.pallas_call(
        functools.partial(conv_kernel, first, count, build),
        in_specs=[vmem] * len(args),
        out_specs=tuple([vmem] * len(out_shape)),
        out_shape=tuple(out_shape),
        scratch_shapes=[pltpu.VMEM(taps, BF), pltpu.VMEM(taps, BF)],
        input_output_aliases={} if build else {4: 0},
        cost_estimate=pl.CostEstimate(
            flops=pixels * 24 * ch * ch, bytes_accessed=4 * pixels * ch, transcendentals=0
        ),
        compiler_params=pltpu.CompilerParams(vmem_limit_bytes=16 * 2**20),
        name="conv_piece",
    )(*args)
    return (out[1], out[2], out[0]) if build else (state[0], state[1], out[0])


def down_kernel(first, count, y_ref, w_ref, b_ref, *refs):
    c_ref, y_out, c_out, taps_0, taps_1, sems = refs[-6:]
    faces, rows, cols, ch = y_ref.shape
    steps, pairs = rows // STEP, STEP // 2
    last = first + count - 1
    order = parting(cols)

    def copies(t):
        face, step = t // steps, lax.rem(t, steps)
        some, cells = pl.ds(step * STEP, STEP), pl.ds(step * pairs, pairs)
        return (
            pltpu.make_async_copy(y_ref.at[face, some], y_out.at[face, some], sems.at[0]),
            pltpu.make_async_copy(c_ref.at[face, cells], c_out.at[face, cells], sems.at[1]),
        )

    def fill(taps, t):
        face, step = t // steps, lax.rem(t, steps)
        for pair in range(pairs):
            row = step * STEP + 2 * pair
            both = jnp.concatenate([y_ref[face, row], y_ref[face, row + 1]], axis=1)
            four = parted(order, both)
            taps[pair] = jnp.concatenate([four[k] for k in (0, 2, 1, 3)], axis=1)

    def product(taps, t):
        face, step = t // steps, lax.rem(t, steps)
        out = jnp.dot(
            taps[...].reshape(pairs * cols // 2, 4 * ch),
            w_ref[...].reshape(4 * ch, -1),
            preferred_element_type=F32,
        )
        out = (out + b_ref[...]).astype(BF)
        c_ref[face, pl.ds(step * pairs, pairs)] = out.reshape(pairs, cols // 2, -1)
        copies(t)[1].start()

    def send(t, carry):
        copies(t)[0].start()
        return carry

    def wait(t, carry):
        for copy in copies(t):
            copy.wait()
        return carry

    lax.fori_loop(first, first + count, send, 0)
    fill(taps_0, first)

    def double(j, carry):
        t = first + 2 * j
        fill(taps_1, t + 1)
        product(taps_0, t)
        fill(taps_0, jnp.minimum(t + 2, last))
        product(taps_1, t + 1)
        return carry

    lax.fori_loop(0, count // 2, double, 0, unroll=True)
    if count % 2:
        product(taps_0, last)
    lax.fori_loop(first, first + count, wait, 0)


def downsample(y, weight, bias, first, count, into):
    faces, rows, cols, ch = y.shape
    shape = (faces, rows // 2, cols // 2, weight.shape[-1])
    vmem = pl.BlockSpec(memory_space=pltpu.VMEM)
    hbm = pl.BlockSpec(memory_space=pltpu.HBM)
    taps = (STEP // 2, cols // 2, 4 * ch)
    args, in_specs = [y, weight, bias], [vmem] * 3
    if into:
        args += [into[0], in_hbm(into[1]), in_hbm(into[2])]
        in_specs += [vmem, hbm, hbm]
    pixels = count * STEP * cols
    return pl.pallas_call(
        functools.partial(down_kernel, first, count),
        in_specs=in_specs,
        out_specs=(vmem, hbm, hbm),
        out_shape=(jax.ShapeDtypeStruct(shape, BF), pltpu.HBM(y.shape, BF), pltpu.HBM(shape, BF)),
        scratch_shapes=[pltpu.VMEM(taps, BF), pltpu.VMEM(taps, BF), pltpu.SemaphoreType.DMA((2,))],
        input_output_aliases={3: 0, 4: 1, 5: 2} if into else {},
        cost_estimate=pl.CostEstimate(
            flops=pixels * 2 * ch * shape[-1], bytes_accessed=4 * pixels * ch, transcendentals=0
        ),
        compiler_params=pltpu.CompilerParams(vmem_limit_bytes=16 * 2**20),
        name="downsample",
    )(*args)


def column(tile, place):
    return tile[pl.ds(place, tile.shape[0] // EDGE, stride=EDGE), :]


def put_strips(i, r, c, lines, top, bottom, u_ref, v_ref, turn_ref, line_ref):
    left, left_in, right_in, right = lines
    size = left.shape[0]
    for place, value in enumerate(lines):
        line_ref[i, place] = value.astype(BF)
    side = jnp.where(c == 0, left, right).astype(BF)
    inner = jnp.where(c == 0, right, left).astype(BF)
    even = lax.rem(r, 2) == 0
    line = jnp.where(even, top, bottom).astype(BF)
    turn_ref[i] = jnp.where(even, bottom, top).astype(BF)
    for ref in (u_ref, v_ref):
        ref[i, 0] = side
        ref[i, 1] = line[:size]
        ref[i, 2] = line[size:]
    u_ref[i, 3] = inner


def strip_shapes(faces, rows, cols, ch):
    return (
        jax.ShapeDtypeStruct((faces, 4, rows, ch), BF),
        jax.ShapeDtypeStruct((faces, 3, rows, ch), BF),
        jax.ShapeDtypeStruct((faces, cols, ch), BF),
        jax.ShapeDtypeStruct((faces, 4, rows, ch), BF),
    )


def whole(shape):
    return pl.BlockSpec(shape, lambda *_: (0,) * len(shape))


def tile_copies(array, tiles, sems, back=False):
    cols = array.shape[2]
    out = []
    for side, start in enumerate((0, cols - EDGE)):
        far, near = array.at[:, :, pl.ds(start, EDGE), :], tiles.at[side]
        out.append(pltpu.make_async_copy(*((near, far) if back else (far, near)), sems.at[side]))
    return out


def strips_kernel(x_ref, u_ref, v_ref, turn_ref, line_ref, tiles, outer, left, right, sems):
    faces, rows, cols, ch = x_ref.shape
    r, c = lax.axis_index("row"), lax.axis_index("col")
    copies = tile_copies(x_ref, tiles, sems)
    for k, row in enumerate((0, rows - 1)):
        copies.append(pltpu.make_async_copy(x_ref.at[:, row], outer.at[k], sems.at[2 + k]))
    for copy in copies:
        copy.start()
    for copy in copies:
        copy.wait()

    def face(i, carry):
        left[...] = tiles[0, i].astype(F32).reshape(rows * EDGE, ch)
        right[...] = tiles[1, i].astype(F32).reshape(rows * EDGE, ch)
        lines = (column(left, 0), column(left, 1), column(right, EDGE - 2), column(right, EDGE - 1))
        put_strips(
            i, r, c, lines, outer[0, i].astype(F32), outer[1, i].astype(F32),
            u_ref, v_ref, turn_ref, line_ref,
        )
        return carry

    lax.fori_loop(0, faces, face, 0, unroll=True)


def strips_of(x):
    faces, rows, cols, ch = x.shape
    shapes = strip_shapes(faces, rows, cols, ch)
    return pl.pallas_call(
        strips_kernel,
        in_specs=[pl.BlockSpec(memory_space=pltpu.HBM)],
        out_specs=(pl.BlockSpec(memory_space=pltpu.VMEM),) * 4,
        out_shape=shapes,
        scratch_shapes=[
            pltpu.VMEM((2, faces, rows, EDGE, ch), BF),
            pltpu.VMEM((2, faces, cols, ch), BF),
            pltpu.VMEM((rows * EDGE, ch), F32),
            pltpu.VMEM((rows * EDGE, ch), F32),
            pltpu.SemaphoreType.DMA((4,)),
        ],
        cost_estimate=pl.CostEstimate(flops=0, bytes_accessed=4 * 2**20, transcendentals=0),
        compiler_params=pltpu.CompilerParams(vmem_limit_bytes=10 * 2**20),
        name="strips_of",
    )(in_hbm(x))


def select_kernel(near_ref, code_ref, *refs):
    stores, outs, held = refs[:8], refs[8:-1], refs[-1]
    faces, _, size, ch = held.shape[1:]
    me, r, c = lax.axis_index("face"), lax.axis_index("row"), lax.axis_index("col")
    for k, store in enumerate(stores):
        for i in range(faces):
            held[k, i] = store[i, 0:3]

    def slot(row, col):
        return ((r ^ row) << 1) | (c ^ col)

    def quarter(edge, q):
        upright = lax.rem(edge, 2) == 1
        row = jnp.where(upright, q, jnp.where(edge == 0, 0, 3))
        col = jnp.where(upright, jnp.where(edge == 3, 0, 1), q >> 1)
        return slot(row, col), jnp.where(upright, 0, 1 + (q & 1))

    def end(n, where, block, last):
        head = held[where, n, block, 0:EXTRA].astype(F32)
        tail = held[where, n, block, size - EXTRA : size].astype(F32)
        return jnp.where(last, tail[EXTRA - 1 : EXTRA], head[0:1])

    spot = lax.broadcasted_iota(jnp.int32, (EXTRA, 1), 0)
    for k, out in enumerate(outs):
        target = me ^ k

        def face(i, carry, k=k, out=out, target=target):
            f = target * faces + i
            edge = 3 - 2 * c
            code = code_ref[edge, f]
            far, flip = code >> 1, code & 1
            n = lax.rem(near_ref[edge, f], faces)
            where, block = quarter(far, jnp.where(flip == 1, 3 - r, r))
            out[i, 0:size] = held[where, n, block]
            corner = jnp.where(r < 2, c, 3 - c)
            tip = code_ref[4 + corner, f]
            tip_n = lax.rem(near_ref[4 + corner, f], faces)
            tip_row = jnp.where(tip < 2, 0, 3)
            tip_col = jnp.where((tip == 1) | (tip == 2), 1, 0)
            tip_pixel = end(tip_n, slot(tip_row, tip_col), 0, tip_row == 3)
            q = jnp.where(flip == 1, 4 - r, r - 1)
            where, block = quarter(far, jnp.clip(q, 0, 3))
            before = jnp.where(r == 0, tip_pixel, end(n, where, block, flip == 0))
            q = jnp.where(flip == 1, 2 - r, r + 1)
            where, block = quarter(far, jnp.clip(q, 0, 3))
            after = jnp.where(r == 3, tip_pixel, end(n, where, block, flip == 1))

            edge = jnp.where(r < 2, 0, 2)
            code = code_ref[edge, f]
            far, flip = code >> 1, code & 1
            n = lax.rem(near_ref[edge, f], faces)
            part = c ^ flip
            for h in range(out.shape[1] // size - 1):
                own = jnp.where((r == 0) | (r == 3), 0, 1) if k else h
                where, block = quarter(far, 2 * part + own)
                out[i, (1 + h) * size : (2 + h) * size] = held[where, n, block]
            where, block = quarter(far, jnp.where(part == 0, 2, 1))
            middle = end(n, where, block, part == 1)
            single = jnp.where(spot == 0, before, jnp.where(spot == 1, after, middle))
            out[i, out.shape[1] - EXTRA :] = single.astype(BF)
            return carry

        lax.fori_loop(0, faces, face, 0, unroll=True)


def select_strips(neighbour_face, orientation, stores, groups):
    faces, _, size, ch = stores[0].shape
    shapes = [
        jax.ShapeDtypeStruct((faces, (2 if k else 3) * size + EXTRA, ch), BF) for k in range(groups)
    ]
    smem = pl.BlockSpec(memory_space=pltpu.SMEM)
    return pl.pallas_call(
        select_kernel,
        in_specs=[smem, smem] + [pl.BlockSpec(memory_space=pltpu.VMEM)] * 8,
        out_specs=(pl.BlockSpec(memory_space=pltpu.VMEM),) * groups,
        out_shape=tuple(shapes),
        scratch_shapes=[pltpu.VMEM((8, faces, 3, size, ch), BF)],
        cost_estimate=pl.CostEstimate(flops=0, bytes_accessed=4 * 2**20, transcendentals=0),
        compiler_params=pltpu.CompilerParams(vmem_limit_bytes=10 * 2**20),
        name="select_strips",
    )(neighbour_face, orientation, *stores)


def ring_kernel(groups, coarse, near_ref, code_ref, x_ref, y_in, line_in, beside, diagonal, across,
                far_diagonal, turned, w_ref, b_ref, *refs):
    seams, seconds, refs = refs[:groups], refs[groups : 2 * groups - 1], refs[2 * groups - 1 :]
    if coarse:
        c_ref, dw_ref, db_ref, _, _, y_out, c_out = refs[:7]
        y_ref = y_in
        scratch = refs[7:]
        *scratch, c_taps, c_tiles, c_rows, c_cols, sems = scratch
    else:
        y_ref, outs, scratch = refs[0], refs[1:5], refs[5:]
    tiles, edge_rows, edge_cols, held, left, right, w_cols, across_taps, along_taps = scratch
    faces, rows, cols, ch = x_ref.shape
    me, r, c = lax.axis_index("face"), lax.axis_index("row"), lax.axis_index("col")
    for k in range(groups):
        seam = seams[k]
        extras = slice(seam.shape[1] - EXTRA, seam.shape[1])
        held[k, :, : 2 * rows] = seam[:, : 2 * rows]
        held[k, :, 2 * rows : 3 * rows] = (
            seconds[k - 1][:, rows : 2 * rows] if k else seam[:, 2 * rows : 3 * rows]
        )
        held[k, :, 3 * rows :] = seam[:, extras]

    def oriented(v, flip):
        n = v.shape[0]
        to = lax.broadcasted_iota(jnp.int32, (n, n), 0)
        source = lax.broadcasted_iota(jnp.int32, (n, n), 1)
        order = jnp.where(source == jnp.where(flip == 1, n - 1 - to, to), 1.0, 0.0).astype(BF)
        return jnp.dot(order, v, preferred_element_type=F32)

    even = lax.rem(r, 2) == 0
    outer = (r == 0) | (r == 3)
    for d in range(3):
        for a in range(3):
            w_cols[(3 * d + a) * ch : (3 * d + a + 1) * ch] = w_ref[a, d]
    bias = b_ref[...]

    def holder(n):
        return jnp.minimum(n, FACES - 1) // faces ^ me

    def put(taps, place, v, before, after, third):
        for k, part in enumerate(shifted(v, before, after)):
            start = (3 * third + k) * ch
            taps[pl.ds(place, v.shape[0]), start : start + ch] = part

    def face(i):
        f = me * faces + i
        edge = 3 - 2 * c
        n = near_ref[edge, f]
        corner = jnp.where(r < 2, c, 3 - c)
        tip_n = near_ref[4 + corner, f]
        seam_side = oriented(held[holder(n), i, 0:rows], code_ref[edge, f] & 1)
        extra = slice(3 * rows, 3 * rows + EXTRA)
        n_before = jnp.where(r == 0, tip_n, n)
        n_after = jnp.where(r == 3, tip_n, n)
        before = held[holder(n_before), i, extra].astype(F32)[0:1]
        after = held[holder(n_after), i, extra].astype(F32)[1:2]
        before = jnp.where(n_before < FACES, before, 0.0)
        after = jnp.where(n_after < FACES, after, 0.0)
        edge = jnp.where(r < 2, 0, 2)
        n = near_ref[edge, f]
        seam_line = oriented(held[holder(n), i, rows : 3 * rows], code_ref[edge, f] & 1)
        middle = held[holder(n), i, extra].astype(F32)[2:3]

        inner = beside[i, 3].astype(F32)
        block_line = jnp.concatenate([across[i, 1], across[i, 2]], axis=0).astype(F32)
        outward = jnp.where(outer, seam_line, block_line)
        inward = turned[i].astype(F32)
        top = jnp.where(even, outward, inward)
        bottom = jnp.where(even, inward, outward)
        lft = jnp.where(c == 0, seam_side, inner)
        rgt = jnp.where(c == 0, inner, seam_side)
        pair_inner = diagonal[i, 3].astype(F32)
        inward_corner = jnp.where(even, pair_inner[0:1], pair_inner[rows - 1 : rows])
        far_first = far_diagonal[i, 1].astype(F32)[0:1]
        far_last = far_diagonal[i, 2].astype(F32)[rows - 1 : rows]
        outward_corner = jnp.where(outer, middle, jnp.where(c == 0, far_first, far_last))
        inner_top = jnp.where(even, outward_corner, inward_corner)
        inner_bottom = jnp.where(even, inward_corner, outward_corner)
        top_left = jnp.where(c == 0, before, inner_top)
        top_right = jnp.where(c == 0, inner_top, before)
        bottom_left = jnp.where(c == 0, after, inner_bottom)
        bottom_right = jnp.where(c == 0, inner_bottom, after)

        row_0, row_1, row_2, row_3 = (
            x_ref[i, k].astype(F32) for k in (0, 1, rows - 2, rows - 1)
        )
        place = 2 * i * cols
        put(across_taps, place, top, top_left, top_right, 0)
        put(across_taps, place, row_0, lft[0:1], rgt[0:1], 1)
        put(across_taps, place, row_1, lft[1:2], rgt[1:2], 2)
        place += cols
        put(across_taps, place, row_2, lft[rows - 2 : rows - 1], rgt[rows - 2 : rows - 1], 0)
        put(across_taps, place, row_3, lft[rows - 1 : rows], rgt[rows - 1 : rows], 1)
        put(across_taps, place, bottom, bottom_left, bottom_right, 2)
        col_0, col_1, col_2, col_3 = (line_in[i, k].astype(F32) for k in range(4))
        place = 2 * i * rows
        put(along_taps, place, lft, top_left, bottom_left, 0)
        put(along_taps, place, col_0, top[0:1], bottom[0:1], 1)
        put(along_taps, place, col_1, top[1:2], bottom[1:2], 2)
        place += rows
        put(along_taps, place, col_2, top[cols - 2 : cols - 1], bottom[cols - 2 : cols - 1], 0)
        put(along_taps, place, col_3, top[cols - 1 : cols], bottom[cols - 1 : cols], 1)
        put(along_taps, place, rgt, top_right, bottom_right, 2)

    for i in range(faces):
        face(i)
    w_rows = w_ref[...].reshape(9 * ch, ch)
    out = gelu(jnp.dot(across_taps[...], w_rows, preferred_element_type=F32) + bias)
    edge_rows[...] = out.astype(BF).reshape(edge_rows.shape)
    out = gelu(jnp.dot(along_taps[...], w_cols[...], preferred_element_type=F32) + bias)
    edge_cols[...] = out.reshape(edge_cols.shape)
    if coarse:
        order_cols, order_rows = parting(cols), parting(rows)

    def with_column(tile, place, value):
        spots = lax.broadcasted_iota(jnp.int32, tile.shape, 1)
        return jnp.where(spots == place, value[:, None, :], tile)

    def update(i, carry):
        new_top, new_bottom = edge_rows[i, 0].astype(F32), edge_rows[i, 1].astype(F32)
        end = (rows - 1) * EDGE
        for tile, side, place in ((left, 0, 0), (right, 1, EDGE - 1)):
            start = side * (cols - EDGE)
            value = y_ref[i, :, start : start + EDGE].astype(F32)
            value = with_column(value, place, edge_cols[i, side * rows : (side + 1) * rows])
            tile[...] = value.reshape(rows * EDGE, ch)
            tile[0:EDGE] = new_top[start : start + EDGE]
            tile[end : end + EDGE] = new_bottom[start : start + EDGE]
            if coarse:
                tiles[side, i] = value.astype(BF)
                tiles[side, i, 0] = edge_rows[i, 0, start : start + EDGE]
                tiles[side, i, rows - 1] = edge_rows[i, 1, start : start + EDGE]
            else:
                y_ref[i, :, start : start + EDGE] = value.astype(BF)
        if not coarse:
            y_ref[i, 0] = edge_rows[i, 0]
            y_ref[i, rows - 1] = edge_rows[i, 1]
        lines = (
            column(left, 0), column(left, 1), column(right, EDGE - 2), column(right, EDGE - 1)
        )
        if not coarse:
            put_strips(i, r, c, lines, new_top, new_bottom, *outs)
            return carry
        spot = lax.broadcasted_iota(jnp.int32, (cols, 1), 0)
        half = cols // 2
        for k, (own, near) in enumerate(((new_top, 1), (new_bottom, rows - 2))):
            first = edge_cols[i, near : near + 1]
            last = edge_cols[i, rows + near : rows + near + 1]
            other = y_ref[i, near].astype(F32)
            other = jnp.where(spot == 0, first, jnp.where(spot == cols - 1, last, other))
            both = (own, other) if k == 0 else (other, own)
            four = parted(order_cols, jnp.concatenate([v.astype(BF) for v in both], axis=1))
            four = jnp.concatenate([four[j] for j in (0, 2, 1, 3)], axis=1)
            c_taps[pl.ds((2 * i + k) * half, half)] = four
        for k, both in enumerate((lines[:2], lines[2:])):
            four = parted(order_rows, jnp.concatenate([v.astype(BF) for v in both], axis=1))
            place = 2 * faces * half + (2 * i + k) * (rows // 2)
            c_taps[pl.ds(place, rows // 2)] = jnp.concatenate(four, axis=1)
        return carry

    lax.fori_loop(0, faces, update, 0, unroll=True)
    if not coarse:
        return
    copies = tile_copies(y_out, tiles, sems, back=True)
    if cols > 2 * EDGE:
        between = pl.ds(EDGE, cols - 2 * EDGE)
        for k, row in enumerate((0, rows - 1)):
            copies.append(
                pltpu.make_async_copy(
                    edge_rows.at[:, k, between], y_out.at[:, row, between], sems.at[2 + k]
                )
            )
    for copy in copies:
        copy.start()
    half = cols // 2
    out = jnp.dot(
        c_taps[...], dw_ref[...].reshape(4 * ch, -1), preferred_element_type=F32
    ) + db_ref[...]
    across_cells = 2 * faces * half
    c_rows[...] = out[:across_cells].astype(BF).reshape(c_rows.shape)
    c_cols[...] = out[across_cells:].reshape(c_cols.shape)

    def cells(i, carry):
        for side in range(2):
            start = side * (half - EDGE)
            value = c_ref[i, :, start : start + EDGE].astype(F32)
            value = with_column(value, side * (EDGE - 1), c_cols[i, side])
            c_tiles[side, i] = value.astype(BF)
            for k in range(2):
                c_tiles[side, i, k * (rows // 2 - 1)] = c_rows[i, k, start : start + EDGE]
        return carry

    lax.fori_loop(0, faces, cells, 0, unroll=True)
    more = []
    for side, start in enumerate((0, half - EDGE)):
        more.append(
            pltpu.make_async_copy(
                c_tiles.at[side], c_out.at[:, :, pl.ds(start, EDGE), :], sems.at[4 + side]
            )
        )
    if half > 2 * EDGE:
        between = pl.ds(EDGE, half - 2 * EDGE)
        for k, row in enumerate((0, rows // 2 - 1)):
            more.append(
                pltpu.make_async_copy(
                    c_rows.at[:, k, between], c_out.at[:, row, between], sems.at[6 + k]
                )
            )
    for copy in more:
        copy.start()
    for copy in copies + more:
        copy.wait()


def ring(
    neighbour_face, orientation, x, buffers, copied, lines, parts, weight, bias, seams, seconds, down
):
    y, *coarse = buffers
    faces, rows, cols, ch = x.shape
    groups = len(seams)
    smem = pl.BlockSpec(memory_space=pltpu.SMEM)
    hbm = pl.BlockSpec(memory_space=pltpu.HBM)
    vmem = pl.BlockSpec(memory_space=pltpu.VMEM)
    args = [neighbour_face, orientation, x, y, lines, *parts, weight, bias, *seams, *seconds]
    in_specs = [smem, smem] + [vmem] * (len(args) - 2)
    scratch = [
        pltpu.VMEM((2, faces, rows, EDGE, ch), BF),
        pltpu.VMEM((faces, 2, cols, ch), BF),
        pltpu.VMEM((faces, 2 * rows, ch), F32),
        pltpu.VMEM((groups, faces, 3 * rows + EXTRA, ch), BF),
        pltpu.VMEM((rows * EDGE, ch), F32),
        pltpu.VMEM((rows * EDGE, ch), F32),
        pltpu.VMEM((9 * ch, ch), BF),
        pltpu.VMEM((2 * faces * cols, 9 * ch), BF),
        pltpu.VMEM((2 * faces * rows, 9 * ch), BF),
    ]
    if down:
        co = down[0].shape[-1]
        args += [coarse[0], *down]
        in_specs += [vmem] * 3
        aliases = {len(args): 0, len(args) + 1: 1}
        args += [in_hbm(buffer) for buffer in copied]
        in_specs += [hbm] * 2
        out_shape = [pltpu.HBM(buffer.shape, BF) for buffer in copied]
        out_specs = [hbm] * 2
        scratch += [
            pltpu.VMEM((faces * (rows + cols), 4 * ch), BF),
            pltpu.VMEM((2, faces, rows // 2, EDGE, co), BF),
            pltpu.VMEM((faces, 2, cols // 2, co), BF),
            pltpu.VMEM((faces, 2, rows // 2, co), F32),
            pltpu.SemaphoreType.DMA((8,)),
        ]
    else:
        aliases = {3: 0}
        out_shape = [jax.ShapeDtypeStruct(y.shape, BF), *strip_shapes(faces, rows, cols, ch)]
        out_specs = [vmem] * 5
    return pl.pallas_call(
        functools.partial(ring_kernel, groups, bool(down)),
        in_specs=in_specs,
        out_specs=tuple(out_specs),
        out_shape=tuple(out_shape),
        scratch_shapes=scratch,
        input_output_aliases=aliases,
        cost_estimate=pl.CostEstimate(
            flops=faces * (rows + cols) * 36 * ch * ch, bytes_accessed=8 * 2**20, transcendentals=0
        ),
        compiler_params=pltpu.CompilerParams(vmem_limit_bytes=20 * 2**20),
        name="ring",
    )(*args)


def blocks(change_row, change_col):
    cols = lax.axis_size("col")
    return [
        (r * cols + c, (r ^ change_row) * cols + (c ^ change_col))
        for r in range(lax.axis_size("row"))
        for c in range(cols)
    ]


def swap(v, change_row, change_col):
    return lax.ppermute(v, ("row", "col"), blocks(change_row, change_col))


def level(neighbour_face, orientation, x, strips, weight, bias, down):
    u, v, turn, lines = strips
    groups = lax.axis_size("face")
    total = x.shape[0] * x.shape[1] // STEP
    early = max(total * (6 if down else 5) // 12, 1)
    late = early + max(total // 12, 1)
    piece = functools.partial(conv_piece, x, weight, bias)
    beside, across, diagonal = swap(u, 0, 1), swap(v, 3, 0), swap(v, 3, 1)
    pair, turned = swap(v, 1, 0), swap(turn, 1, 0)
    state = piece(0, early, None)
    (beside, across, diagonal, turned), state = lax.optimization_barrier(
        ((beside, across, diagonal, turned), state)
    )
    pair_beside, pair_across, pair_diagonal = (swap(a, 1, 0) for a in (beside, across, diagonal))
    state = piece(early, late - early, state)
    stores = (v, beside, pair, pair_beside, pair_across, pair_diagonal, across, diagonal)
    picked = select_strips(neighbour_face, orientation, stores, groups)
    picked, state = lax.optimization_barrier((picked, state))
    seams = list(picked)
    for k in sorted(range(1, groups), key=lambda k: -(k.bit_length())):
        pairs = [(g, g ^ k) for g in range(groups)]
        seams[k] = lax.ppermute(picked[k], "face", pairs)
    y = piece(late, total - late, state)[2]
    done, coarse = total - total // 4, ()
    if down:
        coarse = downsample(y, *down, 0, done, ())
    seams[1:], y, coarse = lax.optimization_barrier((seams[1:], y, coarse))
    seconds = [swap(seam, 1, 0) for seam in seams[1:]]
    if down:
        coarse = downsample(y, *down, done, total - done, coarse)
    buffers, copied = (y, *coarse[:1]), coarse[1:]
    parts = (beside, pair_beside, across, diagonal, turned)
    return ring(
        *(neighbour_face, orientation, x, buffers, copied, lines, parts, weight, bias),
        *(seams, seconds, down),
    )


def per_device(
    field, conv1_w, conv1_b, conv2_w, conv2_b, down_w, down_b, neighbour_face, orientation
):
    tables = (neighbour_face.T, orientation.T)
    hidden, *strips = level(*tables, field, strips_of(field), conv1_w, conv1_b[None], ())
    return level(*tables, hidden, strips, conv2_w, conv2_b[None], (down_w, down_b[None]))


def solution(mesh):
    groups = mesh.shape["face"]
    fast = mesh.shape["row"] == 4 and mesh.shape["col"] == 2 and groups & (groups - 1) == 0
    return jax.shard_map(
        per_device if fast else general_device,
        mesh=mesh,
        in_specs=(P("face", "row", "col", None), P(), P(), P(), P(), P(), P(), P(), P()),
        out_specs=(P("face", "row", "col", None), P("face", "row", "col", None)),
        check_vma=False,
    )
```

```python
import functools

import jax
import jax.numpy as jnp
import numpy as np
from jax import lax
from jax.experimental import pallas as pl
from jax.experimental.pallas import tpu as pltpu
from jax.sharding import PartitionSpec as P


FACES = 12
BF = jnp.bfloat16
F32 = jnp.float32
STEP = 16
EDGE = 8
EXTRA = 16

layout = ("NHWC", "HWIO", "NHWC")


def padded_2(block, sides, width):
    for axis, dim in sides:
        count = lax.axis_size(axis)
        forward = [(i, i + 1) for i in range(count - 1)]
        backward = [(target, source) for source, target in forward]
        low = lax.ppermute(
            lax.slice_in_dim(block, block.shape[dim] - width, None, axis=dim), axis, forward
        )
        high = lax.ppermute(lax.slice_in_dim(block, 0, width, axis=dim), axis, backward)
        block = jnp.concatenate([low, block, high], axis=dim)
    return block


def seam_parts(edges, neighbours, codes):
    seam_faces = neighbours[:, :4]
    seam_codes = codes[:, :4]
    seams = edges[seam_faces, seam_codes // 2]
    seams = jnp.where((seam_codes % 2 == 1)[:, :, None, None], seams[:, :, ::-1], seams)
    corner_values = jnp.stack(
        [edges[:, 0, 0], edges[:, 0, -1], edges[:, 2, -1], edges[:, 2, 0]], axis=1
    )
    corner_faces = neighbours[:, 4:]
    picked = corner_values[jnp.minimum(corner_faces, FACES - 1), codes[:, 4:]]
    picked = jnp.where((corner_faces < FACES)[:, :, None], picked, jnp.zeros_like(picked))
    return (seams, picked)


def convolve(padded, weight, bias):
    summed = lax.conv_general_dilated(
        padded,
        weight,
        (1, 1),
        "VALID",
        dimension_numbers=layout,
        preferred_element_type=jnp.float32,
    )
    return jax.nn.gelu(summed + bias, approximate=False).astype(jnp.bfloat16)


def general_layer(block, weight, bias, neighbour_face, orientation):
    face_count, row_size, col_size, channels = block.shape
    row_total = lax.axis_size("row")
    col_total = lax.axis_size("col")
    row_place = lax.axis_index("row")
    col_place = lax.axis_index("col")
    face_side = row_size * row_total
    padded = padded_2(block, (("row", 1), ("col", 2)), 1)
    top_live = row_place == 0
    bottom_live = row_place == row_total - 1
    left_live = col_place == 0
    right_live = col_place == col_total - 1
    empty_line = jnp.zeros((face_count, face_side, channels), jnp.float32)

    def place(strip, offset, live):
        scaled = strip.astype(jnp.float32) * live.astype(jnp.float32)
        return lax.dynamic_update_slice_in_dim(empty_line, scaled, offset, 1)

    lines = jnp.stack(
        [
            place(block[:, 0], col_place * col_size, top_live),
            place(block[:, :, -1], row_place * row_size, right_live),
            place(block[:, -1], col_place * col_size, bottom_live),
            place(block[:, :, 0], row_place * row_size, left_live),
        ],
        axis=1,
    )
    complete = lax.psum(lax.psum(lines.astype(jnp.bfloat16), "col"), "row").astype(jnp.float32)
    every_edge = lax.all_gather(complete.astype(jnp.bfloat16), "face", axis=0, tiled=True)
    first_face = lax.axis_index("face") * face_count
    own_faces = lax.dynamic_slice_in_dim(neighbour_face, first_face, face_count, 0)
    own_codes = lax.dynamic_slice_in_dim(orientation, first_face, face_count, 0)
    seams, corners = seam_parts(every_edge, own_faces, own_codes)
    upper = jnp.concatenate([corners[:, 0:1], seams[:, 0], corners[:, 1:2]], 1)
    lower = jnp.concatenate([corners[:, 3:4], seams[:, 2], corners[:, 2:3]], 1)
    leftward = jnp.concatenate([corners[:, 0:1], seams[:, 3], corners[:, 3:4]], 1)
    rightward = jnp.concatenate([corners[:, 1:2], seams[:, 1], corners[:, 2:3]], 1)
    upper_cut = lax.dynamic_slice_in_dim(upper, col_place * col_size, col_size + 2, 1)
    lower_cut = lax.dynamic_slice_in_dim(lower, col_place * col_size, col_size + 2, 1)
    left_cut = lax.dynamic_slice_in_dim(leftward, row_place * row_size, row_size + 2, 1)
    right_cut = lax.dynamic_slice_in_dim(rightward, row_place * row_size, row_size + 2, 1)
    padded = padded.at[:, 0].set(jnp.where(top_live, upper_cut, padded[:, 0]))
    padded = padded.at[:, -1].set(jnp.where(bottom_live, lower_cut, padded[:, -1]))
    padded = padded.at[:, :, 0].set(jnp.where(left_live, left_cut, padded[:, :, 0]))
    padded = padded.at[:, :, -1].set(jnp.where(right_live, right_cut, padded[:, :, -1]))
    return convolve(padded, weight, bias)


def general_device(
    field, conv1_w, conv1_b, conv2_w, conv2_b, down_w, down_b, neighbour_face, orientation
):
    hidden = general_layer(field, conv1_w, conv1_b, neighbour_face, orientation)
    skip = general_layer(hidden, conv2_w, conv2_b, neighbour_face, orientation)
    summed = lax.conv_general_dilated(
        skip, down_w, (2, 2), "VALID", dimension_numbers=layout, preferred_element_type=jnp.float32
    )
    coarse = (summed + down_b).astype(jnp.bfloat16)
    return (skip, coarse)


def gelu(v):
    return 0.5 * v * (1.0 + lax.erf(v * np.float32(np.sqrt(0.5))))


def shifted(v, before, after):
    n = v.shape[0]
    spot = lax.broadcasted_iota(jnp.int32, (n, 1), 0)
    low = jnp.where(spot == 0, before, pltpu.roll(v, 1, 0))
    high = jnp.where(spot == n - 1, after, pltpu.roll(v, n - 1, 0))
    return low.astype(BF), v.astype(BF), high.astype(BF)


def parting(n):
    to = lax.broadcasted_iota(jnp.int32, (n, n), 0)
    source = lax.broadcasted_iota(jnp.int32, (n, n), 1)
    half = n // 2
    return jnp.where(source == jnp.where(to < half, 2 * to, 2 * (to - half) + 1), 1.0, 0.0).astype(BF)


def parted(order, v):
    v = jnp.dot(order, v, preferred_element_type=F32).astype(BF)
    half, lanes = v.shape[0] // 2, v.shape[1] // 2
    return v[:half, :lanes], v[:half, lanes:], v[half:, :lanes], v[half:, lanes:]


def conv_kernel(first, count, build, x_ref, b_ref, *refs):
    *refs, taps_0, taps_1 = refs
    if build:
        w_ref, y_ref, w_low, w_high = refs
    else:
        w_low, w_high, _, y_ref = refs
    _, size, cols, ch = x_ref.shape
    steps = size // STEP
    pairs = STEP // 2
    zero_row = jnp.zeros((1, ch), F32)
    half = 3 * ch

    if build:
        zero = jnp.zeros((ch, ch), BF)
        for d in range(3):
            one = slice(d * ch, (d + 1) * ch)
            two = slice(half + d * ch, half + (d + 1) * ch)
            w_low[one, :ch] = w_ref[0, d]
            w_low[one, ch:] = zero
            w_low[two, :ch] = w_ref[1, d]
            w_low[two, ch:] = w_ref[0, d]
            w_high[one, :ch] = w_ref[2, d]
            w_high[one, ch:] = w_ref[1, d]
            w_high[two, :ch] = zero
            w_high[two, ch:] = w_ref[2, d]

    def at(t):
        return t // steps, lax.rem(t, steps)

    def fill(taps, t):
        face, step = at(t)
        base = step * STEP

        def put(v, pair, side):
            low, same, high = shifted(v.astype(F32), zero_row, zero_row)
            place = side * half
            taps[pair, :, place : place + ch] = low
            taps[pair, :, place + ch : place + 2 * ch] = same
            taps[pair, :, place + 2 * ch : place + 3 * ch] = high

        inside = (step > 0).astype(F32)
        put(x_ref[face, jnp.maximum(base - 1, 0)].astype(F32) * inside, 0, 0)
        for row in range(STEP):
            put(x_ref[face, base + row], (row + 1) // 2, (row + 1) % 2)
        inside = (step < steps - 1).astype(F32)
        put(x_ref[face, jnp.minimum(base + STEP, size - 1)].astype(F32) * inside, pairs, 1)

    def product(taps, t):
        face, step = at(t)
        base = step * STEP
        lower = taps[pl.ds(0, pairs)].reshape(pairs * cols, 2 * half)
        upper = taps[pl.ds(1, pairs)].reshape(pairs * cols, 2 * half)
        total = jnp.dot(lower, w_low[...], preferred_element_type=F32)
        total += jnp.dot(upper, w_high[...], preferred_element_type=F32)
        total = total.reshape(pairs, cols, 2 * ch)
        bias = b_ref[...]
        for side in range(2):
            out = gelu(total[:, :, side * ch : (side + 1) * ch] + bias[None]).astype(BF)
            for pair in range(pairs):
                y_ref[face, base + 2 * pair + side] = out[pair]
    last = first + count - 1
    fill(taps_0, first)

    def double(j, carry):
        t = first + 2 * j
        fill(taps_1, t + 1)
        product(taps_0, t)
        fill(taps_0, jnp.minimum(t + 2, last))
        product(taps_1, t + 1)
        return carry

    lax.fori_loop(0, count // 2, double, 0)
    if count % 2:
        product(taps_0, last)


def in_hbm(x):
    return pltpu.with_memory_space_constraint(x, pltpu.HBM)


def conv_piece(x, weight, bias, first, count, state):
    faces, rows, cols, ch = x.shape
    vmem = pl.BlockSpec(memory_space=pltpu.VMEM)
    build = state is None
    taps = (STEP // 2 + 1, cols, 6 * ch)
    arranged = jax.ShapeDtypeStruct((6 * ch, 2 * ch), BF)
    args = [x, bias, weight] if build else [x, bias, *state]
    out_shape = [jax.ShapeDtypeStruct(x.shape, BF)] + [arranged] * (2 if build else 0)
    pixels = count * STEP * cols
    out = pl.pallas_call(
        functools.partial(conv_kernel, first, count, build),
        in_specs=[vmem] * len(args),
        out_specs=tuple([vmem] * len(out_shape)),
        out_shape=tuple(out_shape),
        scratch_shapes=[pltpu.VMEM(taps, BF), pltpu.VMEM(taps, BF)],
        input_output_aliases={} if build else {4: 0},
        cost_estimate=pl.CostEstimate(
            flops=pixels * 24 * ch * ch, bytes_accessed=4 * pixels * ch, transcendentals=0
        ),
        compiler_params=pltpu.CompilerParams(vmem_limit_bytes=16 * 2**20),
        name="conv_piece",
    )(*args)
    return (out[1], out[2], out[0]) if build else (state[0], state[1], out[0])


def down_kernel(first, count, y_ref, w_ref, b_ref, *refs):
    c_ref, y_out, c_out, taps_0, taps_1, wide_0, wide_1, sems = refs[-8:]
    faces, rows, cols, ch = y_ref.shape
    steps, pairs = rows // STEP, STEP // 2
    last = first + count - 1

    def copies(t):
        face, step = t // steps, lax.rem(t, steps)
        some, cells = pl.ds(step * STEP, STEP), pl.ds(step * pairs, pairs)
        return (
            pltpu.make_async_copy(y_ref.at[face, some], y_out.at[face, some], sems.at[0]),
            pltpu.make_async_copy(c_ref.at[face, cells], c_out.at[face, cells], sems.at[1]),
        )

    def fill(taps, wide, t):
        face, step = t // steps, lax.rem(t, steps)
        for pair in range(pairs):
            row = step * STEP + 2 * pair
            for a in range(2):
                wide[2 * pair + a] = y_ref[face, row + a].astype(F32)
            four = [
                wide[2 * pair + a, pl.ds(d, cols // 2, stride=2), :].astype(BF)
                for a in range(2)
                for d in range(2)
            ]
            taps[pair] = jnp.concatenate(four, axis=1)

    def product(taps, t):
        face, step = t // steps, lax.rem(t, steps)
        out = jnp.dot(
            taps[...].reshape(pairs * cols // 2, 4 * ch),
            w_ref[...].reshape(4 * ch, -1),
            preferred_element_type=F32,
        )
        out = (out + b_ref[...]).astype(BF)
        c_ref[face, pl.ds(step * pairs, pairs)] = out.reshape(pairs, cols // 2, -1)
        copies(t)[1].start()

    def send(t, carry):
        copies(t)[0].start()
        return carry

    def wait(t, carry):
        for copy in copies(t):
            copy.wait()
        return carry

    lax.fori_loop(first, first + count, send, 0)
    fill(taps_0, wide_0, first)

    def double(j, carry):
        t = first + 2 * j
        fill(taps_1, wide_1, t + 1)
        product(taps_0, t)
        fill(taps_0, wide_0, jnp.minimum(t + 2, last))
        product(taps_1, t + 1)
        return carry

    lax.fori_loop(0, count // 2, double, 0, unroll=True)
    if count % 2:
        product(taps_0, last)
    lax.fori_loop(first, first + count, wait, 0)


def downsample(y, weight, bias, first, count, into):
    faces, rows, cols, ch = y.shape
    shape = (faces, rows // 2, cols // 2, weight.shape[-1])
    vmem = pl.BlockSpec(memory_space=pltpu.VMEM)
    hbm = pl.BlockSpec(memory_space=pltpu.HBM)
    taps, wide = (STEP // 2, cols // 2, 4 * ch), (STEP, cols, ch)
    args, in_specs = [y, weight, bias], [vmem] * 3
    if into:
        args += [into[0], in_hbm(into[1]), in_hbm(into[2])]
        in_specs += [vmem, hbm, hbm]
    pixels = count * STEP * cols
    return pl.pallas_call(
        functools.partial(down_kernel, first, count),
        in_specs=in_specs,
        out_specs=(vmem, hbm, hbm),
        out_shape=(jax.ShapeDtypeStruct(shape, BF), pltpu.HBM(y.shape, BF), pltpu.HBM(shape, BF)),
        scratch_shapes=[pltpu.VMEM(taps, BF)] * 2
        + [pltpu.VMEM(wide, F32)] * 2
        + [pltpu.SemaphoreType.DMA((2,))],
        input_output_aliases={3: 0, 4: 1, 5: 2} if into else {},
        cost_estimate=pl.CostEstimate(
            flops=pixels * 2 * ch * shape[-1], bytes_accessed=4 * pixels * ch, transcendentals=0
        ),
        compiler_params=pltpu.CompilerParams(vmem_limit_bytes=16 * 2**20),
        name="downsample",
    )(*args)


def column(tile, place):
    return tile[pl.ds(place, tile.shape[0] // EDGE, stride=EDGE), :]


def put_strips(i, r, c, lines, top, bottom, u_ref, v_ref, turn_ref, line_ref):
    left, left_in, right_in, right = lines
    size = left.shape[0]
    for place, value in enumerate(lines):
        line_ref[i, place] = value.astype(BF)
    side = jnp.where(c == 0, left, right).astype(BF)
    inner = jnp.where(c == 0, right, left).astype(BF)
    even = lax.rem(r, 2) == 0
    line = jnp.where(even, top, bottom).astype(BF)
    turn_ref[i] = jnp.where(even, bottom, top).astype(BF)
    for ref in (u_ref, v_ref):
        ref[i, 0] = side
        ref[i, 1] = line[:size]
        ref[i, 2] = line[size:]
    u_ref[i, 3] = inner


def strip_shapes(faces, rows, cols, ch):
    return (
        jax.ShapeDtypeStruct((faces, 4, rows, ch), BF),
        jax.ShapeDtypeStruct((faces, 3, rows, ch), BF),
        jax.ShapeDtypeStruct((faces, cols, ch), BF),
        jax.ShapeDtypeStruct((faces, 4, rows, ch), BF),
    )


def whole(shape):
    return pl.BlockSpec(shape, lambda *_: (0,) * len(shape))


def tile_copies(array, tiles, sems, back=False):
    cols = array.shape[2]
    out = []
    for side, start in enumerate((0, cols - EDGE)):
        far, near = array.at[:, :, pl.ds(start, EDGE), :], tiles.at[side]
        out.append(pltpu.make_async_copy(*((near, far) if back else (far, near)), sems.at[side]))
    return out


def strips_kernel(x_ref, u_ref, v_ref, turn_ref, line_ref, tiles, outer, left, right, sems):
    faces, rows, cols, ch = x_ref.shape
    r, c = lax.axis_index("row"), lax.axis_index("col")
    copies = tile_copies(x_ref, tiles, sems)
    for k, row in enumerate((0, rows - 1)):
        copies.append(pltpu.make_async_copy(x_ref.at[:, row], outer.at[k], sems.at[2 + k]))
    for copy in copies:
        copy.start()
    for copy in copies:
        copy.wait()

    def face(i, carry):
        left[...] = tiles[0, i].astype(F32).reshape(rows * EDGE, ch)
        right[...] = tiles[1, i].astype(F32).reshape(rows * EDGE, ch)
        lines = (column(left, 0), column(left, 1), column(right, EDGE - 2), column(right, EDGE - 1))
        put_strips(
            i, r, c, lines, outer[0, i].astype(F32), outer[1, i].astype(F32),
            u_ref, v_ref, turn_ref, line_ref,
        )
        return carry

    lax.fori_loop(0, faces, face, 0, unroll=True)


def strips_of(x):
    faces, rows, cols, ch = x.shape
    shapes = strip_shapes(faces, rows, cols, ch)
    return pl.pallas_call(
        strips_kernel,
        in_specs=[pl.BlockSpec(memory_space=pltpu.HBM)],
        out_specs=(pl.BlockSpec(memory_space=pltpu.VMEM),) * 4,
        out_shape=shapes,
        scratch_shapes=[
            pltpu.VMEM((2, faces, rows, EDGE, ch), BF),
            pltpu.VMEM((2, faces, cols, ch), BF),
            pltpu.VMEM((rows * EDGE, ch), F32),
            pltpu.VMEM((rows * EDGE, ch), F32),
            pltpu.SemaphoreType.DMA((4,)),
        ],
        cost_estimate=pl.CostEstimate(flops=0, bytes_accessed=4 * 2**20, transcendentals=0),
        compiler_params=pltpu.CompilerParams(vmem_limit_bytes=10 * 2**20),
        name="strips_of",
    )(in_hbm(x))


def select_kernel(near_ref, code_ref, *refs):
    stores, outs, held = refs[:8], refs[8:-1], refs[-1]
    faces, _, size, ch = held.shape[1:]
    me, r, c = lax.axis_index("face"), lax.axis_index("row"), lax.axis_index("col")
    for k, store in enumerate(stores):
        for i in range(faces):
            held[k, i] = store[i, 0:3]

    def slot(row, col):
        return ((r ^ row) << 1) | (c ^ col)

    def quarter(edge, q):
        upright = lax.rem(edge, 2) == 1
        row = jnp.where(upright, q, jnp.where(edge == 0, 0, 3))
        col = jnp.where(upright, jnp.where(edge == 3, 0, 1), q >> 1)
        return slot(row, col), jnp.where(upright, 0, 1 + (q & 1))

    def end(n, where, block, last):
        head = held[where, n, block, 0:EXTRA].astype(F32)
        tail = held[where, n, block, size - EXTRA : size].astype(F32)
        return jnp.where(last, tail[EXTRA - 1 : EXTRA], head[0:1])

    for k, out in enumerate(outs):
        target = me ^ k
        parts = out.shape[0] // (faces * size)
        single = jnp.zeros((out.shape[0] - faces * parts * size, ch), F32)
        spot = lax.broadcasted_iota(jnp.int32, (single.shape[0], 1), 0)
        for i in range(faces):
            start = i * parts * size
            f = target * faces + i
            edge = 3 - 2 * c
            code = code_ref[edge, f]
            far, flip = code >> 1, code & 1
            n = lax.rem(near_ref[edge, f], faces)
            where, block = quarter(far, jnp.where(flip == 1, 3 - r, r))
            out[start : start + size] = held[where, n, block]
            corner = jnp.where(r < 2, c, 3 - c)
            tip = code_ref[4 + corner, f]
            tip_n = lax.rem(near_ref[4 + corner, f], faces)
            tip_row = jnp.where(tip < 2, 0, 3)
            tip_col = jnp.where((tip == 1) | (tip == 2), 1, 0)
            tip_pixel = end(tip_n, slot(tip_row, tip_col), 0, tip_row == 3)
            q = jnp.where(flip == 1, 4 - r, r - 1)
            where, block = quarter(far, jnp.clip(q, 0, 3))
            before = jnp.where(r == 0, tip_pixel, end(n, where, block, flip == 0))
            q = jnp.where(flip == 1, 2 - r, r + 1)
            where, block = quarter(far, jnp.clip(q, 0, 3))
            after = jnp.where(r == 3, tip_pixel, end(n, where, block, flip == 1))

            edge = jnp.where(r < 2, 0, 2)
            code = code_ref[edge, f]
            far, flip = code >> 1, code & 1
            n = lax.rem(near_ref[edge, f], faces)
            part = c ^ flip
            for h in range(parts - 1):
                own = jnp.where((r == 0) | (r == 3), 0, 1) if k else h
                where, block = quarter(far, 2 * part + own)
                out[start + (1 + h) * size : start + (2 + h) * size] = held[where, n, block]
            where, block = quarter(far, jnp.where(part == 0, 2, 1))
            middle = end(n, where, block, part == 1)
            for j, pixel in enumerate((before, after, middle)):
                single = jnp.where(spot == 3 * i + j, pixel, single)
        out[faces * parts * size :] = single.astype(BF)


def select_strips(neighbour_face, orientation, stores, groups):
    faces, _, size, ch = stores[0].shape
    single = -(-3 * faces // EXTRA) * EXTRA
    shapes = [
        jax.ShapeDtypeStruct(((2 if k else 3) * faces * size + single, ch), BF)
        for k in range(groups)
    ]
    smem = pl.BlockSpec(memory_space=pltpu.SMEM)
    return pl.pallas_call(
        select_kernel,
        in_specs=[smem, smem] + [pl.BlockSpec(memory_space=pltpu.VMEM)] * 8,
        out_specs=(pl.BlockSpec(memory_space=pltpu.VMEM),) * groups,
        out_shape=tuple(shapes),
        scratch_shapes=[pltpu.VMEM((8, faces, 3, size, ch), BF)],
        cost_estimate=pl.CostEstimate(flops=0, bytes_accessed=4 * 2**20, transcendentals=0),
        compiler_params=pltpu.CompilerParams(vmem_limit_bytes=10 * 2**20),
        name="select_strips",
    )(neighbour_face, orientation, *stores)


def ring_kernel(groups, coarse, near_ref, code_ref, x_ref, y_in, line_in, beside, diagonal, across,
                far_diagonal, turned, w_ref, b_ref, *refs):
    seams, seconds, refs = refs[:groups], refs[groups : 2 * groups - 1], refs[2 * groups - 1 :]
    if coarse:
        c_ref, dw_ref, db_ref, _, _, y_out, c_out = refs[:7]
        y_ref = y_in
        scratch = refs[7:]
        *scratch, c_taps, c_tiles, c_rows, c_cols, sems = scratch
    else:
        y_ref, outs, scratch = refs[0], refs[1:5], refs[5:]
    tiles, edge_rows, edge_cols, held, held_single, left, right, w_cols, across_taps, along_taps = scratch
    faces, rows, cols, ch = x_ref.shape
    me, r, c = lax.axis_index("face"), lax.axis_index("row"), lax.axis_index("col")
    for k in range(groups):
        seam, parts = seams[k], 2 if k else 3
        for i in range(faces):
            start = i * parts * rows
            held[k, i, : 2 * rows] = seam[start : start + 2 * rows]
            half = seconds[k - 1] if k else seam
            start += (parts - 1) * rows
            held[k, i, 2 * rows :] = half[start : start + rows]
        held_single[k] = seam[faces * parts * rows :]

    def oriented(v, flip):
        n = v.shape[0]
        to = lax.broadcasted_iota(jnp.int32, (n, n), 0)
        source = lax.broadcasted_iota(jnp.int32, (n, n), 1)
        order = jnp.where(source == jnp.where(flip == 1, n - 1 - to, to), 1.0, 0.0).astype(BF)
        return jnp.dot(order, v, preferred_element_type=F32)

    even = lax.rem(r, 2) == 0
    outer = (r == 0) | (r == 3)
    for d in range(3):
        for a in range(3):
            w_cols[(3 * d + a) * ch : (3 * d + a + 1) * ch] = w_ref[a, d]
    bias = b_ref[...]

    def holder(n):
        return jnp.minimum(n, FACES - 1) // faces ^ me

    def put(taps, place, v, before, after, third):
        for k, part in enumerate(shifted(v, before, after)):
            start = (3 * third + k) * ch
            taps[pl.ds(place, v.shape[0]), start : start + ch] = part

    def face(i):
        f = me * faces + i
        edge = 3 - 2 * c
        n = near_ref[edge, f]
        corner = jnp.where(r < 2, c, 3 - c)
        tip_n = near_ref[4 + corner, f]
        seam_side = oriented(held[holder(n), i, 0:rows], code_ref[edge, f] & 1)
        n_before = jnp.where(r == 0, tip_n, n)
        n_after = jnp.where(r == 3, tip_n, n)
        before = held_single[holder(n_before)].astype(F32)[3 * i : 3 * i + 1]
        after = held_single[holder(n_after)].astype(F32)[3 * i + 1 : 3 * i + 2]
        before = jnp.where(n_before < FACES, before, 0.0)
        after = jnp.where(n_after < FACES, after, 0.0)
        edge = jnp.where(r < 2, 0, 2)
        n = near_ref[edge, f]
        seam_line = oriented(held[holder(n), i, rows : 3 * rows], code_ref[edge, f] & 1)
        middle = held_single[holder(n)].astype(F32)[3 * i + 2 : 3 * i + 3]

        inner = beside[i, 3].astype(F32)
        block_line = jnp.concatenate([across[i, 1], across[i, 2]], axis=0).astype(F32)
        outward = jnp.where(outer, seam_line, block_line)
        inward = turned[i].astype(F32)
        top = jnp.where(even, outward, inward)
        bottom = jnp.where(even, inward, outward)
        lft = jnp.where(c == 0, seam_side, inner)
        rgt = jnp.where(c == 0, inner, seam_side)
        pair_inner = diagonal[i, 3].astype(F32)
        inward_corner = jnp.where(even, pair_inner[0:1], pair_inner[rows - 1 : rows])
        far_first = far_diagonal[i, 1].astype(F32)[0:1]
        far_last = far_diagonal[i, 2].astype(F32)[rows - 1 : rows]
        outward_corner = jnp.where(outer, middle, jnp.where(c == 0, far_first, far_last))
        inner_top = jnp.where(even, outward_corner, inward_corner)
        inner_bottom = jnp.where(even, inward_corner, outward_corner)
        top_left = jnp.where(c == 0, before, inner_top)
        top_right = jnp.where(c == 0, inner_top, before)
        bottom_left = jnp.where(c == 0, after, inner_bottom)
        bottom_right = jnp.where(c == 0, inner_bottom, after)

        row_0, row_1, row_2, row_3 = (
            x_ref[i, k].astype(F32) for k in (0, 1, rows - 2, rows - 1)
        )
        place = 2 * i * cols
        put(across_taps, place, top, top_left, top_right, 0)
        put(across_taps, place, row_0, lft[0:1], rgt[0:1], 1)
        put(across_taps, place, row_1, lft[1:2], rgt[1:2], 2)
        place += cols
        put(across_taps, place, row_2, lft[rows - 2 : rows - 1], rgt[rows - 2 : rows - 1], 0)
        put(across_taps, place, row_3, lft[rows - 1 : rows], rgt[rows - 1 : rows], 1)
        put(across_taps, place, bottom, bottom_left, bottom_right, 2)
        col_0, col_1, col_2, col_3 = (line_in[i, k].astype(F32) for k in range(4))
        place = 2 * i * rows
        put(along_taps, place, lft, top_left, bottom_left, 0)
        put(along_taps, place, col_0, top[0:1], bottom[0:1], 1)
        put(along_taps, place, col_1, top[1:2], bottom[1:2], 2)
        place += rows
        put(along_taps, place, col_2, top[cols - 2 : cols - 1], bottom[cols - 2 : cols - 1], 0)
        put(along_taps, place, col_3, top[cols - 1 : cols], bottom[cols - 1 : cols], 1)
        put(along_taps, place, rgt, top_right, bottom_right, 2)

    for i in range(faces):
        face(i)
    w_rows = w_ref[...].reshape(9 * ch, ch)
    out = gelu(jnp.dot(across_taps[...], w_rows, preferred_element_type=F32) + bias)
    edge_rows[...] = out.astype(BF).reshape(edge_rows.shape)
    out = gelu(jnp.dot(along_taps[...], w_cols[...], preferred_element_type=F32) + bias)
    edge_cols[...] = out.reshape(edge_cols.shape)
    if coarse:
        order_cols, order_rows = parting(cols), parting(rows)

    def with_column(tile, place, value):
        spots = lax.broadcasted_iota(jnp.int32, tile.shape, 1)
        return jnp.where(spots == place, value[:, None, :], tile)

    def update(i, carry):
        new_top, new_bottom = edge_rows[i, 0].astype(F32), edge_rows[i, 1].astype(F32)
        end = (rows - 1) * EDGE
        for tile, side, place in ((left, 0, 0), (right, 1, EDGE - 1)):
            start = side * (cols - EDGE)
            value = y_ref[i, :, start : start + EDGE].astype(F32)
            value = with_column(value, place, edge_cols[i, side * rows : (side + 1) * rows])
            tile[...] = value.reshape(rows * EDGE, ch)
            tile[0:EDGE] = new_top[start : start + EDGE]
            tile[end : end + EDGE] = new_bottom[start : start + EDGE]
            if coarse:
                tiles[side, i] = value.astype(BF)
                tiles[side, i, 0] = edge_rows[i, 0, start : start + EDGE]
                tiles[side, i, rows - 1] = edge_rows[i, 1, start : start + EDGE]
            else:
                y_ref[i, :, start : start + EDGE] = value.astype(BF)
        if not coarse:
            y_ref[i, 0] = edge_rows[i, 0]
            y_ref[i, rows - 1] = edge_rows[i, 1]
        lines = (
            column(left, 0), column(left, 1), column(right, EDGE - 2), column(right, EDGE - 1)
        )
        if not coarse:
            put_strips(i, r, c, lines, new_top, new_bottom, *outs)
            return carry
        spot = lax.broadcasted_iota(jnp.int32, (cols, 1), 0)
        half = cols // 2
        for k, (own, near) in enumerate(((new_top, 1), (new_bottom, rows - 2))):
            first = edge_cols[i, near : near + 1]
            last = edge_cols[i, rows + near : rows + near + 1]
            other = y_ref[i, near].astype(F32)
            other = jnp.where(spot == 0, first, jnp.where(spot == cols - 1, last, other))
            both = (own, other) if k == 0 else (other, own)
            four = parted(order_cols, jnp.concatenate([v.astype(BF) for v in both], axis=1))
            four = jnp.concatenate([four[j] for j in (0, 2, 1, 3)], axis=1)
            c_taps[pl.ds((2 * i + k) * half, half)] = four
        for k, both in enumerate((lines[:2], lines[2:])):
            four = parted(order_rows, jnp.concatenate([v.astype(BF) for v in both], axis=1))
            place = 2 * faces * half + (2 * i + k) * (rows // 2)
            c_taps[pl.ds(place, rows // 2)] = jnp.concatenate(four, axis=1)
        return carry

    lax.fori_loop(0, faces, update, 0, unroll=True)
    if not coarse:
        return
    copies = tile_copies(y_out, tiles, sems, back=True)
    if cols > 2 * EDGE:
        between = pl.ds(EDGE, cols - 2 * EDGE)
        for k, row in enumerate((0, rows - 1)):
            copies.append(
                pltpu.make_async_copy(
                    edge_rows.at[:, k, between], y_out.at[:, row, between], sems.at[2 + k]
                )
            )
    for copy in copies:
        copy.start()
    half = cols // 2
    out = jnp.dot(
        c_taps[...], dw_ref[...].reshape(4 * ch, -1), preferred_element_type=F32
    ) + db_ref[...]
    across_cells = 2 * faces * half
    c_rows[...] = out[:across_cells].astype(BF).reshape(c_rows.shape)
    c_cols[...] = out[across_cells:].reshape(c_cols.shape)

    def cells(i):
        for side in range(2):
            start = side * (half - EDGE)
            value = c_ref[i, :, start : start + EDGE].astype(F32)
            value = with_column(value, side * (EDGE - 1), c_cols[i, side])
            c_tiles[side, i] = value.astype(BF)
            for k in range(2):
                c_tiles[side, i, k * (rows // 2 - 1)] = c_rows[i, k, start : start + EDGE]

    more = []
    for i in range(faces):
        cells(i)
        for side, start in enumerate((0, half - EDGE)):
            more.append(
                pltpu.make_async_copy(
                    c_tiles.at[side, i], c_out.at[i, :, pl.ds(start, EDGE), :], sems.at[8 + 2 * i + side]
                )
            )
            more[-1].start()
    first = len(more)
    if half > 2 * EDGE:
        between = pl.ds(EDGE, half - 2 * EDGE)
        for k, row in enumerate((0, rows // 2 - 1)):
            more.append(
                pltpu.make_async_copy(
                    c_rows.at[:, k, between], c_out.at[:, row, between], sems.at[6 + k]
                )
            )
    for copy in more[first:]:
        copy.start()
    for copy in copies + more:
        copy.wait()


def ring(
    neighbour_face, orientation, x, buffers, copied, lines, parts, weight, bias, seams, seconds, down
):
    y, *coarse = buffers
    faces, rows, cols, ch = x.shape
    groups = len(seams)
    smem = pl.BlockSpec(memory_space=pltpu.SMEM)
    hbm = pl.BlockSpec(memory_space=pltpu.HBM)
    vmem = pl.BlockSpec(memory_space=pltpu.VMEM)
    args = [neighbour_face, orientation, x, y, lines, *parts, weight, bias, *seams, *seconds]
    in_specs = [smem, smem] + [vmem] * (len(args) - 2)
    scratch = [
        pltpu.VMEM((2, faces, rows, EDGE, ch), BF),
        pltpu.VMEM((faces, 2, cols, ch), BF),
        pltpu.VMEM((faces, 2 * rows, ch), F32),
        pltpu.VMEM((groups, faces, 3 * rows, ch), BF),
        pltpu.VMEM((groups, seams[0].shape[0] - 3 * faces * rows, ch), BF),
        pltpu.VMEM((rows * EDGE, ch), F32),
        pltpu.VMEM((rows * EDGE, ch), F32),
        pltpu.VMEM((9 * ch, ch), BF),
        pltpu.VMEM((2 * faces * cols, 9 * ch), BF),
        pltpu.VMEM((2 * faces * rows, 9 * ch), BF),
    ]
    if down:
        co = down[0].shape[-1]
        args += [coarse[0], *down]
        in_specs += [vmem] * 3
        aliases = {len(args): 0, len(args) + 1: 1}
        args += [in_hbm(buffer) for buffer in copied]
        in_specs += [hbm] * 2
        out_shape = [pltpu.HBM(buffer.shape, BF) for buffer in copied]
        out_specs = [hbm] * 2
        scratch += [
            pltpu.VMEM((faces * (rows + cols), 4 * ch), BF),
            pltpu.VMEM((2, faces, rows // 2, EDGE, co), BF),
            pltpu.VMEM((faces, 2, cols // 2, co), BF),
            pltpu.VMEM((faces, 2, rows // 2, co), F32),
            pltpu.SemaphoreType.DMA((8 + 2 * faces,)),
        ]
    else:
        aliases = {3: 0}
        out_shape = [jax.ShapeDtypeStruct(y.shape, BF), *strip_shapes(faces, rows, cols, ch)]
        out_specs = [vmem] * 5
    return pl.pallas_call(
        functools.partial(ring_kernel, groups, bool(down)),
        in_specs=in_specs,
        out_specs=tuple(out_specs),
        out_shape=tuple(out_shape),
        scratch_shapes=scratch,
        input_output_aliases=aliases,
        cost_estimate=pl.CostEstimate(
            flops=faces * (rows + cols) * 36 * ch * ch, bytes_accessed=8 * 2**20, transcendentals=0
        ),
        compiler_params=pltpu.CompilerParams(vmem_limit_bytes=20 * 2**20),
        name="ring",
    )(*args)


def blocks(change_row, change_col):
    cols = lax.axis_size("col")
    return [
        (r * cols + c, (r ^ change_row) * cols + (c ^ change_col))
        for r in range(lax.axis_size("row"))
        for c in range(cols)
    ]


def swap(v, change_row, change_col):
    return lax.ppermute(v, ("row", "col"), blocks(change_row, change_col))


def level(neighbour_face, orientation, x, strips, weight, bias, down):
    u, v, turn, lines = strips
    groups = lax.axis_size("face")
    total = x.shape[0] * x.shape[1] // STEP
    early = max(total * (6 if down else 5) // 12, 1)
    late = early + max(total // 12, 1)
    piece = functools.partial(conv_piece, x, weight, bias)
    beside, across, diagonal = swap(u, 0, 1), swap(v, 3, 0), swap(v, 3, 1)
    pair, turned = swap(v, 1, 0), swap(turn, 1, 0)
    state = piece(0, early, None)
    (beside, across, diagonal, turned), state = lax.optimization_barrier(
        ((beside, across, diagonal, turned), state)
    )
    pair_beside, pair_across, pair_diagonal = (swap(a, 1, 0) for a in (beside, across, diagonal))
    state = piece(early, late - early, state)
    stores = (v, beside, pair, pair_beside, pair_across, pair_diagonal, across, diagonal)
    picked = select_strips(neighbour_face, orientation, stores, groups)
    picked, state = lax.optimization_barrier((picked, state))
    seams = list(picked)
    for k in sorted(range(1, groups), key=lambda k: -(k.bit_length())):
        pairs = [(g, g ^ k) for g in range(groups)]
        seams[k] = lax.ppermute(picked[k], "face", pairs)
    y = piece(late, total - late, state)[2]
    done, coarse = total - total // 4, ()
    if down:
        coarse = downsample(y, *down, 0, done, ())
    seams[1:], y, coarse = lax.optimization_barrier((seams[1:], y, coarse))
    seconds = [swap(seam, 1, 0) for seam in seams[1:]]
    if down:
        coarse = downsample(y, *down, done, total - done, coarse)
    buffers, copied = (y, *coarse[:1]), coarse[1:]
    parts = (beside, pair_beside, across, diagonal, turned)
    return ring(
        *(neighbour_face, orientation, x, buffers, copied, lines, parts, weight, bias),
        *(seams, seconds, down),
    )


def per_device(
    field, conv1_w, conv1_b, conv2_w, conv2_b, down_w, down_b, neighbour_face, orientation
):
    tables = (neighbour_face.T, orientation.T)
    hidden, *strips = level(*tables, field, strips_of(field), conv1_w, conv1_b[None], ())
    return level(*tables, hidden, strips, conv2_w, conv2_b[None], (down_w, down_b[None]))


def solution(mesh):
    groups = mesh.shape["face"]
    fast = mesh.shape["row"] == 4 and mesh.shape["col"] == 2 and groups & (groups - 1) == 0
    return jax.shard_map(
        per_device if fast else general_device,
        mesh=mesh,
        in_specs=(P("face", "row", "col", None), P(), P(), P(), P(), P(), P(), P(), P()),
        out_specs=(P("face", "row", "col", None), P("face", "row", "col", None)),
        check_vma=False,
    )
```

```python
import functools

import jax
import jax.numpy as jnp
import numpy as np
from jax import lax
from jax.experimental import pallas as pl
from jax.experimental.pallas import tpu as pltpu
from jax.sharding import PartitionSpec as P


FACES = 12
BF = jnp.bfloat16
F32 = jnp.float32
STEP = 16
EDGE = 8
EXTRA = 16

layout = ("NHWC", "HWIO", "NHWC")


def padded_2(block, sides, width):
    for axis, dim in sides:
        count = lax.axis_size(axis)
        forward = [(i, i + 1) for i in range(count - 1)]
        backward = [(target, source) for source, target in forward]
        low = lax.ppermute(
            lax.slice_in_dim(block, block.shape[dim] - width, None, axis=dim), axis, forward
        )
        high = lax.ppermute(lax.slice_in_dim(block, 0, width, axis=dim), axis, backward)
        block = jnp.concatenate([low, block, high], axis=dim)
    return block


def seam_parts(edges, neighbours, codes):
    seam_faces = neighbours[:, :4]
    seam_codes = codes[:, :4]
    seams = edges[seam_faces, seam_codes // 2]
    seams = jnp.where((seam_codes % 2 == 1)[:, :, None, None], seams[:, :, ::-1], seams)
    corner_values = jnp.stack(
        [edges[:, 0, 0], edges[:, 0, -1], edges[:, 2, -1], edges[:, 2, 0]], axis=1
    )
    corner_faces = neighbours[:, 4:]
    picked = corner_values[jnp.minimum(corner_faces, FACES - 1), codes[:, 4:]]
    picked = jnp.where((corner_faces < FACES)[:, :, None], picked, jnp.zeros_like(picked))
    return (seams, picked)


def convolve(padded, weight, bias):
    summed = lax.conv_general_dilated(
        padded,
        weight,
        (1, 1),
        "VALID",
        dimension_numbers=layout,
        preferred_element_type=jnp.float32,
    )
    return jax.nn.gelu(summed + bias, approximate=False).astype(jnp.bfloat16)


def general_layer(block, weight, bias, neighbour_face, orientation):
    face_count, row_size, col_size, channels = block.shape
    row_total = lax.axis_size("row")
    col_total = lax.axis_size("col")
    row_place = lax.axis_index("row")
    col_place = lax.axis_index("col")
    face_side = row_size * row_total
    padded = padded_2(block, (("row", 1), ("col", 2)), 1)
    top_live = row_place == 0
    bottom_live = row_place == row_total - 1
    left_live = col_place == 0
    right_live = col_place == col_total - 1
    empty_line = jnp.zeros((face_count, face_side, channels), jnp.float32)

    def place(strip, offset, live):
        scaled = strip.astype(jnp.float32) * live.astype(jnp.float32)
        return lax.dynamic_update_slice_in_dim(empty_line, scaled, offset, 1)

    lines = jnp.stack(
        [
            place(block[:, 0], col_place * col_size, top_live),
            place(block[:, :, -1], row_place * row_size, right_live),
            place(block[:, -1], col_place * col_size, bottom_live),
            place(block[:, :, 0], row_place * row_size, left_live),
        ],
        axis=1,
    )
    complete = lax.psum(lax.psum(lines.astype(jnp.bfloat16), "col"), "row").astype(jnp.float32)
    every_edge = lax.all_gather(complete.astype(jnp.bfloat16), "face", axis=0, tiled=True)
    first_face = lax.axis_index("face") * face_count
    own_faces = lax.dynamic_slice_in_dim(neighbour_face, first_face, face_count, 0)
    own_codes = lax.dynamic_slice_in_dim(orientation, first_face, face_count, 0)
    seams, corners = seam_parts(every_edge, own_faces, own_codes)
    upper = jnp.concatenate([corners[:, 0:1], seams[:, 0], corners[:, 1:2]], 1)
    lower = jnp.concatenate([corners[:, 3:4], seams[:, 2], corners[:, 2:3]], 1)
    leftward = jnp.concatenate([corners[:, 0:1], seams[:, 3], corners[:, 3:4]], 1)
    rightward = jnp.concatenate([corners[:, 1:2], seams[:, 1], corners[:, 2:3]], 1)
    upper_cut = lax.dynamic_slice_in_dim(upper, col_place * col_size, col_size + 2, 1)
    lower_cut = lax.dynamic_slice_in_dim(lower, col_place * col_size, col_size + 2, 1)
    left_cut = lax.dynamic_slice_in_dim(leftward, row_place * row_size, row_size + 2, 1)
    right_cut = lax.dynamic_slice_in_dim(rightward, row_place * row_size, row_size + 2, 1)
    padded = padded.at[:, 0].set(jnp.where(top_live, upper_cut, padded[:, 0]))
    padded = padded.at[:, -1].set(jnp.where(bottom_live, lower_cut, padded[:, -1]))
    padded = padded.at[:, :, 0].set(jnp.where(left_live, left_cut, padded[:, :, 0]))
    padded = padded.at[:, :, -1].set(jnp.where(right_live, right_cut, padded[:, :, -1]))
    return convolve(padded, weight, bias)


def general_device(
    field, conv1_w, conv1_b, conv2_w, conv2_b, down_w, down_b, neighbour_face, orientation
):
    hidden = general_layer(field, conv1_w, conv1_b, neighbour_face, orientation)
    skip = general_layer(hidden, conv2_w, conv2_b, neighbour_face, orientation)
    summed = lax.conv_general_dilated(
        skip, down_w, (2, 2), "VALID", dimension_numbers=layout, preferred_element_type=jnp.float32
    )
    coarse = (summed + down_b).astype(jnp.bfloat16)
    return (skip, coarse)


def gelu(v):
    return 0.5 * v * (1.0 + lax.erf(v * np.float32(np.sqrt(0.5))))


def shifted(v, before, after):
    n = v.shape[0]
    spot = lax.broadcasted_iota(jnp.int32, (n, 1), 0)
    low = jnp.where(spot == 0, before, pltpu.roll(v, 1, 0))
    high = jnp.where(spot == n - 1, after, pltpu.roll(v, n - 1, 0))
    return low.astype(BF), v.astype(BF), high.astype(BF)


def parting(n):
    to = lax.broadcasted_iota(jnp.int32, (n, n), 0)
    source = lax.broadcasted_iota(jnp.int32, (n, n), 1)
    half = n // 2
    return jnp.where(source == jnp.where(to < half, 2 * to, 2 * (to - half) + 1), 1.0, 0.0).astype(BF)


def parted(order, v):
    v = jnp.dot(order, v, preferred_element_type=F32).astype(BF)
    half, lanes = v.shape[0] // 2, v.shape[1] // 2
    return v[:half, :lanes], v[:half, lanes:], v[half:, :lanes], v[half:, lanes:]


def conv_kernel(first, count, build, x_ref, b_ref, *refs):
    *refs, taps_0, taps_1 = refs
    if build:
        w_ref, y_ref, w_low, w_high = refs
    else:
        w_low, w_high, _, y_ref = refs
    _, size, cols, ch = x_ref.shape
    steps = size // STEP
    pairs = STEP // 2
    zero_row = jnp.zeros((1, ch), F32)
    half = 3 * ch

    if build:
        zero = jnp.zeros((ch, ch), BF)
        for d in range(3):
            one = slice(d * ch, (d + 1) * ch)
            two = slice(half + d * ch, half + (d + 1) * ch)
            w_low[one, :ch] = w_ref[0, d]
            w_low[one, ch:] = zero
            w_low[two, :ch] = w_ref[1, d]
            w_low[two, ch:] = w_ref[0, d]
            w_high[one, :ch] = w_ref[2, d]
            w_high[one, ch:] = w_ref[1, d]
            w_high[two, :ch] = zero
            w_high[two, ch:] = w_ref[2, d]

    def at(t):
        return t // steps, lax.rem(t, steps)

    def fill(taps, t):
        face, step = at(t)
        base = step * STEP

        def put(v, pair, side):
            low, same, high = shifted(v.astype(F32), zero_row, zero_row)
            place = side * half
            taps[pair, :, place : place + ch] = low
            taps[pair, :, place + ch : place + 2 * ch] = same
            taps[pair, :, place + 2 * ch : place + 3 * ch] = high

        inside = (step > 0).astype(F32)
        put(x_ref[face, jnp.maximum(base - 1, 0)].astype(F32) * inside, 0, 0)
        for row in range(STEP):
            put(x_ref[face, base + row], (row + 1) // 2, (row + 1) % 2)
        inside = (step < steps - 1).astype(F32)
        put(x_ref[face, jnp.minimum(base + STEP, size - 1)].astype(F32) * inside, pairs, 1)

    def product(taps, t):
        face, step = at(t)
        base = step * STEP
        lower = taps[pl.ds(0, pairs)].reshape(pairs * cols, 2 * half)
        upper = taps[pl.ds(1, pairs)].reshape(pairs * cols, 2 * half)
        total = jnp.dot(lower, w_low[...], preferred_element_type=F32)
        total += jnp.dot(upper, w_high[...], preferred_element_type=F32)
        total = total.reshape(pairs, cols, 2 * ch)
        bias = b_ref[...]
        for side in range(2):
            out = gelu(total[:, :, side * ch : (side + 1) * ch] + bias[None]).astype(BF)
            for pair in range(pairs):
                y_ref[face, base + 2 * pair + side] = out[pair]
    last = first + count - 1
    fill(taps_0, first)

    def double(j, carry):
        t = first + 2 * j
        fill(taps_1, t + 1)
        product(taps_0, t)
        fill(taps_0, jnp.minimum(t + 2, last))
        product(taps_1, t + 1)
        return carry

    lax.fori_loop(0, count // 2, double, 0)
    if count % 2:
        product(taps_0, last)


def in_hbm(x):
    return pltpu.with_memory_space_constraint(x, pltpu.HBM)


def conv_piece(x, weight, bias, first, count, state):
    faces, rows, cols, ch = x.shape
    vmem = pl.BlockSpec(memory_space=pltpu.VMEM)
    build = state is None
    taps = (STEP // 2 + 1, cols, 6 * ch)
    arranged = jax.ShapeDtypeStruct((6 * ch, 2 * ch), BF)
    args = [x, bias, weight] if build else [x, bias, *state]
    out_shape = [jax.ShapeDtypeStruct(x.shape, BF)] + [arranged] * (2 if build else 0)
    pixels = count * STEP * cols
    out = pl.pallas_call(
        functools.partial(conv_kernel, first, count, build),
        in_specs=[vmem] * len(args),
        out_specs=tuple([vmem] * len(out_shape)),
        out_shape=tuple(out_shape),
        scratch_shapes=[pltpu.VMEM(taps, BF), pltpu.VMEM(taps, BF)],
        input_output_aliases={} if build else {4: 0},
        cost_estimate=pl.CostEstimate(
            flops=pixels * 24 * ch * ch, bytes_accessed=4 * pixels * ch, transcendentals=0
        ),
        compiler_params=pltpu.CompilerParams(vmem_limit_bytes=16 * 2**20),
        name="conv_piece",
    )(*args)
    return (out[1], out[2], out[0]) if build else (state[0], state[1], out[0])


def down_kernel(first, count, y_ref, w_ref, b_ref, *refs):
    c_ref, y_out, c_out, taps_0, taps_1, wide_0, wide_1, sems = refs[-8:]
    faces, rows, cols, ch = y_ref.shape
    steps, pairs = rows // STEP, STEP // 2
    last = first + count - 1

    def copies(t):
        face, step = t // steps, lax.rem(t, steps)
        some, cells = pl.ds(step * STEP, STEP), pl.ds(step * pairs, pairs)
        return (
            pltpu.make_async_copy(y_ref.at[face, some], y_out.at[face, some], sems.at[0]),
            pltpu.make_async_copy(c_ref.at[face, cells], c_out.at[face, cells], sems.at[1]),
        )

    def fill(taps, wide, t):
        face, step = t // steps, lax.rem(t, steps)
        for pair in range(pairs):
            row = step * STEP + 2 * pair
            for a in range(2):
                wide[2 * pair + a] = y_ref[face, row + a].astype(F32)
            four = [
                wide[2 * pair + a, pl.ds(d, cols // 2, stride=2), :].astype(BF)
                for a in range(2)
                for d in range(2)
            ]
            taps[pair] = jnp.concatenate(four, axis=1)

    def product(taps, t):
        face, step = t // steps, lax.rem(t, steps)
        out = jnp.dot(
            taps[...].reshape(pairs * cols // 2, 4 * ch),
            w_ref[...].reshape(4 * ch, -1),
            preferred_element_type=F32,
        )
        out = (out + b_ref[...]).astype(BF)
        c_ref[face, pl.ds(step * pairs, pairs)] = out.reshape(pairs, cols // 2, -1)
        copies(t)[1].start()

    def send(t, carry):
        copies(t)[0].start()
        return carry

    def wait(t, carry):
        for copy in copies(t):
            copy.wait()
        return carry

    lax.fori_loop(first, first + count, send, 0)
    fill(taps_0, wide_0, first)

    def double(j, carry):
        t = first + 2 * j
        fill(taps_1, wide_1, t + 1)
        product(taps_0, t)
        fill(taps_0, wide_0, jnp.minimum(t + 2, last))
        product(taps_1, t + 1)
        return carry

    lax.fori_loop(0, count // 2, double, 0, unroll=True)
    if count % 2:
        product(taps_0, last)
    lax.fori_loop(first, first + count, wait, 0)


def downsample(y, weight, bias, first, count, into):
    faces, rows, cols, ch = y.shape
    shape = (faces, rows // 2, cols // 2, weight.shape[-1])
    vmem = pl.BlockSpec(memory_space=pltpu.VMEM)
    hbm = pl.BlockSpec(memory_space=pltpu.HBM)
    taps, wide = (STEP // 2, cols // 2, 4 * ch), (STEP, cols, ch)
    args, in_specs = [y, weight, bias], [vmem] * 3
    if into:
        args += [into[0], in_hbm(into[1]), in_hbm(into[2])]
        in_specs += [vmem, hbm, hbm]
    pixels = count * STEP * cols
    return pl.pallas_call(
        functools.partial(down_kernel, first, count),
        in_specs=in_specs,
        out_specs=(vmem, hbm, hbm),
        out_shape=(jax.ShapeDtypeStruct(shape, BF), pltpu.HBM(y.shape, BF), pltpu.HBM(shape, BF)),
        scratch_shapes=[pltpu.VMEM(taps, BF)] * 2
        + [pltpu.VMEM(wide, F32)] * 2
        + [pltpu.SemaphoreType.DMA((2,))],
        input_output_aliases={3: 0, 4: 1, 5: 2} if into else {},
        cost_estimate=pl.CostEstimate(
            flops=pixels * 2 * ch * shape[-1], bytes_accessed=4 * pixels * ch, transcendentals=0
        ),
        compiler_params=pltpu.CompilerParams(vmem_limit_bytes=16 * 2**20),
        name="downsample",
    )(*args)


def column(tile, place):
    return tile[pl.ds(place, tile.shape[0] // EDGE, stride=EDGE), :]


def put_strips(i, r, c, lines, top, bottom, u_ref, v_ref, turn_ref, line_ref):
    left, left_in, right_in, right = lines
    size = left.shape[0]
    for place, value in enumerate(lines):
        line_ref[i, place] = value.astype(BF)
    side = jnp.where(c == 0, left, right).astype(BF)
    inner = jnp.where(c == 0, right, left).astype(BF)
    even = lax.rem(r, 2) == 0
    line = jnp.where(even, top, bottom).astype(BF)
    turn_ref[i] = jnp.where(even, bottom, top).astype(BF)
    for ref in (u_ref, v_ref):
        ref[i, 0] = side
        ref[i, 1] = line[:size]
        ref[i, 2] = line[size:]
    u_ref[i, 3] = inner


def strip_shapes(faces, rows, cols, ch):
    return (
        jax.ShapeDtypeStruct((faces, 4, rows, ch), BF),
        jax.ShapeDtypeStruct((faces, 3, rows, ch), BF),
        jax.ShapeDtypeStruct((faces, cols, ch), BF),
        jax.ShapeDtypeStruct((faces, 4, rows, ch), BF),
    )


def whole(shape):
    return pl.BlockSpec(shape, lambda *_: (0,) * len(shape))


def tile_copies(array, tiles, sems, back=False):
    cols = array.shape[2]
    out = []
    for side, start in enumerate((0, cols - EDGE)):
        far, near = array.at[:, :, pl.ds(start, EDGE), :], tiles.at[side]
        out.append(pltpu.make_async_copy(*((near, far) if back else (far, near)), sems.at[side]))
    return out


def strips_kernel(x_ref, u_ref, v_ref, turn_ref, line_ref, tiles, outer, left, right, sems):
    faces, rows, cols, ch = x_ref.shape
    r, c = lax.axis_index("row"), lax.axis_index("col")
    copies = []
    for i in range(faces):
        for k, start in enumerate((0, cols - EDGE)):
            far, near = x_ref.at[i, :, pl.ds(start, EDGE), :], tiles.at[k, i]
            copies.append(pltpu.make_async_copy(far, near, sems.at[i, k]))
        for k, row in enumerate((0, rows - 1)):
            far, near = x_ref.at[i, row], outer.at[k, i]
            copies.append(pltpu.make_async_copy(far, near, sems.at[i, 2 + k]))
    for copy in copies:
        copy.start()
    for i in range(faces):
        for copy in copies[4 * i : 4 * i + 4]:
            copy.wait()
        left[i] = tiles[0, i].astype(F32).reshape(rows * EDGE, ch)
        right[i] = tiles[1, i].astype(F32).reshape(rows * EDGE, ch)
        ends = [(left.at[i], 0), (left.at[i], 1), (right.at[i], EDGE - 2), (right.at[i], EDGE - 1)]
        lines = [column(*end) for end in ends]
        put_strips(
            i, r, c, lines, outer[0, i].astype(F32), outer[1, i].astype(F32),
            u_ref, v_ref, turn_ref, line_ref,
        )


def strips_of(x):
    faces, rows, cols, ch = x.shape
    shapes = strip_shapes(faces, rows, cols, ch)
    return pl.pallas_call(
        strips_kernel,
        in_specs=[pl.BlockSpec(memory_space=pltpu.HBM)],
        out_specs=(pl.BlockSpec(memory_space=pltpu.VMEM),) * 4,
        out_shape=shapes,
        scratch_shapes=[
            pltpu.VMEM((2, faces, rows, EDGE, ch), BF),
            pltpu.VMEM((2, faces, cols, ch), BF),
            pltpu.VMEM((faces, rows * EDGE, ch), F32),
            pltpu.VMEM((faces, rows * EDGE, ch), F32),
            pltpu.SemaphoreType.DMA((faces, 4)),
        ],
        cost_estimate=pl.CostEstimate(flops=0, bytes_accessed=4 * 2**20, transcendentals=0),
        compiler_params=pltpu.CompilerParams(vmem_limit_bytes=10 * 2**20),
        name="strips_of",
    )(in_hbm(x))


def plan_kernel(near_ref, code_ref, plan_ref):
    faces = near_ref.shape[1] // lax.axis_size("face")
    me, r, c = lax.axis_index("face"), lax.axis_index("row"), lax.axis_index("col")

    def slot(row, col):
        return ((r ^ row) << 1) | (c ^ col)

    def quarter(edge, q):
        upright = lax.rem(edge, 2) == 1
        row = jnp.where(upright, q, jnp.where(edge == 0, 0, 3))
        col = jnp.where(upright, jnp.where(edge == 3, 0, 1), q >> 1)
        return slot(row, col), jnp.where(upright, 0, 1 + (q & 1))

    def one(at, carry):
        k, i = at // faces, lax.rem(at, faces)
        f = (me ^ k) * faces + i
        edge = 3 - 2 * c
        code = code_ref[edge, f]
        far, flip = code >> 1, code & 1
        n = lax.rem(near_ref[edge, f], faces)
        entries = [n, *quarter(far, jnp.where(flip == 1, 3 - r, r))]
        corner = jnp.where(r < 2, c, 3 - c)
        tip = code_ref[4 + corner, f]
        tip_row = jnp.where(tip < 2, 0, 3)
        tip_col = jnp.where((tip == 1) | (tip == 2), 1, 0)
        tip_n = lax.rem(near_ref[4 + corner, f], faces)
        tip_entries = (tip_n, slot(tip_row, tip_col), 0, tip_row // 3)
        pixels = []
        for limit, step in ((0, -1), (3, 1)):
            q = jnp.clip(jnp.where(flip == 1, 3 - r - step, r + step), 0, 3)
            there = (n, *quarter(far, q), flip ^ (1 if step < 0 else 0))
            pixels += [jnp.where(r == limit, t, u) for t, u in zip(tip_entries, there)]
        edge = jnp.where(r < 2, 0, 2)
        code = code_ref[edge, f]
        far, flip = code >> 1, code & 1
        n = lax.rem(near_ref[edge, f], faces)
        part = c ^ flip
        for h in range(2):
            entries += [n, *quarter(far, 2 * part + h)]
        pixels += [n, *quarter(far, jnp.where(part == 0, 2, 1)), part]
        for j, entry in enumerate(entries + pixels):
            plan_ref[at, j] = jnp.asarray(entry, jnp.int32)
        return carry

    lax.fori_loop(0, plan_ref.shape[0], one, 0)


def plan_of(neighbour_face, orientation):
    smem = pl.BlockSpec(memory_space=pltpu.SMEM)
    return pl.pallas_call(
        plan_kernel,
        in_specs=[smem, smem],
        out_specs=smem,
        out_shape=jax.ShapeDtypeStruct((neighbour_face.shape[1], 21), jnp.int32),
        compiler_params=pltpu.CompilerParams(vmem_limit_bytes=2 * 2**20),
        name="plan_of",
    )(neighbour_face, orientation)


def select_kernel(plan_ref, *refs):
    stores, outs, held = refs[:8], refs[8:-1], refs[-1]
    faces, _, size, ch = held.shape[1:]
    r = lax.axis_index("row")
    for k, store in enumerate(stores):
        for i in range(faces):
            held[k, i] = store[i, 0:3]

    for k, out in enumerate(outs):
        parts = out.shape[0] // (faces * size)
        single = jnp.zeros((out.shape[0] - faces * parts * size, ch), F32)
        spot = lax.broadcasted_iota(jnp.int32, (single.shape[0], 1), 0)
        for i in range(faces):
            at, start = k * faces + i, i * parts * size

            def entry(j, at=at):
                return plan_ref[at, j]

            out[start : start + size] = held[entry(1), entry(0), entry(2)]
            for h in range(parts - 1):
                own = 3 + 3 * (jnp.where((r == 0) | (r == 3), 0, 1) if k else h)
                block = held[entry(own + 1), entry(own), entry(own + 2)]
                out[start + (1 + h) * size : start + (2 + h) * size] = block
            for j in range(3):
                first = 9 + 4 * j
                where, n, block = entry(first + 1), entry(first), entry(first + 2)
                head = held[where, n, block, 0:EXTRA].astype(F32)
                tail = held[where, n, block, size - EXTRA : size].astype(F32)
                pixel = jnp.where(entry(first + 3) == 1, tail[EXTRA - 1 : EXTRA], head[0:1])
                single = jnp.where(spot == 3 * i + j, pixel, single)
        out[faces * parts * size :] = single.astype(BF)


def select_strips(plan, stores, groups):
    faces, _, size, ch = stores[0].shape
    single = -(-3 * faces // EXTRA) * EXTRA
    shapes = [
        jax.ShapeDtypeStruct(((2 if k else 3) * faces * size + single, ch), BF)
        for k in range(groups)
    ]
    return pl.pallas_call(
        select_kernel,
        in_specs=[pl.BlockSpec(memory_space=pltpu.SMEM)]
        + [pl.BlockSpec(memory_space=pltpu.VMEM)] * 8,
        out_specs=(pl.BlockSpec(memory_space=pltpu.VMEM),) * groups,
        out_shape=tuple(shapes),
        scratch_shapes=[pltpu.VMEM((8, faces, 3, size, ch), BF)],
        cost_estimate=pl.CostEstimate(flops=0, bytes_accessed=4 * 2**20, transcendentals=0),
        compiler_params=pltpu.CompilerParams(vmem_limit_bytes=10 * 2**20),
        name="select_strips",
    )(plan, *stores)


def ring_kernel(groups, coarse, near_ref, code_ref, x_ref, y_in, line_in, beside, diagonal, across,
                far_diagonal, turned, w_ref, b_ref, *refs):
    seams, seconds, refs = refs[:groups], refs[groups : 2 * groups - 1], refs[2 * groups - 1 :]
    if coarse:
        c_ref, dw_ref, db_ref, _, _, y_out, c_out = refs[:7]
        y_ref = y_in
        scratch = refs[7:]
        *scratch, c_taps, c_tiles, c_rows, c_cols, sems = scratch
    else:
        y_ref, outs, scratch = refs[0], refs[1:5], refs[5:]
    tiles, edge_rows, edge_cols, held, held_single, left, right, w_cols, across_taps, along_taps = scratch
    faces, rows, cols, ch = x_ref.shape
    me, r, c = lax.axis_index("face"), lax.axis_index("row"), lax.axis_index("col")
    for k in range(groups):
        seam, parts = seams[k], 2 if k else 3
        for i in range(faces):
            start = i * parts * rows
            held[k, i, : 2 * rows] = seam[start : start + 2 * rows]
            half = seconds[k - 1] if k else seam
            start += (parts - 1) * rows
            held[k, i, 2 * rows :] = half[start : start + rows]
        held_single[k] = seam[faces * parts * rows :]

    def oriented(v, flip):
        n = v.shape[0]
        to = lax.broadcasted_iota(jnp.int32, (n, n), 0)
        source = lax.broadcasted_iota(jnp.int32, (n, n), 1)
        order = jnp.where(source == jnp.where(flip == 1, n - 1 - to, to), 1.0, 0.0).astype(BF)
        return jnp.dot(order, v, preferred_element_type=F32)

    even = lax.rem(r, 2) == 0
    outer = (r == 0) | (r == 3)
    for d in range(3):
        for a in range(3):
            w_cols[(3 * d + a) * ch : (3 * d + a + 1) * ch] = w_ref[a, d]
    bias = b_ref[...]

    def holder(n):
        return jnp.minimum(n, FACES - 1) // faces ^ me

    def put(taps, place, v, before, after, third):
        for k, part in enumerate(shifted(v, before, after)):
            start = (3 * third + k) * ch
            taps[pl.ds(place, v.shape[0]), start : start + ch] = part

    def face(i):
        f = me * faces + i
        edge = 3 - 2 * c
        n = near_ref[edge, f]
        corner = jnp.where(r < 2, c, 3 - c)
        tip_n = near_ref[4 + corner, f]
        seam_side = oriented(held[holder(n), i, 0:rows], code_ref[edge, f] & 1)
        n_before = jnp.where(r == 0, tip_n, n)
        n_after = jnp.where(r == 3, tip_n, n)
        before = held_single[holder(n_before)].astype(F32)[3 * i : 3 * i + 1]
        after = held_single[holder(n_after)].astype(F32)[3 * i + 1 : 3 * i + 2]
        before = jnp.where(n_before < FACES, before, 0.0)
        after = jnp.where(n_after < FACES, after, 0.0)
        edge = jnp.where(r < 2, 0, 2)
        n = near_ref[edge, f]
        seam_line = oriented(held[holder(n), i, rows : 3 * rows], code_ref[edge, f] & 1)
        middle = held_single[holder(n)].astype(F32)[3 * i + 2 : 3 * i + 3]

        inner = beside[i, 3].astype(F32)
        block_line = jnp.concatenate([across[i, 1], across[i, 2]], axis=0).astype(F32)
        outward = jnp.where(outer, seam_line, block_line)
        inward = turned[i].astype(F32)
        top = jnp.where(even, outward, inward)
        bottom = jnp.where(even, inward, outward)
        lft = jnp.where(c == 0, seam_side, inner)
        rgt = jnp.where(c == 0, inner, seam_side)
        pair_inner = diagonal[i, 3].astype(F32)
        inward_corner = jnp.where(even, pair_inner[0:1], pair_inner[rows - 1 : rows])
        far_first = far_diagonal[i, 1].astype(F32)[0:1]
        far_last = far_diagonal[i, 2].astype(F32)[rows - 1 : rows]
        outward_corner = jnp.where(outer, middle, jnp.where(c == 0, far_first, far_last))
        inner_top = jnp.where(even, outward_corner, inward_corner)
        inner_bottom = jnp.where(even, inward_corner, outward_corner)
        top_left = jnp.where(c == 0, before, inner_top)
        top_right = jnp.where(c == 0, inner_top, before)
        bottom_left = jnp.where(c == 0, after, inner_bottom)
        bottom_right = jnp.where(c == 0, inner_bottom, after)

        row_0, row_1, row_2, row_3 = (
            x_ref[i, k].astype(F32) for k in (0, 1, rows - 2, rows - 1)
        )
        place = 2 * i * cols
        put(across_taps, place, top, top_left, top_right, 0)
        put(across_taps, place, row_0, lft[0:1], rgt[0:1], 1)
        put(across_taps, place, row_1, lft[1:2], rgt[1:2], 2)
        place += cols
        put(across_taps, place, row_2, lft[rows - 2 : rows - 1], rgt[rows - 2 : rows - 1], 0)
        put(across_taps, place, row_3, lft[rows - 1 : rows], rgt[rows - 1 : rows], 1)
        put(across_taps, place, bottom, bottom_left, bottom_right, 2)
        col_0, col_1, col_2, col_3 = (line_in[i, k].astype(F32) for k in range(4))
        place = 2 * i * rows
        put(along_taps, place, lft, top_left, bottom_left, 0)
        put(along_taps, place, col_0, top[0:1], bottom[0:1], 1)
        put(along_taps, place, col_1, top[1:2], bottom[1:2], 2)
        place += rows
        put(along_taps, place, col_2, top[cols - 2 : cols - 1], bottom[cols - 2 : cols - 1], 0)
        put(along_taps, place, col_3, top[cols - 1 : cols], bottom[cols - 1 : cols], 1)
        put(along_taps, place, rgt, top_right, bottom_right, 2)

    for i in range(faces):
        face(i)
    w_rows = w_ref[...].reshape(9 * ch, ch)
    out = gelu(jnp.dot(across_taps[...], w_rows, preferred_element_type=F32) + bias)
    edge_rows[...] = out.astype(BF).reshape(edge_rows.shape)
    out = gelu(jnp.dot(along_taps[...], w_cols[...], preferred_element_type=F32) + bias)
    edge_cols[...] = out.reshape(edge_cols.shape)
    if coarse:
        order_cols, order_rows = parting(cols), parting(rows)

    def with_column(tile, place, value):
        spots = lax.broadcasted_iota(jnp.int32, tile.shape, 1)
        return jnp.where(spots == place, value[:, None, :], tile)

    def update(i, carry):
        new_top, new_bottom = edge_rows[i, 0].astype(F32), edge_rows[i, 1].astype(F32)
        end = (rows - 1) * EDGE
        for tile, side, place in ((left, 0, 0), (right, 1, EDGE - 1)):
            start = side * (cols - EDGE)
            value = y_ref[i, :, start : start + EDGE].astype(F32)
            value = with_column(value, place, edge_cols[i, side * rows : (side + 1) * rows])
            tile[...] = value.reshape(rows * EDGE, ch)
            tile[0:EDGE] = new_top[start : start + EDGE]
            tile[end : end + EDGE] = new_bottom[start : start + EDGE]
            if coarse:
                tiles[side, i] = value.astype(BF)
                tiles[side, i, 0] = edge_rows[i, 0, start : start + EDGE]
                tiles[side, i, rows - 1] = edge_rows[i, 1, start : start + EDGE]
            else:
                y_ref[i, :, start : start + EDGE] = value.astype(BF)
        if not coarse:
            y_ref[i, 0] = edge_rows[i, 0]
            y_ref[i, rows - 1] = edge_rows[i, 1]
        lines = (
            column(left, 0), column(left, 1), column(right, EDGE - 2), column(right, EDGE - 1)
        )
        if not coarse:
            put_strips(i, r, c, lines, new_top, new_bottom, *outs)
            return carry
        spot = lax.broadcasted_iota(jnp.int32, (cols, 1), 0)
        half = cols // 2
        for k, (own, near) in enumerate(((new_top, 1), (new_bottom, rows - 2))):
            first = edge_cols[i, near : near + 1]
            last = edge_cols[i, rows + near : rows + near + 1]
            other = y_ref[i, near].astype(F32)
            other = jnp.where(spot == 0, first, jnp.where(spot == cols - 1, last, other))
            both = (own, other) if k == 0 else (other, own)
            four = parted(order_cols, jnp.concatenate([v.astype(BF) for v in both], axis=1))
            four = jnp.concatenate([four[j] for j in (0, 2, 1, 3)], axis=1)
            c_taps[pl.ds((2 * i + k) * half, half)] = four
        for k, both in enumerate((lines[:2], lines[2:])):
            four = parted(order_rows, jnp.concatenate([v.astype(BF) for v in both], axis=1))
            place = 2 * faces * half + (2 * i + k) * (rows // 2)
            c_taps[pl.ds(place, rows // 2)] = jnp.concatenate(four, axis=1)
        return carry

    lax.fori_loop(0, faces, update, 0, unroll=True)
    if not coarse:
        return
    copies = tile_copies(y_out, tiles, sems, back=True)
    if cols > 2 * EDGE:
        between = pl.ds(EDGE, cols - 2 * EDGE)
        for k, row in enumerate((0, rows - 1)):
            copies.append(
                pltpu.make_async_copy(
                    edge_rows.at[:, k, between], y_out.at[:, row, between], sems.at[2 + k]
                )
            )
    for copy in copies:
        copy.start()
    half = cols // 2
    out = jnp.dot(
        c_taps[...], dw_ref[...].reshape(4 * ch, -1), preferred_element_type=F32
    ) + db_ref[...]
    across_cells = 2 * faces * half
    c_rows[...] = out[:across_cells].astype(BF).reshape(c_rows.shape)
    c_cols[...] = out[across_cells:].reshape(c_cols.shape)

    def cells(i):
        for side in range(2):
            start = side * (half - EDGE)
            value = c_ref[i, :, start : start + EDGE].astype(F32)
            value = with_column(value, side * (EDGE - 1), c_cols[i, side])
            c_tiles[side, i] = value.astype(BF)
            for k in range(2):
                c_tiles[side, i, k * (rows // 2 - 1)] = c_rows[i, k, start : start + EDGE]

    more = []
    for i in range(faces):
        cells(i)
        for side, start in enumerate((0, half - EDGE)):
            more.append(
                pltpu.make_async_copy(
                    c_tiles.at[side, i], c_out.at[i, :, pl.ds(start, EDGE), :], sems.at[8 + 2 * i + side]
                )
            )
            more[-1].start()
    first = len(more)
    if half > 2 * EDGE:
        between = pl.ds(EDGE, half - 2 * EDGE)
        for k, row in enumerate((0, rows // 2 - 1)):
            more.append(
                pltpu.make_async_copy(
                    c_rows.at[:, k, between], c_out.at[:, row, between], sems.at[6 + k]
                )
            )
    for copy in more[first:]:
        copy.start()
    for copy in copies + more:
        copy.wait()


def ring(
    neighbour_face, orientation, x, buffers, copied, lines, parts, weight, bias, seams, seconds, down
):
    y, *coarse = buffers
    faces, rows, cols, ch = x.shape
    groups = len(seams)
    smem = pl.BlockSpec(memory_space=pltpu.SMEM)
    hbm = pl.BlockSpec(memory_space=pltpu.HBM)
    vmem = pl.BlockSpec(memory_space=pltpu.VMEM)
    args = [neighbour_face, orientation, x, y, lines, *parts, weight, bias, *seams, *seconds]
    in_specs = [smem, smem] + [vmem] * (len(args) - 2)
    scratch = [
        pltpu.VMEM((2, faces, rows, EDGE, ch), BF),
        pltpu.VMEM((faces, 2, cols, ch), BF),
        pltpu.VMEM((faces, 2 * rows, ch), F32),
        pltpu.VMEM((groups, faces, 3 * rows, ch), BF),
        pltpu.VMEM((groups, seams[0].shape[0] - 3 * faces * rows, ch), BF),
        pltpu.VMEM((rows * EDGE, ch), F32),
        pltpu.VMEM((rows * EDGE, ch), F32),
        pltpu.VMEM((9 * ch, ch), BF),
        pltpu.VMEM((2 * faces * cols, 9 * ch), BF),
        pltpu.VMEM((2 * faces * rows, 9 * ch), BF),
    ]
    if down:
        co = down[0].shape[-1]
        args += [coarse[0], *down]
        in_specs += [vmem] * 3
        aliases = {len(args): 0, len(args) + 1: 1}
        args += [in_hbm(buffer) for buffer in copied]
        in_specs += [hbm] * 2
        out_shape = [pltpu.HBM(buffer.shape, BF) for buffer in copied]
        out_specs = [hbm] * 2
        scratch += [
            pltpu.VMEM((faces * (rows + cols), 4 * ch), BF),
            pltpu.VMEM((2, faces, rows // 2, EDGE, co), BF),
            pltpu.VMEM((faces, 2, cols // 2, co), BF),
            pltpu.VMEM((faces, 2, rows // 2, co), F32),
            pltpu.SemaphoreType.DMA((8 + 2 * faces,)),
        ]
    else:
        aliases = {3: 0}
        out_shape = [jax.ShapeDtypeStruct(y.shape, BF), *strip_shapes(faces, rows, cols, ch)]
        out_specs = [vmem] * 5
    return pl.pallas_call(
        functools.partial(ring_kernel, groups, bool(down)),
        in_specs=in_specs,
        out_specs=tuple(out_specs),
        out_shape=tuple(out_shape),
        scratch_shapes=scratch,
        input_output_aliases=aliases,
        cost_estimate=pl.CostEstimate(
            flops=faces * (rows + cols) * 36 * ch * ch, bytes_accessed=8 * 2**20, transcendentals=0
        ),
        compiler_params=pltpu.CompilerParams(vmem_limit_bytes=20 * 2**20),
        name="ring",
    )(*args)


def blocks(change_row, change_col):
    cols = lax.axis_size("col")
    return [
        (r * cols + c, (r ^ change_row) * cols + (c ^ change_col))
        for r in range(lax.axis_size("row"))
        for c in range(cols)
    ]


def swap(v, change_row, change_col):
    return lax.ppermute(v, ("row", "col"), blocks(change_row, change_col))


def level(neighbour_face, orientation, plan, x, strips, weight, bias, down):
    u, v, turn, lines = strips
    groups = lax.axis_size("face")
    total = x.shape[0] * x.shape[1] // STEP
    early = max(total * (6 if down else 5) // 12, 1)
    late = early + max(total // 12, 1)
    piece = functools.partial(conv_piece, x, weight, bias)
    beside, across, diagonal = swap(u, 0, 1), swap(v, 3, 0), swap(v, 3, 1)
    pair, turned = swap(v, 1, 0), swap(turn, 1, 0)
    state = piece(0, early, None)
    if plan is None:
        *tables, state = lax.optimization_barrier((neighbour_face, orientation, state))
        plan = plan_of(*tables)
    (beside, across, diagonal, turned), state, plan = lax.optimization_barrier(
        ((beside, across, diagonal, turned), state, plan)
    )
    pair_beside, pair_across, pair_diagonal = (swap(a, 1, 0) for a in (beside, across, diagonal))
    state = piece(early, late - early, state)
    stores = (v, beside, pair, pair_beside, pair_across, pair_diagonal, across, diagonal)
    picked = select_strips(plan, stores, groups)
    picked, state = lax.optimization_barrier((picked, state))
    seams = list(picked)
    for k in sorted(range(1, groups), key=lambda k: -(k.bit_length())):
        pairs = [(g, g ^ k) for g in range(groups)]
        seams[k] = lax.ppermute(picked[k], "face", pairs)
    y = piece(late, total - late, state)[2]
    done, coarse = total - total // 4, ()
    if down:
        coarse = downsample(y, *down, 0, done, ())
    seams[1:], y, coarse = lax.optimization_barrier((seams[1:], y, coarse))
    seconds = [swap(seam, 1, 0) for seam in seams[1:]]
    if down:
        coarse = downsample(y, *down, done, total - done, coarse)
    buffers, copied = (y, *coarse[:1]), coarse[1:]
    parts = (beside, pair_beside, across, diagonal, turned)
    out = ring(
        *(neighbour_face, orientation, x, buffers, copied, lines, parts, weight, bias),
        *(seams, seconds, down),
    )
    return plan, out


def per_device(
    field, conv1_w, conv1_b, conv2_w, conv2_b, down_w, down_b, neighbour_face, orientation
):
    tables = (neighbour_face.T, orientation.T)
    plan, (hidden, *strips) = level(
        *tables, None, field, strips_of(field), conv1_w, conv1_b[None], ()
    )
    _, out = level(*tables, plan, hidden, strips, conv2_w, conv2_b[None], (down_w, down_b[None]))
    return tuple(out)


def solution(mesh):
    groups = mesh.shape["face"]
    fast = mesh.shape["row"] == 4 and mesh.shape["col"] == 2 and groups & (groups - 1) == 0
    return jax.shard_map(
        per_device if fast else general_device,
        mesh=mesh,
        in_specs=(P("face", "row", "col", None), P(), P(), P(), P(), P(), P(), P(), P()),
        out_specs=(P("face", "row", "col", None), P("face", "row", "col", None)),
        check_vma=False,
    )
```

```python
import functools

import jax
import jax.numpy as jnp
import numpy as np
from jax import lax
from jax.experimental import pallas as pl
from jax.experimental.pallas import tpu as pltpu
from jax.sharding import PartitionSpec as P


FACES = 12
BF = jnp.bfloat16
F32 = jnp.float32
STEP = 16
EDGE = 8
EXTRA = 16

layout = ("NHWC", "HWIO", "NHWC")


def padded_2(block, sides, width):
    for axis, dim in sides:
        count = lax.axis_size(axis)
        forward = [(i, i + 1) for i in range(count - 1)]
        backward = [(target, source) for source, target in forward]
        low = lax.ppermute(
            lax.slice_in_dim(block, block.shape[dim] - width, None, axis=dim), axis, forward
        )
        high = lax.ppermute(lax.slice_in_dim(block, 0, width, axis=dim), axis, backward)
        block = jnp.concatenate([low, block, high], axis=dim)
    return block


def seam_parts(edges, neighbours, codes):
    seam_faces = neighbours[:, :4]
    seam_codes = codes[:, :4]
    seams = edges[seam_faces, seam_codes // 2]
    seams = jnp.where((seam_codes % 2 == 1)[:, :, None, None], seams[:, :, ::-1], seams)
    corner_values = jnp.stack(
        [edges[:, 0, 0], edges[:, 0, -1], edges[:, 2, -1], edges[:, 2, 0]], axis=1
    )
    corner_faces = neighbours[:, 4:]
    picked = corner_values[jnp.minimum(corner_faces, FACES - 1), codes[:, 4:]]
    picked = jnp.where((corner_faces < FACES)[:, :, None], picked, jnp.zeros_like(picked))
    return (seams, picked)


def convolve(padded, weight, bias):
    summed = lax.conv_general_dilated(
        padded,
        weight,
        (1, 1),
        "VALID",
        dimension_numbers=layout,
        preferred_element_type=jnp.float32,
    )
    return jax.nn.gelu(summed + bias, approximate=False).astype(jnp.bfloat16)


def general_layer(block, weight, bias, neighbour_face, orientation):
    face_count, row_size, col_size, channels = block.shape
    row_total = lax.axis_size("row")
    col_total = lax.axis_size("col")
    row_place = lax.axis_index("row")
    col_place = lax.axis_index("col")
    face_side = row_size * row_total
    padded = padded_2(block, (("row", 1), ("col", 2)), 1)
    top_live = row_place == 0
    bottom_live = row_place == row_total - 1
    left_live = col_place == 0
    right_live = col_place == col_total - 1
    empty_line = jnp.zeros((face_count, face_side, channels), jnp.float32)

    def place(strip, offset, live):
        scaled = strip.astype(jnp.float32) * live.astype(jnp.float32)
        return lax.dynamic_update_slice_in_dim(empty_line, scaled, offset, 1)

    lines = jnp.stack(
        [
            place(block[:, 0], col_place * col_size, top_live),
            place(block[:, :, -1], row_place * row_size, right_live),
            place(block[:, -1], col_place * col_size, bottom_live),
            place(block[:, :, 0], row_place * row_size, left_live),
        ],
        axis=1,
    )
    complete = lax.psum(lax.psum(lines.astype(jnp.bfloat16), "col"), "row").astype(jnp.float32)
    every_edge = lax.all_gather(complete.astype(jnp.bfloat16), "face", axis=0, tiled=True)
    first_face = lax.axis_index("face") * face_count
    own_faces = lax.dynamic_slice_in_dim(neighbour_face, first_face, face_count, 0)
    own_codes = lax.dynamic_slice_in_dim(orientation, first_face, face_count, 0)
    seams, corners = seam_parts(every_edge, own_faces, own_codes)
    upper = jnp.concatenate([corners[:, 0:1], seams[:, 0], corners[:, 1:2]], 1)
    lower = jnp.concatenate([corners[:, 3:4], seams[:, 2], corners[:, 2:3]], 1)
    leftward = jnp.concatenate([corners[:, 0:1], seams[:, 3], corners[:, 3:4]], 1)
    rightward = jnp.concatenate([corners[:, 1:2], seams[:, 1], corners[:, 2:3]], 1)
    upper_cut = lax.dynamic_slice_in_dim(upper, col_place * col_size, col_size + 2, 1)
    lower_cut = lax.dynamic_slice_in_dim(lower, col_place * col_size, col_size + 2, 1)
    left_cut = lax.dynamic_slice_in_dim(leftward, row_place * row_size, row_size + 2, 1)
    right_cut = lax.dynamic_slice_in_dim(rightward, row_place * row_size, row_size + 2, 1)
    padded = padded.at[:, 0].set(jnp.where(top_live, upper_cut, padded[:, 0]))
    padded = padded.at[:, -1].set(jnp.where(bottom_live, lower_cut, padded[:, -1]))
    padded = padded.at[:, :, 0].set(jnp.where(left_live, left_cut, padded[:, :, 0]))
    padded = padded.at[:, :, -1].set(jnp.where(right_live, right_cut, padded[:, :, -1]))
    return convolve(padded, weight, bias)


def general_device(
    field, conv1_w, conv1_b, conv2_w, conv2_b, down_w, down_b, neighbour_face, orientation
):
    hidden = general_layer(field, conv1_w, conv1_b, neighbour_face, orientation)
    skip = general_layer(hidden, conv2_w, conv2_b, neighbour_face, orientation)
    summed = lax.conv_general_dilated(
        skip, down_w, (2, 2), "VALID", dimension_numbers=layout, preferred_element_type=jnp.float32
    )
    coarse = (summed + down_b).astype(jnp.bfloat16)
    return (skip, coarse)


def gelu(v):
    return 0.5 * v * (1.0 + lax.erf(v * np.float32(np.sqrt(0.5))))


def shifted(v, before, after):
    n = v.shape[0]
    spot = lax.broadcasted_iota(jnp.int32, (n, 1), 0)
    low = jnp.where(spot == 0, before, pltpu.roll(v, 1, 0))
    high = jnp.where(spot == n - 1, after, pltpu.roll(v, n - 1, 0))
    return low.astype(BF), v.astype(BF), high.astype(BF)


def parting(n):
    to = lax.broadcasted_iota(jnp.int32, (n, n), 0)
    source = lax.broadcasted_iota(jnp.int32, (n, n), 1)
    half = n // 2
    return jnp.where(source == jnp.where(to < half, 2 * to, 2 * (to - half) + 1), 1.0, 0.0).astype(BF)


def parted(order, v):
    v = jnp.dot(order, v, preferred_element_type=F32).astype(BF)
    half, lanes = v.shape[0] // 2, v.shape[1] // 2
    return v[:half, :lanes], v[:half, lanes:], v[half:, :lanes], v[half:, lanes:]


def conv_kernel(first, count, build, x_ref, b_ref, *refs):
    *refs, taps_0, taps_1 = refs
    if build:
        w_ref, y_ref, w_low, w_high = refs
    else:
        w_low, w_high, _, y_ref = refs
    _, size, cols, ch = x_ref.shape
    steps = size // STEP
    pairs = STEP // 2
    zero_row = jnp.zeros((1, ch), F32)
    half = 3 * ch

    if build:
        zero = jnp.zeros((ch, ch), BF)
        for d in range(3):
            one = slice(d * ch, (d + 1) * ch)
            two = slice(half + d * ch, half + (d + 1) * ch)
            w_low[one, :ch] = w_ref[0, d]
            w_low[one, ch:] = zero
            w_low[two, :ch] = w_ref[1, d]
            w_low[two, ch:] = w_ref[0, d]
            w_high[one, :ch] = w_ref[2, d]
            w_high[one, ch:] = w_ref[1, d]
            w_high[two, :ch] = zero
            w_high[two, ch:] = w_ref[2, d]

    def at(t):
        return t // steps, lax.rem(t, steps)

    def fill(taps, t):
        face, step = at(t)
        base = step * STEP

        def put(v, pair, side):
            low, same, high = shifted(v.astype(F32), zero_row, zero_row)
            place = side * half
            taps[pair, :, place : place + ch] = low
            taps[pair, :, place + ch : place + 2 * ch] = same
            taps[pair, :, place + 2 * ch : place + 3 * ch] = high

        inside = (step > 0).astype(F32)
        put(x_ref[face, jnp.maximum(base - 1, 0)].astype(F32) * inside, 0, 0)
        for row in range(STEP):
            put(x_ref[face, base + row], (row + 1) // 2, (row + 1) % 2)
        inside = (step < steps - 1).astype(F32)
        put(x_ref[face, jnp.minimum(base + STEP, size - 1)].astype(F32) * inside, pairs, 1)

    def product(taps, t):
        face, step = at(t)
        base = step * STEP
        lower = taps[pl.ds(0, pairs)].reshape(pairs * cols, 2 * half)
        upper = taps[pl.ds(1, pairs)].reshape(pairs * cols, 2 * half)
        total = jnp.dot(lower, w_low[...], preferred_element_type=F32)
        total += jnp.dot(upper, w_high[...], preferred_element_type=F32)
        total = total.reshape(pairs, cols, 2 * ch)
        bias = b_ref[...]
        for side in range(2):
            out = gelu(total[:, :, side * ch : (side + 1) * ch] + bias[None]).astype(BF)
            for pair in range(pairs):
                y_ref[face, base + 2 * pair + side] = out[pair]
    last = first + count - 1
    fill(taps_0, first)

    def double(j, carry):
        t = first + 2 * j
        fill(taps_1, t + 1)
        product(taps_0, t)
        fill(taps_0, jnp.minimum(t + 2, last))
        product(taps_1, t + 1)
        return carry

    lax.fori_loop(0, count // 2, double, 0)
    if count % 2:
        product(taps_0, last)


def in_hbm(x):
    return pltpu.with_memory_space_constraint(x, pltpu.HBM)


def conv_piece(x, weight, bias, first, count, state):
    faces, rows, cols, ch = x.shape
    vmem = pl.BlockSpec(memory_space=pltpu.VMEM)
    build = state is None
    taps = (STEP // 2 + 1, cols, 6 * ch)
    arranged = jax.ShapeDtypeStruct((6 * ch, 2 * ch), BF)
    args = [x, bias, weight] if build else [x, bias, *state]
    out_shape = [jax.ShapeDtypeStruct(x.shape, BF)] + [arranged] * (2 if build else 0)
    pixels = count * STEP * cols
    out = pl.pallas_call(
        functools.partial(conv_kernel, first, count, build),
        in_specs=[vmem] * len(args),
        out_specs=tuple([vmem] * len(out_shape)),
        out_shape=tuple(out_shape),
        scratch_shapes=[pltpu.VMEM(taps, BF), pltpu.VMEM(taps, BF)],
        input_output_aliases={} if build else {4: 0},
        cost_estimate=pl.CostEstimate(
            flops=pixels * 24 * ch * ch, bytes_accessed=4 * pixels * ch, transcendentals=0
        ),
        compiler_params=pltpu.CompilerParams(vmem_limit_bytes=16 * 2**20),
        name="conv_piece",
    )(*args)
    return (out[1], out[2], out[0]) if build else (state[0], state[1], out[0])


def down_kernel(first, count, y_ref, w_ref, b_ref, *refs):
    c_ref, y_out, c_out, taps_0, taps_1, wide_0, wide_1, sems = refs[-8:]
    faces, rows, cols, ch = y_ref.shape
    steps, pairs = rows // STEP, STEP // 2
    last = first + count - 1

    def copies(t):
        face, step = t // steps, lax.rem(t, steps)
        some, cells = pl.ds(step * STEP, STEP), pl.ds(step * pairs, pairs)
        return (
            pltpu.make_async_copy(y_ref.at[face, some], y_out.at[face, some], sems.at[0]),
            pltpu.make_async_copy(c_ref.at[face, cells], c_out.at[face, cells], sems.at[1]),
        )

    def fill(taps, wide, t):
        face, step = t // steps, lax.rem(t, steps)
        for pair in range(pairs):
            row = step * STEP + 2 * pair
            for a in range(2):
                wide[2 * pair + a] = y_ref[face, row + a].astype(F32)
            four = [
                wide[2 * pair + a, pl.ds(d, cols // 2, stride=2), :].astype(BF)
                for a in range(2)
                for d in range(2)
            ]
            taps[pair] = jnp.concatenate(four, axis=1)

    def product(taps, t):
        face, step = t // steps, lax.rem(t, steps)
        out = jnp.dot(
            taps[...].reshape(pairs * cols // 2, 4 * ch),
            w_ref[...].reshape(4 * ch, -1),
            preferred_element_type=F32,
        )
        out = (out + b_ref[...]).astype(BF)
        c_ref[face, pl.ds(step * pairs, pairs)] = out.reshape(pairs, cols // 2, -1)
        copies(t)[1].start()

    def send(t, carry):
        copies(t)[0].start()
        return carry

    def wait(t, carry):
        for copy in copies(t):
            copy.wait()
        return carry

    lax.fori_loop(first, first + count, send, 0)
    fill(taps_0, wide_0, first)

    def double(j, carry):
        t = first + 2 * j
        fill(taps_1, wide_1, t + 1)
        product(taps_0, t)
        fill(taps_0, wide_0, jnp.minimum(t + 2, last))
        product(taps_1, t + 1)
        return carry

    lax.fori_loop(0, count // 2, double, 0, unroll=True)
    if count % 2:
        product(taps_0, last)
    lax.fori_loop(first, first + count, wait, 0)


def downsample(y, weight, bias, first, count, into):
    faces, rows, cols, ch = y.shape
    shape = (faces, rows // 2, cols // 2, weight.shape[-1])
    vmem = pl.BlockSpec(memory_space=pltpu.VMEM)
    hbm = pl.BlockSpec(memory_space=pltpu.HBM)
    taps, wide = (STEP // 2, cols // 2, 4 * ch), (STEP, cols, ch)
    args, in_specs = [y, weight, bias], [vmem] * 3
    if into:
        args += [into[0], in_hbm(into[1]), in_hbm(into[2])]
        in_specs += [vmem, hbm, hbm]
    pixels = count * STEP * cols
    return pl.pallas_call(
        functools.partial(down_kernel, first, count),
        in_specs=in_specs,
        out_specs=(vmem, hbm, hbm),
        out_shape=(jax.ShapeDtypeStruct(shape, BF), pltpu.HBM(y.shape, BF), pltpu.HBM(shape, BF)),
        scratch_shapes=[pltpu.VMEM(taps, BF)] * 2
        + [pltpu.VMEM(wide, F32)] * 2
        + [pltpu.SemaphoreType.DMA((2,))],
        input_output_aliases={3: 0, 4: 1, 5: 2} if into else {},
        cost_estimate=pl.CostEstimate(
            flops=pixels * 2 * ch * shape[-1], bytes_accessed=4 * pixels * ch, transcendentals=0
        ),
        compiler_params=pltpu.CompilerParams(vmem_limit_bytes=16 * 2**20),
        name="downsample",
    )(*args)


def column(tile, place):
    return tile[pl.ds(place, tile.shape[0] // EDGE, stride=EDGE), :]


def put_strips(i, r, c, lines, top, bottom, u_ref, v_ref, turn_ref, line_ref):
    left, left_in, right_in, right = lines
    size = left.shape[0]
    for place, value in enumerate(lines):
        line_ref[i, place] = value.astype(BF)
    side = jnp.where(c == 0, left, right).astype(BF)
    inner = jnp.where(c == 0, right, left).astype(BF)
    even = lax.rem(r, 2) == 0
    line = jnp.where(even, top, bottom).astype(BF)
    turn_ref[i] = jnp.where(even, bottom, top).astype(BF)
    for ref in (u_ref, v_ref):
        ref[i, 0] = side
        ref[i, 1] = line[:size]
        ref[i, 2] = line[size:]
    u_ref[i, 3] = inner


def strip_shapes(faces, rows, cols, ch):
    return (
        jax.ShapeDtypeStruct((faces, 4, rows, ch), BF),
        jax.ShapeDtypeStruct((faces, 3, rows, ch), BF),
        jax.ShapeDtypeStruct((faces, cols, ch), BF),
        jax.ShapeDtypeStruct((faces, 4, rows, ch), BF),
    )


def whole(shape):
    return pl.BlockSpec(shape, lambda *_: (0,) * len(shape))


def tile_copies(array, tiles, sems, back=False):
    cols = array.shape[2]
    out = []
    for side, start in enumerate((0, cols - EDGE)):
        far, near = array.at[:, :, pl.ds(start, EDGE), :], tiles.at[side]
        out.append(pltpu.make_async_copy(*((near, far) if back else (far, near)), sems.at[side]))
    return out


def strips_kernel(x_ref, u_ref, v_ref, turn_ref, line_ref, tiles, outer, left, right, sems):
    faces, rows, cols, ch = x_ref.shape
    r, c = lax.axis_index("row"), lax.axis_index("col")
    copies = []
    for i in range(faces):
        for k, start in enumerate((0, cols - EDGE)):
            far, near = x_ref.at[i, :, pl.ds(start, EDGE), :], tiles.at[k, i]
            copies.append(pltpu.make_async_copy(far, near, sems.at[i, k]))
        for k, row in enumerate((0, rows - 1)):
            far, near = x_ref.at[i, row], outer.at[k, i]
            copies.append(pltpu.make_async_copy(far, near, sems.at[i, 2 + k]))
    for copy in copies:
        copy.start()
    for i in range(faces):
        for copy in copies[4 * i : 4 * i + 4]:
            copy.wait()
        left[i] = tiles[0, i].astype(F32).reshape(rows * EDGE, ch)
        right[i] = tiles[1, i].astype(F32).reshape(rows * EDGE, ch)
        ends = [(left.at[i], 0), (left.at[i], 1), (right.at[i], EDGE - 2), (right.at[i], EDGE - 1)]
        lines = [column(*end) for end in ends]
        put_strips(
            i, r, c, lines, outer[0, i].astype(F32), outer[1, i].astype(F32),
            u_ref, v_ref, turn_ref, line_ref,
        )


def strips_of(x):
    faces, rows, cols, ch = x.shape
    shapes = strip_shapes(faces, rows, cols, ch)
    return pl.pallas_call(
        strips_kernel,
        in_specs=[pl.BlockSpec(memory_space=pltpu.HBM)],
        out_specs=(pl.BlockSpec(memory_space=pltpu.VMEM),) * 4,
        out_shape=shapes,
        scratch_shapes=[
            pltpu.VMEM((2, faces, rows, EDGE, ch), BF),
            pltpu.VMEM((2, faces, cols, ch), BF),
            pltpu.VMEM((faces, rows * EDGE, ch), F32),
            pltpu.VMEM((faces, rows * EDGE, ch), F32),
            pltpu.SemaphoreType.DMA((faces, 4)),
        ],
        cost_estimate=pl.CostEstimate(flops=0, bytes_accessed=4 * 2**20, transcendentals=0),
        compiler_params=pltpu.CompilerParams(vmem_limit_bytes=10 * 2**20),
        name="strips_of",
    )(in_hbm(x))


def plan_kernel(near_ref, code_ref, plan_ref):
    faces = near_ref.shape[1] // lax.axis_size("face")
    me, r, c = lax.axis_index("face"), lax.axis_index("row"), lax.axis_index("col")

    def slot(row, col):
        return ((r ^ row) << 1) | (c ^ col)

    def quarter(edge, q):
        upright = lax.rem(edge, 2) == 1
        row = jnp.where(upright, q, jnp.where(edge == 0, 0, 3))
        col = jnp.where(upright, jnp.where(edge == 3, 0, 1), q >> 1)
        return slot(row, col), jnp.where(upright, 0, 1 + (q & 1))

    def one(at, carry):
        k, i = at // faces, lax.rem(at, faces)
        f = (me ^ k) * faces + i
        edge = 3 - 2 * c
        code = code_ref[edge, f]
        far, flip = code >> 1, code & 1
        n = lax.rem(near_ref[edge, f], faces)
        entries = [n, *quarter(far, jnp.where(flip == 1, 3 - r, r))]
        corner = jnp.where(r < 2, c, 3 - c)
        tip = code_ref[4 + corner, f]
        tip_row = jnp.where(tip < 2, 0, 3)
        tip_col = jnp.where((tip == 1) | (tip == 2), 1, 0)
        tip_n = lax.rem(near_ref[4 + corner, f], faces)
        tip_entries = (tip_n, slot(tip_row, tip_col), 0, tip_row // 3)
        pixels = []
        for limit, step in ((0, -1), (3, 1)):
            q = jnp.clip(jnp.where(flip == 1, 3 - r - step, r + step), 0, 3)
            there = (n, *quarter(far, q), flip ^ (1 if step < 0 else 0))
            pixels += [jnp.where(r == limit, t, u) for t, u in zip(tip_entries, there)]
        edge = jnp.where(r < 2, 0, 2)
        code = code_ref[edge, f]
        far, flip = code >> 1, code & 1
        n = lax.rem(near_ref[edge, f], faces)
        part = c ^ flip
        for h in range(2):
            entries += [n, *quarter(far, 2 * part + h)]
        pixels += [n, *quarter(far, jnp.where(part == 0, 2, 1)), part]
        for j, entry in enumerate(entries + pixels):
            plan_ref[at, j] = jnp.asarray(entry, jnp.int32)
        return carry

    lax.fori_loop(0, plan_ref.shape[0], one, 0)


def plan_of(neighbour_face, orientation):
    smem = pl.BlockSpec(memory_space=pltpu.SMEM)
    return pl.pallas_call(
        plan_kernel,
        in_specs=[smem, smem],
        out_specs=smem,
        out_shape=jax.ShapeDtypeStruct((neighbour_face.shape[1], 21), jnp.int32),
        compiler_params=pltpu.CompilerParams(vmem_limit_bytes=2 * 2**20),
        name="plan_of",
    )(neighbour_face, orientation)


def select_kernel(plan_ref, *refs):
    stores, outs, held = refs[:8], refs[8:-1], refs[-1]
    faces, _, size, ch = held.shape[1:]
    r = lax.axis_index("row")
    for k, store in enumerate(stores):
        for i in range(faces):
            held[k, i] = store[i, 0:3]

    for k, out in enumerate(outs):
        parts = out.shape[0] // (faces * size)
        single = jnp.zeros((out.shape[0] - faces * parts * size, ch), F32)
        spot = lax.broadcasted_iota(jnp.int32, (single.shape[0], 1), 0)
        for i in range(faces):
            at, start = k * faces + i, i * parts * size

            def entry(j, at=at):
                return plan_ref[at, j]

            out[start : start + size] = held[entry(1), entry(0), entry(2)]
            for h in range(parts - 1):
                own = 3 + 3 * (jnp.where((r == 0) | (r == 3), 0, 1) if k else h)
                block = held[entry(own + 1), entry(own), entry(own + 2)]
                out[start + (1 + h) * size : start + (2 + h) * size] = block
            for j in range(3):
                first = 9 + 4 * j
                where, n, block = entry(first + 1), entry(first), entry(first + 2)
                head = held[where, n, block, 0:EXTRA].astype(F32)
                tail = held[where, n, block, size - EXTRA : size].astype(F32)
                pixel = jnp.where(entry(first + 3) == 1, tail[EXTRA - 1 : EXTRA], head[0:1])
                single = jnp.where(spot == 3 * i + j, pixel, single)
        out[faces * parts * size :] = single.astype(BF)


def select_strips(plan, stores, groups):
    faces, _, size, ch = stores[0].shape
    single = -(-3 * faces // EXTRA) * EXTRA
    shapes = [
        jax.ShapeDtypeStruct(((2 if k else 3) * faces * size + single, ch), BF)
        for k in range(groups)
    ]
    return pl.pallas_call(
        select_kernel,
        in_specs=[pl.BlockSpec(memory_space=pltpu.SMEM)]
        + [pl.BlockSpec(memory_space=pltpu.VMEM)] * 8,
        out_specs=(pl.BlockSpec(memory_space=pltpu.VMEM),) * groups,
        out_shape=tuple(shapes),
        scratch_shapes=[pltpu.VMEM((8, faces, 3, size, ch), BF)],
        cost_estimate=pl.CostEstimate(flops=0, bytes_accessed=4 * 2**20, transcendentals=0),
        compiler_params=pltpu.CompilerParams(vmem_limit_bytes=10 * 2**20),
        name="select_strips",
    )(plan, *stores)


def ring_kernel(groups, coarse, near_ref, code_ref, x_ref, y_in, line_in, beside, diagonal, across,
                far_diagonal, turned, w_ref, b_ref, *refs):
    seams, seconds, refs = refs[:groups], refs[groups : 2 * groups - 1], refs[2 * groups - 1 :]
    if coarse:
        c_ref, dw_ref, db_ref, _, _, y_out, c_out = refs[:7]
        y_ref = y_in
        scratch = refs[7:]
        *scratch, c_taps, c_tiles, c_rows, c_cols, sems = scratch
    else:
        y_ref, outs, scratch = refs[0], refs[1:5], refs[5:]
    tiles, edge_rows, edge_cols, held, held_single, left, right, w_cols, across_taps, along_taps = scratch
    faces, rows, cols, ch = x_ref.shape
    me, r, c = lax.axis_index("face"), lax.axis_index("row"), lax.axis_index("col")
    for k in range(groups):
        seam, parts = seams[k], 2 if k else 3
        for i in range(faces):
            start = i * parts * rows
            held[k, i, : 2 * rows] = seam[start : start + 2 * rows]
            half = seconds[k - 1] if k else seam
            start += (parts - 1) * rows
            held[k, i, 2 * rows :] = half[start : start + rows]
        held_single[k] = seam[faces * parts * rows :]

    def oriented(v, flip):
        n = v.shape[0]
        to = lax.broadcasted_iota(jnp.int32, (n, n), 0)
        source = lax.broadcasted_iota(jnp.int32, (n, n), 1)
        order = jnp.where(source == jnp.where(flip == 1, n - 1 - to, to), 1.0, 0.0).astype(BF)
        return jnp.dot(order, v, preferred_element_type=F32)

    even = lax.rem(r, 2) == 0
    outer = (r == 0) | (r == 3)
    for d in range(3):
        for a in range(3):
            w_cols[(3 * d + a) * ch : (3 * d + a + 1) * ch] = w_ref[a, d]
    bias = b_ref[...]

    def holder(n):
        return jnp.minimum(n, FACES - 1) // faces ^ me

    def put(taps, place, v, before, after, third):
        for k, part in enumerate(shifted(v, before, after)):
            start = (3 * third + k) * ch
            taps[pl.ds(place, v.shape[0]), start : start + ch] = part

    def face(i):
        f = me * faces + i
        edge = 3 - 2 * c
        n = near_ref[edge, f]
        corner = jnp.where(r < 2, c, 3 - c)
        tip_n = near_ref[4 + corner, f]
        seam_side = oriented(held[holder(n), i, 0:rows], code_ref[edge, f] & 1)
        n_before = jnp.where(r == 0, tip_n, n)
        n_after = jnp.where(r == 3, tip_n, n)
        before = held_single[holder(n_before)].astype(F32)[3 * i : 3 * i + 1]
        after = held_single[holder(n_after)].astype(F32)[3 * i + 1 : 3 * i + 2]
        before = jnp.where(n_before < FACES, before, 0.0)
        after = jnp.where(n_after < FACES, after, 0.0)
        edge = jnp.where(r < 2, 0, 2)
        n = near_ref[edge, f]
        seam_line = oriented(held[holder(n), i, rows : 3 * rows], code_ref[edge, f] & 1)
        middle = held_single[holder(n)].astype(F32)[3 * i + 2 : 3 * i + 3]

        inner = beside[i, 3].astype(F32)
        block_line = jnp.concatenate([across[i, 1], across[i, 2]], axis=0).astype(F32)
        outward = jnp.where(outer, seam_line, block_line)
        inward = turned[i].astype(F32)
        top = jnp.where(even, outward, inward)
        bottom = jnp.where(even, inward, outward)
        lft = jnp.where(c == 0, seam_side, inner)
        rgt = jnp.where(c == 0, inner, seam_side)
        pair_inner = diagonal[i, 3].astype(F32)
        inward_corner = jnp.where(even, pair_inner[0:1], pair_inner[rows - 1 : rows])
        far_first = far_diagonal[i, 1].astype(F32)[0:1]
        far_last = far_diagonal[i, 2].astype(F32)[rows - 1 : rows]
        outward_corner = jnp.where(outer, middle, jnp.where(c == 0, far_first, far_last))
        inner_top = jnp.where(even, outward_corner, inward_corner)
        inner_bottom = jnp.where(even, inward_corner, outward_corner)
        top_left = jnp.where(c == 0, before, inner_top)
        top_right = jnp.where(c == 0, inner_top, before)
        bottom_left = jnp.where(c == 0, after, inner_bottom)
        bottom_right = jnp.where(c == 0, inner_bottom, after)

        row_0, row_1, row_2, row_3 = (
            x_ref[i, k].astype(F32) for k in (0, 1, rows - 2, rows - 1)
        )
        place = 2 * i * cols
        put(across_taps, place, top, top_left, top_right, 0)
        put(across_taps, place, row_0, lft[0:1], rgt[0:1], 1)
        put(across_taps, place, row_1, lft[1:2], rgt[1:2], 2)
        place += cols
        put(across_taps, place, row_2, lft[rows - 2 : rows - 1], rgt[rows - 2 : rows - 1], 0)
        put(across_taps, place, row_3, lft[rows - 1 : rows], rgt[rows - 1 : rows], 1)
        put(across_taps, place, bottom, bottom_left, bottom_right, 2)
        col_0, col_1, col_2, col_3 = (line_in[i, k].astype(F32) for k in range(4))
        place = 2 * i * rows
        put(along_taps, place, lft, top_left, bottom_left, 0)
        put(along_taps, place, col_0, top[0:1], bottom[0:1], 1)
        put(along_taps, place, col_1, top[1:2], bottom[1:2], 2)
        place += rows
        put(along_taps, place, col_2, top[cols - 2 : cols - 1], bottom[cols - 2 : cols - 1], 0)
        put(along_taps, place, col_3, top[cols - 1 : cols], bottom[cols - 1 : cols], 1)
        put(along_taps, place, rgt, top_right, bottom_right, 2)

    for i in range(faces):
        face(i)
    w_rows = w_ref[...].reshape(9 * ch, ch)
    out = gelu(jnp.dot(across_taps[...], w_rows, preferred_element_type=F32) + bias)
    edge_rows[...] = out.astype(BF).reshape(edge_rows.shape)
    out = gelu(jnp.dot(along_taps[...], w_cols[...], preferred_element_type=F32) + bias)
    edge_cols[...] = out.reshape(edge_cols.shape)
    if coarse:
        order_cols, order_rows = parting(cols), parting(rows)

    def with_column(tile, place, value):
        spots = lax.broadcasted_iota(jnp.int32, tile.shape, 1)
        return jnp.where(spots == place, value[:, None, :], tile)

    def update(i, carry):
        new_top, new_bottom = edge_rows[i, 0].astype(F32), edge_rows[i, 1].astype(F32)
        end = (rows - 1) * EDGE
        for tile, side, place in ((left, 0, 0), (right, 1, EDGE - 1)):
            start = side * (cols - EDGE)
            value = y_ref[i, :, start : start + EDGE].astype(F32)
            value = with_column(value, place, edge_cols[i, side * rows : (side + 1) * rows])
            tile[...] = value.reshape(rows * EDGE, ch)
            tile[0:EDGE] = new_top[start : start + EDGE]
            tile[end : end + EDGE] = new_bottom[start : start + EDGE]
            if coarse:
                tiles[side, i] = value.astype(BF)
                tiles[side, i, 0] = edge_rows[i, 0, start : start + EDGE]
                tiles[side, i, rows - 1] = edge_rows[i, 1, start : start + EDGE]
            else:
                y_ref[i, :, start : start + EDGE] = value.astype(BF)
        if not coarse:
            y_ref[i, 0] = edge_rows[i, 0]
            y_ref[i, rows - 1] = edge_rows[i, 1]
        lines = (
            column(left, 0), column(left, 1), column(right, EDGE - 2), column(right, EDGE - 1)
        )
        if not coarse:
            put_strips(i, r, c, lines, new_top, new_bottom, *outs)
            return carry
        spot = lax.broadcasted_iota(jnp.int32, (cols, 1), 0)
        half = cols // 2
        for k, (own, near) in enumerate(((new_top, 1), (new_bottom, rows - 2))):
            first = edge_cols[i, near : near + 1]
            last = edge_cols[i, rows + near : rows + near + 1]
            other = y_ref[i, near].astype(F32)
            other = jnp.where(spot == 0, first, jnp.where(spot == cols - 1, last, other))
            both = (own, other) if k == 0 else (other, own)
            four = parted(order_cols, jnp.concatenate([v.astype(BF) for v in both], axis=1))
            four = jnp.concatenate([four[j] for j in (0, 2, 1, 3)], axis=1)
            c_taps[pl.ds((2 * i + k) * half, half)] = four
        for k, both in enumerate((lines[:2], lines[2:])):
            four = parted(order_rows, jnp.concatenate([v.astype(BF) for v in both], axis=1))
            place = 2 * faces * half + (2 * i + k) * (rows // 2)
            c_taps[pl.ds(place, rows // 2)] = jnp.concatenate(four, axis=1)
        return carry

    lax.fori_loop(0, faces, update, 0, unroll=True)
    if not coarse:
        return
    copies = tile_copies(y_out, tiles, sems, back=True)
    if cols > 2 * EDGE:
        between = pl.ds(EDGE, cols - 2 * EDGE)
        for k, row in enumerate((0, rows - 1)):
            copies.append(
                pltpu.make_async_copy(
                    edge_rows.at[:, k, between], y_out.at[:, row, between], sems.at[2 + k]
                )
            )
    for copy in copies:
        copy.start()
    half = cols // 2
    out = jnp.dot(
        c_taps[...], dw_ref[...].reshape(4 * ch, -1), preferred_element_type=F32
    ) + db_ref[...]
    across_cells = 2 * faces * half
    c_rows[...] = out[:across_cells].astype(BF).reshape(c_rows.shape)
    c_cols[...] = out[across_cells:].reshape(c_cols.shape)

    def cells(i):
        for side in range(2):
            start = side * (half - EDGE)
            value = c_ref[i, :, start : start + EDGE].astype(F32)
            value = with_column(value, side * (EDGE - 1), c_cols[i, side])
            c_tiles[side, i] = value.astype(BF)
            for k in range(2):
                c_tiles[side, i, k * (rows // 2 - 1)] = c_rows[i, k, start : start + EDGE]

    more = []
    for i in range(faces):
        cells(i)
        for side, start in enumerate((0, half - EDGE)):
            more.append(
                pltpu.make_async_copy(
                    c_tiles.at[side, i], c_out.at[i, :, pl.ds(start, EDGE), :], sems.at[8 + 2 * i + side]
                )
            )
            more[-1].start()
    first = len(more)
    if half > 2 * EDGE:
        between = pl.ds(EDGE, half - 2 * EDGE)
        for k, row in enumerate((0, rows // 2 - 1)):
            more.append(
                pltpu.make_async_copy(
                    c_rows.at[:, k, between], c_out.at[:, row, between], sems.at[6 + k]
                )
            )
    for copy in more[first:]:
        copy.start()
    for copy in copies + more:
        copy.wait()


def ring(
    neighbour_face, orientation, x, buffers, copied, lines, parts, weight, bias, seams, seconds, down
):
    y, *coarse = buffers
    faces, rows, cols, ch = x.shape
    groups = len(seams)
    smem = pl.BlockSpec(memory_space=pltpu.SMEM)
    hbm = pl.BlockSpec(memory_space=pltpu.HBM)
    vmem = pl.BlockSpec(memory_space=pltpu.VMEM)
    args = [neighbour_face, orientation, x, y, lines, *parts, weight, bias, *seams, *seconds]
    in_specs = [smem, smem] + [vmem] * (len(args) - 2)
    scratch = [
        pltpu.VMEM((2, faces, rows, EDGE, ch), BF),
        pltpu.VMEM((faces, 2, cols, ch), BF),
        pltpu.VMEM((faces, 2 * rows, ch), F32),
        pltpu.VMEM((groups, faces, 3 * rows, ch), BF),
        pltpu.VMEM((groups, seams[0].shape[0] - 3 * faces * rows, ch), BF),
        pltpu.VMEM((rows * EDGE, ch), F32),
        pltpu.VMEM((rows * EDGE, ch), F32),
        pltpu.VMEM((9 * ch, ch), BF),
        pltpu.VMEM((2 * faces * cols, 9 * ch), BF),
        pltpu.VMEM((2 * faces * rows, 9 * ch), BF),
    ]
    if down:
        co = down[0].shape[-1]
        args += [coarse[0], *down]
        in_specs += [vmem] * 3
        aliases = {len(args): 0, len(args) + 1: 1}
        args += [in_hbm(buffer) for buffer in copied]
        in_specs += [hbm] * 2
        out_shape = [pltpu.HBM(buffer.shape, BF) for buffer in copied]
        out_specs = [hbm] * 2
        scratch += [
            pltpu.VMEM((faces * (rows + cols), 4 * ch), BF),
            pltpu.VMEM((2, faces, rows // 2, EDGE, co), BF),
            pltpu.VMEM((faces, 2, cols // 2, co), BF),
            pltpu.VMEM((faces, 2, rows // 2, co), F32),
            pltpu.SemaphoreType.DMA((8 + 2 * faces,)),
        ]
    else:
        aliases = {3: 0}
        out_shape = [jax.ShapeDtypeStruct(y.shape, BF), *strip_shapes(faces, rows, cols, ch)]
        out_specs = [vmem] * 5
    return pl.pallas_call(
        functools.partial(ring_kernel, groups, bool(down)),
        in_specs=in_specs,
        out_specs=tuple(out_specs),
        out_shape=tuple(out_shape),
        scratch_shapes=scratch,
        input_output_aliases=aliases,
        cost_estimate=pl.CostEstimate(
            flops=faces * (rows + cols) * 36 * ch * ch, bytes_accessed=8 * 2**20, transcendentals=0
        ),
        compiler_params=pltpu.CompilerParams(vmem_limit_bytes=20 * 2**20),
        name="ring",
    )(*args)


def blocks(change_row, change_col):
    cols = lax.axis_size("col")
    return [
        (r * cols + c, (r ^ change_row) * cols + (c ^ change_col))
        for r in range(lax.axis_size("row"))
        for c in range(cols)
    ]


def swap(v, change_row, change_col):
    return lax.ppermute(v, ("row", "col"), blocks(change_row, change_col))


def level(neighbour_face, orientation, plan, x, strips, weight, bias, down):
    u, v, turn, lines = strips
    groups = lax.axis_size("face")
    total = x.shape[0] * x.shape[1] // STEP
    early = max(total * (6 if down else 4) // 12, 1)
    late = early + max(total // 12, 1)
    piece = functools.partial(conv_piece, x, weight, bias)
    beside, across, diagonal = swap(u, 0, 1), swap(v, 3, 0), swap(v, 3, 1)
    pair, turned = swap(v, 1, 0), swap(turn, 1, 0)
    state = piece(0, early, None)
    if plan is None:
        *tables, state = lax.optimization_barrier((neighbour_face, orientation, state))
        plan = plan_of(*tables)
    (beside, across, diagonal, turned), state, plan = lax.optimization_barrier(
        ((beside, across, diagonal, turned), state, plan)
    )
    pair_beside, pair_across, pair_diagonal = (swap(a, 1, 0) for a in (beside, across, diagonal))
    state = piece(early, late - early, state)
    stores = (v, beside, pair, pair_beside, pair_across, pair_diagonal, across, diagonal)
    picked = select_strips(plan, stores, groups)
    picked, state = lax.optimization_barrier((picked, state))
    seams = list(picked)
    for k in sorted(range(1, groups), key=lambda k: -(k.bit_length())):
        pairs = [(g, g ^ k) for g in range(groups)]
        seams[k] = lax.ppermute(picked[k], "face", pairs)
    y = piece(late, total - late, state)[2]
    done, coarse = total - total // 4, ()
    if down:
        coarse = downsample(y, *down, 0, done, ())
    seams[1:], y, coarse = lax.optimization_barrier((seams[1:], y, coarse))
    seconds = [swap(seam, 1, 0) for seam in seams[1:]]
    if down:
        coarse = downsample(y, *down, done, total - done, coarse)
    buffers, copied = (y, *coarse[:1]), coarse[1:]
    parts = (beside, pair_beside, across, diagonal, turned)
    out = ring(
        *(neighbour_face, orientation, x, buffers, copied, lines, parts, weight, bias),
        *(seams, seconds, down),
    )
    return plan, out


def per_device(
    field, conv1_w, conv1_b, conv2_w, conv2_b, down_w, down_b, neighbour_face, orientation
):
    tables = (neighbour_face.T, orientation.T)
    plan, (hidden, *strips) = level(
        *tables, None, field, strips_of(field), conv1_w, conv1_b[None], ()
    )
    _, out = level(*tables, plan, hidden, strips, conv2_w, conv2_b[None], (down_w, down_b[None]))
    return tuple(out)


def solution(mesh):
    groups = mesh.shape["face"]
    fast = mesh.shape["row"] == 4 and mesh.shape["col"] == 2 and groups & (groups - 1) == 0
    return jax.shard_map(
        per_device if fast else general_device,
        mesh=mesh,
        in_specs=(P("face", "row", "col", None), P(), P(), P(), P(), P(), P(), P(), P()),
        out_specs=(P("face", "row", "col", None), P("face", "row", "col", None)),
        check_vma=False,
    )
```

```python
import functools

import jax
import jax.numpy as jnp
import numpy as np
from jax import lax
from jax.experimental import pallas as pl
from jax.experimental.pallas import tpu as pltpu
from jax.sharding import PartitionSpec as P


FACES = 12
BF = jnp.bfloat16
F32 = jnp.float32
STEP = 16
EDGE = 8
EXTRA = 16

layout = ("NHWC", "HWIO", "NHWC")


def padded_2(block, sides, width):
    for axis, dim in sides:
        count = lax.axis_size(axis)
        forward = [(i, i + 1) for i in range(count - 1)]
        backward = [(target, source) for source, target in forward]
        low = lax.ppermute(
            lax.slice_in_dim(block, block.shape[dim] - width, None, axis=dim), axis, forward
        )
        high = lax.ppermute(lax.slice_in_dim(block, 0, width, axis=dim), axis, backward)
        block = jnp.concatenate([low, block, high], axis=dim)
    return block


def seam_parts(edges, neighbours, codes):
    seam_faces = neighbours[:, :4]
    seam_codes = codes[:, :4]
    seams = edges[seam_faces, seam_codes // 2]
    seams = jnp.where((seam_codes % 2 == 1)[:, :, None, None], seams[:, :, ::-1], seams)
    corner_values = jnp.stack(
        [edges[:, 0, 0], edges[:, 0, -1], edges[:, 2, -1], edges[:, 2, 0]], axis=1
    )
    corner_faces = neighbours[:, 4:]
    picked = corner_values[jnp.minimum(corner_faces, FACES - 1), codes[:, 4:]]
    picked = jnp.where((corner_faces < FACES)[:, :, None], picked, jnp.zeros_like(picked))
    return (seams, picked)


def convolve(padded, weight, bias):
    summed = lax.conv_general_dilated(
        padded,
        weight,
        (1, 1),
        "VALID",
        dimension_numbers=layout,
        preferred_element_type=jnp.float32,
    )
    return jax.nn.gelu(summed + bias, approximate=False).astype(jnp.bfloat16)


def general_layer(block, weight, bias, neighbour_face, orientation):
    face_count, row_size, col_size, channels = block.shape
    row_total = lax.axis_size("row")
    col_total = lax.axis_size("col")
    row_place = lax.axis_index("row")
    col_place = lax.axis_index("col")
    face_side = row_size * row_total
    padded = padded_2(block, (("row", 1), ("col", 2)), 1)
    top_live = row_place == 0
    bottom_live = row_place == row_total - 1
    left_live = col_place == 0
    right_live = col_place == col_total - 1
    empty_line = jnp.zeros((face_count, face_side, channels), jnp.float32)

    def place(strip, offset, live):
        scaled = strip.astype(jnp.float32) * live.astype(jnp.float32)
        return lax.dynamic_update_slice_in_dim(empty_line, scaled, offset, 1)

    lines = jnp.stack(
        [
            place(block[:, 0], col_place * col_size, top_live),
            place(block[:, :, -1], row_place * row_size, right_live),
            place(block[:, -1], col_place * col_size, bottom_live),
            place(block[:, :, 0], row_place * row_size, left_live),
        ],
        axis=1,
    )
    complete = lax.psum(lax.psum(lines.astype(jnp.bfloat16), "col"), "row").astype(jnp.float32)
    every_edge = lax.all_gather(complete.astype(jnp.bfloat16), "face", axis=0, tiled=True)
    first_face = lax.axis_index("face") * face_count
    own_faces = lax.dynamic_slice_in_dim(neighbour_face, first_face, face_count, 0)
    own_codes = lax.dynamic_slice_in_dim(orientation, first_face, face_count, 0)
    seams, corners = seam_parts(every_edge, own_faces, own_codes)
    upper = jnp.concatenate([corners[:, 0:1], seams[:, 0], corners[:, 1:2]], 1)
    lower = jnp.concatenate([corners[:, 3:4], seams[:, 2], corners[:, 2:3]], 1)
    leftward = jnp.concatenate([corners[:, 0:1], seams[:, 3], corners[:, 3:4]], 1)
    rightward = jnp.concatenate([corners[:, 1:2], seams[:, 1], corners[:, 2:3]], 1)
    upper_cut = lax.dynamic_slice_in_dim(upper, col_place * col_size, col_size + 2, 1)
    lower_cut = lax.dynamic_slice_in_dim(lower, col_place * col_size, col_size + 2, 1)
    left_cut = lax.dynamic_slice_in_dim(leftward, row_place * row_size, row_size + 2, 1)
    right_cut = lax.dynamic_slice_in_dim(rightward, row_place * row_size, row_size + 2, 1)
    padded = padded.at[:, 0].set(jnp.where(top_live, upper_cut, padded[:, 0]))
    padded = padded.at[:, -1].set(jnp.where(bottom_live, lower_cut, padded[:, -1]))
    padded = padded.at[:, :, 0].set(jnp.where(left_live, left_cut, padded[:, :, 0]))
    padded = padded.at[:, :, -1].set(jnp.where(right_live, right_cut, padded[:, :, -1]))
    return convolve(padded, weight, bias)


def general_device(
    field, conv1_w, conv1_b, conv2_w, conv2_b, down_w, down_b, neighbour_face, orientation
):
    hidden = general_layer(field, conv1_w, conv1_b, neighbour_face, orientation)
    skip = general_layer(hidden, conv2_w, conv2_b, neighbour_face, orientation)
    summed = lax.conv_general_dilated(
        skip, down_w, (2, 2), "VALID", dimension_numbers=layout, preferred_element_type=jnp.float32
    )
    coarse = (summed + down_b).astype(jnp.bfloat16)
    return (skip, coarse)


def gelu(v):
    return 0.5 * v * (1.0 + lax.erf(v * np.float32(np.sqrt(0.5))))


def shifted(v, before, after):
    n = v.shape[0]
    spot = lax.broadcasted_iota(jnp.int32, (n, 1), 0)
    low = jnp.where(spot == 0, before, pltpu.roll(v, 1, 0))
    high = jnp.where(spot == n - 1, after, pltpu.roll(v, n - 1, 0))
    return low.astype(BF), v.astype(BF), high.astype(BF)


def parting(n):
    to = lax.broadcasted_iota(jnp.int32, (n, n), 0)
    source = lax.broadcasted_iota(jnp.int32, (n, n), 1)
    half = n // 2
    return jnp.where(source == jnp.where(to < half, 2 * to, 2 * (to - half) + 1), 1.0, 0.0).astype(BF)


def parted(order, v):
    v = jnp.dot(order, v, preferred_element_type=F32).astype(BF)
    half, lanes = v.shape[0] // 2, v.shape[1] // 2
    return v[:half, :lanes], v[:half, lanes:], v[half:, :lanes], v[half:, lanes:]


def conv_kernel(first, count, build, x_ref, b_ref, *refs):
    *refs, taps_0, taps_1 = refs
    if build:
        w_ref, y_ref, w_low, w_high = refs
    else:
        w_low, w_high, _, y_ref = refs
    _, size, cols, ch = x_ref.shape
    steps = size // STEP
    pairs = STEP // 2
    zero_row = jnp.zeros((1, ch), F32)
    half = 3 * ch

    if build:
        zero = jnp.zeros((ch, ch), BF)
        for d in range(3):
            one = slice(d * ch, (d + 1) * ch)
            two = slice(half + d * ch, half + (d + 1) * ch)
            w_low[one, :ch] = w_ref[0, d]
            w_low[one, ch:] = zero
            w_low[two, :ch] = w_ref[1, d]
            w_low[two, ch:] = w_ref[0, d]
            w_high[one, :ch] = w_ref[2, d]
            w_high[one, ch:] = w_ref[1, d]
            w_high[two, :ch] = zero
            w_high[two, ch:] = w_ref[2, d]

    def at(t):
        return t // steps, lax.rem(t, steps)

    def fill(taps, t):
        face, step = at(t)
        base = step * STEP

        def put(v, pair, side):
            low, same, high = shifted(v.astype(F32), zero_row, zero_row)
            place = side * half
            taps[pair, :, place : place + ch] = low
            taps[pair, :, place + ch : place + 2 * ch] = same
            taps[pair, :, place + 2 * ch : place + 3 * ch] = high

        inside = (step > 0).astype(F32)
        put(x_ref[face, jnp.maximum(base - 1, 0)].astype(F32) * inside, 0, 0)
        for row in range(STEP):
            put(x_ref[face, base + row], (row + 1) // 2, (row + 1) % 2)
        inside = (step < steps - 1).astype(F32)
        put(x_ref[face, jnp.minimum(base + STEP, size - 1)].astype(F32) * inside, pairs, 1)

    def product(taps, t):
        face, step = at(t)
        base = step * STEP
        lower = taps[pl.ds(0, pairs)].reshape(pairs * cols, 2 * half)
        upper = taps[pl.ds(1, pairs)].reshape(pairs * cols, 2 * half)
        total = jnp.dot(lower, w_low[...], preferred_element_type=F32)
        total += jnp.dot(upper, w_high[...], preferred_element_type=F32)
        total = total.reshape(pairs, cols, 2 * ch)
        bias = b_ref[...]
        for side in range(2):
            out = gelu(total[:, :, side * ch : (side + 1) * ch] + bias[None]).astype(BF)
            for pair in range(pairs):
                y_ref[face, base + 2 * pair + side] = out[pair]
    last = first + count - 1
    fill(taps_0, first)

    def double(j, carry):
        t = first + 2 * j
        fill(taps_1, t + 1)
        product(taps_0, t)
        fill(taps_0, jnp.minimum(t + 2, last))
        product(taps_1, t + 1)
        return carry

    lax.fori_loop(0, count // 2, double, 0)
    if count % 2:
        product(taps_0, last)


def in_hbm(x):
    return pltpu.with_memory_space_constraint(x, pltpu.HBM)


def conv_piece(x, weight, bias, first, count, state):
    faces, rows, cols, ch = x.shape
    vmem = pl.BlockSpec(memory_space=pltpu.VMEM)
    build = state is None
    taps = (STEP // 2 + 1, cols, 6 * ch)
    arranged = jax.ShapeDtypeStruct((6 * ch, 2 * ch), BF)
    args = [x, bias, weight] if build else [x, bias, *state]
    out_shape = [jax.ShapeDtypeStruct(x.shape, BF)] + [arranged] * (2 if build else 0)
    pixels = count * STEP * cols
    out = pl.pallas_call(
        functools.partial(conv_kernel, first, count, build),
        in_specs=[vmem] * len(args),
        out_specs=tuple([vmem] * len(out_shape)),
        out_shape=tuple(out_shape),
        scratch_shapes=[pltpu.VMEM(taps, BF), pltpu.VMEM(taps, BF)],
        input_output_aliases={} if build else {4: 0},
        cost_estimate=pl.CostEstimate(
            flops=pixels * 24 * ch * ch, bytes_accessed=4 * pixels * ch, transcendentals=0
        ),
        compiler_params=pltpu.CompilerParams(vmem_limit_bytes=16 * 2**20),
        name="conv_piece",
    )(*args)
    return (out[1], out[2], out[0]) if build else (state[0], state[1], out[0])


def down_kernel(first, count, y_ref, w_ref, b_ref, *refs):
    c_ref, y_out, c_out, taps_0, taps_1, wide_0, wide_1, sems = refs[-8:]
    faces, rows, cols, ch = y_ref.shape
    steps, pairs = rows // STEP, STEP // 2
    last = first + count - 1

    def copies(t):
        face, step = t // steps, lax.rem(t, steps)
        some, cells = pl.ds(step * STEP, STEP), pl.ds(step * pairs, pairs)
        return (
            pltpu.make_async_copy(y_ref.at[face, some], y_out.at[face, some], sems.at[0]),
            pltpu.make_async_copy(c_ref.at[face, cells], c_out.at[face, cells], sems.at[1]),
        )

    def fill(taps, wide, t):
        face, step = t // steps, lax.rem(t, steps)
        for pair in range(pairs):
            row = step * STEP + 2 * pair
            for a in range(2):
                wide[2 * pair + a] = y_ref[face, row + a].astype(F32)
            four = [
                wide[2 * pair + a, pl.ds(d, cols // 2, stride=2), :].astype(BF)
                for a in range(2)
                for d in range(2)
            ]
            taps[pair] = jnp.concatenate(four, axis=1)

    def product(taps, t):
        face, step = t // steps, lax.rem(t, steps)
        out = jnp.dot(
            taps[...].reshape(pairs * cols // 2, 4 * ch),
            w_ref[...].reshape(4 * ch, -1),
            preferred_element_type=F32,
        )
        out = (out + b_ref[...]).astype(BF)
        c_ref[face, pl.ds(step * pairs, pairs)] = out.reshape(pairs, cols // 2, -1)
        copies(t)[1].start()

    def send(t, carry):
        copies(t)[0].start()
        return carry

    def wait(t, carry):
        for copy in copies(t):
            copy.wait()
        return carry

    lax.fori_loop(first, first + count, send, 0)
    fill(taps_0, wide_0, first)

    def double(j, carry):
        t = first + 2 * j
        fill(taps_1, wide_1, t + 1)
        product(taps_0, t)
        fill(taps_0, wide_0, jnp.minimum(t + 2, last))
        product(taps_1, t + 1)
        return carry

    lax.fori_loop(0, count // 2, double, 0, unroll=True)
    if count % 2:
        product(taps_0, last)
    lax.fori_loop(first, first + count, wait, 0)


def downsample(y, weight, bias, first, count, into):
    faces, rows, cols, ch = y.shape
    shape = (faces, rows // 2, cols // 2, weight.shape[-1])
    vmem = pl.BlockSpec(memory_space=pltpu.VMEM)
    hbm = pl.BlockSpec(memory_space=pltpu.HBM)
    taps, wide = (STEP // 2, cols // 2, 4 * ch), (STEP, cols, ch)
    args, in_specs = [y, weight, bias], [vmem] * 3
    if into:
        args += [into[0], in_hbm(into[1]), in_hbm(into[2])]
        in_specs += [vmem, hbm, hbm]
    pixels = count * STEP * cols
    return pl.pallas_call(
        functools.partial(down_kernel, first, count),
        in_specs=in_specs,
        out_specs=(vmem, hbm, hbm),
        out_shape=(jax.ShapeDtypeStruct(shape, BF), pltpu.HBM(y.shape, BF), pltpu.HBM(shape, BF)),
        scratch_shapes=[pltpu.VMEM(taps, BF)] * 2
        + [pltpu.VMEM(wide, F32)] * 2
        + [pltpu.SemaphoreType.DMA((2,))],
        input_output_aliases={3: 0, 4: 1, 5: 2} if into else {},
        cost_estimate=pl.CostEstimate(
            flops=pixels * 2 * ch * shape[-1], bytes_accessed=4 * pixels * ch, transcendentals=0
        ),
        compiler_params=pltpu.CompilerParams(vmem_limit_bytes=16 * 2**20),
        name="downsample",
    )(*args)


def column(tile, place):
    return tile[pl.ds(place, tile.shape[0] // EDGE, stride=EDGE), :]


def put_strips(i, r, c, lines, top, bottom, u_ref, v_ref, turn_ref, line_ref):
    left, left_in, right_in, right = lines
    size = left.shape[0]
    for place, value in enumerate(lines):
        line_ref[i, place] = value.astype(BF)
    side = jnp.where(c == 0, left, right).astype(BF)
    inner = jnp.where(c == 0, right, left).astype(BF)
    even = lax.rem(r, 2) == 0
    line = jnp.where(even, top, bottom).astype(BF)
    turn_ref[i] = jnp.where(even, bottom, top).astype(BF)
    for ref in (u_ref, v_ref):
        ref[i, 0] = side
        ref[i, 1] = line[:size]
        ref[i, 2] = line[size:]
    u_ref[i, 3] = inner


def strip_shapes(faces, rows, cols, ch):
    return (
        jax.ShapeDtypeStruct((faces, 4, rows, ch), BF),
        jax.ShapeDtypeStruct((faces, 3, rows, ch), BF),
        jax.ShapeDtypeStruct((faces, cols, ch), BF),
        jax.ShapeDtypeStruct((faces, 4, rows, ch), BF),
    )


def whole(shape):
    return pl.BlockSpec(shape, lambda *_: (0,) * len(shape))


def tile_copies(array, tiles, sems, back=False):
    cols = array.shape[2]
    out = []
    for side, start in enumerate((0, cols - EDGE)):
        far, near = array.at[:, :, pl.ds(start, EDGE), :], tiles.at[side]
        out.append(pltpu.make_async_copy(*((near, far) if back else (far, near)), sems.at[side]))
    return out


def strips_kernel(x_ref, u_ref, v_ref, turn_ref, line_ref, tiles, outer, left, right, sems):
    faces, rows, cols, ch = x_ref.shape
    r, c = lax.axis_index("row"), lax.axis_index("col")
    copies = []
    for i in range(faces):
        for k, start in enumerate((0, cols - EDGE)):
            far, near = x_ref.at[i, :, pl.ds(start, EDGE), :], tiles.at[k, i]
            copies.append(pltpu.make_async_copy(far, near, sems.at[i, k]))
        for k, row in enumerate((0, rows - 1)):
            far, near = x_ref.at[i, row], outer.at[k, i]
            copies.append(pltpu.make_async_copy(far, near, sems.at[i, 2 + k]))
    for copy in copies:
        copy.start()
    for i in range(faces):
        for copy in copies[4 * i : 4 * i + 4]:
            copy.wait()
        left[i] = tiles[0, i].astype(F32).reshape(rows * EDGE, ch)
        right[i] = tiles[1, i].astype(F32).reshape(rows * EDGE, ch)
        ends = [(left.at[i], 0), (left.at[i], 1), (right.at[i], EDGE - 2), (right.at[i], EDGE - 1)]
        lines = [column(*end) for end in ends]
        put_strips(
            i, r, c, lines, outer[0, i].astype(F32), outer[1, i].astype(F32),
            u_ref, v_ref, turn_ref, line_ref,
        )


def strips_of(x):
    faces, rows, cols, ch = x.shape
    shapes = strip_shapes(faces, rows, cols, ch)
    return pl.pallas_call(
        strips_kernel,
        in_specs=[pl.BlockSpec(memory_space=pltpu.HBM)],
        out_specs=(pl.BlockSpec(memory_space=pltpu.VMEM),) * 4,
        out_shape=shapes,
        scratch_shapes=[
            pltpu.VMEM((2, faces, rows, EDGE, ch), BF),
            pltpu.VMEM((2, faces, cols, ch), BF),
            pltpu.VMEM((faces, rows * EDGE, ch), F32),
            pltpu.VMEM((faces, rows * EDGE, ch), F32),
            pltpu.SemaphoreType.DMA((faces, 4)),
        ],
        cost_estimate=pl.CostEstimate(flops=0, bytes_accessed=4 * 2**20, transcendentals=0),
        compiler_params=pltpu.CompilerParams(vmem_limit_bytes=10 * 2**20),
        name="strips_of",
    )(in_hbm(x))


def plan_kernel(near_ref, code_ref, plan_ref):
    faces = near_ref.shape[1] // lax.axis_size("face")
    me, r, c = lax.axis_index("face"), lax.axis_index("row"), lax.axis_index("col")

    def slot(row, col):
        return ((r ^ row) << 1) | (c ^ col)

    def quarter(edge, q):
        upright = lax.rem(edge, 2) == 1
        row = jnp.where(upright, q, jnp.where(edge == 0, 0, 3))
        col = jnp.where(upright, jnp.where(edge == 3, 0, 1), q >> 1)
        return slot(row, col), jnp.where(upright, 0, 1 + (q & 1))

    def one(at, carry):
        k, i = at // faces, lax.rem(at, faces)
        f = (me ^ k) * faces + i
        edge = 3 - 2 * c
        code = code_ref[edge, f]
        far, flip = code >> 1, code & 1
        n = lax.rem(near_ref[edge, f], faces)
        entries = [n, *quarter(far, jnp.where(flip == 1, 3 - r, r))]
        corner = jnp.where(r < 2, c, 3 - c)
        tip = code_ref[4 + corner, f]
        tip_row = jnp.where(tip < 2, 0, 3)
        tip_col = jnp.where((tip == 1) | (tip == 2), 1, 0)
        tip_n = lax.rem(near_ref[4 + corner, f], faces)
        tip_entries = (tip_n, slot(tip_row, tip_col), 0, tip_row // 3)
        pixels = []
        for limit, step in ((0, -1), (3, 1)):
            q = jnp.clip(jnp.where(flip == 1, 3 - r - step, r + step), 0, 3)
            there = (n, *quarter(far, q), flip ^ (1 if step < 0 else 0))
            pixels += [jnp.where(r == limit, t, u) for t, u in zip(tip_entries, there)]
        edge = jnp.where(r < 2, 0, 2)
        code = code_ref[edge, f]
        far, flip = code >> 1, code & 1
        n = lax.rem(near_ref[edge, f], faces)
        part = c ^ flip
        for h in range(2):
            entries += [n, *quarter(far, 2 * part + h)]
        pixels += [n, *quarter(far, jnp.where(part == 0, 2, 1)), part]
        for j, entry in enumerate(entries + pixels):
            plan_ref[at, j] = jnp.asarray(entry, jnp.int32)
        return carry

    lax.fori_loop(0, plan_ref.shape[0], one, 0)


def plan_of(neighbour_face, orientation):
    smem = pl.BlockSpec(memory_space=pltpu.SMEM)
    return pl.pallas_call(
        plan_kernel,
        in_specs=[smem, smem],
        out_specs=smem,
        out_shape=jax.ShapeDtypeStruct((neighbour_face.shape[1], 21), jnp.int32),
        compiler_params=pltpu.CompilerParams(vmem_limit_bytes=2 * 2**20),
        name="plan_of",
    )(neighbour_face, orientation)


def select_kernel(plan_ref, *refs):
    stores, outs, held = refs[:8], refs[8:-1], refs[-1]
    faces, _, size, ch = held.shape[1:]
    r = lax.axis_index("row")
    for k, store in enumerate(stores):
        for i in range(faces):
            held[k, i] = store[i, 0:3]

    for k, out in enumerate(outs):
        parts = out.shape[0] // (faces * size)
        single = jnp.zeros((out.shape[0] - faces * parts * size, ch), F32)
        spot = lax.broadcasted_iota(jnp.int32, (single.shape[0], 1), 0)
        for i in range(faces):
            at, start = k * faces + i, i * parts * size

            def entry(j, at=at):
                return plan_ref[at, j]

            out[start : start + size] = held[entry(1), entry(0), entry(2)]
            for h in range(parts - 1):
                own = 3 + 3 * (jnp.where((r == 0) | (r == 3), 0, 1) if k else h)
                block = held[entry(own + 1), entry(own), entry(own + 2)]
                out[start + (1 + h) * size : start + (2 + h) * size] = block
            for j in range(3):
                first = 9 + 4 * j
                where, n, block = entry(first + 1), entry(first), entry(first + 2)
                head = held[where, n, block, 0:EXTRA].astype(F32)
                tail = held[where, n, block, size - EXTRA : size].astype(F32)
                pixel = jnp.where(entry(first + 3) == 1, tail[EXTRA - 1 : EXTRA], head[0:1])
                single = jnp.where(spot == 3 * i + j, pixel, single)
        out[faces * parts * size :] = single.astype(BF)


def select_strips(plan, stores, groups):
    faces, _, size, ch = stores[0].shape
    single = -(-3 * faces // EXTRA) * EXTRA
    shapes = [
        jax.ShapeDtypeStruct(((2 if k else 3) * faces * size + single, ch), BF)
        for k in range(groups)
    ]
    return pl.pallas_call(
        select_kernel,
        in_specs=[pl.BlockSpec(memory_space=pltpu.SMEM)]
        + [pl.BlockSpec(memory_space=pltpu.VMEM)] * 8,
        out_specs=(pl.BlockSpec(memory_space=pltpu.VMEM),) * groups,
        out_shape=tuple(shapes),
        scratch_shapes=[pltpu.VMEM((8, faces, 3, size, ch), BF)],
        cost_estimate=pl.CostEstimate(flops=0, bytes_accessed=4 * 2**20, transcendentals=0),
        compiler_params=pltpu.CompilerParams(vmem_limit_bytes=10 * 2**20),
        name="select_strips",
    )(plan, *stores)


def ring_kernel(groups, coarse, near_ref, code_ref, x_ref, y_in, line_in, beside, diagonal, across,
                far_diagonal, turned, w_ref, b_ref, *refs):
    seams, seconds, refs = refs[:groups], refs[groups : 2 * groups - 1], refs[2 * groups - 1 :]
    if coarse:
        c_ref, dw_ref, db_ref, _, _, y_out, c_out = refs[:7]
        y_ref = y_in
        scratch = refs[7:]
        *scratch, c_taps, c_tiles, c_rows, c_cols, sems = scratch
    else:
        y_ref, outs, scratch = refs[0], refs[1:5], refs[5:]
    tiles, edge_rows, edge_cols, held, held_single, left, right, w_cols, across_taps, along_taps = scratch
    faces, rows, cols, ch = x_ref.shape
    me, r, c = lax.axis_index("face"), lax.axis_index("row"), lax.axis_index("col")
    for k in range(groups):
        seam, parts = seams[k], 2 if k else 3
        for i in range(faces):
            start = i * parts * rows
            held[k, i, : 2 * rows] = seam[start : start + 2 * rows]
            half = seconds[k - 1] if k else seam
            start += (parts - 1) * rows
            held[k, i, 2 * rows :] = half[start : start + rows]
        held_single[k] = seam[faces * parts * rows :]

    def oriented(v, flip):
        n = v.shape[0]
        to = lax.broadcasted_iota(jnp.int32, (n, n), 0)
        source = lax.broadcasted_iota(jnp.int32, (n, n), 1)
        order = jnp.where(source == jnp.where(flip == 1, n - 1 - to, to), 1.0, 0.0).astype(BF)
        return jnp.dot(order, v, preferred_element_type=F32)

    even = lax.rem(r, 2) == 0
    outer = (r == 0) | (r == 3)
    for d in range(3):
        for a in range(3):
            w_cols[(3 * d + a) * ch : (3 * d + a + 1) * ch] = w_ref[a, d]
    bias = b_ref[...]

    def holder(n):
        return jnp.minimum(n, FACES - 1) // faces ^ me

    def put(taps, place, v, before, after, third):
        for k, part in enumerate(shifted(v, before, after)):
            start = (3 * third + k) * ch
            taps[pl.ds(place, v.shape[0]), start : start + ch] = part

    def face(i):
        f = me * faces + i
        edge = 3 - 2 * c
        n = near_ref[edge, f]
        corner = jnp.where(r < 2, c, 3 - c)
        tip_n = near_ref[4 + corner, f]
        seam_side = oriented(held[holder(n), i, 0:rows], code_ref[edge, f] & 1)
        n_before = jnp.where(r == 0, tip_n, n)
        n_after = jnp.where(r == 3, tip_n, n)
        before = held_single[holder(n_before)].astype(F32)[3 * i : 3 * i + 1]
        after = held_single[holder(n_after)].astype(F32)[3 * i + 1 : 3 * i + 2]
        before = jnp.where(n_before < FACES, before, 0.0)
        after = jnp.where(n_after < FACES, after, 0.0)
        edge = jnp.where(r < 2, 0, 2)
        n = near_ref[edge, f]
        seam_line = oriented(held[holder(n), i, rows : 3 * rows], code_ref[edge, f] & 1)
        middle = held_single[holder(n)].astype(F32)[3 * i + 2 : 3 * i + 3]

        inner = beside[i, 3].astype(F32)
        block_line = jnp.concatenate([across[i, 1], across[i, 2]], axis=0).astype(F32)
        outward = jnp.where(outer, seam_line, block_line)
        inward = turned[i].astype(F32)
        top = jnp.where(even, outward, inward)
        bottom = jnp.where(even, inward, outward)
        lft = jnp.where(c == 0, seam_side, inner)
        rgt = jnp.where(c == 0, inner, seam_side)
        pair_inner = diagonal[i, 3].astype(F32)
        inward_corner = jnp.where(even, pair_inner[0:1], pair_inner[rows - 1 : rows])
        far_first = far_diagonal[i, 1].astype(F32)[0:1]
        far_last = far_diagonal[i, 2].astype(F32)[rows - 1 : rows]
        outward_corner = jnp.where(outer, middle, jnp.where(c == 0, far_first, far_last))
        inner_top = jnp.where(even, outward_corner, inward_corner)
        inner_bottom = jnp.where(even, inward_corner, outward_corner)
        top_left = jnp.where(c == 0, before, inner_top)
        top_right = jnp.where(c == 0, inner_top, before)
        bottom_left = jnp.where(c == 0, after, inner_bottom)
        bottom_right = jnp.where(c == 0, inner_bottom, after)

        row_0, row_1, row_2, row_3 = (
            x_ref[i, k].astype(F32) for k in (0, 1, rows - 2, rows - 1)
        )
        place = 2 * i * cols
        put(across_taps, place, top, top_left, top_right, 0)
        put(across_taps, place, row_0, lft[0:1], rgt[0:1], 1)
        put(across_taps, place, row_1, lft[1:2], rgt[1:2], 2)
        place += cols
        put(across_taps, place, row_2, lft[rows - 2 : rows - 1], rgt[rows - 2 : rows - 1], 0)
        put(across_taps, place, row_3, lft[rows - 1 : rows], rgt[rows - 1 : rows], 1)
        put(across_taps, place, bottom, bottom_left, bottom_right, 2)
        col_0, col_1, col_2, col_3 = (line_in[i, k].astype(F32) for k in range(4))
        place = 2 * i * rows
        put(along_taps, place, lft, top_left, bottom_left, 0)
        put(along_taps, place, col_0, top[0:1], bottom[0:1], 1)
        put(along_taps, place, col_1, top[1:2], bottom[1:2], 2)
        place += rows
        put(along_taps, place, col_2, top[cols - 2 : cols - 1], bottom[cols - 2 : cols - 1], 0)
        put(along_taps, place, col_3, top[cols - 1 : cols], bottom[cols - 1 : cols], 1)
        put(along_taps, place, rgt, top_right, bottom_right, 2)

    for i in range(faces):
        face(i)
    w_rows = w_ref[...].reshape(9 * ch, ch)
    out = gelu(jnp.dot(across_taps[...], w_rows, preferred_element_type=F32) + bias)
    edge_rows[...] = out.astype(BF).reshape(edge_rows.shape)
    out = gelu(jnp.dot(along_taps[...], w_cols[...], preferred_element_type=F32) + bias)
    edge_cols[...] = out.reshape(edge_cols.shape)
    if coarse:
        order_cols, order_rows = parting(cols), parting(rows)

    def with_column(tile, place, value):
        spots = lax.broadcasted_iota(jnp.int32, tile.shape, 1)
        return jnp.where(spots == place, value[:, None, :], tile)

    def update(i, carry):
        new_top, new_bottom = edge_rows[i, 0].astype(F32), edge_rows[i, 1].astype(F32)
        end = (rows - 1) * EDGE
        for tile, side, place in ((left, 0, 0), (right, 1, EDGE - 1)):
            start = side * (cols - EDGE)
            value = y_ref[i, :, start : start + EDGE].astype(F32)
            value = with_column(value, place, edge_cols[i, side * rows : (side + 1) * rows])
            tile[...] = value.reshape(rows * EDGE, ch)
            tile[0:EDGE] = new_top[start : start + EDGE]
            tile[end : end + EDGE] = new_bottom[start : start + EDGE]
            if coarse:
                tiles[side, i] = value.astype(BF)
                tiles[side, i, 0] = edge_rows[i, 0, start : start + EDGE]
                tiles[side, i, rows - 1] = edge_rows[i, 1, start : start + EDGE]
            else:
                y_ref[i, :, start : start + EDGE] = value.astype(BF)
        if not coarse:
            y_ref[i, 0] = edge_rows[i, 0]
            y_ref[i, rows - 1] = edge_rows[i, 1]
        lines = (
            column(left, 0), column(left, 1), column(right, EDGE - 2), column(right, EDGE - 1)
        )
        if not coarse:
            put_strips(i, r, c, lines, new_top, new_bottom, *outs)
            return carry
        spot = lax.broadcasted_iota(jnp.int32, (cols, 1), 0)
        half = cols // 2
        for k, (own, near) in enumerate(((new_top, 1), (new_bottom, rows - 2))):
            first = edge_cols[i, near : near + 1]
            last = edge_cols[i, rows + near : rows + near + 1]
            other = y_ref[i, near].astype(F32)
            other = jnp.where(spot == 0, first, jnp.where(spot == cols - 1, last, other))
            both = (own, other) if k == 0 else (other, own)
            four = parted(order_cols, jnp.concatenate([v.astype(BF) for v in both], axis=1))
            four = jnp.concatenate([four[j] for j in (0, 2, 1, 3)], axis=1)
            c_taps[pl.ds((2 * i + k) * half, half)] = four
        for k, both in enumerate((lines[:2], lines[2:])):
            four = parted(order_rows, jnp.concatenate([v.astype(BF) for v in both], axis=1))
            place = 2 * faces * half + (2 * i + k) * (rows // 2)
            c_taps[pl.ds(place, rows // 2)] = jnp.concatenate(four, axis=1)
        return carry

    lax.fori_loop(0, faces, update, 0, unroll=True)
    if not coarse:
        return
    copies = tile_copies(y_out, tiles, sems, back=True)
    if cols > 2 * EDGE:
        between = pl.ds(EDGE, cols - 2 * EDGE)
        for k, row in enumerate((0, rows - 1)):
            copies.append(
                pltpu.make_async_copy(
                    edge_rows.at[:, k, between], y_out.at[:, row, between], sems.at[2 + k]
                )
            )
    for copy in copies:
        copy.start()
    half = cols // 2
    out = jnp.dot(
        c_taps[...], dw_ref[...].reshape(4 * ch, -1), preferred_element_type=F32
    ) + db_ref[...]
    across_cells = 2 * faces * half
    c_rows[...] = out[:across_cells].astype(BF).reshape(c_rows.shape)
    c_cols[...] = out[across_cells:].reshape(c_cols.shape)

    def cells(i):
        for side in range(2):
            start = side * (half - EDGE)
            value = c_ref[i, :, start : start + EDGE].astype(F32)
            value = with_column(value, side * (EDGE - 1), c_cols[i, side])
            c_tiles[side, i] = value.astype(BF)
            for k in range(2):
                c_tiles[side, i, k * (rows // 2 - 1)] = c_rows[i, k, start : start + EDGE]

    more = []
    for i in range(faces):
        cells(i)
        for side, start in enumerate((0, half - EDGE)):
            more.append(
                pltpu.make_async_copy(
                    c_tiles.at[side, i], c_out.at[i, :, pl.ds(start, EDGE), :], sems.at[8 + 2 * i + side]
                )
            )
            more[-1].start()
    first = len(more)
    if half > 2 * EDGE:
        between = pl.ds(EDGE, half - 2 * EDGE)
        for k, row in enumerate((0, rows // 2 - 1)):
            more.append(
                pltpu.make_async_copy(
                    c_rows.at[:, k, between], c_out.at[:, row, between], sems.at[6 + k]
                )
            )
    for copy in more[first:]:
        copy.start()
    for copy in copies + more:
        copy.wait()


def ring(
    neighbour_face, orientation, x, buffers, copied, lines, parts, weight, bias, seams, seconds, down
):
    y, *coarse = buffers
    faces, rows, cols, ch = x.shape
    groups = len(seams)
    smem = pl.BlockSpec(memory_space=pltpu.SMEM)
    hbm = pl.BlockSpec(memory_space=pltpu.HBM)
    vmem = pl.BlockSpec(memory_space=pltpu.VMEM)
    args = [neighbour_face, orientation, x, y, lines, *parts, weight, bias, *seams, *seconds]
    in_specs = [smem, smem] + [vmem] * (len(args) - 2)
    scratch = [
        pltpu.VMEM((2, faces, rows, EDGE, ch), BF),
        pltpu.VMEM((faces, 2, cols, ch), BF),
        pltpu.VMEM((faces, 2 * rows, ch), F32),
        pltpu.VMEM((groups, faces, 3 * rows, ch), BF),
        pltpu.VMEM((groups, seams[0].shape[0] - 3 * faces * rows, ch), BF),
        pltpu.VMEM((rows * EDGE, ch), F32),
        pltpu.VMEM((rows * EDGE, ch), F32),
        pltpu.VMEM((9 * ch, ch), BF),
        pltpu.VMEM((2 * faces * cols, 9 * ch), BF),
        pltpu.VMEM((2 * faces * rows, 9 * ch), BF),
    ]
    if down:
        co = down[0].shape[-1]
        args += [coarse[0], *down]
        in_specs += [vmem] * 3
        aliases = {len(args): 0, len(args) + 1: 1}
        args += [in_hbm(buffer) for buffer in copied]
        in_specs += [hbm] * 2
        out_shape = [pltpu.HBM(buffer.shape, BF) for buffer in copied]
        out_specs = [hbm] * 2
        scratch += [
            pltpu.VMEM((faces * (rows + cols), 4 * ch), BF),
            pltpu.VMEM((2, faces, rows // 2, EDGE, co), BF),
            pltpu.VMEM((faces, 2, cols // 2, co), BF),
            pltpu.VMEM((faces, 2, rows // 2, co), F32),
            pltpu.SemaphoreType.DMA((8 + 2 * faces,)),
        ]
    else:
        aliases = {3: 0}
        out_shape = [jax.ShapeDtypeStruct(y.shape, BF), *strip_shapes(faces, rows, cols, ch)]
        out_specs = [vmem] * 5
    return pl.pallas_call(
        functools.partial(ring_kernel, groups, bool(down)),
        in_specs=in_specs,
        out_specs=tuple(out_specs),
        out_shape=tuple(out_shape),
        scratch_shapes=scratch,
        input_output_aliases=aliases,
        cost_estimate=pl.CostEstimate(
            flops=faces * (rows + cols) * 36 * ch * ch, bytes_accessed=8 * 2**20, transcendentals=0
        ),
        compiler_params=pltpu.CompilerParams(vmem_limit_bytes=20 * 2**20),
        name="ring",
    )(*args)


def blocks(change_row, change_col):
    cols = lax.axis_size("col")
    return [
        (r * cols + c, (r ^ change_row) * cols + (c ^ change_col))
        for r in range(lax.axis_size("row"))
        for c in range(cols)
    ]


def swap(v, change_row, change_col):
    return lax.ppermute(v, ("row", "col"), blocks(change_row, change_col))


def level(neighbour_face, orientation, plan, x, strips, weight, bias, down):
    u, v, turn, lines = strips
    groups = lax.axis_size("face")
    total = x.shape[0] * x.shape[1] // STEP
    early = max(total * (7 if down else 4) // 12, 1)
    late = early + max(total // 12, 1)
    piece = functools.partial(conv_piece, x, weight, bias)
    beside, across, diagonal = swap(u, 0, 1), swap(v, 3, 0), swap(v, 3, 1)
    pair, turned = swap(v, 1, 0), swap(turn, 1, 0)
    state = piece(0, early, None)
    if plan is None:
        *tables, state = lax.optimization_barrier((neighbour_face, orientation, state))
        plan = plan_of(*tables)
    (beside, across, diagonal, turned), state, plan = lax.optimization_barrier(
        ((beside, across, diagonal, turned), state, plan)
    )
    pair_beside, pair_across, pair_diagonal = (swap(a, 1, 0) for a in (beside, across, diagonal))
    state = piece(early, late - early, state)
    stores = (v, beside, pair, pair_beside, pair_across, pair_diagonal, across, diagonal)
    picked = select_strips(plan, stores, groups)
    picked, state = lax.optimization_barrier((picked, state))
    seams = list(picked)
    for k in sorted(range(1, groups), key=lambda k: -(k.bit_length())):
        pairs = [(g, g ^ k) for g in range(groups)]
        seams[k] = lax.ppermute(picked[k], "face", pairs)
    y = piece(late, total - late, state)[2]
    done, coarse = total - total // 4, ()
    if down:
        coarse = downsample(y, *down, 0, done, ())
    seams[1:], y, coarse = lax.optimization_barrier((seams[1:], y, coarse))
    seconds = [swap(seam, 1, 0) for seam in seams[1:]]
    if down:
        coarse = downsample(y, *down, done, total - done, coarse)
    buffers, copied = (y, *coarse[:1]), coarse[1:]
    parts = (beside, pair_beside, across, diagonal, turned)
    out = ring(
        *(neighbour_face, orientation, x, buffers, copied, lines, parts, weight, bias),
        *(seams, seconds, down),
    )
    return plan, out


def per_device(
    field, conv1_w, conv1_b, conv2_w, conv2_b, down_w, down_b, neighbour_face, orientation
):
    tables = (neighbour_face.T, orientation.T)
    plan, (hidden, *strips) = level(
        *tables, None, field, strips_of(field), conv1_w, conv1_b[None], ()
    )
    _, out = level(*tables, plan, hidden, strips, conv2_w, conv2_b[None], (down_w, down_b[None]))
    return tuple(out)


def solution(mesh):
    groups = mesh.shape["face"]
    fast = mesh.shape["row"] == 4 and mesh.shape["col"] == 2 and groups & (groups - 1) == 0
    return jax.shard_map(
        per_device if fast else general_device,
        mesh=mesh,
        in_specs=(P("face", "row", "col", None), P(), P(), P(), P(), P(), P(), P(), P()),
        out_specs=(P("face", "row", "col", None), P("face", "row", "col", None)),
        check_vma=False,
    )
```
